32 devices in a mesh: seq: 8 (over z, y), tp: 4 (over x, core).
Axes of the slice: x: 2, y: 2, z: 4, core: 2. Of those that a mesh axis runs over, the one named last changes fastest.
Arguments:
- layer_input: bfloat16 [8, 2048, 1024], P('tp', 'seq'), may hold values from -6 to 6
- first_values: bfloat16 [8, 1024, 2048], P(None, 'tp', 'seq'), may hold values from -16 to 16
- doc_lengths: int32 [8, 16], replicated, may hold values from 1 to 1024, 2048 in all within a row
- attn_gain: bfloat16 [1024], replicated, may hold values from 0.25 to 1.75
- query_weight: bfloat16 [1024, 1024], P('tp'), may hold values from -0.1875 to 0.1875
- key_weight: bfloat16 [1024, 1024], P('tp'), may hold values from -0.1875 to 0.1875
- value_weight: bfloat16 [1024, 1024], P('tp'), may hold values from -0.1875 to 0.1875
- output_weight: bfloat16 [1024, 1024], P('tp'), may hold values from -0.75 to 0.75
- feed_gain: bfloat16 [1024], replicated, may hold values from 0.25 to 1.75
- gate_weight: bfloat16 [1024, 2816], P(None, 'tp'), may hold values from -0.1875 to 0.1875
- up_weight: bfloat16 [1024, 2816], P(None, 'tp'), may hold values from -0.1875 to 0.1875
- down_weight: bfloat16 [2816, 1024], P('tp'), may hold values from -0.21875 to 0.21875
- out_cotangent: bfloat16 [8, 2048, 1024], P('tp', 'seq'), may hold values from -6 to 6
Outputs:
- layer_output: bfloat16 [8, 2048, 1024], P('tp', 'seq')
- input_grad: bfloat16 [8, 2048, 1024], P('tp', 'seq')
- first_grad: float32 [8, 1024, 2048], P(None, 'tp', 'seq')
- attn_gain_grad: float32 [1024], replicated
- query_grad: float32 [1024, 1024], P('tp')
- key_grad: float32 [1024, 1024], P('tp')
- value_grad: float32 [1024, 1024], P('tp')
- output_proj_grad: float32 [1024, 1024], P('tp')
- feed_gain_grad: float32 [1024], replicated
- gate_grad: float32 [1024, 2816], P(None, 'tp')
- up_grad: float32 [1024, 2816], P(None, 'tp')
- down_grad: float32 [2816, 1024], P('tp')
- value_norms: float32 [2], replicated
The draws below stay inside these ranges and needn't reach their ends.
Inputs may be any that keep to these rules, and one draw needn't show every extreme that they name: `doc_lengths`: each row's 16 lengths sum to 2048, and its longest document has exactly 1024 tokens.
All inputs are finite; a program needn't handle non-finite values.
Results may differ from the reference program's by a relative error of at most 0.019.
Values may be sent and summed in bfloat16 or wider, within the bound.
A program may use at most 256 MiB of HBM per device.

```python
import functools
import math
import jax
import jax.numpy as jnp
import numpy as np
from jax import lax

D = 1024
H = 16
HD = 64
FF = 2816
ROW = 2048
DOCS = 16
ROWS = 8


def draw_first_values(key, part):
    places = jnp.arange(ROW, dtype=jnp.float32) / (ROW - 1)
    heads_pos = (jnp.arange(H * HD) // HD).astype(jnp.float32) / (H - 1)
    base = jnp.clip(jax.random.normal(key, (ROWS, H * HD, ROW), jnp.float32), -5.0, 5.0)
    scale = (1.0 + 0.75 * places)[None, None, :] * (1.0 + 0.75 * heads_pos)[None, :, None]
    return (base * scale).astype(jnp.bfloat16)


def block_scale(key, extent, split, smallest, high):
    factor_of = 1.0
    for dim, shards_of in split:
        draws = jax.random.uniform(jax.random.fold_in(jax.random.fold_in(key, 6), dim), (shards_of,), jnp.float32, smallest / len(split), high / len(split))
        factor_of = factor_of * jnp.repeat(jnp.exp(draws), extent[dim] // shards_of).reshape((-1,) + (1,) * (len(extent) - 1 - dim))
    return factor_of


def length_profile(number_of, total, bound, slope):
    portions = [(1 << 20) // math.isqrt(rank ** slope) + 1 for rank in range(2, number_of + 1)]
    spare, holding = total - bound - (number_of - 1), [1] * (number_of - 1)
    while spare > 0:
        candidates = [i for i in range(number_of - 1) if holding[i] < bound]
        pool, remaining = sum([portions[i] for i in candidates]), spare
        for i in candidates:
            addition = min(bound - holding[i], max(1, remaining * portions[i] // pool), spare)
            holding[i] = holding[i] + addition
            spare = spare - addition
    return np.array([bound] + holding)


def ragged(key, count, total, bound, skew):
    if count == 2:
        one = jax.random.randint(key, (), max(1, total - bound), min(bound, total - 1) + 1)
        return jnp.stack([one, total - one])
    lengths = jnp.asarray(length_profile(count, total, bound, skew), jnp.int32)
    twos = (count - 1) // 2
    donor, receiver = lengths[1:1 + 2 * twos:2], lengths[2:2 + 2 * twos:2]
    room = jnp.minimum(donor - 1, bound - receiver)
    shifted = jax.random.randint(jax.random.fold_in(key, 1), (twos,), 0, 1 << 20) % (room + 1)
    lengths = lengths.at[1:1 + 2 * twos:2].set(donor - shifted).at[2:2 + 2 * twos:2].set(receiver + shifted)
    return lengths[jax.random.permutation(jax.random.fold_in(key, 2), count)]


def noise(stream_key, extent, deviation, most, shards=(), held_as=jnp.bfloat16):
    loudness = block_scale(stream_key, extent, shards, -0.22, 0.18) if shards else 1.0
    values = jax.random.normal(stream_key, extent, jnp.float32) * deviation * loudness
    return jnp.minimum(jnp.maximum(values, -most), most).astype(held_as)


def setup_inputs(seed: int = 0) -> dict:
    key_of = jax.random.split(jax.random.key(seed), 14)
    return {
        "layer_input": noise(key_of[0], (ROWS, ROW, D), 1.0, 6.0, ((0, 4), (1, 8))),
        "first_values": draw_first_values(jax.random.fold_in(key_of[13], 71), 0),
        "doc_lengths": jax.vmap(lambda own: ragged(own, DOCS, ROW, ROW // 2, 2))(jax.random.split(key_of[2], ROWS)).reshape((ROWS, DOCS)).astype(jnp.int32),
        "attn_gain": jnp.clip(1.0 + 0.15 * jax.random.normal(key_of[3], (D,), jnp.float32), 0.25, 1.75).astype(jnp.bfloat16),
        "query_weight": noise(key_of[4], (H * HD, D), D ** -0.5, 0.1875, ((0, 4),)),
        "key_weight": noise(key_of[5], (H * HD, D), D ** -0.5, 0.1875, ((0, 4),)),
        "value_weight": noise(key_of[6], (H * HD, D), D ** -0.5, 0.1875, ((0, 4),)),
        "output_weight": noise(key_of[7], (H * HD, D), (D // 16) ** -0.5, 0.75, ((0, 4),)),
        "feed_gain": jnp.clip(1.0 + 0.15 * jax.random.normal(key_of[8], (D,), jnp.float32), 0.25, 1.75).astype(jnp.bfloat16),
        "gate_weight": noise(key_of[9], (D, FF), D ** -0.5, 0.1875, ((1, 4),)),
        "up_weight": noise(key_of[10], (D, FF), D ** -0.5, 0.1875, ((1, 4),)),
        "down_weight": noise(key_of[11], (FF, D), (FF // 4) ** -0.5, 0.21875, ((0, 4),)),
        "out_cotangent": noise(key_of[12], (ROWS, ROW, D), 1.0, 6.0, ((0, 4), (1, 8))),
    }


@jax.custom_vjp
def low(v):
    return lax.optimization_barrier(v.astype(jnp.bfloat16)).astype(jnp.float32)

@jax.custom_vjp
def low_back(v):
    return v

def low_keep(v):
    return (low(v), None)

def low_pass(kept, grad):
    return (grad,)

def back_keep(v):
    return (v, None)

def back_low(kept, grad):
    return (low(grad),)
low.defvjp(low_keep, low_pass)
low_back.defvjp(back_keep, back_low)
norm_eps = 1e-06
rope_base = 10000.0
masked_score = -1e+30

def project(values_in, weight):
    return jnp.einsum('rtd,de->rte', values_in, weight, precision=lax.Precision.HIGHEST)

def project_rows(values_in, weight):
    return jnp.einsum('rtd,ed->rte', values_in, weight, precision=lax.Precision.HIGHEST)

def rms_scale(values_in, gain):
    inverse = lax.rsqrt(lax.optimization_barrier(jnp.mean(values_in * values_in, axis=-1, keepdims=True)) + norm_eps)
    return values_in * inverse * gain

def doc_layout(doc_lengths):
    doc_ends = jnp.cumsum(doc_lengths, axis=-1).astype(jnp.int32)
    places = jnp.arange(ROW, dtype=jnp.int32)
    passed = doc_ends[:, None, :] <= places[None, :, None]
    segment = lax.optimization_barrier(jnp.sum(passed.astype(jnp.int32), axis=-1)).astype(jnp.int32)
    starts = lax.optimization_barrier(jnp.max(jnp.where(passed, doc_ends[:, None, :], 0), axis=-1)).astype(jnp.int32)
    return (segment, (places[None, :] - starts).astype(jnp.int32))

def rotate(values_in, offsets):
    half_dim = HD // 2
    frequency = rope_base ** (-jnp.arange(half_dim, dtype=jnp.float32) * 2.0 / HD)
    angles = offsets.astype(jnp.float32)[..., None] * frequency
    cosine = jnp.cos(angles)[..., None, :]
    sine_part = jnp.sin(angles)[..., None, :]
    first_half = values_in[..., :half_dim]
    second_half = values_in[..., half_dim:]
    return jnp.concatenate([first_half * cosine - second_half * sine_part, second_half * cosine + first_half * sine_part], axis=-1)

def attend_row(pieces):
    queries, keys_in, values_in, segment = pieces
    scores = low_back(jnp.einsum('qhd,khd->hqk', queries, keys_in, precision=lax.Precision.HIGHEST) * HD ** (-0.5))
    places = jnp.arange(ROW, dtype=jnp.int32)
    allowed = (segment[:, None] == segment[None, :]) & (places[None, :] <= places[:, None])
    scores = jnp.where(allowed[None], scores, masked_score)
    highest = lax.optimization_barrier(jnp.max(scores, axis=-1, keepdims=True))
    weights = jnp.exp(scores - highest)
    softmax_out = low(weights / lax.optimization_barrier(jnp.sum(weights, axis=-1, keepdims=True)))
    return jnp.einsum('hqk,khd->qhd', softmax_out, values_in, precision=lax.Precision.HIGHEST)

def forward(layer_input, first_values, attn_gain, query_weight, key_weight, value_weight, output_weight, feed_gain, gate_weight, up_weight, down_weight, segment=None, offsets=None):
    row_count = layer_input.shape[0]
    first_rows = jnp.swapaxes(first_values, 1, 2)
    normed = low(rms_scale(layer_input, attn_gain))
    queries = low_back(project_rows(normed, query_weight)).reshape(row_count, ROW, H, HD)
    keys_in = low_back(project_rows(normed, key_weight)).reshape(row_count, ROW, H, HD)
    own_values = low_back(project_rows(normed, value_weight))
    queries = low(rotate(queries, offsets))
    keys_in = low(rotate(keys_in, offsets))
    mixed = low(0.5 * own_values + 0.5 * first_rows).reshape(row_count, ROW, H, HD)
    attended = lax.map(jax.checkpoint(attend_row), (queries, keys_in, mixed, segment))
    attended = low(low_back(attended.reshape(row_count, ROW, H * HD)))
    middle = layer_input + low_back(project(attended, output_weight))
    feed_in = low(rms_scale(middle, feed_gain))
    gate = low_back(project(feed_in, gate_weight))
    up_part = low_back(project(feed_in, up_weight))
    hidden = low(gate * jax.nn.sigmoid(gate) * up_part)
    result = middle + low_back(project(hidden, down_weight))
    return (result, mixed)

def reference(layer_input, first_values, doc_lengths, attn_gain, query_weight, key_weight, value_weight, output_weight, feed_gain, gate_weight, up_weight, down_weight, out_cotangent):
    segment, offsets = doc_layout(doc_lengths)
    floats = [array_in.astype(jnp.float32) for array_in in (layer_input, first_values, attn_gain, query_weight, key_weight, value_weight, output_weight, feed_gain, gate_weight, up_weight, down_weight)]
    result, pullback, mixed = jax.vjp(functools.partial(forward, segment=segment, offsets=offsets), *floats, has_aux=True)
    grads = pullback(out_cotangent.astype(jnp.float32))
    first_sq = jnp.sum(floats[1] * floats[1])
    mixed_sq = jnp.sum(mixed * mixed)
    value_norms = jnp.sqrt(jnp.stack([first_sq, mixed_sq]))
    return (result.astype(jnp.bfloat16), grads[0].astype(jnp.bfloat16), grads[1], grads[2], grads[3], grads[4], grads[5], grads[6], grads[7], grads[8], grads[9], grads[10], value_norms)
```

```python
import functools
import math

import jax
import jax.numpy as jnp
from jax import lax
from jax.experimental import pallas as pl
from jax.experimental.pallas import tpu as pltpu
from jax.sharding import PartitionSpec as P

HD = 64
ROW = 2048
BLOCK = 256
LOG2E = math.log2(math.e)
LN2 = math.log(2.0)
MESH = pl.DeviceIdType.MESH


norm_eps = 1e-06
rope_base = 10000.0
masked_score = -1e30


def doc_layout(doc_lengths):
    doc_ends = jnp.cumsum(doc_lengths, axis=-1)
    places = jnp.arange(ROW, dtype=jnp.int32)
    passed = doc_ends[:, None, :] <= places[None, :, None]
    segment = jnp.sum(passed.astype(jnp.int32), axis=-1)
    starts = jnp.max(jnp.where(passed, doc_ends[:, None, :], 0), axis=-1)
    return (segment, places[None, :] - starts)


def rotary_tables(offsets):
    half_dim = HD // 2
    frequency = rope_base ** (-jnp.arange(half_dim, dtype=jnp.float32) * 2.0 / HD)
    angles = offsets.astype(jnp.float32)[..., None] * frequency
    return (jnp.cos(angles)[..., None, :], jnp.sin(angles)[..., None, :])


def rotate(values_in, tables):
    cosine, sine_part = tables
    half_dim = HD // 2
    first_half = values_in[..., :half_dim]
    second_half = values_in[..., half_dim:]
    return jnp.concatenate(
        [
            first_half * cosine - second_half * sine_part,
            second_half * cosine + first_half * sine_part,
        ],
        axis=-1,
    )


def unrotate(grads_in, tables):
    cosine, sine_part = tables
    half_dim = HD // 2
    first_half = grads_in[..., :half_dim]
    second_half = grads_in[..., half_dim:]
    return jnp.concatenate(
        [
            first_half * cosine + second_half * sine_part,
            second_half * cosine - first_half * sine_part,
        ],
        axis=-1,
    )


def norm_rows(values_in):
    inverse = lax.rsqrt(jnp.mean(values_in * values_in, axis=-1, keepdims=True) + norm_eps)
    return (values_in * inverse, inverse)


def norm_back(grads_in, unit_rows, inverse, gain):
    scaled = grads_in * gain
    extra = inverse * (scaled - unit_rows * jnp.mean(scaled * unit_rows, axis=-1, keepdims=True))
    return (extra, jnp.sum(grads_in * unit_rows, axis=(0, 1)))


def rows_dot(left, right):
    return lax.dot_general(left, right, (((1,), (1,)), ((), ())), preferred_element_type=jnp.float32)


def plain_dot(left, right):
    return lax.dot_general(left, right, (((1,), (0,)), ((), ())), preferred_element_type=jnp.float32)


def head_masked(block, head, heads):
    if heads == 1:
        return block
    lanes = lax.broadcasted_iota(jnp.int32, block.shape, 1)
    return jnp.where(lanes // HD == head, block, jnp.zeros_like(block))


def attend_kernel(low_ref, q_ref, k_ref, v_ref, start_ref, o_ref, lse_ref, v_cols):
    row = pl.program_id(0)
    length, lanes = q_ref.shape[1:]
    heads = lanes // HD
    blocks = length // BLOCK
    for j in range(blocks):
        v_cols[:, j * BLOCK : (j + 1) * BLOCK] = v_ref[0, j * BLOCK : (j + 1) * BLOCK, :].T

    def query_block(i, carry):
        first = pl.multiple_of(i * BLOCK, BLOCK)
        q_block = q_ref[0, pl.ds(first, BLOCK), :]
        q_heads = [head_masked(q_block, h, heads) for h in range(heads)]
        start = start_ref[0, :, pl.ds(first, BLOCK)]
        places = first + lax.broadcasted_iota(jnp.int32, (1, BLOCK), 1)

        def key_block(j, state):
            at = pl.multiple_of(j * BLOCK, BLOCK)
            k_block = k_ref[0, pl.ds(at, BLOCK), :]
            keys = at + lax.broadcasted_iota(jnp.int32, (BLOCK, BLOCK), 0)
            allowed = (keys >= start) & (keys <= places)
            out = []
            for h in range(heads):
                top, total, acc = state[h]
                scores = jnp.where(allowed, rows_dot(k_block, q_heads[h]), masked_score)
                new_top = jnp.maximum(top, jnp.max(scores, axis=0, keepdims=True))
                weights = jnp.exp2(scores - new_top)
                shrink = jnp.exp2(top - new_top)
                total = total * shrink + jnp.sum(weights, axis=0, keepdims=True)
                acc = acc * shrink + plain_dot(
                    v_cols[h * HD : (h + 1) * HD, pl.ds(at, BLOCK)], weights.astype(jnp.bfloat16)
                )
                out.append((new_top, total, acc))
            return tuple(out)

        begin = tuple(
            (
                jnp.full((1, BLOCK), masked_score, jnp.float32),
                jnp.zeros((1, BLOCK), jnp.float32),
                jnp.zeros((HD, BLOCK), jnp.float32),
            )
            for _ in range(heads)
        )
        state = key_block(i, begin)
        state = lax.fori_loop(low_ref[row * blocks + i], i, key_block, state)
        columns = jnp.concatenate([acc / total for _, total, acc in state], axis=0)
        o_ref[0, pl.ds(first, BLOCK), :] = columns.T.astype(jnp.bfloat16)
        for h in range(heads):
            top, total, _ = state[h]
            lse_ref[0, 0, pl.ds(h, 1), pl.ds(first, BLOCK)] = top + jnp.log2(total)
        return carry

    lax.fori_loop(0, blocks, query_block, 0)


def attend(low, queries, keys, values, starts):
    rows, length, width = queries.shape
    lanes = min(width, 128)
    groups = width // lanes
    heads = lanes // HD
    wide = pl.BlockSpec((1, length, lanes), lambda r, g, low: (r, 0, g))
    return pl.pallas_call(
        attend_kernel,
        grid_spec=pltpu.PrefetchScalarGridSpec(
            num_scalar_prefetch=1,
            grid=(rows, groups),
            in_specs=[wide, wide, wide, pl.BlockSpec((1, 1, length), lambda r, g, low: (r, 0, 0))],
            out_specs=[
                wide,
                pl.BlockSpec((1, 1, heads, length), lambda r, g, low: (r, g, 0, 0)),
            ],
            scratch_shapes=[pltpu.VMEM((lanes, length), jnp.bfloat16)],
        ),
        out_shape=[
            jax.ShapeDtypeStruct(queries.shape, jnp.bfloat16),
            jax.ShapeDtypeStruct((rows, groups, heads, length), jnp.float32),
        ],
        name="attend",
    )(low, queries, keys, values, starts)


def attend_back_kernel(
    low_ref, q_ref, k_ref, v_ref, o_ref, g_ref, lse_ref, start_ref,
    qg_ref, kg_ref, vg_ref, k_cols, k_acc, v_acc,
):
    row = pl.program_id(0)
    length, lanes = q_ref.shape[1:]
    heads = lanes // HD
    blocks = length // BLOCK
    for j in range(blocks):
        k_cols[:, j * BLOCK : (j + 1) * BLOCK] = k_ref[0, j * BLOCK : (j + 1) * BLOCK, :].T
    k_acc[...] = jnp.zeros_like(k_acc)
    v_acc[...] = jnp.zeros_like(v_acc)
    select = (
        lax.broadcasted_iota(jnp.int32, (8, lanes), 1) // HD
        == lax.broadcasted_iota(jnp.int32, (8, lanes), 0)
    ).astype(jnp.float32)

    def query_block(i, carry):
        first = pl.multiple_of(i * BLOCK, BLOCK)
        q_block = q_ref[0, pl.ds(first, BLOCK), :]
        g_block = g_ref[0, pl.ds(first, BLOCK), :]
        q_heads = [head_masked(q_block, h, heads) for h in range(heads)]
        g_heads = [head_masked(g_block, h, heads) for h in range(heads)]
        product = g_block.astype(jnp.float32) * o_ref[0, pl.ds(first, BLOCK), :].astype(jnp.float32)
        centre = lax.dot_general(
            select, product, (((1,), (1,)), ((), ())),
            precision=lax.Precision.HIGHEST, preferred_element_type=jnp.float32,
        )
        lse = lse_ref[0, 0, :, pl.ds(first, BLOCK)]
        start = start_ref[0, :, pl.ds(first, BLOCK)]
        places = first + lax.broadcasted_iota(jnp.int32, (1, BLOCK), 1)

        def key_block(j, state):
            at = pl.multiple_of(j * BLOCK, BLOCK)
            k_block = k_ref[0, pl.ds(at, BLOCK), :]
            v_block = v_ref[0, pl.ds(at, BLOCK), :]
            keys = at + lax.broadcasted_iota(jnp.int32, (BLOCK, BLOCK), 0)
            allowed = (keys >= start) & (keys <= places)
            k_add = jnp.zeros((BLOCK, lanes), jnp.float32)
            v_add = jnp.zeros((BLOCK, lanes), jnp.float32)
            out = []
            for h in range(heads):
                scores = jnp.where(allowed, rows_dot(k_block, q_heads[h]), masked_score)
                probs = jnp.exp2(scores - lse[h : h + 1, :])
                prob_g = rows_dot(v_block, g_heads[h])
                score_g = (probs * (prob_g - centre[h : h + 1, :])).astype(jnp.bfloat16)
                v_add = v_add + plain_dot(probs.astype(jnp.bfloat16), g_heads[h])
                k_add = k_add + plain_dot(score_g, q_heads[h])
                out.append(
                    state[h] + plain_dot(k_cols[h * HD : (h + 1) * HD, pl.ds(at, BLOCK)], score_g)
                )
            k_acc[pl.ds(at, BLOCK), :] += k_add
            v_acc[pl.ds(at, BLOCK), :] += v_add
            return tuple(out)

        begin = tuple(jnp.zeros((HD, BLOCK), jnp.float32) for _ in range(heads))
        state = lax.fori_loop(low_ref[row * blocks + i], i + 1, key_block, begin)
        columns = jnp.concatenate(state, axis=0) * HD ** (-0.5)
        qg_ref[0, pl.ds(first, BLOCK), :] = columns.T.astype(jnp.bfloat16)
        return carry

    lax.fori_loop(0, blocks, query_block, 0)
    kg_ref[0] = (k_acc[...] * LN2).astype(jnp.bfloat16)
    vg_ref[0] = v_acc[...].astype(jnp.bfloat16)


def attend_back(low, queries, keys, values, attended, grads, lse, starts):
    rows, length, width = queries.shape
    lanes = min(width, 128)
    groups = width // lanes
    heads = lanes // HD
    wide = pl.BlockSpec((1, length, lanes), lambda r, g, low: (r, 0, g))
    return pl.pallas_call(
        attend_back_kernel,
        grid_spec=pltpu.PrefetchScalarGridSpec(
            num_scalar_prefetch=1,
            grid=(rows, groups),
            in_specs=[wide] * 5
            + [
                pl.BlockSpec((1, 1, heads, length), lambda r, g, low: (r, g, 0, 0)),
                pl.BlockSpec((1, 1, length), lambda r, g, low: (r, 0, 0)),
            ],
            out_specs=[wide] * 3,
            scratch_shapes=[
                pltpu.VMEM((lanes, length), jnp.bfloat16),
                pltpu.VMEM((length, lanes), jnp.float32),
                pltpu.VMEM((length, lanes), jnp.float32),
            ],
        ),
        out_shape=[jax.ShapeDtypeStruct(queries.shape, jnp.bfloat16)] * 3,
        name="attend_back",
    )(low, queries, keys, values, attended, grads, lse, starts)


def exchange(arrays, out_shapes, plan, number):
    count = len(arrays)

    def kernel(*refs):
        sources, targets = refs[:count], refs[count : 2 * count]
        local_sem, send_sem, receive_sem = refs[2 * count :]
        me = (lax.axis_index("seq"), lax.axis_index("tp"))
        sends, receives = plan(*me)
        barrier = pltpu.get_barrier_semaphore()

        def is_me(place):
            return (place[0] == me[0]) & (place[1] == me[1])

        for origin, _, _ in receives:
            @pl.when(jnp.logical_not(is_me(origin)))
            def _():
                pl.semaphore_signal(barrier, inc=1, device_id=origin, device_id_type=MESH)
        others = sum(jnp.where(is_me(destination), 0, 1) for destination, _, _, _ in sends)
        pl.semaphore_wait(barrier, others)

        def remote(a, n, destination, source, target, at):
            return pltpu.make_async_remote_copy(
                src_ref=sources[a].at[source],
                dst_ref=targets[a].at[target],
                send_sem=send_sem.at[n * count + a],
                recv_sem=receive_sem.at[at * count + a],
                device_id=destination,
                device_id_type=MESH,
            )

        def local(a, n, source, target):
            return pltpu.make_async_copy(
                sources[a].at[source], targets[a].at[target], local_sem.at[n * count + a]
            )

        for wait in (False, True):
            for n, (destination, source, target, at) in enumerate(sends):
                for a in range(count):
                    @pl.when(is_me(destination))
                    def _():
                        copy = local(a, n, source, target)
                        copy.wait() if wait else copy.start()

                    @pl.when(jnp.logical_not(is_me(destination)))
                    def _():
                        copy = remote(a, n, destination, source, target, at)
                        copy.wait_send() if wait else copy.start()
        for origin, target, at in receives:
            for a in range(count):
                @pl.when(jnp.logical_not(is_me(origin)))
                def _():
                    pltpu.make_async_remote_copy(
                        src_ref=targets[a].at[target],
                        dst_ref=targets[a].at[target],
                        send_sem=send_sem.at[0],
                        recv_sem=receive_sem.at[at * count + a],
                        device_id=origin,
                        device_id_type=MESH,
                    ).wait_recv()

    total = len(plan(0, 0)[0]) * count
    return pl.pallas_call(
        kernel,
        out_shape=[jax.ShapeDtypeStruct(shape, jnp.bfloat16) for shape in out_shapes],
        in_specs=[pl.BlockSpec(memory_space=pl.ANY)] * count,
        out_specs=[pl.BlockSpec(memory_space=pl.ANY)] * count,
        scratch_shapes=[
            pltpu.SemaphoreType.DMA((total,)),
            pltpu.SemaphoreType.DMA((total,)),
            pltpu.SemaphoreType.DMA((total,)),
        ],
        compiler_params=pltpu.CompilerParams(collective_id=number, has_side_effects=True),
        name=f"exchange_{number}",
    )(*arrays)


def places_to_rows(seq_size, rows_each):
    def plan(s, t):
        sends, receives = [], []
        for i in range(seq_size):
            other = lax.rem(s + i, seq_size)
            sends.append(((other, t), (pl.ds(other * rows_each, rows_each),), (slice(None), s), s))
            origin = lax.rem(s + seq_size - i, seq_size)
            receives.append(((origin, t), (slice(None), origin), origin))
        return sends, receives

    return plan


def rows_to_places(seq_size, rows_each):
    def plan(s, t):
        sends, receives = [], []
        for i in range(seq_size):
            other = lax.rem(s + i, seq_size)
            sends.append(((other, t), (slice(None), other), (pl.ds(s * rows_each, rows_each),), s))
            origin = lax.rem(s + seq_size - i, seq_size)
            receives.append(((origin, t), (pl.ds(origin * rows_each, rows_each),), origin))
        return sends, receives

    return plan


def heads_to_owner(seq_size, tp_size, rows_each, rows_local):
    def plan(s, t):
        sends, receives = [], []
        for i in range(seq_size):
            other = lax.rem(s + i, seq_size)
            for j in range(rows_each):
                row = s * rows_each + j
                slot = lax.rem(row, rows_local)
                sends.append(((other, row // rows_local), (j, other), (t, slot), t * rows_local + slot))
        for i in range(tp_size):
            for slot in range(rows_local):
                row = t * rows_local + slot
                receives.append(((row // rows_each, i), (i, slot), i * rows_local + slot))
        return sends, receives

    return plan


def owner_to_heads(seq_size, tp_size, rows_each, rows_local):
    def plan(s, t):
        sends, receives = [], []
        for i in range(tp_size):
            for slot in range(rows_local):
                row = t * rows_local + slot
                j = lax.rem(row, rows_each)
                sends.append(((row // rows_each, i), (i, slot), (j, s), j * seq_size + s))
        for j in range(rows_each):
            row = s * rows_each + j
            for i in range(seq_size):
                receives.append(((i, row // rows_local), (j, i), j * seq_size + i))
        return sends, receives

    return plan


def shards(
    layer_input,
    first_values,
    doc_lengths,
    attn_gain,
    query_weight,
    key_weight,
    value_weight,
    output_weight,
    feed_gain,
    gate_weight,
    up_weight,
    down_weight,
    out_cotangent,
):
    local_len = layer_input.shape[1]
    row_count = first_values.shape[0]
    width_local = query_weight.shape[0]
    head_count = width_local // HD
    _, offsets = doc_layout(doc_lengths)
    begin = lax.axis_index("seq") * local_len
    off_own = lax.dynamic_slice_in_dim(offsets, begin, local_len, 1)
    places_all = jnp.arange(ROW, dtype=jnp.int32)
    tables = rotary_tables(off_own)
    attn_scale = attn_gain.astype(jnp.float32)
    feed_scale = feed_gain.astype(jnp.float32)
    first_rows = jnp.swapaxes(first_values, 1, 2)
    source = layer_input.astype(jnp.float32)
    unit_attn, inv_attn = norm_rows(source)
    normed = (unit_attn * attn_scale).astype(jnp.bfloat16)
    normed_all = lax.all_gather(normed, "tp", axis=0, tiled=True)
    stacked_weights = jnp.concatenate([query_weight, key_weight, value_weight], axis=0)
    projected = jnp.einsum(
        "rtd,ed->rte", normed_all, stacked_weights, preferred_element_type=jnp.float32
    )
    queries = (
        rotate(projected[..., :width_local].reshape(row_count, local_len, head_count, HD), tables)
        * (HD ** (-0.5) * LOG2E)
    ).astype(jnp.bfloat16)
    keys_rot = rotate(
        projected[..., width_local : 2 * width_local].reshape(row_count, local_len, head_count, HD),
        tables,
    ).astype(jnp.bfloat16)
    mixed = (0.5 * projected[..., 2 * width_local :] + 0.5 * first_rows.astype(jnp.float32)).astype(
        jnp.bfloat16
    )
    seq_size = lax.axis_size("seq")
    tp_size = lax.axis_size("tp")
    rows_local = layer_input.shape[0]
    rows_each = row_count // seq_size
    rows_shape = (rows_each, seq_size, local_len, width_local)
    my_rows = lax.axis_index("seq") * rows_each
    starts = lax.dynamic_slice_in_dim(places_all[None, :] - offsets, my_rows, rows_each, 0)
    low = (starts[:, ::BLOCK] // BLOCK).reshape(-1)
    starts = starts[:, None, :]
    queries, keys, values = (
        part.reshape(rows_each, ROW, width_local)
        for part in exchange(
            [
                queries.reshape(row_count, local_len, width_local),
                keys_rot.reshape(row_count, local_len, width_local),
                mixed,
            ],
            [rows_shape] * 3,
            places_to_rows(seq_size, rows_each),
            0,
        )
    )
    result, logsum = attend(low, queries, keys, values, starts)
    (pieces,) = exchange(
        [result.reshape(rows_shape)],
        [(tp_size, rows_local, local_len, width_local)],
        heads_to_owner(seq_size, tp_size, rows_each, rows_local),
        1,
    )
    attended = jnp.transpose(pieces, (1, 2, 0, 3)).reshape(rows_local, local_len, -1)
    output_full = lax.all_gather(output_weight, "tp", axis=0, tiled=True)
    middle = source + jnp.einsum(
        "rte,ed->rtd", attended, output_full, preferred_element_type=jnp.float32
    )
    unit_feed, inv_feed = norm_rows(middle)
    feed_in = (unit_feed * feed_scale).astype(jnp.bfloat16)
    feed_all = lax.all_gather(feed_in, "tp", axis=0, tiled=True)
    gate = jnp.einsum("rtd,df->rtf", feed_all, gate_weight, preferred_element_type=jnp.float32)
    up_part = jnp.einsum("rtd,df->rtf", feed_all, up_weight, preferred_element_type=jnp.float32)
    sigmoid_gate = jax.nn.sigmoid(gate)
    activated = gate * sigmoid_gate
    hidden = (activated * up_part).astype(jnp.bfloat16)
    piece = hidden
    layer_output = (
        middle
        + lax.psum_scatter(
            jnp.einsum(
                "rtf,fd->rtd", piece, down_weight, preferred_element_type=jnp.float32
            ).astype(jnp.bfloat16),
            "tp",
            scatter_dimension=0,
            tiled=True,
        ).astype(jnp.float32)
    ).astype(jnp.bfloat16)
    cotangent = out_cotangent.astype(jnp.float32)
    cot_all = lax.all_gather(out_cotangent, "tp", axis=0, tiled=True)
    down_grad = jnp.einsum("rtf,rtd->fd", hidden, cot_all, preferred_element_type=jnp.float32)
    hidden_g = jnp.einsum("rtd,fd->rtf", cot_all, down_weight, preferred_element_type=jnp.float32)
    gate_g = (hidden_g * up_part * sigmoid_gate * (1.0 + gate * (1.0 - sigmoid_gate))).astype(
        jnp.bfloat16
    )
    up_g = (hidden_g * activated).astype(jnp.bfloat16)
    gate_grad = jnp.einsum("rtd,rtf->df", feed_all, gate_g, preferred_element_type=jnp.float32)
    up_grad = jnp.einsum("rtd,rtf->df", feed_all, up_g, preferred_element_type=jnp.float32)
    feed_in_g = lax.psum_scatter(
        (
            jnp.einsum("rtf,df->rtd", gate_g, gate_weight, preferred_element_type=jnp.float32)
            + jnp.einsum("rtf,df->rtd", up_g, up_weight, preferred_element_type=jnp.float32)
        ).astype(jnp.bfloat16),
        "tp",
        scatter_dimension=0,
        tiled=True,
    ).astype(jnp.float32)
    middle_extra, feed_gain_part = norm_back(feed_in_g, unit_feed, inv_feed, feed_scale)
    middle_g = cotangent + middle_extra
    branch_g = middle_g.astype(jnp.bfloat16)
    output_proj_grad = lax.psum_scatter(
        jnp.einsum("rte,rtd->ed", attended, branch_g, preferred_element_type=jnp.float32).astype(
            jnp.bfloat16
        ),
        "tp",
        scatter_dimension=0,
        tiled=True,
    )
    attended_g = jnp.einsum(
        "rtd,ed->rte", branch_g, output_full, preferred_element_type=jnp.float32
    ).astype(jnp.bfloat16)
    (attended_g,) = exchange(
        [
            jnp.transpose(
                attended_g.reshape(rows_local, local_len, tp_size, width_local), (2, 0, 1, 3)
            )
        ],
        [rows_shape],
        owner_to_heads(seq_size, tp_size, rows_each, rows_local),
        2,
    )
    query_rows, key_rows, value_rows = attend_back(
        low, queries, keys, values, result, attended_g.reshape(result.shape), logsum, starts
    )
    query_own_g, keys_own_g, values_own_g = exchange(
        [query_rows.reshape(rows_shape), key_rows.reshape(rows_shape), value_rows.reshape(rows_shape)],
        [(row_count, local_len, width_local)] * 3,
        rows_to_places(seq_size, rows_each),
        3,
    )
    query_g = query_own_g.astype(jnp.float32).reshape(row_count, local_len, head_count, HD)
    keys_own_g = keys_own_g.astype(jnp.float32)
    values_own_g = values_own_g.astype(jnp.float32)
    first_grad = jnp.swapaxes(0.5 * values_own_g, 1, 2)
    value_low = (0.5 * values_own_g).astype(jnp.bfloat16)
    key_low = (
        unrotate(keys_own_g.reshape(row_count, local_len, head_count, HD), tables)
        .astype(jnp.bfloat16)
        .reshape(row_count, local_len, width_local)
    )
    query_low = (
        unrotate(query_g, tables).astype(jnp.bfloat16).reshape(row_count, local_len, width_local)
    )
    stacked_g = jnp.concatenate([query_low, key_low, value_low], axis=-1)
    stacked_grad = jnp.einsum(
        "rte,rtd->ed", stacked_g, normed_all, preferred_element_type=jnp.float32
    )
    piece = stacked_g
    normed_g = lax.psum_scatter(
        jnp.einsum(
            "rte,ed->rtd", piece, stacked_weights, preferred_element_type=jnp.float32
        ).astype(jnp.bfloat16),
        "tp",
        scatter_dimension=0,
        tiled=True,
    ).astype(jnp.float32)
    input_extra, attn_gain_part = norm_back(normed_g, unit_attn, inv_attn, attn_scale)
    input_grad = (middle_g + input_extra).astype(jnp.bfloat16)
    summed = (
        lax.psum(stacked_grad.astype(jnp.bfloat16), "seq").astype(jnp.float32),
        lax.psum(output_proj_grad.astype(jnp.bfloat16), "seq").astype(jnp.float32),
        lax.psum(gate_grad.astype(jnp.bfloat16), "seq").astype(jnp.float32),
        lax.psum(up_grad.astype(jnp.bfloat16), "seq").astype(jnp.float32),
        lax.psum(down_grad.astype(jnp.bfloat16), "seq").astype(jnp.float32),
    )
    first_float = first_values.astype(jnp.float32)
    mixed_float = mixed.astype(jnp.float32)
    squares = jnp.stack([jnp.sum(first_float * first_float), jnp.sum(mixed_float * mixed_float)])
    small = lax.psum((attn_gain_part, feed_gain_part, squares), ("seq", "tp"))
    stacked_total = summed[0]
    return (
        layer_output,
        input_grad,
        first_grad,
        small[0],
        stacked_total[:width_local],
        stacked_total[width_local : 2 * width_local],
        stacked_total[2 * width_local :],
        summed[1],
        small[1],
        summed[2],
        summed[3],
        summed[4],
        jnp.sqrt(small[2]),
    )


def solution(mesh):
    placed = (
        P("tp", "seq", None),
        P(None, "tp", "seq"),
        P(),
        P(),
        P("tp", None),
        P("tp", None),
        P("tp", None),
        P("tp", None),
        P(),
        P(None, "tp"),
        P(None, "tp"),
        P("tp", None),
        P("tp", "seq", None),
    )
    return jax.shard_map(
        shards,
        mesh=mesh,
        in_specs=placed,
        out_specs=(
            P("tp", "seq", None),
            P("tp", "seq", None),
            P(None, "tp", "seq"),
            P(),
            P("tp", None),
            P("tp", None),
            P("tp", None),
            P("tp", None),
            P(),
            P(None, "tp"),
            P(None, "tp"),
            P("tp", None),
            P(),
        ),
        check_vma=False,
    )
```

```python
import functools
import math

import jax
import jax.numpy as jnp
from jax import lax
from jax.experimental import pallas as pl
from jax.experimental.pallas import tpu as pltpu
from jax.sharding import PartitionSpec as P

HD = 64
ROW = 2048
BLOCK = 256
LOG2E = math.log2(math.e)
LN2 = math.log(2.0)
MESH = pl.DeviceIdType.MESH


norm_eps = 1e-06
rope_base = 10000.0
masked_score = -1e30


def doc_layout(doc_lengths):
    doc_ends = jnp.cumsum(doc_lengths, axis=-1)
    places = jnp.arange(ROW, dtype=jnp.int32)
    passed = doc_ends[:, None, :] <= places[None, :, None]
    segment = jnp.sum(passed.astype(jnp.int32), axis=-1)
    starts = jnp.max(jnp.where(passed, doc_ends[:, None, :], 0), axis=-1)
    return (segment, places[None, :] - starts)


def norm_rows(values_in):
    inverse = lax.rsqrt(jnp.mean(values_in * values_in, axis=-1, keepdims=True) + norm_eps)
    return (values_in * inverse, inverse)


def norm_back(grads_in, unit_rows, inverse, gain):
    scaled = grads_in * gain
    extra = inverse * (scaled - unit_rows * jnp.mean(scaled * unit_rows, axis=-1, keepdims=True))
    return (extra, jnp.sum(grads_in * unit_rows, axis=0))


def rows_dot(left, right):
    return lax.dot_general(left, right, (((1,), (1,)), ((), ())), preferred_element_type=jnp.float32)


def plain_dot(left, right):
    return lax.dot_general(left, right, (((1,), (0,)), ((), ())), preferred_element_type=jnp.float32)


def head_masked(block, head, heads):
    if heads == 1:
        return block
    lanes = lax.broadcasted_iota(jnp.int32, block.shape, 1)
    return jnp.where(lanes // HD == head, block, jnp.zeros_like(block))


def attend_kernel(low_ref, q_ref, k_ref, v_ref, start_ref, o_ref, lse_ref, v_cols):
    row = pl.program_id(0)
    length, lanes = q_ref.shape[1:]
    heads = lanes // HD
    blocks = length // BLOCK
    for j in range(blocks):
        v_cols[:, j * BLOCK : (j + 1) * BLOCK] = v_ref[0, j * BLOCK : (j + 1) * BLOCK, :].T

    def query_block(i, carry):
        first = pl.multiple_of(i * BLOCK, BLOCK)
        q_block = q_ref[0, pl.ds(first, BLOCK), :]
        q_heads = [head_masked(q_block, h, heads) for h in range(heads)]
        start = start_ref[0, :, pl.ds(first, BLOCK)]
        places = first + lax.broadcasted_iota(jnp.int32, (1, BLOCK), 1)

        def key_block(j, state):
            at = pl.multiple_of(j * BLOCK, BLOCK)
            k_block = k_ref[0, pl.ds(at, BLOCK), :]
            keys = at + lax.broadcasted_iota(jnp.int32, (BLOCK, BLOCK), 0)
            allowed = (keys >= start) & (keys <= places)
            out = []
            for h in range(heads):
                top, total, acc = state[h]
                scores = jnp.where(allowed, rows_dot(k_block, q_heads[h]), masked_score)
                new_top = jnp.maximum(top, jnp.max(scores, axis=0, keepdims=True))
                weights = jnp.exp2(scores - new_top)
                shrink = jnp.exp2(top - new_top)
                total = total * shrink + jnp.sum(weights, axis=0, keepdims=True)
                acc = acc * shrink + plain_dot(
                    v_cols[h * HD : (h + 1) * HD, pl.ds(at, BLOCK)], weights.astype(jnp.bfloat16)
                )
                out.append((new_top, total, acc))
            return tuple(out)

        begin = tuple(
            (
                jnp.full((1, BLOCK), masked_score, jnp.float32),
                jnp.zeros((1, BLOCK), jnp.float32),
                jnp.zeros((HD, BLOCK), jnp.float32),
            )
            for _ in range(heads)
        )
        state = key_block(i, begin)
        state = lax.fori_loop(low_ref[row * blocks + i], i, key_block, state)
        columns = jnp.concatenate([acc / total for _, total, acc in state], axis=0)
        o_ref[0, pl.ds(first, BLOCK), :] = columns.T.astype(jnp.bfloat16)
        for h in range(heads):
            top, total, _ = state[h]
            lse_ref[0, 0, pl.ds(h, 1), pl.ds(first, BLOCK)] = top + jnp.log2(total)
        return carry

    lax.fori_loop(0, blocks, query_block, 0)


def attend(low, queries, keys, values, starts):
    rows, length, width = queries.shape
    lanes = min(width, 128)
    groups = width // lanes
    heads = lanes // HD
    wide = pl.BlockSpec((1, length, lanes), lambda r, g, low: (r, 0, g))
    return pl.pallas_call(
        attend_kernel,
        grid_spec=pltpu.PrefetchScalarGridSpec(
            num_scalar_prefetch=1,
            grid=(rows, groups),
            in_specs=[wide, wide, wide, pl.BlockSpec((1, 1, length), lambda r, g, low: (r, 0, 0))],
            out_specs=[
                wide,
                pl.BlockSpec((1, 1, heads, length), lambda r, g, low: (r, g, 0, 0)),
            ],
            scratch_shapes=[pltpu.VMEM((lanes, length), jnp.bfloat16)],
        ),
        out_shape=[
            jax.ShapeDtypeStruct(queries.shape, jnp.bfloat16),
            jax.ShapeDtypeStruct((rows, groups, heads, length), jnp.float32),
        ],
        name="attend",
    )(low, queries, keys, values, starts)


def attend_back_kernel(
    low_ref, q_ref, k_ref, v_ref, o_ref, g_ref, lse_ref, start_ref,
    qg_ref, kg_ref, vg_ref, k_cols, k_acc, v_acc,
):
    row = pl.program_id(0)
    length, lanes = q_ref.shape[1:]
    heads = lanes // HD
    blocks = length // BLOCK
    for j in range(blocks):
        k_cols[:, j * BLOCK : (j + 1) * BLOCK] = k_ref[0, j * BLOCK : (j + 1) * BLOCK, :].T
    k_acc[...] = jnp.zeros_like(k_acc)
    v_acc[...] = jnp.zeros_like(v_acc)
    select = (
        lax.broadcasted_iota(jnp.int32, (8, lanes), 1) // HD
        == lax.broadcasted_iota(jnp.int32, (8, lanes), 0)
    ).astype(jnp.float32)

    def query_block(i, carry):
        first = pl.multiple_of(i * BLOCK, BLOCK)
        q_block = q_ref[0, pl.ds(first, BLOCK), :]
        g_block = g_ref[0, pl.ds(first, BLOCK), :]
        q_heads = [head_masked(q_block, h, heads) for h in range(heads)]
        g_heads = [head_masked(g_block, h, heads) for h in range(heads)]
        product = g_block.astype(jnp.float32) * o_ref[0, pl.ds(first, BLOCK), :].astype(jnp.float32)
        centre = lax.dot_general(
            select, product, (((1,), (1,)), ((), ())),
            precision=lax.Precision.HIGHEST, preferred_element_type=jnp.float32,
        )
        lse = lse_ref[0, 0, :, pl.ds(first, BLOCK)]
        start = start_ref[0, :, pl.ds(first, BLOCK)]
        places = first + lax.broadcasted_iota(jnp.int32, (1, BLOCK), 1)

        def key_block(j, state):
            at = pl.multiple_of(j * BLOCK, BLOCK)
            k_block = k_ref[0, pl.ds(at, BLOCK), :]
            v_block = v_ref[0, pl.ds(at, BLOCK), :]
            keys = at + lax.broadcasted_iota(jnp.int32, (BLOCK, BLOCK), 0)
            allowed = (keys >= start) & (keys <= places)
            k_add = jnp.zeros((BLOCK, lanes), jnp.float32)
            v_add = jnp.zeros((BLOCK, lanes), jnp.float32)
            out = []
            for h in range(heads):
                scores = jnp.where(allowed, rows_dot(k_block, q_heads[h]), masked_score)
                probs = jnp.exp2(scores - lse[h : h + 1, :])
                prob_g = rows_dot(v_block, g_heads[h])
                score_g = (probs * (prob_g - centre[h : h + 1, :])).astype(jnp.bfloat16)
                v_add = v_add + plain_dot(probs.astype(jnp.bfloat16), g_heads[h])
                k_add = k_add + plain_dot(score_g, q_heads[h])
                out.append(
                    state[h] + plain_dot(k_cols[h * HD : (h + 1) * HD, pl.ds(at, BLOCK)], score_g)
                )
            k_acc[pl.ds(at, BLOCK), :] += k_add
            v_acc[pl.ds(at, BLOCK), :] += v_add
            return tuple(out)

        begin = tuple(jnp.zeros((HD, BLOCK), jnp.float32) for _ in range(heads))
        state = lax.fori_loop(low_ref[row * blocks + i], i + 1, key_block, begin)
        columns = jnp.concatenate(state, axis=0) * HD ** (-0.5)
        qg_ref[0, pl.ds(first, BLOCK), :] = columns.T.astype(jnp.bfloat16)
        return carry

    lax.fori_loop(0, blocks, query_block, 0)
    kg_ref[0] = (k_acc[...] * LN2).astype(jnp.bfloat16)
    vg_ref[0] = v_acc[...].astype(jnp.bfloat16)


def attend_back(low, queries, keys, values, attended, grads, lse, starts):
    rows, length, width = queries.shape
    lanes = min(width, 128)
    groups = width // lanes
    heads = lanes // HD
    wide = pl.BlockSpec((1, length, lanes), lambda r, g, low: (r, 0, g))
    return pl.pallas_call(
        attend_back_kernel,
        grid_spec=pltpu.PrefetchScalarGridSpec(
            num_scalar_prefetch=1,
            grid=(rows, groups),
            in_specs=[wide] * 5
            + [
                pl.BlockSpec((1, 1, heads, length), lambda r, g, low: (r, g, 0, 0)),
                pl.BlockSpec((1, 1, length), lambda r, g, low: (r, 0, 0)),
            ],
            out_specs=[wide] * 3,
            scratch_shapes=[
                pltpu.VMEM((lanes, length), jnp.bfloat16),
                pltpu.VMEM((length, lanes), jnp.float32),
                pltpu.VMEM((length, lanes), jnp.float32),
            ],
        ),
        out_shape=[jax.ShapeDtypeStruct(queries.shape, jnp.bfloat16)] * 3,
        name="attend_back",
    )(low, queries, keys, values, attended, grads, lse, starts)


def columns_dot(left, right):
    return lax.dot_general(left, right, (((0,), (0,)), ((), ())), preferred_element_type=jnp.float32)


def feed_kernel(
    chunk, feed_ref, cot_ref, gate_w, up_w, down_w,
    feed_g_ref, out_ref, gate_grad_ref, up_grad_ref, down_grad_ref,
    feed_all, part, core_in, pair_in, gate_acc, up_acc, down_acc,
    feed_send, feed_core, feed_pair, relay_send, part_send, part_core, sum_send, sum_pair,
):
    tokens = feed_ref.shape[0]
    chunks = tokens // chunk
    seq = lax.axis_index("seq")
    me = lax.axis_index("tp")
    pairs = lax.axis_size("tp") // 2
    pair, core = me // 2, lax.rem(me, 2)
    other = pair * 2 + 1 - core

    def peer(offset):
        return lax.rem(pair + offset, pairs) * 2 + core

    def copy(source, target, send, receive, to):
        return pltpu.make_async_remote_copy(
            src_ref=source, dst_ref=target, send_sem=send, recv_sem=receive,
            device_id=(seq, to), device_id_type=MESH,
        )

    barrier = pltpu.get_barrier_semaphore()
    for to in [other] + [peer(offset) for offset in range(1, pairs)]:
        pl.semaphore_signal(barrier, inc=1, device_id=(seq, to), device_id_type=MESH)
    pl.semaphore_wait(barrier, pairs)

    def rows(c):
        return pl.ds(pl.multiple_of(c * chunk, chunk), chunk)

    def feed_to_core(c):
        return copy(
            feed_ref.at[rows(c)], feed_all.at[me, rows(c)],
            feed_send.at[c], feed_core.at[c], other,
        )

    def feed_to_pair(offset, c):
        return copy(
            feed_ref.at[rows(c)], feed_all.at[me, rows(c)],
            feed_send.at[offset * chunks + c],
            feed_pair.at[(pairs - offset) * chunks + c], peer(offset),
        )

    def feed_from_pair(offset, c):
        return copy(
            feed_all.at[peer(offset), rows(c)], feed_all.at[peer(offset), rows(c)],
            feed_send.at[0], feed_pair.at[offset * chunks + c], other,
        )

    def relay(offset, c):
        return copy(
            feed_all.at[peer(offset), rows(c)], feed_all.at[peer(offset), rows(c)],
            relay_send.at[offset * chunks + c], feed_core.at[offset * chunks + c], other,
        )

    def part_to_core(offset, c):
        at = lax.rem(pair + offset, pairs) * 2 + 1 - core
        return copy(
            part.at[at, rows(c)], core_in.at[offset, rows(c)],
            part_send.at[offset * chunks + c], part_core.at[offset * chunks + c], other,
        )

    def sum_to_pair(offset, c):
        return copy(
            part.at[peer(offset), rows(c)], pair_in.at[pairs - offset, rows(c)],
            sum_send.at[offset * chunks + c],
            sum_pair.at[(pairs - offset) * chunks + c], peer(offset),
        )

    for c in range(chunks):
        feed_to_core(c).start()
        for offset in range(1, pairs):
            feed_to_pair(offset, c).start()
    feed_all[me] = feed_ref[...]
    gate_acc[...] = jnp.zeros_like(gate_acc)
    up_acc[...] = jnp.zeros_like(up_acc)
    down_acc[...] = jnp.zeros_like(down_acc)

    def step(n, carry):
        which = lax.rem(n, 2)
        c = lax.rem(n // 2, chunks)
        offset = n // (2 * chunks)
        owner = lax.rem(pair + offset, pairs) * 2 + lax.rem(core + which, 2)

        @pl.when((which == 0) & (offset > 0))
        def _():
            feed_from_pair(offset, c).wait_recv()
            relay(offset, c).start()

        @pl.when(which == 1)
        def _():
            relay(offset, c).wait_recv()

        feed = feed_all[owner, rows(c), :]
        cot = cot_ref[owner, rows(c), :]
        gate = plain_dot(feed, gate_w[...])
        up = plain_dot(feed, up_w[...])
        sigmoid = jax.nn.sigmoid(gate)
        activated = gate * sigmoid
        hidden = (activated * up).astype(jnp.bfloat16)
        hidden_g = rows_dot(cot, down_w[...])
        up_g = (hidden_g * activated).astype(jnp.bfloat16)
        gate_g = (hidden_g * up * sigmoid * (1.0 + gate * (1.0 - sigmoid))).astype(jnp.bfloat16)
        part[owner, rows(c), :] = (
            rows_dot(gate_g, gate_w[...]) + rows_dot(up_g, up_w[...])
        ).astype(jnp.bfloat16)

        @pl.when(which == 1)
        def _():
            part_to_core(offset, c).start()

        out_ref[owner, rows(c), :] = plain_dot(hidden, down_w[...]).astype(jnp.bfloat16)
        gate_acc[...] += columns_dot(feed, gate_g)
        up_acc[...] += columns_dot(feed, up_g)
        down_acc[...] += columns_dot(hidden, cot)

        @pl.when((which == 1) & (offset > 0))
        def _():
            part_to_core(offset, c).wait_recv()
            to = peer(offset)
            part[to, rows(c), :] = (
                part[to, rows(c), :].astype(jnp.float32)
                + core_in[offset, rows(c), :].astype(jnp.float32)
            ).astype(jnp.bfloat16)
            sum_to_pair(offset, c).start()

        return carry

    lax.fori_loop(0, 2 * chunks * pairs, step, 0)
    gate_grad_ref[...] = gate_acc[...].astype(jnp.bfloat16)
    up_grad_ref[...] = up_acc[...].astype(jnp.bfloat16)
    down_grad_ref[...] = down_acc[...].astype(jnp.bfloat16)
    for c in range(chunks):
        part_to_core(0, c).wait_recv()
        for offset in range(1, pairs):
            sum_to_pair(offset, c).wait_recv()
        total = part[me, rows(c), :].astype(jnp.float32) + core_in[0, rows(c), :].astype(jnp.float32)
        for offset in range(1, pairs):
            total = total + pair_in[offset, rows(c), :].astype(jnp.float32)
        feed_g_ref[rows(c), :] = total
    for c in range(chunks):
        feed_to_core(c).wait_send()
        part_to_core(0, c).wait_send()
        for offset in range(1, pairs):
            feed_to_pair(offset, c).wait_send()
            relay(offset, c).wait_send()
            part_to_core(offset, c).wait_send()
            sum_to_pair(offset, c).wait_send()


def feed_forward(feed_in, cot_all, gate_weight, up_weight, down_weight):
    tokens, width = feed_in.shape
    tp_size = cot_all.shape[0]
    pairs = tp_size // 2
    chunk = min(tokens, 256)
    chunks = tokens // chunk
    hidden = gate_weight.shape[1]
    whole = pl.BlockSpec(memory_space=pltpu.VMEM)
    dma = pltpu.SemaphoreType.DMA
    return pl.pallas_call(
        functools.partial(feed_kernel, chunk),
        out_shape=[
            jax.ShapeDtypeStruct((tokens, width), jnp.float32),
            jax.ShapeDtypeStruct(cot_all.shape, jnp.bfloat16),
            jax.ShapeDtypeStruct((width, hidden), jnp.bfloat16),
            jax.ShapeDtypeStruct((width, hidden), jnp.bfloat16),
            jax.ShapeDtypeStruct((hidden, width), jnp.bfloat16),
        ],
        in_specs=[whole] * 5,
        out_specs=[whole] * 5,
        scratch_shapes=[
            pltpu.VMEM(cot_all.shape, jnp.bfloat16),
            pltpu.VMEM(cot_all.shape, jnp.bfloat16),
            pltpu.VMEM((pairs, tokens, width), jnp.bfloat16),
            pltpu.VMEM((pairs, tokens, width), jnp.bfloat16),
            pltpu.VMEM((width, hidden), jnp.float32),
            pltpu.VMEM((width, hidden), jnp.float32),
            pltpu.VMEM((hidden, width), jnp.float32),
        ]
        + [dma((pairs * chunks,))] * 8,
        compiler_params=pltpu.CompilerParams(
            collective_id=4, has_side_effects=True, vmem_limit_bytes=67043328
        ),
        name="feed_forward",
    )(feed_in, cot_all, gate_weight, up_weight, down_weight)


def group_of(place, seq_size):
    half = seq_size // 2
    low = place // 2
    return lax.rem(place + low, 2) * half + low


def place_of(group, seq_size):
    half = seq_size // 2
    low = lax.rem(group, half)
    return low * 2 + lax.rem(low + group // half, 2)


def remote(source, target, send, receive, to):
    return pltpu.make_async_remote_copy(
        src_ref=source, dst_ref=target, send_sem=send, recv_sem=receive,
        device_id=to, device_id_type=MESH,
    )


def same(left, right):
    return (left[0] == right[0]) & (left[1] == right[1])


class Exchange:
    def __init__(self, plan, me, source, target, local_sem, send_sem, receive_sem):
        self.me = me
        self.sends, self.receives = plan(*me)
        self.source, self.target = source, target
        self.local_sem, self.send_sem, self.receive_sem = local_sem, send_sem, receive_sem

    def greet(self, barrier):
        for origin, _, _ in self.receives:
            @pl.when(jnp.logical_not(same(origin, self.me)))
            def _():
                pl.semaphore_signal(barrier, inc=1, device_id=origin, device_id_type=MESH)

    def others(self):
        return sum(jnp.where(same(to, self.me), 0, 1) for to, _, _, _ in self.sends)

    def each_send(self, wait):
        for n, (to, source, target, at) in enumerate(self.sends):
            here = same(to, self.me)

            @pl.when(here)
            def _():
                copy = pltpu.make_async_copy(
                    self.source.at[source], self.target.at[target], self.local_sem.at[n]
                )
                copy.wait() if wait else copy.start()

            @pl.when(jnp.logical_not(here))
            def _():
                copy = remote(
                    self.source.at[source], self.target.at[target],
                    self.send_sem.at[n], self.receive_sem.at[at], to,
                )
                copy.wait_send() if wait else copy.start()

    def start(self):
        self.each_send(False)

    def wait_sends(self):
        self.each_send(True)

    def wait_receive(self, origin, target, at):
        @pl.when(jnp.logical_not(same(origin, self.me)))
        def _():
            remote(
                self.target.at[target], self.target.at[target],
                self.send_sem.at[0], self.receive_sem.at[at], origin,
            ).wait_recv()

    def wait_receives(self):
        for receive in self.receives:
            self.wait_receive(*receive)


def exchange(arrays, out_shapes, plans, number):
    count = len(arrays)

    def kernel(*refs):
        me = (lax.axis_index("seq"), lax.axis_index("tp"))
        moves = [
            Exchange(plan, me, refs[n], refs[count + n], *refs[2 * count + 3 * n :][:3])
            for n, plan in enumerate(plans)
        ]
        barrier = pltpu.get_barrier_semaphore()
        for move in moves:
            move.greet(barrier)
        pl.semaphore_wait(barrier, sum(move.others() for move in moves))
        for move in moves:
            move.start()
        for move in moves:
            move.wait_sends()
        for move in moves:
            move.wait_receives()

    semaphores = []
    for plan in plans:
        semaphores += [pltpu.SemaphoreType.DMA((len(plan(0, 0)[0]),))] * 3
    return pl.pallas_call(
        kernel,
        out_shape=[
            jax.ShapeDtypeStruct(shape, array.dtype) for shape, array in zip(out_shapes, arrays)
        ],
        in_specs=[pl.BlockSpec(memory_space=pl.ANY)] * count,
        out_specs=[pl.BlockSpec(memory_space=pl.ANY)] * count,
        scratch_shapes=semaphores,
        compiler_params=pltpu.CompilerParams(collective_id=number, has_side_effects=True),
        name=f"exchange_{number}",
    )(*arrays)


def owner_to_quarter(seq_size, tp_size, rows_each, rows_local, piece_first):
    def plan(s, t):
        sends, receives = [], []
        for slot in range(rows_local):
            row = t * rows_local + slot
            to = place_of(row // rows_each, seq_size)
            j = lax.rem(row, rows_each)
            for i in range(tp_size):
                target = (i, j, s) if piece_first else (j, s, i)
                sends.append(((to, i), (slot, i), target, j * seq_size + s))
        group = group_of(s, seq_size)
        for j in range(rows_each):
            row = group * rows_each + j
            for i in range(seq_size):
                origin = lax.rem(s + i, seq_size)
                target = (t, j, origin) if piece_first else (j, origin, t)
                receives.append(((origin, row // rows_local), target, j * seq_size + origin))
        return sends, receives

    return plan


def quarter_to_owner(seq_size, tp_size, rows_each, rows_local):
    def plan(s, t):
        sends, receives = [], []
        group = group_of(s, seq_size)
        for i in range(seq_size):
            to = lax.rem(s + i, seq_size)
            for j in range(rows_each):
                row = group * rows_each + j
                slot = lax.rem(row, rows_local)
                sends.append(((to, row // rows_local), (j, to), (slot, t), slot * tp_size + t))
        for slot in range(rows_local):
            row = t * rows_local + slot
            for i in range(tp_size):
                receives.append(
                    ((place_of(row // rows_each, seq_size), i), (slot, i), slot * tp_size + i)
                )
        return sends, receives

    return plan


def places_to_rows(seq_size, rows_each):
    def plan(s, t):
        sends, receives = [], []
        for i in range(seq_size):
            to = lax.rem(s + i, seq_size)
            rows = pl.ds(group_of(to, seq_size) * rows_each, rows_each)
            sends.append(((to, t), (rows,), (slice(None), s), s))
            origin = lax.rem(s + seq_size - i, seq_size)
            receives.append(((origin, t), (slice(None), origin), origin))
        return sends, receives

    return plan


def rows_to_places(seq_size, rows_each):
    def plan(s, t):
        sends, receives = [], []
        rows = pl.ds(group_of(s, seq_size) * rows_each, rows_each)
        for i in range(seq_size):
            to = lax.rem(s + i, seq_size)
            sends.append(((to, t), (slice(None), to), (rows,), s))
            origin = lax.rem(s + seq_size - i, seq_size)
            source_rows = pl.ds(group_of(origin, seq_size) * rows_each, rows_each)
            receives.append(((origin, t), (source_rows,), origin))
        return sends, receives

    return plan


def heads_to_tokens(tp_size):
    def plan(s, t):
        sends, receives = [], []
        for i in range(tp_size):
            to = lax.rem(t + i, tp_size)
            sends.append(((s, to), (slice(None), slice(None), to), (t,), t))
            origin = lax.rem(t + tp_size - i, tp_size)
            receives.append(((s, origin), (origin,), origin))
        return sends, receives

    return plan


def tokens_to_heads(tp_size):
    def plan(s, t):
        sends, receives = [], []
        for i in range(tp_size):
            to = lax.rem(t + i, tp_size)
            sends.append(((s, to), (to,), (slice(None), slice(None), t), t))
            origin = lax.rem(t + tp_size - i, tp_size)
            receives.append(((s, origin), (slice(None), slice(None), origin), origin))
        return sends, receives

    return plan


def spread_kernel(
    plans, sizes, x_ref, cot_ref, first_ref, x_out, cot_out, first_out,
    x_local, x_send, x_receive, cot_local, cot_send, cot_receive,
    first_local, first_send, first_receive,
    core_send, core_receive, pair_send, pair_receive, relay_send,
):
    seq_size, tp_size, rows_each, rows_local, parts = sizes
    me = (lax.axis_index("seq"), lax.axis_index("tp"))
    s, t = me
    pairs = tp_size // 2
    pair, core = t // 2, lax.rem(t, 2)
    other = pair * 2 + 1 - core
    each = seq_size // parts

    def peer(offset):
        return lax.rem(pair + offset, pairs) * 2 + core

    x_move = Exchange(plans[0], me, x_ref, x_out, x_local, x_send, x_receive)
    cot_move = Exchange(plans[1], me, cot_ref, cot_out, cot_local, cot_send, cot_receive)
    first_move = Exchange(plans[2], me, first_ref, first_out, first_local, first_send, first_receive)
    moves = (x_move, first_move, cot_move)
    barrier = pltpu.get_barrier_semaphore()
    for move in moves:
        move.greet(barrier)
    for to in [other] + [peer(offset) for offset in range(1, pairs)]:
        pl.semaphore_signal(barrier, inc=1, device_id=(s, to), device_id_type=MESH)
    pl.semaphore_wait(barrier, sum(move.others() for move in moves) + pairs)
    for move in moves:
        move.start()

    def block(out, tensor, piece, part):
        span = pl.ds(part * each, each)
        return out.at[:, span, piece] if tensor == 0 else out.at[piece, :, span]

    def number(tensor, offset, part):
        return (tensor * pairs + offset) * parts + part

    def to_core(out, tensor, part):
        view, at = block(out, tensor, t, part), number(tensor, 0, part)
        return remote(view, view, core_send.at[at], core_receive.at[at], (s, other))

    def to_pair(out, tensor, offset, part):
        view = block(out, tensor, t, part)
        return remote(
            view, view, pair_send.at[number(tensor, offset, part)],
            pair_receive.at[number(tensor, pairs - offset, part)], (s, peer(offset)),
        )

    def from_pair(out, tensor, offset, part):
        view, at = block(out, tensor, peer(offset), part), number(tensor, offset, part)
        return remote(view, view, pair_send.at[at], pair_receive.at[at], (s, peer(offset)))

    def relay(out, tensor, offset, part):
        view, at = block(out, tensor, peer(offset), part), number(tensor, offset, part)
        return remote(view, view, relay_send.at[at], core_receive.at[at], (s, other))

    def from_core(out, tensor, offset, part):
        piece = lax.rem(pair + offset, pairs) * 2 + 1 - core
        view, at = block(out, tensor, piece, part), number(tensor, offset, part)
        return remote(view, view, relay_send.at[at], core_receive.at[at], (s, other))

    def forward(move, out, tensor):
        def receive(n, carry):
            part = lax.rem(s // each + n, parts)
            for j in range(rows_each):
                for i in range(each):
                    origin = part * each + i
                    group = group_of(s, seq_size)
                    owner = (origin, (group * rows_each + j) // rows_local)
                    target = (t, j, origin) if tensor else (j, origin, t)
                    move.wait_receive(owner, target, j * seq_size + origin)
                    slot = lax.rem(group * rows_each + j, rows_local)

                    @pl.when(same(owner, me))
                    def _():
                        pltpu.make_async_copy(
                            move.source.at[slot, t], move.target.at[target],
                            move.local_sem.at[slot * tp_size + t],
                        ).wait()
            to_core(out, tensor, part).start()
            for offset in range(1, pairs):
                to_pair(out, tensor, offset, part).start()
            return carry

        def relays(n, carry):
            part = lax.rem(s // each + n, parts)
            for offset in range(1, pairs):
                from_pair(out, tensor, offset, part).wait_recv()
                relay(out, tensor, offset, part).start()
            return carry

        lax.fori_loop(0, parts, receive, 0)
        lax.fori_loop(0, parts, relays, 0)

    def finish(move, out, tensor):
        def one(part, carry):
            for offset in range(pairs):
                from_core(out, tensor, offset, part).wait_recv()
            to_core(out, tensor, part).wait_send()
            for offset in range(1, pairs):
                to_pair(out, tensor, offset, part).wait_send()
                relay(out, tensor, offset, part).wait_send()
            return carry

        lax.fori_loop(0, parts, one, 0)
        for n, (to, source, target, at) in enumerate(move.sends):
            @pl.when(jnp.logical_not(same(to, me)))
            def _():
                remote(
                    move.source.at[source], move.target.at[target],
                    move.send_sem.at[n], move.receive_sem.at[at], to,
                ).wait_send()

    forward(x_move, x_out, 0)
    forward(cot_move, cot_out, 1)
    finish(x_move, x_out, 0)
    finish(cot_move, cot_out, 1)
    first_move.wait_sends()
    first_move.wait_receives()


def spread(layer_input, cotangent, first_values, sizes):
    seq_size, tp_size, rows_each, rows_local, parts = sizes
    pieces = layer_input.shape[2:]
    plans = (
        owner_to_quarter(seq_size, tp_size, rows_each, rows_local, False),
        owner_to_quarter(seq_size, tp_size, rows_each, rows_local, True),
        places_to_rows(seq_size, rows_each),
    )
    dma = pltpu.SemaphoreType.DMA
    quarter = [
        dma((rows_local * tp_size,)), dma((rows_local * tp_size,)), dma((rows_each * seq_size,)),
    ]
    stage = tp_size // 2 * parts * 2
    return pl.pallas_call(
        functools.partial(spread_kernel, plans, sizes),
        out_shape=[
            jax.ShapeDtypeStruct((rows_each, seq_size, tp_size) + pieces, jnp.bfloat16),
            jax.ShapeDtypeStruct((tp_size, rows_each, seq_size) + pieces, jnp.bfloat16),
            jax.ShapeDtypeStruct((rows_each, seq_size) + first_values.shape[1:], jnp.bfloat16),
        ],
        in_specs=[pl.BlockSpec(memory_space=pl.ANY)] * 3,
        out_specs=[pl.BlockSpec(memory_space=pl.ANY)] * 3,
        scratch_shapes=quarter + quarter + [dma((seq_size,))] * 3 + [dma((stage,))] * 5,
        compiler_params=pltpu.CompilerParams(collective_id=5, has_side_effects=True),
        name="spread",
    )(layer_input, cotangent, first_values)


def widen(table, width):
    return jnp.concatenate([table] * (width // table.shape[1]), axis=1)


def project_kernel(
    x_ref, first_ref, cos_ref, sin_ref, gain_ref, weight_ref, swapped_ref,
    q_ref, k_ref, v_ref, square_ref,
):
    width = q_ref.shape[1]
    x = x_ref[...].astype(jnp.float32)
    inverse = lax.rsqrt(jnp.mean(x * x, axis=-1, keepdims=True) + norm_eps)
    normed = (x * inverse * gain_ref[...]).astype(jnp.bfloat16)
    straight = rows_dot(normed, weight_ref[...])
    swapped = rows_dot(normed, swapped_ref[...])
    cosine, sine = widen(cos_ref[...], width), widen(sin_ref[...], width)
    q_ref[...] = (
        (straight[:, :width] * cosine + swapped[:, :width] * sine) * (HD ** (-0.5) * LOG2E)
    ).astype(jnp.bfloat16)
    k_ref[...] = (
        straight[:, width : 2 * width] * cosine + swapped[:, width:] * sine
    ).astype(jnp.bfloat16)
    first = first_ref[0, 0].astype(jnp.float32)
    mixed = (0.5 * straight[:, 2 * width :] + 0.5 * first.T).astype(jnp.bfloat16)
    v_ref[...] = mixed
    wide = mixed.astype(jnp.float32)

    @pl.when(pl.program_id(0) == 0)
    def _():
        square_ref[...] = jnp.zeros_like(square_ref)

    square_ref[0:1, :] += jnp.sum(first * first, axis=0, keepdims=True)
    square_ref[1:2, : wide.shape[1]] += jnp.sum(wide * wide, axis=0, keepdims=True)


def project(x_rows, first_rows, cosine, sine, gain, weights, swapped):
    tokens, depth = x_rows.shape
    rows_each, seq_size, width, places = first_rows.shape
    lanes = cosine.shape[1]

    def tile(columns):
        return pl.BlockSpec((places, columns), lambda n: (n, 0))

    def fixed(array):
        return pl.BlockSpec(array.shape, lambda n: (0,) * array.ndim)

    square = jax.ShapeDtypeStruct((8, max(width, places)), jnp.float32)
    return pl.pallas_call(
        project_kernel,
        grid=(rows_each * seq_size,),
        in_specs=[
            tile(depth),
            pl.BlockSpec((1, 1, width, places), lambda n: (n // seq_size, n % seq_size, 0, 0)),
            tile(lanes),
            tile(lanes),
            fixed(gain),
            fixed(weights),
            fixed(swapped),
        ],
        out_specs=[tile(width)] * 3 + [fixed(square)],
        out_shape=[jax.ShapeDtypeStruct((tokens, width), jnp.bfloat16)] * 3 + [square],
        compiler_params=pltpu.CompilerParams(vmem_limit_bytes=67043328),
        name="project",
    )(x_rows, first_rows, cosine, sine, gain, weights, swapped)


def project_back_kernel(
    x_ref, q_ref, k_ref, v_ref, cos_ref, sin_ref, gain_ref, weight_ref, turn_ref,
    normed_g_ref, grad_ref, grad_acc,
):
    width = q_ref.shape[1]
    x = x_ref[...].astype(jnp.float32)
    inverse = lax.rsqrt(jnp.mean(x * x, axis=-1, keepdims=True) + norm_eps)
    normed = (x * inverse * gain_ref[...]).astype(jnp.bfloat16)
    cosine, sine = widen(cos_ref[...], width), widen(sin_ref[...], width)

    def unrotate(grad):
        turned = plain_dot(grad, turn_ref[...])
        return (grad.astype(jnp.float32) * cosine + turned * sine).astype(jnp.bfloat16)

    stacked = jnp.concatenate(
        [
            unrotate(q_ref[...]),
            unrotate(k_ref[...]),
            (0.5 * v_ref[...].astype(jnp.float32)).astype(jnp.bfloat16),
        ],
        axis=1,
    )
    normed_g_ref[...] = plain_dot(stacked, weight_ref[...]).astype(jnp.bfloat16).reshape(
        normed_g_ref.shape
    )

    @pl.when(pl.program_id(0) == 0)
    def _():
        grad_acc[...] = jnp.zeros_like(grad_acc)

    grad_acc[...] += columns_dot(stacked, normed)

    @pl.when(pl.program_id(0) == pl.num_programs(0) - 1)
    def _():
        grad_ref[...] = grad_acc[...].astype(jnp.bfloat16)


def project_back(x_rows, query_g, key_g, value_g, cosine, sine, gain, weights, turn, sizes):
    seq_size, tp_size, rows_each, _, _ = sizes
    tokens, depth = x_rows.shape
    places = tokens // (rows_each * seq_size)
    width, lanes = query_g.shape[1], cosine.shape[1]
    piece = places // tp_size

    def tile(columns):
        return pl.BlockSpec((places, columns), lambda n: (n, 0))

    def fixed(array):
        return pl.BlockSpec(array.shape, lambda n: (0,) * array.ndim)

    return pl.pallas_call(
        project_back_kernel,
        grid=(rows_each * seq_size,),
        in_specs=[
            tile(depth), tile(width), tile(width), tile(width), tile(lanes), tile(lanes),
            fixed(gain), fixed(weights), fixed(turn),
        ],
        out_specs=[
            pl.BlockSpec((tp_size, 1, piece, depth), lambda n: (0, n, 0, 0)),
            fixed(weights),
        ],
        out_shape=[
            jax.ShapeDtypeStruct((tp_size, rows_each * seq_size, piece, depth), jnp.bfloat16),
            jax.ShapeDtypeStruct(weights.shape, jnp.bfloat16),
        ],
        scratch_shapes=[pltpu.VMEM(weights.shape, jnp.float32)],
        compiler_params=pltpu.CompilerParams(vmem_limit_bytes=67043328),
        name="project_back",
    )(x_rows, query_g, key_g, value_g, cosine, sine, gain, weights, turn)


def total_kernel(seq_size, tp_size, in_ref, out_ref, held, sums, seq_held, send_sem, tp_sem, seq_sem):
    s, t = lax.axis_index("seq"), lax.axis_index("tp")
    barrier = pltpu.get_barrier_semaphore()
    tp_peers = [lax.rem(t + i, tp_size) for i in range(1, tp_size)]
    seq_peers = [lax.rem(s + i, seq_size) for i in range(1, seq_size)]
    for other in tp_peers:
        pl.semaphore_signal(barrier, inc=1, device_id=(s, other), device_id_type=MESH)
    for other in seq_peers:
        pl.semaphore_signal(barrier, inc=1, device_id=(other, t), device_id_type=MESH)
    pl.semaphore_wait(barrier, tp_size + seq_size - 2)

    def tp_copy(n):
        return remote(
            in_ref, held.at[tp_size - n], send_sem.at[n], tp_sem.at[tp_size - n], (s, tp_peers[n - 1])
        )

    def seq_copy(n):
        return remote(
            sums, seq_held.at[seq_size - n], send_sem.at[tp_size + n],
            seq_sem.at[seq_size - n], (seq_peers[n - 1], t),
        )

    for n in range(1, tp_size):
        tp_copy(n).start()
    for n in range(1, tp_size):
        tp_copy(n).wait()
    held[0] = in_ref[...]
    total = held[lax.rem(tp_size - t, tp_size)]
    for n in range(1, tp_size):
        total = total + held[lax.rem(n + tp_size - t, tp_size)]
    sums[...] = total
    for n in range(1, seq_size):
        seq_copy(n).start()
    seq_held[0] = total
    for n in range(1, seq_size):
        seq_copy(n).wait()
    total = seq_held[lax.rem(seq_size - s, seq_size)]
    for n in range(1, seq_size):
        total = total + seq_held[lax.rem(n + seq_size - s, seq_size)]
    out_ref[...] = total


def total_of(values, seq_size, tp_size):
    whole = pl.BlockSpec(memory_space=pltpu.VMEM)
    dma = pltpu.SemaphoreType.DMA
    return pl.pallas_call(
        functools.partial(total_kernel, seq_size, tp_size),
        out_shape=jax.ShapeDtypeStruct(values.shape, jnp.float32),
        in_specs=[whole],
        out_specs=whole,
        scratch_shapes=[
            pltpu.VMEM((tp_size,) + values.shape, jnp.float32),
            pltpu.VMEM(values.shape, jnp.float32),
            pltpu.VMEM((seq_size,) + values.shape, jnp.float32),
            dma((tp_size + seq_size,)),
            dma((tp_size,)),
            dma((seq_size,)),
        ],
        compiler_params=pltpu.CompilerParams(collective_id=6, has_side_effects=True),
        name="total",
    )(values)


def half_swap(weight):
    parts = weight.reshape(-1, 2, HD // 2, weight.shape[1])
    return jnp.stack([-parts[:, 1], parts[:, 0]], axis=1).reshape(weight.shape)


def shards(
    layer_input,
    first_values,
    doc_lengths,
    attn_gain,
    query_weight,
    key_weight,
    value_weight,
    output_weight,
    feed_gain,
    gate_weight,
    up_weight,
    down_weight,
    out_cotangent,
):
    seq_size = lax.axis_size("seq")
    tp_size = lax.axis_size("tp")
    rows_local, local_len, depth = layer_input.shape
    row_count = first_values.shape[0]
    width = query_weight.shape[0]
    rows_each = row_count // seq_size
    piece = local_len // tp_size
    tokens = rows_each * seq_size * piece
    sizes = (seq_size, tp_size, rows_each, rows_local, 4)
    me = lax.axis_index("tp")
    my_rows = group_of(lax.axis_index("seq"), seq_size) * rows_each

    _, offsets = doc_layout(doc_lengths)
    offsets = lax.dynamic_slice_in_dim(offsets, my_rows, rows_each, 0)
    starts = jnp.arange(ROW, dtype=jnp.int32)[None, :] - offsets
    low = (starts[:, ::BLOCK] // BLOCK).reshape(-1)
    starts = starts[:, None, :]
    lane = jnp.arange(min(width, 128), dtype=jnp.int32)
    frequency = rope_base ** (-(lane % (HD // 2)).astype(jnp.float32) * 2.0 / HD)
    angles = offsets.astype(jnp.float32).reshape(-1, 1) * frequency
    cosine, sine = jnp.cos(angles), jnp.sin(angles)
    attn_scale = attn_gain.astype(jnp.float32)[None, :]
    feed_scale = feed_gain.astype(jnp.float32)[None, :]
    weights = jnp.concatenate([query_weight, key_weight, value_weight], axis=0)
    swapped = jnp.concatenate([half_swap(query_weight), half_swap(key_weight)], axis=0)
    turn = half_swap(jnp.eye(width, dtype=jnp.bfloat16))

    x_rows, cot_all, first_rows = spread(
        layer_input.reshape(rows_local, tp_size, piece, depth),
        out_cotangent.reshape(rows_local, tp_size, piece, depth),
        first_values,
        sizes,
    )
    source = lax.dynamic_index_in_dim(x_rows, me, 2, keepdims=False).reshape(tokens, depth)
    source = source.astype(jnp.float32)
    cotangent = lax.dynamic_index_in_dim(cot_all, me, 0, keepdims=False).reshape(tokens, depth)
    cotangent = cotangent.astype(jnp.float32)
    x_rows = x_rows.reshape(rows_each * ROW, depth)
    queries, keys, values, squares = project(
        x_rows, first_rows, cosine, sine, attn_scale, weights, swapped
    )
    queries, keys, values = (
        part.reshape(rows_each, ROW, width) for part in (queries, keys, values)
    )
    result, logsum = attend(low, queries, keys, values, starts)
    by_piece = (rows_each, seq_size, tp_size, piece, width)
    by_head = (tp_size, rows_each, seq_size, piece, width)
    (pieces,) = exchange([result.reshape(by_piece)], [by_head], [heads_to_tokens(tp_size)], 1)
    attended = jnp.transpose(pieces.reshape(tp_size, tokens, width), (1, 0, 2)).reshape(tokens, -1)
    output_full = lax.all_gather(output_weight, "tp", axis=0, tiled=True)
    attended, output_full = lax.optimization_barrier((attended, output_full))
    middle = source + jnp.dot(attended, output_full, preferred_element_type=jnp.float32)
    unit_feed, inv_feed = norm_rows(middle)
    feed_in = (unit_feed * feed_scale).astype(jnp.bfloat16)
    feed_in_g, out_part, gate_grad, up_grad, down_grad = feed_forward(
        feed_in, cot_all.reshape(tp_size, tokens, depth), gate_weight, up_weight, down_weight
    )
    out_sum = lax.psum_scatter(out_part, "tp", scatter_dimension=0, tiled=False)
    layer_output = (middle + out_sum.astype(jnp.float32)).astype(jnp.bfloat16)
    middle_extra, feed_gain_part = norm_back(feed_in_g, unit_feed, inv_feed, feed_scale)
    middle_g = cotangent + middle_extra
    branch_g = middle_g.astype(jnp.bfloat16)
    attended_g = jnp.einsum(
        "td,ed->te", branch_g, output_full, preferred_element_type=jnp.float32
    ).astype(jnp.bfloat16)
    (attended_g,) = exchange(
        [jnp.transpose(attended_g.reshape(tokens, tp_size, width), (1, 0, 2)).reshape(by_head)],
        [by_piece],
        [tokens_to_heads(tp_size)],
        2,
    )
    query_g, key_g, value_g = attend_back(
        low, queries, keys, values, result, attended_g.reshape(result.shape), logsum, starts
    )
    normed_g, stacked_grad = project_back(
        x_rows,
        query_g.reshape(-1, width),
        key_g.reshape(-1, width),
        value_g.reshape(-1, width),
        cosine,
        sine,
        attn_scale,
        weights,
        turn,
        sizes,
    )
    output_proj_grad = lax.psum_scatter(
        jnp.einsum("te,td->ed", attended, branch_g, preferred_element_type=jnp.float32).astype(
            jnp.bfloat16
        ),
        "tp",
        scatter_dimension=0,
        tiled=True,
    )
    normed_g = lax.psum_scatter(
        normed_g.reshape(tp_size, tokens, depth), "tp", scatter_dimension=0, tiled=False
    ).astype(jnp.float32)
    unit_attn, inv_attn = norm_rows(source)
    input_extra, attn_gain_part = norm_back(normed_g, unit_attn, inv_attn, attn_scale)
    input_grad = (middle_g + input_extra).astype(jnp.bfloat16)
    quarter = (rows_each, seq_size, piece, depth)
    owned = (rows_local, tp_size, piece, depth)
    back = quarter_to_owner(seq_size, tp_size, rows_each, rows_local)
    layer_output, input_grad, value_own_g = exchange(
        [
            layer_output.reshape(quarter),
            input_grad.reshape(quarter),
            value_g.reshape(rows_each, seq_size, local_len, width),
        ],
        [owned, owned, (row_count, local_len, width)],
        [back, back, rows_to_places(seq_size, rows_each)],
        3,
    )
    first_grad = jnp.swapaxes(0.5 * value_own_g.astype(jnp.float32), 1, 2)
    feed_sums = lax.psum((gate_grad, up_grad, down_grad), "seq")
    stacked_grad, output_proj_grad, feed_sums = lax.optimization_barrier(
        (stacked_grad, output_proj_grad, feed_sums)
    )
    stacked_total, output_proj_total = lax.psum((stacked_grad, output_proj_grad), "seq")
    stacked_total = stacked_total.astype(jnp.float32)
    squares = jnp.pad(jnp.sum(squares, axis=1)[:2], (0, 126))
    small = total_of(
        jnp.concatenate([attn_gain_part, feed_gain_part, jnp.pad(squares, (0, 7 * 128))]).reshape(
            -1, 128
        ),
        seq_size,
        tp_size,
    ).reshape(-1)
    return (
        layer_output.reshape(layer_input.shape),
        input_grad.reshape(layer_input.shape),
        first_grad,
        small[:depth],
        stacked_total[:width],
        stacked_total[width : 2 * width],
        stacked_total[2 * width :],
        output_proj_total.astype(jnp.float32),
        small[depth : 2 * depth],
        feed_sums[0].astype(jnp.float32),
        feed_sums[1].astype(jnp.float32),
        feed_sums[2].astype(jnp.float32),
        jnp.sqrt(small[2 * depth : 2 * depth + 2]),
    )


def solution(mesh):
    placed = (
        P("tp", "seq", None),
        P(None, "tp", "seq"),
        P(),
        P(),
        P("tp", None),
        P("tp", None),
        P("tp", None),
        P("tp", None),
        P(),
        P(None, "tp"),
        P(None, "tp"),
        P("tp", None),
        P("tp", "seq", None),
    )
    return jax.shard_map(
        shards,
        mesh=mesh,
        in_specs=placed,
        out_specs=(
            P("tp", "seq", None),
            P("tp", "seq", None),
            P(None, "tp", "seq"),
            P(),
            P("tp", None),
            P("tp", None),
            P("tp", None),
            P("tp", None),
            P(),
            P(None, "tp"),
            P(None, "tp"),
            P("tp", None),
            P(),
        ),
        check_vma=False,
    )
```

```python
import functools
import math

import jax
import jax.numpy as jnp
from jax import lax
from jax.experimental import pallas as pl
from jax.experimental.pallas import tpu as pltpu
from jax.sharding import PartitionSpec as P

HD = 64
ROW = 2048
BLOCK = 256
LOG2E = math.log2(math.e)
LN2 = math.log(2.0)
MESH = pl.DeviceIdType.MESH


norm_eps = 1e-06
rope_base = 10000.0
masked_score = -1e30


def doc_layout(doc_lengths):
    doc_ends = jnp.cumsum(doc_lengths, axis=-1)
    places = jnp.arange(ROW, dtype=jnp.int32)
    passed = doc_ends[:, None, :] <= places[None, :, None]
    segment = jnp.sum(passed.astype(jnp.int32), axis=-1)
    starts = jnp.max(jnp.where(passed, doc_ends[:, None, :], 0), axis=-1)
    return (segment, places[None, :] - starts)


def norm_rows(values_in):
    inverse = lax.rsqrt(jnp.mean(values_in * values_in, axis=-1, keepdims=True) + norm_eps)
    return (values_in * inverse, inverse)


def norm_back(grads_in, unit_rows, inverse, gain):
    scaled = grads_in * gain
    extra = inverse * (scaled - unit_rows * jnp.mean(scaled * unit_rows, axis=-1, keepdims=True))
    return (extra, jnp.sum(grads_in * unit_rows, axis=0))


def rows_dot(left, right):
    return lax.dot_general(left, right, (((1,), (1,)), ((), ())), preferred_element_type=jnp.float32)


def plain_dot(left, right):
    return lax.dot_general(left, right, (((1,), (0,)), ((), ())), preferred_element_type=jnp.float32)


def head_masked(block, head, heads):
    if heads == 1:
        return block
    lanes = lax.broadcasted_iota(jnp.int32, block.shape, 1)
    return jnp.where(lanes // HD == head, block, jnp.zeros_like(block))


def attend_kernel(low_ref, q_ref, k_ref, v_ref, start_ref, o_ref, lse_ref, v_cols):
    row = pl.program_id(0)
    length, lanes = q_ref.shape[1:]
    heads = lanes // HD
    blocks = length // BLOCK
    for j in range(blocks):
        v_cols[:, j * BLOCK : (j + 1) * BLOCK] = v_ref[0, j * BLOCK : (j + 1) * BLOCK, :].T

    def query_block(i, carry):
        first = pl.multiple_of(i * BLOCK, BLOCK)
        q_block = q_ref[0, pl.ds(first, BLOCK), :]
        q_heads = [head_masked(q_block, h, heads) for h in range(heads)]
        start = start_ref[0, :, pl.ds(first, BLOCK)]
        places = first + lax.broadcasted_iota(jnp.int32, (1, BLOCK), 1)

        def key_block(j, state):
            at = pl.multiple_of(j * BLOCK, BLOCK)
            k_block = k_ref[0, pl.ds(at, BLOCK), :]
            keys = at + lax.broadcasted_iota(jnp.int32, (BLOCK, BLOCK), 0)
            allowed = (keys >= start) & (keys <= places)
            out = []
            for h in range(heads):
                top, total, acc = state[h]
                scores = jnp.where(allowed, rows_dot(k_block, q_heads[h]), masked_score)
                new_top = jnp.maximum(top, jnp.max(scores, axis=0, keepdims=True))
                weights = jnp.exp2(scores - new_top)
                shrink = jnp.exp2(top - new_top)
                total = total * shrink + jnp.sum(weights, axis=0, keepdims=True)
                acc = acc * shrink + plain_dot(
                    v_cols[h * HD : (h + 1) * HD, pl.ds(at, BLOCK)], weights.astype(jnp.bfloat16)
                )
                out.append((new_top, total, acc))
            return tuple(out)

        begin = tuple(
            (
                jnp.full((1, BLOCK), masked_score, jnp.float32),
                jnp.zeros((1, BLOCK), jnp.float32),
                jnp.zeros((HD, BLOCK), jnp.float32),
            )
            for _ in range(heads)
        )
        state = key_block(i, begin)
        state = lax.fori_loop(low_ref[row * blocks + i], i, key_block, state)
        columns = jnp.concatenate([acc / total for _, total, acc in state], axis=0)
        o_ref[0, pl.ds(first, BLOCK), :] = columns.T.astype(jnp.bfloat16)
        for h in range(heads):
            top, total, _ = state[h]
            lse_ref[0, 0, pl.ds(h, 1), pl.ds(first, BLOCK)] = top + jnp.log2(total)
        return carry

    lax.fori_loop(0, blocks, query_block, 0)


def attend(low, queries, keys, values, starts):
    rows, length, width = queries.shape
    lanes = min(width, 128)
    groups = width // lanes
    heads = lanes // HD
    wide = pl.BlockSpec((1, length, lanes), lambda r, g, low: (r, 0, g))
    return pl.pallas_call(
        attend_kernel,
        grid_spec=pltpu.PrefetchScalarGridSpec(
            num_scalar_prefetch=1,
            grid=(rows, groups),
            in_specs=[wide, wide, wide, pl.BlockSpec((1, 1, length), lambda r, g, low: (r, 0, 0))],
            out_specs=[
                wide,
                pl.BlockSpec((1, 1, heads, length), lambda r, g, low: (r, g, 0, 0)),
            ],
            scratch_shapes=[pltpu.VMEM((lanes, length), jnp.bfloat16)],
        ),
        out_shape=[
            jax.ShapeDtypeStruct(queries.shape, jnp.bfloat16),
            jax.ShapeDtypeStruct((rows, groups, heads, length), jnp.float32),
        ],
        name="attend",
    )(low, queries, keys, values, starts)


def attend_back_kernel(
    low_ref, q_ref, k_ref, v_ref, o_ref, g_ref, lse_ref, start_ref,
    qg_ref, kg_ref, vg_ref, k_cols, k_acc, v_acc,
):
    row = pl.program_id(0)
    length, lanes = q_ref.shape[1:]
    heads = lanes // HD
    blocks = length // BLOCK
    for j in range(blocks):
        k_cols[:, j * BLOCK : (j + 1) * BLOCK] = k_ref[0, j * BLOCK : (j + 1) * BLOCK, :].T
    k_acc[...] = jnp.zeros_like(k_acc)
    v_acc[...] = jnp.zeros_like(v_acc)
    select = (
        lax.broadcasted_iota(jnp.int32, (8, lanes), 1) // HD
        == lax.broadcasted_iota(jnp.int32, (8, lanes), 0)
    ).astype(jnp.float32)

    def query_block(i, carry):
        first = pl.multiple_of(i * BLOCK, BLOCK)
        q_block = q_ref[0, pl.ds(first, BLOCK), :]
        g_block = g_ref[0, pl.ds(first, BLOCK), :]
        q_heads = [head_masked(q_block, h, heads) for h in range(heads)]
        g_heads = [head_masked(g_block, h, heads) for h in range(heads)]
        product = g_block.astype(jnp.float32) * o_ref[0, pl.ds(first, BLOCK), :].astype(jnp.float32)
        centre = lax.dot_general(
            select, product, (((1,), (1,)), ((), ())),
            precision=lax.Precision.HIGHEST, preferred_element_type=jnp.float32,
        )
        lse = lse_ref[0, 0, :, pl.ds(first, BLOCK)]
        start = start_ref[0, :, pl.ds(first, BLOCK)]
        places = first + lax.broadcasted_iota(jnp.int32, (1, BLOCK), 1)

        def key_block(j, state):
            at = pl.multiple_of(j * BLOCK, BLOCK)
            k_block = k_ref[0, pl.ds(at, BLOCK), :]
            v_block = v_ref[0, pl.ds(at, BLOCK), :]
            keys = at + lax.broadcasted_iota(jnp.int32, (BLOCK, BLOCK), 0)
            allowed = (keys >= start) & (keys <= places)
            k_add = jnp.zeros((BLOCK, lanes), jnp.float32)
            v_add = jnp.zeros((BLOCK, lanes), jnp.float32)
            out = []
            for h in range(heads):
                scores = jnp.where(allowed, rows_dot(k_block, q_heads[h]), masked_score)
                probs = jnp.exp2(scores - lse[h : h + 1, :])
                prob_g = rows_dot(v_block, g_heads[h])
                score_g = (probs * (prob_g - centre[h : h + 1, :])).astype(jnp.bfloat16)
                v_add = v_add + plain_dot(probs.astype(jnp.bfloat16), g_heads[h])
                k_add = k_add + plain_dot(score_g, q_heads[h])
                out.append(
                    state[h] + plain_dot(k_cols[h * HD : (h + 1) * HD, pl.ds(at, BLOCK)], score_g)
                )
            k_acc[pl.ds(at, BLOCK), :] += k_add
            v_acc[pl.ds(at, BLOCK), :] += v_add
            return tuple(out)

        begin = tuple(jnp.zeros((HD, BLOCK), jnp.float32) for _ in range(heads))
        state = lax.fori_loop(low_ref[row * blocks + i], i + 1, key_block, begin)
        columns = jnp.concatenate(state, axis=0) * HD ** (-0.5)
        qg_ref[0, pl.ds(first, BLOCK), :] = columns.T.astype(jnp.bfloat16)
        return carry

    lax.fori_loop(0, blocks, query_block, 0)
    kg_ref[0] = (k_acc[...] * LN2).astype(jnp.bfloat16)
    vg_ref[0] = v_acc[...].astype(jnp.bfloat16)


def attend_back(low, queries, keys, values, attended, grads, lse, starts):
    rows, length, width = queries.shape
    lanes = min(width, 128)
    groups = width // lanes
    heads = lanes // HD
    wide = pl.BlockSpec((1, length, lanes), lambda r, g, low: (r, 0, g))
    return pl.pallas_call(
        attend_back_kernel,
        grid_spec=pltpu.PrefetchScalarGridSpec(
            num_scalar_prefetch=1,
            grid=(rows, groups),
            in_specs=[wide] * 5
            + [
                pl.BlockSpec((1, 1, heads, length), lambda r, g, low: (r, g, 0, 0)),
                pl.BlockSpec((1, 1, length), lambda r, g, low: (r, 0, 0)),
            ],
            out_specs=[wide] * 3,
            scratch_shapes=[
                pltpu.VMEM((lanes, length), jnp.bfloat16),
                pltpu.VMEM((length, lanes), jnp.float32),
                pltpu.VMEM((length, lanes), jnp.float32),
            ],
        ),
        out_shape=[jax.ShapeDtypeStruct(queries.shape, jnp.bfloat16)] * 3,
        name="attend_back",
    )(low, queries, keys, values, attended, grads, lse, starts)


def columns_dot(left, right):
    return lax.dot_general(left, right, (((0,), (0,)), ((), ())), preferred_element_type=jnp.float32)


def feed_kernel(
    chunk, feed_ref, cot_ref, gate_w, up_w, down_w,
    feed_g_ref, out_ref, gate_grad_ref, up_grad_ref, down_grad_ref,
    feed_all, part, core_in, pair_in, gate_acc, up_acc, down_acc,
    feed_send, feed_core, feed_pair, relay_send, part_send, part_core, sum_send, sum_pair,
):
    tokens = feed_ref.shape[0]
    chunks = tokens // chunk
    seq = lax.axis_index("seq")
    me = lax.axis_index("tp")
    pairs = lax.axis_size("tp") // 2
    pair, core = me // 2, lax.rem(me, 2)
    other = pair * 2 + 1 - core

    def peer(offset):
        return lax.rem(pair + offset, pairs) * 2 + core

    def copy(source, target, send, receive, to):
        return pltpu.make_async_remote_copy(
            src_ref=source, dst_ref=target, send_sem=send, recv_sem=receive,
            device_id=(seq, to), device_id_type=MESH,
        )

    barrier = pltpu.get_barrier_semaphore()
    for to in [other] + [peer(offset) for offset in range(1, pairs)]:
        pl.semaphore_signal(barrier, inc=1, device_id=(seq, to), device_id_type=MESH)
    pl.semaphore_wait(barrier, pairs)

    def rows(c):
        return pl.ds(pl.multiple_of(c * chunk, chunk), chunk)

    def feed_to_core(c):
        return copy(
            feed_ref.at[rows(c)], feed_all.at[me, rows(c)],
            feed_send.at[c], feed_core.at[c], other,
        )

    def feed_to_pair(offset, c):
        return copy(
            feed_ref.at[rows(c)], feed_all.at[me, rows(c)],
            feed_send.at[offset * chunks + c],
            feed_pair.at[(pairs - offset) * chunks + c], peer(offset),
        )

    def feed_from_pair(offset, c):
        return copy(
            feed_all.at[peer(offset), rows(c)], feed_all.at[peer(offset), rows(c)],
            feed_send.at[0], feed_pair.at[offset * chunks + c], other,
        )

    def relay(offset, c):
        return copy(
            feed_all.at[peer(offset), rows(c)], feed_all.at[peer(offset), rows(c)],
            relay_send.at[offset * chunks + c], feed_core.at[offset * chunks + c], other,
        )

    def part_to_core(offset, c):
        at = lax.rem(pair + offset, pairs) * 2 + 1 - core
        return copy(
            part.at[at, rows(c)], core_in.at[offset, rows(c)],
            part_send.at[offset * chunks + c], part_core.at[offset * chunks + c], other,
        )

    def sum_to_pair(offset, c):
        return copy(
            part.at[peer(offset), rows(c)], pair_in.at[pairs - offset, rows(c)],
            sum_send.at[offset * chunks + c],
            sum_pair.at[(pairs - offset) * chunks + c], peer(offset),
        )

    for c in range(chunks):
        feed_to_core(c).start()
        for offset in range(1, pairs):
            feed_to_pair(offset, c).start()
    feed_all[me] = feed_ref[...]
    gate_acc[...] = jnp.zeros_like(gate_acc)
    up_acc[...] = jnp.zeros_like(up_acc)
    down_acc[...] = jnp.zeros_like(down_acc)

    def step(n, carry):
        which = lax.rem(n, 2)
        c = lax.rem(n // 2, chunks)
        offset = n // (2 * chunks)
        owner = lax.rem(pair + offset, pairs) * 2 + lax.rem(core + which, 2)

        @pl.when((which == 0) & (offset > 0))
        def _():
            feed_from_pair(offset, c).wait_recv()
            relay(offset, c).start()

        @pl.when(which == 1)
        def _():
            relay(offset, c).wait_recv()

        feed = feed_all[owner, rows(c), :]
        cot = cot_ref[owner, rows(c), :]
        gate = plain_dot(feed, gate_w[...])
        up = plain_dot(feed, up_w[...])
        sigmoid = jax.nn.sigmoid(gate)
        activated = gate * sigmoid
        hidden = (activated * up).astype(jnp.bfloat16)
        hidden_g = rows_dot(cot, down_w[...])
        up_g = (hidden_g * activated).astype(jnp.bfloat16)
        gate_g = (hidden_g * up * sigmoid * (1.0 + gate * (1.0 - sigmoid))).astype(jnp.bfloat16)
        part[owner, rows(c), :] = (
            rows_dot(gate_g, gate_w[...]) + rows_dot(up_g, up_w[...])
        ).astype(jnp.bfloat16)

        @pl.when(which == 1)
        def _():
            part_to_core(offset, c).start()

        out_ref[owner, rows(c), :] = plain_dot(hidden, down_w[...]).astype(jnp.bfloat16)
        gate_acc[...] += columns_dot(feed, gate_g)
        up_acc[...] += columns_dot(feed, up_g)
        down_acc[...] += columns_dot(hidden, cot)

        @pl.when((which == 1) & (offset > 0))
        def _():
            part_to_core(offset, c).wait_recv()
            to = peer(offset)
            part[to, rows(c), :] = (
                part[to, rows(c), :].astype(jnp.float32)
                + core_in[offset, rows(c), :].astype(jnp.float32)
            ).astype(jnp.bfloat16)
            sum_to_pair(offset, c).start()

        return carry

    lax.fori_loop(0, 2 * chunks * pairs, step, 0)
    gate_grad_ref[...] = gate_acc[...].astype(jnp.bfloat16)
    up_grad_ref[...] = up_acc[...].astype(jnp.bfloat16)
    down_grad_ref[...] = down_acc[...].astype(jnp.bfloat16)
    for c in range(chunks):
        part_to_core(0, c).wait_recv()
        for offset in range(1, pairs):
            sum_to_pair(offset, c).wait_recv()
        total = part[me, rows(c), :].astype(jnp.float32) + core_in[0, rows(c), :].astype(jnp.float32)
        for offset in range(1, pairs):
            total = total + pair_in[offset, rows(c), :].astype(jnp.float32)
        feed_g_ref[rows(c), :] = total
    for c in range(chunks):
        feed_to_core(c).wait_send()
        part_to_core(0, c).wait_send()
        for offset in range(1, pairs):
            feed_to_pair(offset, c).wait_send()
            relay(offset, c).wait_send()
            part_to_core(offset, c).wait_send()
            sum_to_pair(offset, c).wait_send()


def feed_forward(feed_in, cot_all, gate_weight, up_weight, down_weight):
    tokens, width = feed_in.shape
    tp_size = cot_all.shape[0]
    pairs = tp_size // 2
    chunk = min(tokens, 256)
    chunks = tokens // chunk
    hidden = gate_weight.shape[1]
    whole = pl.BlockSpec(memory_space=pltpu.VMEM)
    dma = pltpu.SemaphoreType.DMA
    return pl.pallas_call(
        functools.partial(feed_kernel, chunk),
        out_shape=[
            jax.ShapeDtypeStruct((tokens, width), jnp.float32),
            jax.ShapeDtypeStruct(cot_all.shape, jnp.bfloat16),
            jax.ShapeDtypeStruct((width, hidden), jnp.bfloat16),
            jax.ShapeDtypeStruct((width, hidden), jnp.bfloat16),
            jax.ShapeDtypeStruct((hidden, width), jnp.bfloat16),
        ],
        in_specs=[whole] * 5,
        out_specs=[whole] * 5,
        scratch_shapes=[
            pltpu.VMEM(cot_all.shape, jnp.bfloat16),
            pltpu.VMEM(cot_all.shape, jnp.bfloat16),
            pltpu.VMEM((pairs, tokens, width), jnp.bfloat16),
            pltpu.VMEM((pairs, tokens, width), jnp.bfloat16),
            pltpu.VMEM((width, hidden), jnp.float32),
            pltpu.VMEM((width, hidden), jnp.float32),
            pltpu.VMEM((hidden, width), jnp.float32),
        ]
        + [dma((pairs * chunks,))] * 8,
        compiler_params=pltpu.CompilerParams(
            collective_id=4, has_side_effects=True, vmem_limit_bytes=67043328
        ),
        name="feed_forward",
    )(feed_in, cot_all, gate_weight, up_weight, down_weight)


def group_of(place, seq_size):
    half = seq_size // 2
    low = place // 2
    return lax.rem(place + low, 2) * half + low


def place_of(group, seq_size):
    half = seq_size // 2
    low = lax.rem(group, half)
    return low * 2 + lax.rem(low + group // half, 2)


def remote(source, target, send, receive, to):
    return pltpu.make_async_remote_copy(
        src_ref=source, dst_ref=target, send_sem=send, recv_sem=receive,
        device_id=to, device_id_type=MESH,
    )


def same(left, right):
    return (left[0] == right[0]) & (left[1] == right[1])


class Exchange:
    def __init__(self, plan, me, source, target, local_sem, send_sem, receive_sem):
        self.me = me
        self.sends, self.receives = plan(*me)
        self.source, self.target = source, target
        self.local_sem, self.send_sem, self.receive_sem = local_sem, send_sem, receive_sem

    def greet(self, barrier):
        for origin, _, _ in self.receives:
            @pl.when(jnp.logical_not(same(origin, self.me)))
            def _():
                pl.semaphore_signal(barrier, inc=1, device_id=origin, device_id_type=MESH)

    def others(self):
        return sum(jnp.where(same(to, self.me), 0, 1) for to, _, _, _ in self.sends)

    def each_send(self, wait):
        for n, (to, source, target, at) in enumerate(self.sends):
            here = same(to, self.me)

            @pl.when(here)
            def _():
                copy = pltpu.make_async_copy(
                    self.source.at[source], self.target.at[target], self.local_sem.at[n]
                )
                copy.wait() if wait else copy.start()

            @pl.when(jnp.logical_not(here))
            def _():
                copy = remote(
                    self.source.at[source], self.target.at[target],
                    self.send_sem.at[n], self.receive_sem.at[at], to,
                )
                copy.wait_send() if wait else copy.start()

    def start(self):
        self.each_send(False)

    def wait_sends(self):
        self.each_send(True)

    def wait_receive(self, origin, target, at):
        @pl.when(jnp.logical_not(same(origin, self.me)))
        def _():
            remote(
                self.target.at[target], self.target.at[target],
                self.send_sem.at[0], self.receive_sem.at[at], origin,
            ).wait_recv()

    def wait_receives(self):
        for receive in self.receives:
            self.wait_receive(*receive)


def exchange(arrays, out_shapes, plans, number):
    count = len(arrays)

    def kernel(*refs):
        me = (lax.axis_index("seq"), lax.axis_index("tp"))
        moves = [
            Exchange(plan, me, refs[n], refs[count + n], *refs[2 * count + 3 * n :][:3])
            for n, plan in enumerate(plans)
        ]
        barrier = pltpu.get_barrier_semaphore()
        for move in moves:
            move.greet(barrier)
        pl.semaphore_wait(barrier, sum(move.others() for move in moves))
        for move in moves:
            move.start()
        for move in moves:
            move.wait_sends()
        for move in moves:
            move.wait_receives()

    semaphores = []
    for plan in plans:
        semaphores += [pltpu.SemaphoreType.DMA((len(plan(0, 0)[0]),))] * 3
    return pl.pallas_call(
        kernel,
        out_shape=[
            jax.ShapeDtypeStruct(shape, array.dtype) for shape, array in zip(out_shapes, arrays)
        ],
        in_specs=[pl.BlockSpec(memory_space=pl.ANY)] * count,
        out_specs=[pl.BlockSpec(memory_space=pl.ANY)] * count,
        scratch_shapes=semaphores,
        compiler_params=pltpu.CompilerParams(collective_id=number, has_side_effects=True),
        name=f"exchange_{number}",
    )(*arrays)


def owner_to_quarter(seq_size, tp_size, rows_each, rows_local, piece_first):
    def plan(s, t):
        sends, receives = [], []
        for slot in range(rows_local):
            row = t * rows_local + slot
            to = place_of(row // rows_each, seq_size)
            j = lax.rem(row, rows_each)
            for i in range(tp_size):
                target = (i, j, s) if piece_first else (j, s, i)
                sends.append(((to, i), (slot, i), target, j * seq_size + s))
        group = group_of(s, seq_size)
        for j in range(rows_each):
            row = group * rows_each + j
            for i in range(seq_size):
                origin = lax.rem(s + i, seq_size)
                target = (t, j, origin) if piece_first else (j, origin, t)
                receives.append(((origin, row // rows_local), target, j * seq_size + origin))
        return sends, receives

    return plan


def quarter_to_owner(seq_size, tp_size, rows_each, rows_local):
    def plan(s, t):
        sends, receives = [], []
        group = group_of(s, seq_size)
        for i in range(seq_size):
            to = lax.rem(s + i, seq_size)
            for j in range(rows_each):
                row = group * rows_each + j
                slot = lax.rem(row, rows_local)
                sends.append(((to, row // rows_local), (j, to), (slot, t), slot * tp_size + t))
        for slot in range(rows_local):
            row = t * rows_local + slot
            for i in range(tp_size):
                receives.append(
                    ((place_of(row // rows_each, seq_size), i), (slot, i), slot * tp_size + i)
                )
        return sends, receives

    return plan


def places_to_rows(seq_size, rows_each):
    def plan(s, t):
        sends, receives = [], []
        for i in range(seq_size):
            to = lax.rem(s + i, seq_size)
            rows = pl.ds(group_of(to, seq_size) * rows_each, rows_each)
            sends.append(((to, t), (rows,), (slice(None), s), s))
            origin = lax.rem(s + seq_size - i, seq_size)
            receives.append(((origin, t), (slice(None), origin), origin))
        return sends, receives

    return plan


def rows_to_places(seq_size, rows_each):
    def plan(s, t):
        sends, receives = [], []
        rows = pl.ds(group_of(s, seq_size) * rows_each, rows_each)
        for i in range(seq_size):
            to = lax.rem(s + i, seq_size)
            sends.append(((to, t), (slice(None), to), (rows,), s))
            origin = lax.rem(s + seq_size - i, seq_size)
            source_rows = pl.ds(group_of(origin, seq_size) * rows_each, rows_each)
            receives.append(((origin, t), (source_rows,), origin))
        return sends, receives

    return plan


def heads_to_tokens(tp_size):
    def plan(s, t):
        sends, receives = [], []
        for i in range(tp_size):
            to = lax.rem(t + i, tp_size)
            sends.append(((s, to), (slice(None), slice(None), to), (t,), t))
            origin = lax.rem(t + tp_size - i, tp_size)
            receives.append(((s, origin), (origin,), origin))
        return sends, receives

    return plan


def tokens_to_heads(tp_size):
    def plan(s, t):
        sends, receives = [], []
        for i in range(tp_size):
            to = lax.rem(t + i, tp_size)
            sends.append(((s, to), (to,), (slice(None), slice(None), t), t))
            origin = lax.rem(t + tp_size - i, tp_size)
            receives.append(((s, origin), (slice(None), slice(None), origin), origin))
        return sends, receives

    return plan


def spread_kernel(
    plans, sizes, x_ref, cot_ref, first_ref, x_out, cot_out, first_out,
    x_local, x_send, x_receive, cot_local, cot_send, cot_receive,
    first_local, first_send, first_receive,
    core_send, core_receive, pair_send, pair_receive, relay_send,
):
    seq_size, tp_size, rows_each, rows_local, parts = sizes
    me = (lax.axis_index("seq"), lax.axis_index("tp"))
    s, t = me
    pairs = tp_size // 2
    pair, core = t // 2, lax.rem(t, 2)
    other = pair * 2 + 1 - core
    each = seq_size // parts

    def peer(offset):
        return lax.rem(pair + offset, pairs) * 2 + core

    x_move = Exchange(plans[0], me, x_ref, x_out, x_local, x_send, x_receive)
    cot_move = Exchange(plans[1], me, cot_ref, cot_out, cot_local, cot_send, cot_receive)
    first_move = Exchange(plans[2], me, first_ref, first_out, first_local, first_send, first_receive)
    moves = (x_move, first_move, cot_move)
    barrier = pltpu.get_barrier_semaphore()
    for move in moves:
        move.greet(barrier)
    for to in [other] + [peer(offset) for offset in range(1, pairs)]:
        pl.semaphore_signal(barrier, inc=1, device_id=(s, to), device_id_type=MESH)
    pl.semaphore_wait(barrier, sum(move.others() for move in moves) + pairs)
    for move in moves:
        move.start()

    def block(out, tensor, piece, part):
        span = pl.ds(part * each, each)
        return out.at[:, span, piece] if tensor == 0 else out.at[piece, :, span]

    def number(tensor, offset, part):
        return (tensor * pairs + offset) * parts + part

    def to_core(out, tensor, part):
        view, at = block(out, tensor, t, part), number(tensor, 0, part)
        return remote(view, view, core_send.at[at], core_receive.at[at], (s, other))

    def to_pair(out, tensor, offset, part):
        view = block(out, tensor, t, part)
        return remote(
            view, view, pair_send.at[number(tensor, offset, part)],
            pair_receive.at[number(tensor, pairs - offset, part)], (s, peer(offset)),
        )

    def from_pair(out, tensor, offset, part):
        view, at = block(out, tensor, peer(offset), part), number(tensor, offset, part)
        return remote(view, view, pair_send.at[at], pair_receive.at[at], (s, peer(offset)))

    def relay(out, tensor, offset, part):
        view, at = block(out, tensor, peer(offset), part), number(tensor, offset, part)
        return remote(view, view, relay_send.at[at], core_receive.at[at], (s, other))

    def from_core(out, tensor, offset, part):
        piece = lax.rem(pair + offset, pairs) * 2 + 1 - core
        view, at = block(out, tensor, piece, part), number(tensor, offset, part)
        return remote(view, view, relay_send.at[at], core_receive.at[at], (s, other))

    def forward(move, out, tensor):
        def receive(n, carry):
            part = lax.rem(s // each + n, parts)
            for j in range(rows_each):
                for i in range(each):
                    origin = part * each + i
                    group = group_of(s, seq_size)
                    owner = (origin, (group * rows_each + j) // rows_local)
                    target = (t, j, origin) if tensor else (j, origin, t)
                    move.wait_receive(owner, target, j * seq_size + origin)
                    slot = lax.rem(group * rows_each + j, rows_local)

                    @pl.when(same(owner, me))
                    def _():
                        pltpu.make_async_copy(
                            move.source.at[slot, t], move.target.at[target],
                            move.local_sem.at[slot * tp_size + t],
                        ).wait()
            to_core(out, tensor, part).start()
            for offset in range(1, pairs):
                to_pair(out, tensor, offset, part).start()
            return carry

        def relays(n, carry):
            part = lax.rem(s // each + n, parts)
            for offset in range(1, pairs):
                from_pair(out, tensor, offset, part).wait_recv()
                relay(out, tensor, offset, part).start()
            return carry

        lax.fori_loop(0, parts, receive, 0)
        lax.fori_loop(0, parts, relays, 0)

    def finish(move, out, tensor):
        def one(part, carry):
            for offset in range(pairs):
                from_core(out, tensor, offset, part).wait_recv()
            to_core(out, tensor, part).wait_send()
            for offset in range(1, pairs):
                to_pair(out, tensor, offset, part).wait_send()
                relay(out, tensor, offset, part).wait_send()
            return carry

        lax.fori_loop(0, parts, one, 0)
        for n, (to, source, target, at) in enumerate(move.sends):
            @pl.when(jnp.logical_not(same(to, me)))
            def _():
                remote(
                    move.source.at[source], move.target.at[target],
                    move.send_sem.at[n], move.receive_sem.at[at], to,
                ).wait_send()

    forward(x_move, x_out, 0)
    forward(cot_move, cot_out, 1)
    finish(x_move, x_out, 0)
    finish(cot_move, cot_out, 1)
    first_move.wait_sends()
    first_move.wait_receives()


def spread(layer_input, cotangent, first_values, sizes):
    seq_size, tp_size, rows_each, rows_local, parts = sizes
    pieces = layer_input.shape[2:]
    plans = (
        owner_to_quarter(seq_size, tp_size, rows_each, rows_local, False),
        owner_to_quarter(seq_size, tp_size, rows_each, rows_local, True),
        places_to_rows(seq_size, rows_each),
    )
    dma = pltpu.SemaphoreType.DMA
    quarter = [
        dma((rows_local * tp_size,)), dma((rows_local * tp_size,)), dma((rows_each * seq_size,)),
    ]
    stage = tp_size // 2 * parts * 2
    return pl.pallas_call(
        functools.partial(spread_kernel, plans, sizes),
        out_shape=[
            jax.ShapeDtypeStruct((rows_each, seq_size, tp_size) + pieces, jnp.bfloat16),
            jax.ShapeDtypeStruct((tp_size, rows_each, seq_size) + pieces, jnp.bfloat16),
            jax.ShapeDtypeStruct((rows_each, seq_size) + first_values.shape[1:], jnp.bfloat16),
        ],
        in_specs=[pl.BlockSpec(memory_space=pl.ANY)] * 3,
        out_specs=[pl.BlockSpec(memory_space=pl.ANY)] * 3,
        scratch_shapes=quarter + quarter + [dma((seq_size,))] * 3 + [dma((stage,))] * 5,
        compiler_params=pltpu.CompilerParams(collective_id=5, has_side_effects=True),
        name="spread",
    )(layer_input, cotangent, first_values)


def widen(table, width):
    return jnp.concatenate([table] * (width // table.shape[1]), axis=1)


def project_kernel(
    x_ref, first_ref, cos_ref, sin_ref, gain_ref, weight_ref, swapped_ref,
    q_ref, k_ref, v_ref, square_ref,
):
    width = q_ref.shape[1]
    x = x_ref[...].astype(jnp.float32)
    inverse = lax.rsqrt(jnp.mean(x * x, axis=-1, keepdims=True) + norm_eps)
    normed = (x * inverse * gain_ref[...]).astype(jnp.bfloat16)
    straight = rows_dot(normed, weight_ref[...])
    swapped = rows_dot(normed, swapped_ref[...])
    cosine, sine = widen(cos_ref[...], width), widen(sin_ref[...], width)
    q_ref[...] = (
        (straight[:, :width] * cosine + swapped[:, :width] * sine) * (HD ** (-0.5) * LOG2E)
    ).astype(jnp.bfloat16)
    k_ref[...] = (
        straight[:, width : 2 * width] * cosine + swapped[:, width:] * sine
    ).astype(jnp.bfloat16)
    first = first_ref[0, 0].astype(jnp.float32)
    mixed = (0.5 * straight[:, 2 * width :] + 0.5 * first.T).astype(jnp.bfloat16)
    v_ref[...] = mixed
    wide = mixed.astype(jnp.float32)

    @pl.when(pl.program_id(0) == 0)
    def _():
        square_ref[...] = jnp.zeros_like(square_ref)

    square_ref[0:1, :] += jnp.sum(first * first, axis=0, keepdims=True)
    square_ref[1:2, : wide.shape[1]] += jnp.sum(wide * wide, axis=0, keepdims=True)


def project(x_rows, first_rows, cosine, sine, gain, weights, swapped):
    tokens, depth = x_rows.shape
    rows_each, seq_size, width, places = first_rows.shape
    lanes = cosine.shape[1]

    def tile(columns):
        return pl.BlockSpec((places, columns), lambda n: (n, 0))

    def fixed(array):
        return pl.BlockSpec(array.shape, lambda n: (0,) * array.ndim)

    square = jax.ShapeDtypeStruct((8, max(width, places)), jnp.float32)
    return pl.pallas_call(
        project_kernel,
        grid=(rows_each * seq_size,),
        in_specs=[
            tile(depth),
            pl.BlockSpec((1, 1, width, places), lambda n: (n // seq_size, n % seq_size, 0, 0)),
            tile(lanes),
            tile(lanes),
            fixed(gain),
            fixed(weights),
            fixed(swapped),
        ],
        out_specs=[tile(width)] * 3 + [fixed(square)],
        out_shape=[jax.ShapeDtypeStruct((tokens, width), jnp.bfloat16)] * 3 + [square],
        compiler_params=pltpu.CompilerParams(vmem_limit_bytes=67043328),
        name="project",
    )(x_rows, first_rows, cosine, sine, gain, weights, swapped)


def project_back_kernel(
    x_ref, q_ref, k_ref, v_ref, cos_ref, sin_ref, gain_ref, weight_ref, turn_ref,
    normed_g_ref, grad_ref, grad_acc,
):
    width = q_ref.shape[1]
    x = x_ref[...].astype(jnp.float32)
    inverse = lax.rsqrt(jnp.mean(x * x, axis=-1, keepdims=True) + norm_eps)
    normed = (x * inverse * gain_ref[...]).astype(jnp.bfloat16)
    cosine, sine = widen(cos_ref[...], width), widen(sin_ref[...], width)

    def unrotate(grad):
        turned = plain_dot(grad, turn_ref[...])
        return (grad.astype(jnp.float32) * cosine + turned * sine).astype(jnp.bfloat16)

    stacked = jnp.concatenate(
        [
            unrotate(q_ref[...]),
            unrotate(k_ref[...]),
            (0.5 * v_ref[...].astype(jnp.float32)).astype(jnp.bfloat16),
        ],
        axis=1,
    )
    normed_g_ref[...] = plain_dot(stacked, weight_ref[...]).astype(jnp.bfloat16).reshape(
        normed_g_ref.shape
    )

    @pl.when(pl.program_id(0) == 0)
    def _():
        grad_acc[...] = jnp.zeros_like(grad_acc)

    grad_acc[...] += columns_dot(stacked, normed)

    @pl.when(pl.program_id(0) == pl.num_programs(0) - 1)
    def _():
        grad_ref[...] = grad_acc[...].astype(jnp.bfloat16)


def project_back(x_rows, query_g, key_g, value_g, cosine, sine, gain, weights, turn, sizes):
    seq_size, tp_size, rows_each, _, _ = sizes
    tokens, depth = x_rows.shape
    places = tokens // (rows_each * seq_size)
    width, lanes = query_g.shape[1], cosine.shape[1]
    piece = places // tp_size

    def tile(columns):
        return pl.BlockSpec((places, columns), lambda n: (n, 0))

    def fixed(array):
        return pl.BlockSpec(array.shape, lambda n: (0,) * array.ndim)

    return pl.pallas_call(
        project_back_kernel,
        grid=(rows_each * seq_size,),
        in_specs=[
            tile(depth), tile(width), tile(width), tile(width), tile(lanes), tile(lanes),
            fixed(gain), fixed(weights), fixed(turn),
        ],
        out_specs=[
            pl.BlockSpec((tp_size, 1, piece, depth), lambda n: (0, n, 0, 0)),
            fixed(weights),
        ],
        out_shape=[
            jax.ShapeDtypeStruct((tp_size, rows_each * seq_size, piece, depth), jnp.bfloat16),
            jax.ShapeDtypeStruct(weights.shape, jnp.bfloat16),
        ],
        scratch_shapes=[pltpu.VMEM(weights.shape, jnp.float32)],
        compiler_params=pltpu.CompilerParams(vmem_limit_bytes=67043328),
        name="project_back",
    )(x_rows, query_g, key_g, value_g, cosine, sine, gain, weights, turn)


class Reduce:
    def __init__(self, place, hbm, part, core_in, pair_in, chunks, sems):
        self.seq, self.tp, self.pairs = place
        self.pair, self.core = self.tp // 2, lax.rem(self.tp, 2)
        self.other = self.pair * 2 + 1 - self.core
        self.hbm, self.part, self.core_in, self.pair_in = hbm, part, core_in, pair_in
        self.chunks = chunks
        self.load_sem, self.core_send, self.core_recv, self.pair_send, self.pair_recv = sems

    def peer(self, offset):
        return lax.rem(self.pair + offset, self.pairs) * 2 + self.core

    def cut(self, ref, lead, c):
        return ref.at[lead, :, c]

    def load(self, offset):
        return pltpu.make_async_copy(
            self.hbm.at[self.peer(offset)], self.part.at[offset], self.load_sem.at[offset]
        )

    def to_core(self, offset, c):
        lead = lax.rem(self.pair + offset, self.pairs) * 2 + 1 - self.core
        at = offset * self.chunks + c
        return remote(
            self.cut(self.hbm, lead, c), self.cut(self.core_in, offset, c),
            self.core_send.at[at], self.core_recv.at[at], (self.seq, self.other),
        )

    def to_pair(self, offset, c):
        back = self.pairs - offset
        return remote(
            self.cut(self.part, offset, c), self.cut(self.pair_in, back, c),
            self.pair_send.at[offset * self.chunks + c],
            self.pair_recv.at[back * self.chunks + c], (self.seq, self.peer(offset)),
        )

    def from_pair(self, offset, c):
        view, at = self.cut(self.pair_in, offset, c), offset * self.chunks + c
        return remote(
            view, view, self.pair_send.at[at], self.pair_recv.at[at], (self.seq, self.peer(offset))
        )

    def start(self):
        for offset in list(range(1, self.pairs)) + [0]:
            self.load(offset).start()
        for c in range(self.chunks):
            for offset in list(range(1, self.pairs)) + [0]:
                self.to_core(offset, c).start()

    def wait_loads(self):
        for offset in range(self.pairs):
            self.load(offset).wait()

    def pass_on(self, c):
        for offset in range(1, self.pairs):
            self.to_core(offset, c).wait_recv()

            def add(b, carry):
                self.part[offset, b, c] = (
                    self.part[offset, b, c].astype(jnp.float32)
                    + self.core_in[offset, b, c].astype(jnp.float32)
                ).astype(jnp.bfloat16)
                return carry

            lax.fori_loop(0, self.part.shape[1], add, 0)
            self.to_pair(offset, c).start()

    def arrive(self, c):
        self.to_core(0, c).wait_recv()
        for offset in range(1, self.pairs):
            self.from_pair(offset, c).wait_recv()

    def total(self, b, c):
        value = self.part[0, b, c].astype(jnp.float32) + self.core_in[0, b, c].astype(jnp.float32)
        for offset in range(1, self.pairs):
            value = value + self.pair_in[offset, b, c].astype(jnp.float32)
        return value

    def finish(self):
        for c in range(self.chunks):
            for offset in range(self.pairs):
                self.to_core(offset, c).wait_send()
            for offset in range(1, self.pairs):
                self.to_pair(offset, c).wait_send()


class SeqSum:
    def __init__(self, place, color, bits, blocks, held, sums, send_sem, recv_sem):
        self.seq, self.tp = place
        self.sums = sums
        self.bits, self.blocks, self.held, self.color = bits, blocks, held, color
        self.size = 1 << len(bits)
        self.send_sem, self.recv_sem = send_sem, recv_sem
        low, self.lows = color * self.size, []
        self.flags = []
        for n, bit in enumerate(bits):
            flag = lax.rem(self.seq // (1 << bit), 2)
            self.flags.append(flag)
            self.lows.append(low)
            low = low + flag * (self.size >> (n + 1))
        self.lows.append(low)

    def partner(self, n):
        return (self.seq + (1 - 2 * self.flags[n]) * (1 << self.bits[n]), self.tp)

    def span(self, n):
        return pl.ds(self.lows[n + 1], self.size >> (n + 1))

    def give(self, n):
        half = self.size >> (n + 1)
        begin = self.size - (self.size >> n)
        source = self.blocks.at[pl.ds(self.lows[n] + (1 - self.flags[n]) * half, half)]
        steps = len(self.bits)
        return remote(
            source, self.held.at[self.color, pl.ds(begin, half)],
            self.send_sem.at[self.color * 2 * steps + n],
            self.recv_sem.at[self.color * 2 * steps + n], self.partner(n),
        )

    def take(self, n):
        copy = self.give(n)
        copy.wait_recv()
        copy.wait_send()
        half = self.size >> (n + 1)
        begin = self.size - (self.size >> n)

        target = self.sums if n + 1 == len(self.bits) else self.blocks

        def add(b, carry):
            at = self.lows[n + 1] + b
            target[at] = (
                self.blocks[at].astype(jnp.float32)
                + self.held[self.color, begin + b].astype(jnp.float32)
            ).astype(jnp.bfloat16)
            return carry

        lax.fori_loop(0, half, add, 0)

    def spread(self, n):
        view = self.sums.at[self.span(n)]
        at = self.color * 2 * len(self.bits) + len(self.bits) + n
        return remote(view, view, self.send_sem.at[at], self.recv_sem.at[at], self.partner(n))

    def collect(self, n):
        half = self.size >> (n + 1)
        view = self.sums.at[pl.ds(self.lows[n] + (1 - self.flags[n]) * half, half)]
        at = self.color * 2 * len(self.bits) + len(self.bits) + n
        remote(view, view, self.send_sem.at[at], self.recv_sem.at[at], self.partner(n)).wait_recv()

    def steps(self):
        count = len(self.bits)
        self.give(0).start()
        yield
        for n in range(count):
            self.take(n)
            if n + 1 < count:
                self.give(n + 1).start()
            else:
                self.spread(n).start()
            yield
        for n in range(count - 1, -1, -1):
            self.collect(n)
            if n > 0:
                self.spread(n - 1).start()
            yield
        for n in range(count):
            self.spread(n).wait_send()


def tail_kernel(
    sizes, dv_plan, normed_hbm, proj_hbm, out_hbm, grad_hbm, source_hbm, middle_hbm,
    middle_g_hbm, dv_hbm, gain_ref, small_ref,
    out_ref, input_g_ref, dv_ref, sums_ref, total_ref,
    normed_part, normed_core, normed_pair, proj_part, proj_core, proj_pair,
    out_part, out_core, out_pair, source, middle, middle_g, input_g, result,
    blocks, held, sums, small, tp_held, tp_sum, seq_held,
    *sems,
):
    seq_size, tp_size, rows_each, rows_local, _ = sizes
    s, t = lax.axis_index("seq"), lax.axis_index("tp")
    me = (s, t)
    pairs = tp_size // 2
    normed_sems, proj_sems, out_sems = sems[:5], sems[5:10], sems[10:15]
    dv_sems, back_sems, lo_sems = sems[15:18], sems[18:21], sems[21:24]
    load_sem, grad_send, grad_recv, small_send, tp_sem, seq_sem = sems[24:]
    place = (s, t, pairs)
    normed = Reduce(place, normed_hbm, normed_part, normed_core, normed_pair, 2, normed_sems)
    proj = Reduce(place, proj_hbm, proj_part, proj_core, proj_pair, 1, proj_sems)
    out = Reduce(place, out_hbm, out_part, out_core, out_pair, 2, out_sems)
    dv_move = Exchange(dv_plan, me, dv_hbm, dv_ref, *dv_sems)
    half = source.shape[0]
    piece = source.shape[2]

    group = group_of(s, seq_size)
    origins = []
    for slot in range(rows_local):
        row = t * rows_local + slot
        for i in range(tp_size):
            origins.append(((place_of(row // rows_each, seq_size), i), (slot, i), slot * tp_size + i))

    tp_peers = [lax.rem(t + i, tp_size) for i in range(1, tp_size)]
    seq_peers = [lax.rem(s + i, seq_size) for i in range(1, seq_size)]
    barrier = pltpu.get_barrier_semaphore()
    dv_move.greet(barrier)
    for origin, _, _ in origins:
        @pl.when(jnp.logical_not(same(origin, me)))
        def _():
            pl.semaphore_signal(barrier, inc=1, device_id=origin, device_id_type=MESH)
    for to in tp_peers:
        pl.semaphore_signal(barrier, inc=1, device_id=(s, to), device_id_type=MESH)
    for to in seq_peers:
        pl.semaphore_signal(barrier, inc=1, device_id=(to, t), device_id_type=MESH)
    back_others = sum(
        jnp.where(
            same((to, (group * rows_each + j) // rows_local), me), 0, 1
        )
        for j in range(rows_each)
        for to in range(seq_size)
    )
    pl.semaphore_wait(barrier, dv_move.others() + back_others + tp_size + seq_size - 2)

    loads = [
        pltpu.make_async_copy(grad_hbm, blocks.at[pl.ds(0, grad_hbm.shape[0])], load_sem.at[0]),
        pltpu.make_async_copy(source_hbm, source, load_sem.at[1]),
        pltpu.make_async_copy(middle_g_hbm, middle_g, load_sem.at[2]),
        pltpu.make_async_copy(middle_hbm, middle, load_sem.at[3]),
    ]
    loads[0].start()
    proj.start()
    normed.start()
    loads[1].start()
    loads[2].start()
    dv_move.start()
    out.start()
    loads[3].start()

    order = list(range(seq_size.bit_length() - 1))
    first = SeqSum(me, 0, order, blocks, held, sums, grad_send, grad_recv).steps()
    second = SeqSum(me, 1, order[1:] + order[:1], blocks, held, sums, grad_send, grad_recv).steps()

    loads[0].wait()
    next(first)
    proj.wait_loads()
    proj.pass_on(0)
    normed.wait_loads()
    normed.pass_on(0)
    normed.pass_on(1)
    proj.arrive(0)

    def put(b, carry):
        at = grad_hbm.shape[0] + b
        blocks[at] = proj.total(b, 0).astype(jnp.bfloat16)
        return carry

    lax.fori_loop(0, blocks.shape[0] - grad_hbm.shape[0], put, 0)
    next(second)
    next(first)
    out.wait_loads()
    out.pass_on(0)
    out.pass_on(1)

    def send_back(source_ref, target, trio, b, c, wait):
        local_sem, send_sem, recv_sem = trio
        flat = 2 * b + c
        j, to = flat // seq_size, lax.rem(flat, seq_size)
        row = group * rows_each + j
        slot = lax.rem(row, rows_local)
        place = (to, row // rows_local)
        here = same(place, me)
        view = target.at[slot, t]

        @pl.when(here)
        def _():
            copy = pltpu.make_async_copy(source_ref.at[b, c], view, local_sem.at[flat])
            copy.wait() if wait else copy.start()

        @pl.when(jnp.logical_not(here))
        def _():
            copy = remote(
                source_ref.at[b, c], view, send_sem.at[flat], recv_sem.at[slot * tp_size + t], place
            )
            copy.wait_send() if wait else copy.start()

    gain = gain_ref[...]
    small[...] = small_ref[...]

    def back(c):
        normed.arrive(c)

        def one(n, carry):
            b = lax.rem(n + s // 2, half)
            grads = normed.total(b, c)
            x = source[b, c].astype(jnp.float32)
            inverse = lax.rsqrt(jnp.mean(x * x, axis=-1, keepdims=True) + norm_eps)
            unit = x * inverse
            scaled = grads * gain
            extra = inverse * (scaled - unit * jnp.mean(scaled * unit, axis=-1, keepdims=True))
            input_g[b, c] = (middle_g[b, c] + extra).astype(jnp.bfloat16)
            small[0:1, :] += jnp.sum(grads * unit, axis=0, keepdims=True)
            send_back(input_g, input_g_ref, back_sems, b, c, False)
            return carry

        lax.fori_loop(0, half, one, 0)

    def forward(c):
        out.arrive(c)

        def one(n, carry):
            b = lax.rem(n + s // 2, half)
            result[b, c] = (middle[b, c] + out.total(b, c)).astype(jnp.bfloat16)
            send_back(result, out_ref, lo_sems, b, c, False)
            return carry

        lax.fori_loop(0, half, one, 0)

    def tp_copy(n):
        return remote(
            small, tp_held.at[tp_size - n], small_send.at[n],
            tp_sem.at[tp_size - n], (s, tp_peers[n - 1]),
        )

    def seq_copy(n):
        return remote(
            tp_sum, seq_held.at[seq_size - n], small_send.at[tp_size + n],
            seq_sem.at[seq_size - n], (seq_peers[n - 1], t),
        )

    next(first)
    next(second)
    loads[1].wait()
    loads[2].wait()
    back(0)
    next(first)
    next(second)
    back(1)
    for n in range(1, tp_size):
        tp_copy(n).start()
    next(first)
    next(second)
    loads[3].wait()
    forward(0)
    for n in range(1, tp_size):
        tp_copy(n).wait()
    tp_held[0] = small[...]
    total = tp_held[lax.rem(tp_size - t, tp_size)]
    for n in range(1, tp_size):
        total = total + tp_held[lax.rem(n + tp_size - t, tp_size)]
    tp_sum[...] = total
    for n in range(1, seq_size):
        seq_copy(n).start()
    seq_held[0] = total
    next(first)
    next(second)
    forward(1)
    for _ in first:
        pass
    for _ in second:
        pass
    for n in range(1, seq_size):
        seq_copy(n).wait()
    total = seq_held[lax.rem(seq_size - s, seq_size)]
    for n in range(1, seq_size):
        total = total + seq_held[lax.rem(n + seq_size - s, seq_size)]
    total_ref[...] = total
    store = pltpu.make_async_copy(sums, sums_ref, load_sem.at[0])
    store.start()

    for reduce in (normed, proj, out):
        reduce.finish()
    for c in range(2):
        def done(b, carry):
            send_back(input_g, input_g_ref, back_sems, b, c, True)
            send_back(result, out_ref, lo_sems, b, c, True)
            return carry

        lax.fori_loop(0, half, done, 0)
    dv_move.wait_sends()
    dv_move.wait_receives()
    for origin, target, at in origins:
        @pl.when(jnp.logical_not(same(origin, me)))
        def _():
            for ref, trio in ((input_g_ref, back_sems), (out_ref, lo_sems)):
                view = ref.at[target]
                remote(view, view, trio[1].at[0], trio[2].at[at], origin).wait_recv()
    store.wait()


def tail(normed_g, proj_grad, out_part, grads, source, middle, middle_g, value_g, gain, small, sizes):
    seq_size, tp_size, rows_each, rows_local, _ = sizes
    pairs = tp_size // 2
    blocks = rows_each * seq_size
    tokens, depth = source.shape
    piece = tokens // blocks
    width = proj_grad.shape[0] // tp_size
    fine = 2 * width // seq_size
    places = value_g.shape[2]
    bf16, f32 = jnp.bfloat16, jnp.float32
    shape = (blocks // 2, 2, piece, depth)
    proj_shape = (width // fine, 1, fine, depth)
    anywhere = pl.BlockSpec(memory_space=pl.ANY)
    vmem = pl.BlockSpec(memory_space=pltpu.VMEM)
    dma = pltpu.SemaphoreType.DMA
    plan = rows_to_places(seq_size, rows_each)
    steps = seq_size.bit_length() - 1
    owned = jax.ShapeDtypeStruct((rows_local, tp_size, piece, depth), bf16)

    def reduce_sems(chunks):
        return [dma((pairs,))] + [dma((pairs * chunks,))] * 4

    return pl.pallas_call(
        functools.partial(tail_kernel, sizes, plan),
        out_shape=[
            owned,
            owned,
            jax.ShapeDtypeStruct((rows_each * seq_size, places, width), bf16),
            jax.ShapeDtypeStruct((2 * seq_size, fine, depth), bf16),
            jax.ShapeDtypeStruct(small.shape, f32),
        ],
        in_specs=[anywhere] * 8 + [vmem] * 2,
        out_specs=[anywhere] * 4 + [vmem],
        scratch_shapes=[pltpu.VMEM((pairs,) + shape, bf16)] * 3
        + [pltpu.VMEM((pairs,) + proj_shape, bf16)] * 3
        + [pltpu.VMEM((pairs,) + shape, bf16)] * 3
        + [
            pltpu.VMEM(shape, bf16),
            pltpu.VMEM(shape, f32),
            pltpu.VMEM(shape, f32),
            pltpu.VMEM(shape, bf16),
            pltpu.VMEM(shape, bf16),
            pltpu.VMEM((2 * seq_size, fine, depth), bf16),
            pltpu.VMEM((2, seq_size, fine, depth), bf16),
            pltpu.VMEM((2 * seq_size, fine, depth), bf16),
            pltpu.VMEM(small.shape, f32),
            pltpu.VMEM((tp_size,) + small.shape, f32),
            pltpu.VMEM(small.shape, f32),
            pltpu.VMEM((seq_size,) + small.shape, f32),
        ]
        + reduce_sems(2)
        + reduce_sems(1)
        + reduce_sems(2)
        + [dma((seq_size,))] * 3
        + ([dma((blocks,))] * 2 + [dma((rows_local * tp_size,))]) * 2
        + [
            dma((4,)),
            dma((4 * steps,)),
            dma((4 * steps,)),
            dma((tp_size + seq_size,)),
            dma((tp_size,)),
            dma((seq_size,)),
        ],
        compiler_params=pltpu.CompilerParams(
            collective_id=6, has_side_effects=True, vmem_limit_bytes=67043328
        ),
        name="tail",
    )(
        normed_g.reshape((tp_size,) + shape),
        proj_grad.reshape((tp_size,) + proj_shape),
        out_part.reshape((tp_size,) + shape),
        grads.reshape(-1, fine, depth),
        source.reshape(shape),
        middle.reshape(shape),
        middle_g.reshape(shape),
        value_g,
        gain,
        small,
    )


def half_swap(weight):
    parts = weight.reshape(-1, 2, HD // 2, weight.shape[1])
    return jnp.stack([-parts[:, 1], parts[:, 0]], axis=1).reshape(weight.shape)


def shards(
    layer_input,
    first_values,
    doc_lengths,
    attn_gain,
    query_weight,
    key_weight,
    value_weight,
    output_weight,
    feed_gain,
    gate_weight,
    up_weight,
    down_weight,
    out_cotangent,
):
    seq_size = lax.axis_size("seq")
    tp_size = lax.axis_size("tp")
    rows_local, local_len, depth = layer_input.shape
    row_count = first_values.shape[0]
    width = query_weight.shape[0]
    rows_each = row_count // seq_size
    piece = local_len // tp_size
    tokens = rows_each * seq_size * piece
    sizes = (seq_size, tp_size, rows_each, rows_local, 4)
    me = lax.axis_index("tp")
    my_rows = group_of(lax.axis_index("seq"), seq_size) * rows_each

    _, offsets = doc_layout(doc_lengths)
    offsets = lax.dynamic_slice_in_dim(offsets, my_rows, rows_each, 0)
    starts = jnp.arange(ROW, dtype=jnp.int32)[None, :] - offsets
    low = (starts[:, ::BLOCK] // BLOCK).reshape(-1)
    starts = starts[:, None, :]
    lane = jnp.arange(min(width, 128), dtype=jnp.int32)
    frequency = rope_base ** (-(lane % (HD // 2)).astype(jnp.float32) * 2.0 / HD)
    angles = offsets.astype(jnp.float32).reshape(-1, 1) * frequency
    cosine, sine = jnp.cos(angles), jnp.sin(angles)
    attn_scale = attn_gain.astype(jnp.float32)[None, :]
    feed_scale = feed_gain.astype(jnp.float32)[None, :]
    weights = jnp.concatenate([query_weight, key_weight, value_weight], axis=0)
    swapped = jnp.concatenate([half_swap(query_weight), half_swap(key_weight)], axis=0)
    turn = half_swap(jnp.eye(width, dtype=jnp.bfloat16))

    x_rows, cot_all, first_rows = spread(
        layer_input.reshape(rows_local, tp_size, piece, depth),
        out_cotangent.reshape(rows_local, tp_size, piece, depth),
        first_values,
        sizes,
    )
    source_low = lax.dynamic_index_in_dim(x_rows, me, 2, keepdims=False).reshape(tokens, depth)
    source = source_low.astype(jnp.float32)
    cotangent = lax.dynamic_index_in_dim(cot_all, me, 0, keepdims=False).reshape(tokens, depth)
    cotangent = cotangent.astype(jnp.float32)
    x_rows = x_rows.reshape(rows_each * ROW, depth)
    queries, keys, values, squares = project(
        x_rows, first_rows, cosine, sine, attn_scale, weights, swapped
    )
    queries, keys, values = (
        part.reshape(rows_each, ROW, width) for part in (queries, keys, values)
    )
    result, logsum = attend(low, queries, keys, values, starts)
    by_piece = (rows_each, seq_size, tp_size, piece, width)
    by_head = (tp_size, rows_each, seq_size, piece, width)
    (pieces,) = exchange([result.reshape(by_piece)], [by_head], [heads_to_tokens(tp_size)], 1)
    attended = jnp.transpose(pieces.reshape(tp_size, tokens, width), (1, 0, 2)).reshape(tokens, -1)
    output_full = lax.all_gather(output_weight, "tp", axis=0, tiled=True)
    attended, output_full = lax.optimization_barrier((attended, output_full))
    middle = source + jnp.dot(attended, output_full, preferred_element_type=jnp.float32)
    unit_feed, inv_feed = norm_rows(middle)
    feed_in = (unit_feed * feed_scale).astype(jnp.bfloat16)
    feed_in_g, out_part, gate_grad, up_grad, down_grad = feed_forward(
        feed_in, cot_all.reshape(tp_size, tokens, depth), gate_weight, up_weight, down_weight
    )
    feed_sums = lax.psum((gate_grad, up_grad, down_grad), "seq")
    middle_extra, feed_gain_part = norm_back(feed_in_g, unit_feed, inv_feed, feed_scale)
    middle_g = cotangent + middle_extra
    branch_g = middle_g.astype(jnp.bfloat16)
    attended_g = jnp.einsum(
        "td,ed->te", branch_g, output_full, preferred_element_type=jnp.float32
    ).astype(jnp.bfloat16)
    (attended_g,) = exchange(
        [jnp.transpose(attended_g.reshape(tokens, tp_size, width), (1, 0, 2)).reshape(by_head)],
        [by_piece],
        [tokens_to_heads(tp_size)],
        2,
    )
    query_g, key_g, value_g = attend_back(
        low, queries, keys, values, result, attended_g.reshape(result.shape), logsum, starts
    )
    normed_g, stacked_grad = project_back(
        x_rows,
        query_g.reshape(-1, width),
        key_g.reshape(-1, width),
        value_g.reshape(-1, width),
        cosine,
        sine,
        attn_scale,
        weights,
        turn,
        sizes,
    )
    output_proj_grad = jnp.einsum(
        "te,td->ed", attended, branch_g, preferred_element_type=jnp.float32
    ).astype(jnp.bfloat16)
    squares = jnp.pad(jnp.sum(squares, axis=1)[:2], (0, depth - 2))
    small = jnp.stack([jnp.zeros_like(squares), feed_gain_part, squares])
    layer_output, input_grad, value_own_g, grad_sums, small = tail(
        normed_g,
        output_proj_grad,
        out_part,
        stacked_grad,
        source_low,
        middle,
        middle_g,
        value_g.reshape(rows_each, seq_size, local_len, width),
        attn_scale,
        jnp.pad(small, ((0, 5), (0, 0))),
        sizes,
    )
    first_grad = jnp.swapaxes(0.5 * value_own_g.astype(jnp.float32), 1, 2)
    grad_sums = grad_sums.reshape(4 * width, depth).astype(jnp.float32)
    return (
        layer_output.reshape(layer_input.shape),
        input_grad.reshape(layer_input.shape),
        first_grad,
        small[0],
        grad_sums[:width],
        grad_sums[width : 2 * width],
        grad_sums[2 * width : 3 * width],
        grad_sums[3 * width :],
        small[1],
        feed_sums[0].astype(jnp.float32),
        feed_sums[1].astype(jnp.float32),
        feed_sums[2].astype(jnp.float32),
        jnp.sqrt(small[2, :2]),
    )


def solution(mesh):
    placed = (
        P("tp", "seq", None),
        P(None, "tp", "seq"),
        P(),
        P(),
        P("tp", None),
        P("tp", None),
        P("tp", None),
        P("tp", None),
        P(),
        P(None, "tp"),
        P(None, "tp"),
        P("tp", None),
        P("tp", "seq", None),
    )
    return jax.shard_map(
        shards,
        mesh=mesh,
        in_specs=placed,
        out_specs=(
            P("tp", "seq", None),
            P("tp", "seq", None),
            P(None, "tp", "seq"),
            P(),
            P("tp", None),
            P("tp", None),
            P("tp", None),
            P("tp", None),
            P(),
            P(None, "tp"),
            P(None, "tp"),
            P("tp", None),
            P(),
        ),
        check_vma=False,
    )
```

```python
import functools
import math

import jax
import jax.numpy as jnp
from jax import lax
from jax.experimental import pallas as pl
from jax.experimental.pallas import tpu as pltpu
from jax.sharding import PartitionSpec as P

HD = 64
ROW = 2048
BLOCK = 256
LOG2E = math.log2(math.e)
LN2 = math.log(2.0)
MESH = pl.DeviceIdType.MESH


norm_eps = 1e-06
rope_base = 10000.0
masked_score = -1e30


def doc_layout(doc_lengths):
    doc_ends = jnp.cumsum(doc_lengths, axis=-1)
    places = jnp.arange(ROW, dtype=jnp.int32)
    passed = doc_ends[:, None, :] <= places[None, :, None]
    segment = jnp.sum(passed.astype(jnp.int32), axis=-1)
    starts = jnp.max(jnp.where(passed, doc_ends[:, None, :], 0), axis=-1)
    return (segment, places[None, :] - starts)


def norm_rows(values_in):
    inverse = lax.rsqrt(jnp.mean(values_in * values_in, axis=-1, keepdims=True) + norm_eps)
    return (values_in * inverse, inverse)


def norm_back(grads_in, unit_rows, inverse, gain):
    scaled = grads_in * gain
    extra = inverse * (scaled - unit_rows * jnp.mean(scaled * unit_rows, axis=-1, keepdims=True))
    return (extra, jnp.sum(grads_in * unit_rows, axis=0))


def rows_dot(left, right):
    return lax.dot_general(left, right, (((1,), (1,)), ((), ())), preferred_element_type=jnp.float32)


def plain_dot(left, right):
    return lax.dot_general(left, right, (((1,), (0,)), ((), ())), preferred_element_type=jnp.float32)


def head_masked(block, head, heads):
    if heads == 1:
        return block
    lanes = lax.broadcasted_iota(jnp.int32, block.shape, 1)
    return jnp.where(lanes // HD == head, block, jnp.zeros_like(block))


def lane_group(head, width):
    lanes = min(width, 128)
    return slice(head * HD // lanes * lanes, head * HD // lanes * lanes + lanes), head % (lanes // HD)


def attend_kernel(low_ref, q_ref, k_ref, v_ref, start_ref, o_ref, lse_ref, v_cols):
    row = pl.program_id(0)
    length, width = q_ref.shape[1:]
    heads = width // HD
    together = min(width, 128) // HD
    blocks = length // BLOCK
    for j in range(blocks):
        v_cols[:, j * BLOCK : (j + 1) * BLOCK] = v_ref[0, j * BLOCK : (j + 1) * BLOCK, :].T

    def query_block(i, carry):
        first = pl.multiple_of(i * BLOCK, BLOCK)
        q_heads = []
        for h in range(heads):
            lanes, at = lane_group(h, width)
            q_heads.append(head_masked(q_ref[0, pl.ds(first, BLOCK), lanes], at, together))
        start = start_ref[0, :, pl.ds(first, BLOCK)]
        places = first + lax.broadcasted_iota(jnp.int32, (1, BLOCK), 1)

        def key_block(j, state):
            at = pl.multiple_of(j * BLOCK, BLOCK)
            keys = at + lax.broadcasted_iota(jnp.int32, (BLOCK, BLOCK), 0)
            allowed = (keys >= start) & (keys <= places)
            scores = [
                rows_dot(k_ref[0, pl.ds(at, BLOCK), lane_group(h, width)[0]], q_heads[h])
                for h in range(heads)
            ]
            out = []
            for h in range(heads):
                top, total, acc = state[h]
                masked = jnp.where(allowed, scores[h], masked_score)
                new_top = jnp.maximum(top, jnp.max(masked, axis=0, keepdims=True))
                weights = jnp.exp2(masked - new_top)
                shrink = jnp.exp2(top - new_top)
                total = total * shrink + jnp.sum(weights, axis=0, keepdims=True)
                acc = acc * shrink + plain_dot(
                    v_cols[h * HD : (h + 1) * HD, pl.ds(at, BLOCK)], weights.astype(jnp.bfloat16)
                )
                out.append((new_top, total, acc))
            return tuple(out)

        begin = tuple(
            (
                jnp.full((1, BLOCK), masked_score, jnp.float32),
                jnp.zeros((1, BLOCK), jnp.float32),
                jnp.zeros((HD, BLOCK), jnp.float32),
            )
            for _ in range(heads)
        )
        state = key_block(i, begin)
        state = lax.fori_loop(low_ref[row * blocks + i], i, key_block, state)
        columns = jnp.concatenate([acc / total for _, total, acc in state], axis=0)
        o_ref[0, pl.ds(first, BLOCK), :] = columns.T.astype(jnp.bfloat16)
        for h in range(heads):
            top, total, _ = state[h]
            lse_ref[0, pl.ds(h, 1), pl.ds(first, BLOCK)] = top + jnp.log2(total)
        return carry

    lax.fori_loop(0, blocks, query_block, 0)


def attend(low, queries, keys, values, starts):
    rows, length, width = queries.shape
    heads = width // HD
    wide = pl.BlockSpec((1, length, width), lambda r, low: (r, 0, 0))
    return pl.pallas_call(
        attend_kernel,
        grid_spec=pltpu.PrefetchScalarGridSpec(
            num_scalar_prefetch=1,
            grid=(rows,),
            in_specs=[wide, wide, wide, pl.BlockSpec((1, 1, length), lambda r, low: (r, 0, 0))],
            out_specs=[wide, pl.BlockSpec((1, heads, length), lambda r, low: (r, 0, 0))],
            scratch_shapes=[pltpu.VMEM((width, length), jnp.bfloat16)],
        ),
        out_shape=[
            jax.ShapeDtypeStruct(queries.shape, jnp.bfloat16),
            jax.ShapeDtypeStruct((rows, heads, length), jnp.float32),
        ],
        compiler_params=pltpu.CompilerParams(vmem_limit_bytes=67043328),
        name="attend",
    )(low, queries, keys, values, starts)


def attend_back_kernel(
    low_ref, q_ref, k_ref, v_ref, o_ref, g_ref, lse_ref, start_ref,
    qg_ref, kg_ref, vg_ref, k_cols, k_acc, v_acc,
):
    row = pl.program_id(0)
    length, width = q_ref.shape[1:]
    heads = width // HD
    together = min(width, 128) // HD
    blocks = length // BLOCK
    for j in range(blocks):
        k_cols[:, j * BLOCK : (j + 1) * BLOCK] = k_ref[0, j * BLOCK : (j + 1) * BLOCK, :].T
    k_acc[...] = jnp.zeros_like(k_acc)
    v_acc[...] = jnp.zeros_like(v_acc)
    select = (
        lax.broadcasted_iota(jnp.int32, (8, width), 1) // HD
        == lax.broadcasted_iota(jnp.int32, (8, width), 0)
    ).astype(jnp.float32)

    def query_block(i, carry):
        first = pl.multiple_of(i * BLOCK, BLOCK)
        q_heads, g_heads = [], []
        for h in range(heads):
            lanes, at = lane_group(h, width)
            q_heads.append(head_masked(q_ref[0, pl.ds(first, BLOCK), lanes], at, together))
            g_heads.append(head_masked(g_ref[0, pl.ds(first, BLOCK), lanes], at, together))
        product = g_ref[0, pl.ds(first, BLOCK), :].astype(jnp.float32) * o_ref[
            0, pl.ds(first, BLOCK), :
        ].astype(jnp.float32)
        centre = lax.dot_general(
            select, product, (((1,), (1,)), ((), ())),
            precision=lax.Precision.HIGHEST, preferred_element_type=jnp.float32,
        )
        lse = lse_ref[0, :, pl.ds(first, BLOCK)]
        start = start_ref[0, :, pl.ds(first, BLOCK)]
        places = first + lax.broadcasted_iota(jnp.int32, (1, BLOCK), 1)

        def key_block(j, state):
            at = pl.multiple_of(j * BLOCK, BLOCK)
            keys = at + lax.broadcasted_iota(jnp.int32, (BLOCK, BLOCK), 0)
            allowed = (keys >= start) & (keys <= places)
            scores, prob_gs = [], []
            for h in range(heads):
                lanes, _ = lane_group(h, width)
                scores.append(rows_dot(k_ref[0, pl.ds(at, BLOCK), lanes], q_heads[h]))
                prob_gs.append(rows_dot(v_ref[0, pl.ds(at, BLOCK), lanes], g_heads[h]))
            out = []
            for h in range(heads):
                lanes, _ = lane_group(h, width)
                probs = jnp.exp2(jnp.where(allowed, scores[h], masked_score) - lse[h : h + 1, :])
                score_g = (probs * (prob_gs[h] - centre[h : h + 1, :])).astype(jnp.bfloat16)
                v_acc[pl.ds(at, BLOCK), lanes] += plain_dot(probs.astype(jnp.bfloat16), g_heads[h])
                k_acc[pl.ds(at, BLOCK), lanes] += plain_dot(score_g, q_heads[h])
                out.append(
                    state[h] + plain_dot(k_cols[h * HD : (h + 1) * HD, pl.ds(at, BLOCK)], score_g)
                )
            return tuple(out)

        begin = tuple(jnp.zeros((HD, BLOCK), jnp.float32) for _ in range(heads))
        state = lax.fori_loop(low_ref[row * blocks + i], i + 1, key_block, begin)
        columns = jnp.concatenate(state, axis=0) * HD ** (-0.5)
        qg_ref[0, pl.ds(first, BLOCK), :] = columns.T.astype(jnp.bfloat16)
        return carry

    lax.fori_loop(0, blocks, query_block, 0)
    kg_ref[0] = (k_acc[...] * LN2).astype(jnp.bfloat16)
    vg_ref[0] = v_acc[...].astype(jnp.bfloat16)


def attend_back(low, queries, keys, values, attended, grads, lse, starts):
    rows, length, width = queries.shape
    heads = width // HD
    wide = pl.BlockSpec((1, length, width), lambda r, low: (r, 0, 0))
    return pl.pallas_call(
        attend_back_kernel,
        grid_spec=pltpu.PrefetchScalarGridSpec(
            num_scalar_prefetch=1,
            grid=(rows,),
            in_specs=[wide] * 5
            + [
                pl.BlockSpec((1, heads, length), lambda r, low: (r, 0, 0)),
                pl.BlockSpec((1, 1, length), lambda r, low: (r, 0, 0)),
            ],
            out_specs=[wide] * 3,
            scratch_shapes=[
                pltpu.VMEM((width, length), jnp.bfloat16),
                pltpu.VMEM((length, width), jnp.float32),
                pltpu.VMEM((length, width), jnp.float32),
            ],
        ),
        out_shape=[jax.ShapeDtypeStruct(queries.shape, jnp.bfloat16)] * 3,
        compiler_params=pltpu.CompilerParams(vmem_limit_bytes=67043328),
        name="attend_back",
    )(low, queries, keys, values, attended, grads, lse, starts)


def columns_dot(left, right):
    return lax.dot_general(left, right, (((0,), (0,)), ((), ())), preferred_element_type=jnp.float32)


def feed_kernel(
    chunk, feed_ref, cot_ref, gate_w, up_w, down_w,
    feed_g_ref, out_ref, keep_ref, give_ref,
    feed_all, part, core_in, pair_in, acc,
    feed_send, feed_core, feed_pair, relay_send, part_send, part_core, sum_send, sum_pair,
):
    tokens = feed_ref.shape[0]
    chunks = tokens // chunk
    seq = lax.axis_index("seq")
    me = lax.axis_index("tp")
    pairs = lax.axis_size("tp") // 2
    pair, core = me // 2, lax.rem(me, 2)
    other = pair * 2 + 1 - core

    def peer(offset):
        return lax.rem(pair + offset, pairs) * 2 + core

    def copy(source, target, send, receive, to):
        return pltpu.make_async_remote_copy(
            src_ref=source, dst_ref=target, send_sem=send, recv_sem=receive,
            device_id=(seq, to), device_id_type=MESH,
        )

    barrier = pltpu.get_barrier_semaphore()
    for to in [other] + [peer(offset) for offset in range(1, pairs)]:
        pl.semaphore_signal(barrier, inc=1, device_id=(seq, to), device_id_type=MESH)
    pl.semaphore_wait(barrier, pairs)

    def rows(c):
        return pl.ds(pl.multiple_of(c * chunk, chunk), chunk)

    def feed_to_core(c):
        return copy(
            feed_ref.at[rows(c)], feed_all.at[me, rows(c)],
            feed_send.at[c], feed_core.at[c], other,
        )

    def feed_to_pair(offset, c):
        return copy(
            feed_ref.at[rows(c)], feed_all.at[me, rows(c)],
            feed_send.at[offset * chunks + c],
            feed_pair.at[(pairs - offset) * chunks + c], peer(offset),
        )

    def feed_from_pair(offset, c):
        return copy(
            feed_all.at[peer(offset), rows(c)], feed_all.at[peer(offset), rows(c)],
            feed_send.at[0], feed_pair.at[offset * chunks + c], other,
        )

    def relay(offset, c):
        return copy(
            feed_all.at[peer(offset), rows(c)], feed_all.at[peer(offset), rows(c)],
            relay_send.at[offset * chunks + c], feed_core.at[offset * chunks + c], other,
        )

    def part_to_core(offset, c):
        at = lax.rem(pair + offset, pairs) * 2 + 1 - core
        return copy(
            part.at[at, rows(c)], core_in.at[offset, rows(c)],
            part_send.at[offset * chunks + c], part_core.at[offset * chunks + c], other,
        )

    def sum_to_pair(offset, c):
        return copy(
            part.at[peer(offset), rows(c)], pair_in.at[pairs - offset, rows(c)],
            sum_send.at[offset * chunks + c],
            sum_pair.at[(pairs - offset) * chunks + c], peer(offset),
        )

    for c in range(chunks):
        feed_to_core(c).start()
        for offset in range(1, pairs):
            feed_to_pair(offset, c).start()
    feed_all[me] = feed_ref[...]
    acc[...] = jnp.zeros_like(acc)

    def step(n, carry):
        which = lax.rem(n, 2)
        c = lax.rem(n // 2, chunks)
        offset = n // (2 * chunks)
        owner = lax.rem(pair + offset, pairs) * 2 + lax.rem(core + which, 2)

        @pl.when((which == 0) & (offset > 0))
        def _():
            feed_from_pair(offset, c).wait_recv()
            relay(offset, c).start()

        @pl.when(which == 1)
        def _():
            relay(offset, c).wait_recv()

        feed = feed_all[owner, rows(c), :]
        cot = cot_ref[owner, rows(c), :]
        gate = rows_dot(feed, gate_w[...])
        up = rows_dot(feed, up_w[...])
        sigmoid = jax.nn.sigmoid(gate)
        activated = gate * sigmoid
        hidden = (activated * up).astype(jnp.bfloat16)
        hidden_g = rows_dot(cot, down_w[...])
        up_g = (hidden_g * activated).astype(jnp.bfloat16)
        gate_g = (hidden_g * up * sigmoid * (1.0 + gate * (1.0 - sigmoid))).astype(jnp.bfloat16)
        part[owner, rows(c), :] = (
            plain_dot(gate_g, gate_w[...]) + plain_dot(up_g, up_w[...])
        ).astype(jnp.bfloat16)

        @pl.when(which == 1)
        def _():
            part_to_core(offset, c).start()

        out_ref[owner, rows(c), :] = plain_dot(hidden, down_w[...]).astype(jnp.bfloat16)
        acc[0] += columns_dot(gate_g, feed)
        acc[1] += columns_dot(up_g, feed)
        acc[2] += columns_dot(hidden, cot)

        @pl.when((which == 1) & (offset > 0))
        def _():
            part_to_core(offset, c).wait_recv()
            to = peer(offset)
            part[to, rows(c), :] = (
                part[to, rows(c), :].astype(jnp.float32)
                + core_in[offset, rows(c), :].astype(jnp.float32)
            ).astype(jnp.bfloat16)
            sum_to_pair(offset, c).start()

        return carry

    lax.fori_loop(0, 2 * chunks * pairs, step, 0)
    half = acc.shape[1] // 2
    flag = lax.rem(seq, 2)
    for n in range(3):
        keep_ref[n] = acc[n, pl.ds(pl.multiple_of(flag * half, 8), half), :].astype(jnp.bfloat16)
        give_ref[n] = acc[n, pl.ds(pl.multiple_of((1 - flag) * half, 8), half), :].astype(
            jnp.bfloat16
        )
    for c in range(chunks):
        part_to_core(0, c).wait_recv()
        for offset in range(1, pairs):
            sum_to_pair(offset, c).wait_recv()
        total = part[me, rows(c), :].astype(jnp.float32) + core_in[0, rows(c), :].astype(jnp.float32)
        for offset in range(1, pairs):
            total = total + pair_in[offset, rows(c), :].astype(jnp.float32)
        feed_g_ref[rows(c), :] = total
    for c in range(chunks):
        feed_to_core(c).wait_send()
        part_to_core(0, c).wait_send()
        for offset in range(1, pairs):
            feed_to_pair(offset, c).wait_send()
            relay(offset, c).wait_send()
            part_to_core(offset, c).wait_send()
            sum_to_pair(offset, c).wait_send()


def feed_forward(feed_in, cot_all, gate_weight, up_weight, down_weight):
    tokens, width = feed_in.shape
    tp_size = cot_all.shape[0]
    pairs = tp_size // 2
    chunk = min(tokens, 256)
    chunks = tokens // chunk
    hidden = gate_weight.shape[0]
    whole = pl.BlockSpec(memory_space=pltpu.VMEM)
    dma = pltpu.SemaphoreType.DMA
    return pl.pallas_call(
        functools.partial(feed_kernel, chunk),
        out_shape=[
            jax.ShapeDtypeStruct((tokens, width), jnp.float32),
            jax.ShapeDtypeStruct(cot_all.shape, jnp.bfloat16),
            jax.ShapeDtypeStruct((3, hidden // 2, width), jnp.bfloat16),
            jax.ShapeDtypeStruct((3, hidden // 2, width), jnp.bfloat16),
        ],
        in_specs=[whole] * 5,
        out_specs=[whole] * 4,
        scratch_shapes=[
            pltpu.VMEM(cot_all.shape, jnp.bfloat16),
            pltpu.VMEM(cot_all.shape, jnp.bfloat16),
            pltpu.VMEM((pairs, tokens, width), jnp.bfloat16),
            pltpu.VMEM((pairs, tokens, width), jnp.bfloat16),
            pltpu.VMEM((3, hidden, width), jnp.float32),
        ]
        + [dma((pairs * chunks,))] * 8,
        compiler_params=pltpu.CompilerParams(
            collective_id=4, has_side_effects=True, vmem_limit_bytes=67043328
        ),
        name="feed_forward",
    )(feed_in, cot_all, gate_weight, up_weight, down_weight)


def group_of(place, seq_size):
    half = seq_size // 2
    low = place // 2
    return lax.rem(place + low, 2) * half + low


def place_of(group, seq_size):
    half = seq_size // 2
    low = lax.rem(group, half)
    return low * 2 + lax.rem(low + group // half, 2)


def remote(source, target, send, receive, to):
    return pltpu.make_async_remote_copy(
        src_ref=source, dst_ref=target, send_sem=send, recv_sem=receive,
        device_id=to, device_id_type=MESH,
    )


def same(left, right):
    return (left[0] == right[0]) & (left[1] == right[1])


class Exchange:
    def __init__(self, plan, me, source, target, local_sem, send_sem, receive_sem):
        self.me = me
        self.sends, self.receives = plan(*me)
        self.source, self.target = source, target
        self.local_sem, self.send_sem, self.receive_sem = local_sem, send_sem, receive_sem

    def greet(self, barrier):
        for origin, _, _ in self.receives:
            @pl.when(jnp.logical_not(same(origin, self.me)))
            def _():
                pl.semaphore_signal(barrier, inc=1, device_id=origin, device_id_type=MESH)

    def others(self):
        return sum(jnp.where(same(to, self.me), 0, 1) for to, _, _, _ in self.sends)

    def each_send(self, wait):
        for n, (to, source, target, at) in enumerate(self.sends):
            here = same(to, self.me)

            @pl.when(here)
            def _():
                copy = pltpu.make_async_copy(
                    self.source.at[source], self.target.at[target], self.local_sem.at[n]
                )
                copy.wait() if wait else copy.start()

            @pl.when(jnp.logical_not(here))
            def _():
                copy = remote(
                    self.source.at[source], self.target.at[target],
                    self.send_sem.at[n], self.receive_sem.at[at], to,
                )
                copy.wait_send() if wait else copy.start()

    def start(self):
        self.each_send(False)

    def wait_sends(self):
        self.each_send(True)

    def wait_receive(self, origin, target, at):
        @pl.when(jnp.logical_not(same(origin, self.me)))
        def _():
            remote(
                self.target.at[target], self.target.at[target],
                self.send_sem.at[0], self.receive_sem.at[at], origin,
            ).wait_recv()

    def wait_receives(self):
        for receive in self.receives:
            self.wait_receive(*receive)


def exchange(arrays, out_shapes, plans, number):
    count = len(arrays)

    def kernel(*refs):
        me = (lax.axis_index("seq"), lax.axis_index("tp"))
        moves = [
            Exchange(plan, me, refs[n], refs[count + n], *refs[2 * count + 3 * n :][:3])
            for n, plan in enumerate(plans)
        ]
        barrier = pltpu.get_barrier_semaphore()
        for move in moves:
            move.greet(barrier)
        pl.semaphore_wait(barrier, sum(move.others() for move in moves))
        for move in moves:
            move.start()
        for move in moves:
            move.wait_sends()
        for move in moves:
            move.wait_receives()

    semaphores = []
    for plan in plans:
        semaphores += [pltpu.SemaphoreType.DMA((len(plan(0, 0)[0]),))] * 3
    return pl.pallas_call(
        kernel,
        out_shape=[
            jax.ShapeDtypeStruct(shape, array.dtype) for shape, array in zip(out_shapes, arrays)
        ],
        in_specs=[pl.BlockSpec(memory_space=pl.ANY)] * count,
        out_specs=[pl.BlockSpec(memory_space=pl.ANY)] * count,
        scratch_shapes=semaphores,
        compiler_params=pltpu.CompilerParams(collective_id=number, has_side_effects=True),
        name=f"exchange_{number}",
    )(*arrays)


def owner_to_quarter(seq_size, tp_size, rows_each, rows_local, piece_first):
    def plan(s, t):
        sends, receives = [], []
        for slot in range(rows_local):
            row = t * rows_local + slot
            to = place_of(row // rows_each, seq_size)
            j = lax.rem(row, rows_each)
            for i in range(tp_size):
                target = (i, j, s) if piece_first else (j, s, i)
                sends.append(((to, i), (slot, i), target, j * seq_size + s))
        group = group_of(s, seq_size)
        for j in range(rows_each):
            row = group * rows_each + j
            for i in range(seq_size):
                origin = lax.rem(s + i, seq_size)
                target = (t, j, origin) if piece_first else (j, origin, t)
                receives.append(((origin, row // rows_local), target, j * seq_size + origin))
        return sends, receives

    return plan


def quarter_to_owner(seq_size, tp_size, rows_each, rows_local):
    def plan(s, t):
        sends, receives = [], []
        group = group_of(s, seq_size)
        for i in range(seq_size):
            to = lax.rem(s + i, seq_size)
            for j in range(rows_each):
                row = group * rows_each + j
                slot = lax.rem(row, rows_local)
                sends.append(((to, row // rows_local), (j, to), (slot, t), slot * tp_size + t))
        for slot in range(rows_local):
            row = t * rows_local + slot
            for i in range(tp_size):
                receives.append(
                    ((place_of(row // rows_each, seq_size), i), (slot, i), slot * tp_size + i)
                )
        return sends, receives

    return plan


def places_to_rows(seq_size, rows_each):
    def plan(s, t):
        sends, receives = [], []
        for i in range(seq_size):
            to = lax.rem(s + i, seq_size)
            rows = pl.ds(group_of(to, seq_size) * rows_each, rows_each)
            sends.append(((to, t), (rows,), (slice(None), s), s))
            origin = lax.rem(s + seq_size - i, seq_size)
            receives.append(((origin, t), (slice(None), origin), origin))
        return sends, receives

    return plan


def rows_to_places(seq_size, rows_each):
    def plan(s, t):
        sends, receives = [], []
        rows = pl.ds(group_of(s, seq_size) * rows_each, rows_each)
        for i in range(seq_size):
            to = lax.rem(s + i, seq_size)
            sends.append(((to, t), (slice(None), to), (rows,), s))
            origin = lax.rem(s + seq_size - i, seq_size)
            source_rows = pl.ds(group_of(origin, seq_size) * rows_each, rows_each)
            receives.append(((origin, t), (source_rows,), origin))
        return sends, receives

    return plan


def heads_to_tokens(tp_size):
    def plan(s, t):
        sends, receives = [], []
        for i in range(tp_size):
            to = lax.rem(t + i, tp_size)
            sends.append(((s, to), (slice(None), slice(None), to), (t,), t))
            origin = lax.rem(t + tp_size - i, tp_size)
            receives.append(((s, origin), (origin,), origin))
        return sends, receives

    return plan


def tokens_to_heads(tp_size):
    def plan(s, t):
        sends, receives = [], []
        for i in range(tp_size):
            to = lax.rem(t + i, tp_size)
            sends.append(((s, to), (to,), (slice(None), slice(None), t), t))
            origin = lax.rem(t + tp_size - i, tp_size)
            receives.append(((s, origin), (slice(None), slice(None), origin), origin))
        return sends, receives

    return plan


def spread_kernel(
    plans, sizes, x_ref, cot_ref, first_ref, output_ref, q_w, k_w, v_w, offset_ref, frequency_ref,
    gain_ref,
    x_out, cot_out, first_out, output_out, q_ref, k_ref, v_ref, cos_ref, sin_ref, square_ref,
    x_rows, first_rows, q_turned, k_turned,
    x_local, x_send, x_receive, cot_local, cot_send, cot_receive,
    first_local, first_send, first_receive,
    core_send, core_receive, pair_send, pair_receive, relay_send, load_sem, output_sem,
):
    seq_size, tp_size, rows_each, rows_local, parts = sizes
    me = (lax.axis_index("seq"), lax.axis_index("tp"))
    s, t = me
    pairs = tp_size // 2
    pair, core = t // 2, lax.rem(t, 2)
    other = pair * 2 + 1 - core
    each = seq_size // parts

    def peer(offset):
        return lax.rem(pair + offset, pairs) * 2 + core

    x_move = Exchange(plans[0], me, x_ref, x_out, x_local, x_send, x_receive)
    cot_move = Exchange(plans[1], me, cot_ref, cot_out, cot_local, cot_send, cot_receive)
    first_move = Exchange(plans[2], me, first_ref, first_out, first_local, first_send, first_receive)
    moves = (x_move, first_move, cot_move)
    barrier = pltpu.get_barrier_semaphore()
    for move in moves:
        move.greet(barrier)
    for to in [other] + [peer(offset) for offset in range(1, pairs)]:
        pl.semaphore_signal(barrier, inc=1, device_id=(s, to), device_id_type=MESH)
    pl.semaphore_wait(barrier, sum(move.others() for move in moves) + pairs)
    for move in moves:
        move.start()

    def block(out, tensor, piece, part):
        if tensor == 2:
            return out.at[piece]
        span = pl.ds(part * each, each)
        return out.at[:, span, piece] if tensor == 0 else out.at[piece, :, span]

    def number(tensor, offset, part):
        return (tensor * pairs + offset) * parts + part

    def own(out, tensor, part):
        return output_ref if tensor == 2 else block(out, tensor, t, part)

    def to_core(out, tensor, part):
        view, at = block(out, tensor, t, part), number(tensor, 0, part)
        return remote(own(out, tensor, part), view, core_send.at[at], core_receive.at[at], (s, other))

    def to_pair(out, tensor, offset, part):
        view = block(out, tensor, t, part)
        return remote(
            own(out, tensor, part), view, pair_send.at[number(tensor, offset, part)],
            pair_receive.at[number(tensor, pairs - offset, part)], (s, peer(offset)),
        )

    def from_pair(out, tensor, offset, part):
        view, at = block(out, tensor, peer(offset), part), number(tensor, offset, part)
        return remote(view, view, pair_send.at[at], pair_receive.at[at], (s, peer(offset)))

    def relay(out, tensor, offset, part):
        view, at = block(out, tensor, peer(offset), part), number(tensor, offset, part)
        return remote(view, view, relay_send.at[at], core_receive.at[at], (s, other))

    def from_core(out, tensor, offset, part):
        piece = lax.rem(pair + offset, pairs) * 2 + 1 - core
        view, at = block(out, tensor, piece, part), number(tensor, offset, part)
        return remote(view, view, relay_send.at[at], core_receive.at[at], (s, other))

    def forward(move, out, tensor):
        def receive(n, carry):
            part = lax.rem(s // each + n, parts)
            for j in range(rows_each):
                for i in range(each):
                    origin = part * each + i
                    group = group_of(s, seq_size)
                    owner = (origin, (group * rows_each + j) // rows_local)
                    target = (t, j, origin) if tensor else (j, origin, t)
                    move.wait_receive(owner, target, j * seq_size + origin)
                    slot = lax.rem(group * rows_each + j, rows_local)

                    @pl.when(same(owner, me))
                    def _():
                        pltpu.make_async_copy(
                            move.source.at[slot, t], move.target.at[target],
                            move.local_sem.at[slot * tp_size + t],
                        ).wait()
            to_core(out, tensor, part).start()
            for offset in range(1, pairs):
                to_pair(out, tensor, offset, part).start()
            return carry

        def relays(n, carry):
            part = lax.rem(s // each + n, parts)
            for offset in range(1, pairs):
                from_pair(out, tensor, offset, part).wait_recv()
                relay(out, tensor, offset, part).start()
            return carry

        lax.fori_loop(0, parts, receive, 0)
        lax.fori_loop(0, parts, relays, 0)

    def arrive(out, tensor):
        def one(part, carry):
            for offset in range(pairs):
                from_core(out, tensor, offset, part).wait_recv()
            return carry

        lax.fori_loop(0, parts, one, 0)

    def finish(move, out, tensor):
        def one(part, carry):
            to_core(out, tensor, part).wait_send()
            for offset in range(1, pairs):
                to_pair(out, tensor, offset, part).wait_send()
                relay(out, tensor, offset, part).wait_send()
            return carry

        lax.fori_loop(0, parts, one, 0)
        for n, (to, source, target, at) in enumerate(move.sends):
            @pl.when(jnp.logical_not(same(to, me)))
            def _():
                remote(
                    move.source.at[source], move.target.at[target],
                    move.send_sem.at[n], move.receive_sem.at[at], to,
                ).wait_send()

    blocks, _, piece, depth = x_rows.shape
    places = tp_size * piece
    width = q_w.shape[0]
    lanes = cos_ref.shape[2]
    output_copy = pltpu.make_async_copy(output_ref, output_out.at[t], output_sem)
    output_copy.start()
    turn = half_turn(width)
    q_turned[...] = plain_dot(turn, q_w[...]).astype(jnp.bfloat16)
    k_turned[...] = plain_dot(turn, k_w[...]).astype(jnp.bfloat16)
    square_ref[...] = jnp.zeros_like(square_ref)

    def tables(n, carry):
        angles = frequency_ref[...] * offset_ref[n]
        cos_ref[n] = jnp.concatenate([jnp.cos(angles)] * (2 * lanes // HD), axis=0).T
        sin_ref[n] = jnp.concatenate([jnp.sin(angles)] * (2 * lanes // HD), axis=0).T
        return carry

    lax.fori_loop(0, blocks, tables, 0)

    def x_load(n):
        source = x_out.at[n // seq_size, lax.rem(n, seq_size)]
        return pltpu.make_async_copy(source, x_rows.at[n], load_sem.at[n])

    def first_load(n):
        source = first_out.at[n // seq_size, lax.rem(n, seq_size)]
        return pltpu.make_async_copy(source, first_rows.at[n], load_sem.at[n])

    def start_loads(load):
        def one(n, carry):
            load(n).start()
            return carry

        lax.fori_loop(0, blocks, one, 0)

    def query_key(n, carry):
        x_load(n).wait()
        x = x_rows[n].reshape(places, depth).astype(jnp.float32)
        inverse = lax.rsqrt(jnp.mean(x * x, axis=-1, keepdims=True) + norm_eps)
        normed = (x * inverse * gain_ref[...]).astype(jnp.bfloat16)
        cosine, sine = widen(cos_ref[n], width), widen(sin_ref[n], width)
        q_ref[n] = (
            (rows_dot(normed, q_w[...]) * cosine + rows_dot(normed, q_turned[...]) * sine)
            * (HD ** (-0.5) * LOG2E)
        ).astype(jnp.bfloat16)
        k_ref[n] = (
            rows_dot(normed, k_w[...]) * cosine + rows_dot(normed, k_turned[...]) * sine
        ).astype(jnp.bfloat16)
        x_rows[n] = normed.reshape(x_rows.shape[1:])
        return carry

    def mix(n, carry):
        first_load(n).wait()
        first = first_rows[n].astype(jnp.float32)
        value = rows_dot(x_rows[n].reshape(places, depth), v_w[...])
        mixed = (0.5 * value + 0.5 * first.T).astype(jnp.bfloat16)
        v_ref[n] = mixed
        wide = mixed.astype(jnp.float32)
        square_ref[0:1, : first.shape[1]] += jnp.sum(first * first, axis=0, keepdims=True)
        square_ref[1:2, : wide.shape[1]] += jnp.sum(wide * wide, axis=0, keepdims=True)
        return carry

    forward(x_move, x_out, 0)
    to_core(output_out, 2, 0).start()
    for offset in range(1, pairs):
        to_pair(output_out, 2, offset, 0).start()
    arrive(x_out, 0)
    start_loads(x_load)
    lax.fori_loop(0, blocks, query_key, 0)
    first_move.wait_sends()
    first_move.wait_receives()
    start_loads(first_load)
    lax.fori_loop(0, blocks, mix, 0)
    for offset in range(1, pairs):
        from_pair(output_out, 2, offset, 0).wait_recv()
        relay(output_out, 2, offset, 0).start()
    forward(cot_move, cot_out, 1)
    arrive(cot_out, 1)
    for offset in range(pairs):
        from_core(output_out, 2, offset, 0).wait_recv()
    to_core(output_out, 2, 0).wait_send()
    for offset in range(1, pairs):
        to_pair(output_out, 2, offset, 0).wait_send()
        relay(output_out, 2, offset, 0).wait_send()
    finish(x_move, x_out, 0)
    finish(cot_move, cot_out, 1)
    output_copy.wait()


def half_turn(width):
    row = lax.broadcasted_iota(jnp.int32, (width, width), 0)
    column = lax.broadcasted_iota(jnp.int32, (width, width), 1)
    low = lax.rem(row, HD) < HD // 2
    minus = low & (column == row + HD // 2)
    plus = jnp.logical_not(low) & (column == row - HD // 2)
    return jnp.where(plus, 1.0, jnp.where(minus, -1.0, 0.0)).astype(jnp.bfloat16)


def spread(
    layer_input, cotangent, first_values, output_weight, query_weight, key_weight, value_weight,
    offsets, frequency, gain, sizes,
):
    seq_size, tp_size, rows_each, rows_local, parts = sizes
    pieces = layer_input.shape[2:]
    width, depth = query_weight.shape
    features, places = first_values.shape[1:]
    blocks = rows_each * seq_size
    lanes = min(width, 128)
    plans = (
        owner_to_quarter(seq_size, tp_size, rows_each, rows_local, False),
        owner_to_quarter(seq_size, tp_size, rows_each, rows_local, True),
        places_to_rows(seq_size, rows_each),
    )
    dma = pltpu.SemaphoreType.DMA
    quarter = [
        dma((rows_local * tp_size,)), dma((rows_local * tp_size,)), dma((rows_each * seq_size,)),
    ]
    stage = tp_size // 2 * parts * 3
    bf16, f32 = jnp.bfloat16, jnp.float32
    anywhere = pl.BlockSpec(memory_space=pl.ANY)
    vmem = pl.BlockSpec(memory_space=pltpu.VMEM)
    part = jax.ShapeDtypeStruct((blocks, places, width), bf16)
    table = jax.ShapeDtypeStruct((blocks, places, lanes), f32)
    return pl.pallas_call(
        functools.partial(spread_kernel, plans, sizes),
        out_shape=[
            jax.ShapeDtypeStruct((rows_each, seq_size, tp_size) + pieces, bf16),
            jax.ShapeDtypeStruct((tp_size, rows_each, seq_size) + pieces, bf16),
            jax.ShapeDtypeStruct((rows_each, seq_size, features, places), bf16),
            jax.ShapeDtypeStruct((tp_size,) + output_weight.shape, bf16),
            part,
            part,
            part,
            table,
            table,
            jax.ShapeDtypeStruct((8, max(width, places)), f32),
        ],
        in_specs=[anywhere] * 3 + [vmem] * 7,
        out_specs=[anywhere] * 4 + [vmem] * 6,
        scratch_shapes=[
            pltpu.VMEM((blocks, tp_size) + pieces, bf16),
            pltpu.VMEM((blocks, features, places), bf16),
            pltpu.VMEM((width, depth), bf16),
            pltpu.VMEM((width, depth), bf16),
        ]
        + quarter
        + quarter
        + [dma((seq_size,))] * 3
        + [dma((stage,))] * 5
        + [dma((blocks,)), dma],
        compiler_params=pltpu.CompilerParams(
            collective_id=5, has_side_effects=True, vmem_limit_bytes=67043328
        ),
        name="spread",
    )(
        layer_input, cotangent, first_values, output_weight, query_weight, key_weight,
        value_weight, offsets, frequency, gain,
    )


def widen(table, width):
    return jnp.concatenate([table] * (width // table.shape[1]), axis=1)


class Reduce:
    def __init__(self, place, full, core_in, pair_in, chunks, sems):
        self.seq, self.tp, self.pairs = place
        self.pair, self.core = self.tp // 2, lax.rem(self.tp, 2)
        self.other = self.pair * 2 + 1 - self.core
        self.full, self.core_in, self.pair_in = full, core_in, pair_in
        self.chunks = chunks
        self.core_send, self.core_recv, self.pair_send, self.pair_recv = sems

    def peer(self, offset):
        return lax.rem(self.pair + offset, self.pairs) * 2 + self.core

    def cut(self, ref, lead, c):
        return ref.at[lead, :, c]

    def to_core(self, offset, c):
        lead = lax.rem(self.pair + offset, self.pairs) * 2 + 1 - self.core
        at = offset * self.chunks + c
        return remote(
            self.cut(self.full, lead, c), self.cut(self.core_in, offset, c),
            self.core_send.at[at], self.core_recv.at[at], (self.seq, self.other),
        )

    def to_pair(self, offset, c):
        back = self.pairs - offset
        return remote(
            self.cut(self.full, self.peer(offset), c), self.cut(self.pair_in, back - 1, c),
            self.pair_send.at[offset * self.chunks + c],
            self.pair_recv.at[back * self.chunks + c], (self.seq, self.peer(offset)),
        )

    def from_pair(self, offset, c):
        view, at = self.cut(self.pair_in, offset - 1, c), offset * self.chunks + c
        return remote(
            view, view, self.pair_send.at[at], self.pair_recv.at[at], (self.seq, self.peer(offset))
        )

    def start(self, c):
        for offset in list(range(1, self.pairs)) + [0]:
            self.to_core(offset, c).start()

    def pass_on(self, c):
        for offset in range(1, self.pairs):
            self.to_core(offset, c).wait_recv()
            to = self.peer(offset)

            def add(b, carry):
                self.full[to, b, c] = (
                    self.full[to, b, c].astype(jnp.float32)
                    + self.core_in[offset, b, c].astype(jnp.float32)
                ).astype(jnp.bfloat16)
                return carry

            lax.fori_loop(0, self.full.shape[1], add, 0)
            self.to_pair(offset, c).start()

    def arrive(self, c):
        self.to_core(0, c).wait_recv()
        for offset in range(1, self.pairs):
            self.from_pair(offset, c).wait_recv()

    def total(self, b, c):
        value = self.full[self.tp, b, c].astype(jnp.float32)
        value = value + self.core_in[0, b, c].astype(jnp.float32)
        for offset in range(1, self.pairs):
            value = value + self.pair_in[offset - 1, b, c].astype(jnp.float32)
        return value

    def finish(self):
        for c in range(self.chunks):
            for offset in range(self.pairs):
                self.to_core(offset, c).wait_send()
            for offset in range(1, self.pairs):
                self.to_pair(offset, c).wait_send()


class SeqSum:
    def __init__(self, place, steps, done, blocks, held, mine, sums, local_sem, send_sem, recv_sem):
        self.seq, self.tp = place
        self.count, self.done, self.size = steps, done, 1 << steps
        self.blocks, self.held, self.mine, self.sums = blocks, held, mine, sums
        self.local_sem, self.send_sem, self.recv_sem = local_sem, send_sem, recv_sem
        self.flags = [lax.rem(self.seq // (1 << n), 2) for n in range(steps)]
        low, self.lows = 0, [0]
        for n in range(steps):
            low = low + self.flags[n] * (self.size >> (n + 1))
            self.lows.append(low)

    def partner(self, n):
        return (self.seq + (1 - 2 * self.flags[n]) * (1 << n), self.tp)

    def half(self, n):
        return self.size >> (n + 1)

    def begin(self, n):
        return (self.size >> self.done) - (self.size >> n)

    def give(self, n):
        half = self.half(n)
        low = self.lows[n] - self.lows[self.done] + (1 - self.flags[n]) * half
        return remote(
            self.blocks.at[pl.ds(low, half)], self.held.at[pl.ds(self.begin(n), half)],
            self.send_sem.at[n], self.recv_sem.at[n], self.partner(n),
        )

    def take(self, n):
        copy = self.give(n)
        copy.wait_recv()
        copy.wait_send()
        last = n + 1 == self.count

        def add(b, carry):
            at = self.lows[n + 1] - self.lows[self.done] + b
            value = (
                self.blocks[at].astype(jnp.float32)
                + self.held[self.begin(n) + b].astype(jnp.float32)
            ).astype(jnp.bfloat16)
            if last:
                self.mine[b] = value
            else:
                self.blocks[at] = value
            return carry

        lax.fori_loop(0, self.half(n), add, 0)

    def store(self):
        return pltpu.make_async_copy(
            self.mine, self.sums.at[pl.ds(self.lows[self.count], 1)], self.local_sem
        )

    def spread(self, n):
        target = self.sums.at[pl.ds(self.lows[n + 1], self.half(n))]
        source = self.mine if n + 1 == self.count else target
        at = self.count + n
        return remote(source, target, self.send_sem.at[at], self.recv_sem.at[at], self.partner(n))

    def collect(self, n):
        half = self.half(n)
        view = self.sums.at[pl.ds(self.lows[n] + (1 - self.flags[n]) * half, half)]
        at = self.count + n
        remote(view, view, self.send_sem.at[at], self.recv_sem.at[at], self.partner(n)).wait_recv()

    def steps(self):
        self.give(self.done).start()
        yield
        for n in range(self.done, self.count):
            self.take(n)
            if n + 1 < self.count:
                self.give(n + 1).start()
            else:
                self.spread(n).start()
                self.store().start()
            yield
        for n in range(self.count - 1, -1, -1):
            self.collect(n)
            if n + 1 == self.count:
                self.store().wait()
            if n > 0:
                self.spread(n - 1).start()
            yield
        for n in range(self.count):
            self.spread(n).wait_send()


def tail_kernel(
    sizes, dv_plan, out_hbm, keep_hbm, got_hbm, x_hbm, q_hbm, k_hbm, v_hbm, cos_hbm, sin_hbm,
    qw_hbm, kw_hbm, vw_hbm, attended_hbm, source_hbm, middle_hbm, middle_g_hbm, dv_hbm, gain_ref, small_ref,
    out_ref, input_g_ref, dv_ref, sums_ref, feed_ref, total_ref,
    x_rows, q_rows, k_rows, v_rows, cos_rows, sin_rows, weights, attended, grad_acc,
    normed_full, normed_core, normed_pair, proj_full, proj_core, proj_pair,
    out_full, out_core, out_pair, source, middle, middle_g, input_g, result,
    blocks, held, mine, feed_blocks, feed_got, feed_held, feed_mine,
    small, tp_held, tp_sum, seq_held,
    *sems,
):
    seq_size, tp_size, rows_each, rows_local, _ = sizes
    s, t = lax.axis_index("seq"), lax.axis_index("tp")
    me = (s, t)
    pairs = tp_size // 2
    count = seq_size.bit_length() - 1
    normed_sems, proj_sems, out_sems = sems[:4], sems[4:8], sems[8:12]
    dv_sems, back_sems, lo_sems = sems[12:15], sems[15:18], sems[18:21]
    load_sem, x_sem, feed_sem, store_sem, grad_send, grad_recv = sems[21:27]
    feed_send, feed_recv, small_send, tp_sem, seq_sem = sems[27:]
    place = (s, t, pairs)
    normed = Reduce(place, normed_full, normed_core, normed_pair, 2, normed_sems)
    proj = Reduce(place, proj_full, proj_core, proj_pair, 1, proj_sems)
    out = Reduce(place, out_full, out_core, out_pair, 2, out_sems)
    dv_move = Exchange(dv_plan, me, dv_hbm, dv_ref, *dv_sems)
    half = source.shape[0]
    places, depth = x_rows.shape[1:]
    width = q_rows.shape[2]

    group = group_of(s, seq_size)
    origins = []
    for slot in range(rows_local):
        row = t * rows_local + slot
        for i in range(tp_size):
            origins.append(((place_of(row // rows_each, seq_size), i), (slot, i), slot * tp_size + i))

    tp_peers = [lax.rem(t + i, tp_size) for i in range(1, tp_size)]
    seq_peers = [lax.rem(s + i, seq_size) for i in range(1, seq_size)]

    names = (
        (q_hbm, q_rows), (k_hbm, k_rows), (v_hbm, v_rows), (cos_hbm, cos_rows),
        (sin_hbm, sin_rows), (qw_hbm, weights.at[pl.ds(0, width)]),
        (kw_hbm, weights.at[pl.ds(width, width)]), (vw_hbm, weights.at[pl.ds(2 * width, width)]),
        (out_hbm, out_full), (attended_hbm, attended),
        (middle_g_hbm, middle_g), (source_hbm, source), (middle_hbm, middle),
    )
    loads = [
        pltpu.make_async_copy(origin, target, load_sem.at[n])
        for n, (origin, target) in enumerate(names)
    ]
    feed_loads = [
        (
            pltpu.make_async_copy(keep_hbm.at[n], feed_blocks.at[n], feed_sem.at[2 * n]),
            pltpu.make_async_copy(got_hbm.at[n], feed_got.at[n], feed_sem.at[2 * n + 1]),
        )
        for n in range(3)
    ]

    def x_load(n):
        return pltpu.make_async_copy(x_hbm.at[n], x_rows.at[n], x_sem.at[n])

    def ordered(n):
        return 2 * lax.rem(n, half) + n // half

    for pair in feed_loads:
        for copy in pair:
            copy.start()
    loads[8].start()
    for copy in loads[:8]:
        copy.start()
    for n in range(2 * half):
        x_load(ordered(n)).start()
    for copy in loads[9:]:
        copy.start()

    barrier = pltpu.get_barrier_semaphore()
    dv_move.greet(barrier)
    for origin, _, _ in origins:
        @pl.when(jnp.logical_not(same(origin, me)))
        def _():
            pl.semaphore_signal(barrier, inc=1, device_id=origin, device_id_type=MESH)
    for to in tp_peers:
        pl.semaphore_signal(barrier, inc=1, device_id=(s, to), device_id_type=MESH)
    for to in seq_peers:
        pl.semaphore_signal(barrier, inc=1, device_id=(to, t), device_id_type=MESH)
    back_others = sum(
        jnp.where(same((to, (group * rows_each + j) // rows_local), me), 0, 1)
        for j in range(rows_each)
        for to in range(seq_size)
    )
    pl.semaphore_wait(barrier, dv_move.others() + back_others + tp_size + seq_size - 2)

    def seq_sum(n, done, *refs):
        return SeqSum(
            me, count, done, *refs, store_sem.at[n],
            (grad_send if done == 0 else feed_send).at[n if done == 0 else n - 2],
            (grad_recv if done == 0 else feed_recv).at[n if done == 0 else n - 2],
        ).steps()

    sums = [
        seq_sum(n, 0, blocks.at[n], held.at[n], mine.at[n], sums_ref.at[n]) for n in range(2)
    ]
    feeds = [
        seq_sum(
            n + 2, 1, feed_blocks.at[n], feed_held.at[n], feed_mine.at[n], feed_ref.at[n]
        )
        for n in range(3)
    ]

    for n in range(3):
        for copy in feed_loads[n]:
            copy.wait()

        def join(b, carry):
            feed_blocks[n, b] = (
                feed_blocks[n, b].astype(jnp.float32) + feed_got[n, b].astype(jnp.float32)
            ).astype(jnp.bfloat16)
            return carry

        lax.fori_loop(0, feed_blocks.shape[1], join, 0)
        next(feeds[n])
    loads[8].wait()
    out.start(0)
    out.start(1)
    dv_move.start()
    for copy in loads[:8]:
        copy.wait()
    turn = half_turn(width)
    grad_acc[...] = jnp.zeros_like(grad_acc)
    gain = gain_ref[...]

    def project_back(first, last):
        def one(n, carry):
            at = ordered(n)
            x_load(at).wait()
            x = x_rows[at].astype(jnp.float32)
            inverse = lax.rsqrt(jnp.mean(x * x, axis=-1, keepdims=True) + norm_eps)
            rows = (x * inverse * gain).astype(jnp.bfloat16)
            cosine, sine = widen(cos_rows[at], width), widen(sin_rows[at], width)

            def unrotate(grad):
                turned = plain_dot(grad, turn)
                return (grad.astype(jnp.float32) * cosine + turned * sine).astype(jnp.bfloat16)

            stacked = jnp.concatenate(
                [
                    unrotate(q_rows[at]),
                    unrotate(k_rows[at]),
                    (0.5 * v_rows[at].astype(jnp.float32)).astype(jnp.bfloat16),
                ],
                axis=1,
            )
            b, c = at // 2, lax.rem(at, 2)
            product = plain_dot(stacked, weights[...])
            for i in range(tp_size):
                piece = places // tp_size
                normed_full[i, b, c] = product[i * piece : (i + 1) * piece].astype(jnp.bfloat16)
            grad_acc[...] += columns_dot(stacked, rows)
            return carry

        lax.fori_loop(first, last, one, 0)

    quarter = half // 2
    project_back(0, quarter)
    out.pass_on(0)
    out.pass_on(1)
    next(feeds[0])
    project_back(quarter, half)
    normed.start(0)
    next(feeds[1])
    project_back(half, half + quarter)
    normed.pass_on(0)
    next(feeds[2])
    next(feeds[0])
    project_back(half + quarter, 2 * half)
    normed.start(1)
    fine = blocks.shape[2]
    for n in range(3 * seq_size // 2):
        blocks[n // seq_size, n % seq_size] = grad_acc[n * fine : (n + 1) * fine].astype(
            jnp.bfloat16
        )
    next(sums[0])
    next(feeds[1])
    loads[9].wait()
    loads[10].wait()
    branch = middle_g[...].reshape(2 * half * middle_g.shape[2], depth).astype(jnp.bfloat16)
    for i in range(tp_size):
        product = columns_dot(attended[i], branch)
        for n in range(seq_size // 2):
            proj_full[i, n, 0] = product[n * fine : (n + 1) * fine].astype(jnp.bfloat16)
    proj.start(0)
    normed.pass_on(1)
    proj.pass_on(0)
    next(feeds[2])
    next(feeds[0])

    def send_back(source_ref, target, trio, b, c, wait):
        local_sem, send_sem, recv_sem = trio
        flat = 2 * b + c
        j, to = flat // seq_size, lax.rem(flat, seq_size)
        row = group * rows_each + j
        slot = lax.rem(row, rows_local)
        place = (to, row // rows_local)
        here = same(place, me)
        view = target.at[slot, t]

        @pl.when(here)
        def _():
            copy = pltpu.make_async_copy(source_ref.at[b, c], view, local_sem.at[flat])
            copy.wait() if wait else copy.start()

        @pl.when(jnp.logical_not(here))
        def _():
            copy = remote(
                source_ref.at[b, c], view, send_sem.at[flat], recv_sem.at[slot * tp_size + t], place
            )
            copy.wait_send() if wait else copy.start()

    small[...] = small_ref[...]

    def back(c):
        normed.arrive(c)

        def one(n, carry):
            b = lax.rem(n + s // 2, half)
            grads = normed.total(b, c)
            x = source[b, c].astype(jnp.float32)
            inverse = lax.rsqrt(jnp.mean(x * x, axis=-1, keepdims=True) + norm_eps)
            unit = x * inverse
            scaled = grads * gain
            extra = inverse * (scaled - unit * jnp.mean(scaled * unit, axis=-1, keepdims=True))
            input_g[b, c] = (middle_g[b, c] + extra).astype(jnp.bfloat16)
            small[0:1, :] += jnp.sum(grads * unit, axis=0, keepdims=True)
            send_back(input_g, input_g_ref, back_sems, b, c, False)
            return carry

        lax.fori_loop(0, half, one, 0)

    def forward(c):
        out.arrive(c)

        def one(n, carry):
            b = lax.rem(n + s // 2, half)
            result[b, c] = (middle[b, c] + out.total(b, c)).astype(jnp.bfloat16)
            send_back(result, out_ref, lo_sems, b, c, False)
            return carry

        lax.fori_loop(0, half, one, 0)

    def tp_copy(n):
        return remote(
            small, tp_held.at[tp_size - n], small_send.at[n],
            tp_sem.at[tp_size - n], (s, tp_peers[n - 1]),
        )

    def seq_copy(n):
        return remote(
            tp_sum, seq_held.at[seq_size - n], small_send.at[tp_size + n],
            seq_sem.at[seq_size - n], (seq_peers[n - 1], t),
        )

    def all_steps(generators):
        for generator in generators:
            next(generator, None)

    loads[12].wait()
    forward(0)
    forward(1)
    next(feeds[1])
    loads[11].wait()
    back(0)
    proj.arrive(0)

    def put(b, carry):
        blocks[1, seq_size // 2 + b] = proj.total(b, 0).astype(jnp.bfloat16)
        return carry

    lax.fori_loop(0, seq_size // 2, put, 0)
    next(sums[1])
    next(sums[0])
    next(feeds[2])
    back(1)
    for n in range(1, tp_size):
        tp_copy(n).start()
    all_steps([feeds[0], sums[0], sums[1]])
    for n in range(1, tp_size):
        tp_copy(n).wait()
    tp_held[0] = small[...]
    total = tp_held[lax.rem(tp_size - t, tp_size)]
    for n in range(1, tp_size):
        total = total + tp_held[lax.rem(n + tp_size - t, tp_size)]
    tp_sum[...] = total
    for n in range(1, seq_size):
        seq_copy(n).start()
    seq_held[0] = total
    for _ in range(2 * count):
        all_steps([feeds[1], sums[0], feeds[2], sums[1], feeds[0]])
    for generator in sums + feeds:
        for _ in generator:
            pass
    for n in range(1, seq_size):
        seq_copy(n).wait()
    total = seq_held[lax.rem(seq_size - s, seq_size)]
    for n in range(1, seq_size):
        total = total + seq_held[lax.rem(n + seq_size - s, seq_size)]
    total_ref[...] = total

    for reduce in (normed, proj, out):
        reduce.finish()
    for c in range(2):
        def done(b, carry):
            send_back(input_g, input_g_ref, back_sems, b, c, True)
            send_back(result, out_ref, lo_sems, b, c, True)
            return carry

        lax.fori_loop(0, half, done, 0)
    dv_move.wait_sends()
    dv_move.wait_receives()
    for origin, target, at in origins:
        @pl.when(jnp.logical_not(same(origin, me)))
        def _():
            for ref, trio in ((input_g_ref, back_sems), (out_ref, lo_sems)):
                view = ref.at[target]
                remote(view, view, trio[1].at[0], trio[2].at[at], origin).wait_recv()


def tail(
    out_part, keep, got, x_rows, query_g, key_g, value_g, cosine, sine, query_weight, key_weight, value_weight,
    attended, source, middle, middle_g, gain, small, sizes,
):
    seq_size, tp_size, rows_each, rows_local, _ = sizes
    pairs = tp_size // 2
    blocks = rows_each * seq_size
    tokens, depth = source.shape
    piece = tokens // blocks
    width = query_g.shape[-1]
    places = x_rows.shape[0] // blocks
    lanes = cosine.shape[2]
    fine = 2 * width // seq_size
    bf16, f32 = jnp.bfloat16, jnp.float32
    shape = (blocks // 2, 2, piece, depth)
    proj_shape = (width // fine, 1, fine, depth)
    hidden = 2 * keep.shape[1] // seq_size
    feed_shape = (3, seq_size // 2, hidden, depth)
    anywhere = pl.BlockSpec(memory_space=pl.ANY)
    vmem = pl.BlockSpec(memory_space=pltpu.VMEM)
    dma = pltpu.SemaphoreType.DMA
    plan = rows_to_places(seq_size, rows_each)
    steps = seq_size.bit_length() - 1
    owned = jax.ShapeDtypeStruct((rows_local, tp_size, piece, depth), bf16)

    def reduce_shapes(part):
        return [
            pltpu.VMEM((tp_size,) + part, bf16),
            pltpu.VMEM((pairs,) + part, bf16),
            pltpu.VMEM((pairs - 1,) + part, bf16),
        ]

    def reduce_sems(chunks):
        return [dma((pairs * chunks,))] * 4

    return pl.pallas_call(
        functools.partial(tail_kernel, sizes, plan),
        out_shape=[
            owned,
            owned,
            jax.ShapeDtypeStruct((rows_each * seq_size, places, width), bf16),
            jax.ShapeDtypeStruct((2, seq_size, fine, depth), bf16),
            jax.ShapeDtypeStruct((3, seq_size, hidden, depth), bf16),
            jax.ShapeDtypeStruct(small.shape, f32),
        ],
        in_specs=[anywhere] * 17 + [vmem] * 2,
        out_specs=[anywhere] * 5 + [vmem],
        scratch_shapes=[
            pltpu.VMEM((blocks, places, depth), bf16),
            pltpu.VMEM((blocks, places, width), bf16),
            pltpu.VMEM((blocks, places, width), bf16),
            pltpu.VMEM((blocks, places, width), bf16),
            pltpu.VMEM((blocks, places, lanes), f32),
            pltpu.VMEM((blocks, places, lanes), f32),
            pltpu.VMEM((3 * width, depth), bf16),
            pltpu.VMEM(attended.shape, bf16),
            pltpu.VMEM((3 * width, depth), f32),
        ]
        + reduce_shapes(shape)
        + reduce_shapes(proj_shape)
        + reduce_shapes(shape)
        + [
            pltpu.VMEM(shape, bf16),
            pltpu.VMEM(shape, f32),
            pltpu.VMEM(shape, f32),
            pltpu.VMEM(shape, bf16),
            pltpu.VMEM(shape, bf16),
            pltpu.VMEM((2, seq_size, fine, depth), bf16),
            pltpu.VMEM((2, seq_size, fine, depth), bf16),
            pltpu.VMEM((2, 1, fine, depth), bf16),
            pltpu.VMEM(feed_shape, bf16),
            pltpu.VMEM(feed_shape, bf16),
            pltpu.VMEM(feed_shape, bf16),
            pltpu.VMEM((3, 1, hidden, depth), bf16),
            pltpu.VMEM(small.shape, f32),
            pltpu.VMEM((tp_size,) + small.shape, f32),
            pltpu.VMEM(small.shape, f32),
            pltpu.VMEM((seq_size,) + small.shape, f32),
        ]
        + reduce_sems(2)
        + reduce_sems(1)
        + reduce_sems(2)
        + [dma((seq_size,))] * 3
        + ([dma((blocks,))] * 2 + [dma((rows_local * tp_size,))]) * 2
        + [
            dma((13,)),
            dma((blocks,)),
            dma((6,)),
            dma((5,)),
            dma((2, 2 * steps)),
            dma((2, 2 * steps)),
            dma((3, 2 * steps)),
            dma((3, 2 * steps)),
            dma((tp_size + seq_size,)),
            dma((tp_size,)),
            dma((seq_size,)),
        ],
        compiler_params=pltpu.CompilerParams(
            collective_id=6, has_side_effects=True, vmem_limit_bytes=67043328
        ),
        name="tail",
    )(
        out_part.reshape((tp_size,) + shape),
        keep.reshape(feed_shape),
        got.reshape(feed_shape),
        x_rows.reshape(blocks, places, depth),
        query_g.reshape(blocks, places, width),
        key_g.reshape(blocks, places, width),
        value_g.reshape(blocks, places, width),
        cosine,
        sine,
        query_weight,
        key_weight,
        value_weight,
        attended,
        source.reshape(shape),
        middle.reshape(shape),
        middle_g.reshape(shape),
        value_g.reshape(rows_each, seq_size, places, width),
        gain,
        small,
    )


def shards(
    layer_input,
    first_values,
    doc_lengths,
    attn_gain,
    query_weight,
    key_weight,
    value_weight,
    output_weight,
    feed_gain,
    gate_weight,
    up_weight,
    down_weight,
    out_cotangent,
):
    seq_size = lax.axis_size("seq")
    tp_size = lax.axis_size("tp")
    rows_local, local_len, depth = layer_input.shape
    row_count = first_values.shape[0]
    width = query_weight.shape[0]
    rows_each = row_count // seq_size
    piece = local_len // tp_size
    tokens = rows_each * seq_size * piece
    sizes = (seq_size, tp_size, rows_each, rows_local, 4)
    me = lax.axis_index("tp")
    my_rows = group_of(lax.axis_index("seq"), seq_size) * rows_each

    _, offsets = doc_layout(doc_lengths)
    offsets = lax.dynamic_slice_in_dim(offsets, my_rows, rows_each, 0)
    starts = jnp.arange(ROW, dtype=jnp.int32)[None, :] - offsets
    low = (starts[:, ::BLOCK] // BLOCK).reshape(-1)
    starts = starts[:, None, :]
    half_dim = HD // 2
    frequency = rope_base ** (-jnp.arange(half_dim, dtype=jnp.float32) * 2.0 / HD)
    attn_scale = attn_gain.astype(jnp.float32)[None, :]
    feed_scale = feed_gain.astype(jnp.float32)[None, :]
    (
        x_rows, cot_all, _, output_full, queries, keys, values, cosine, sine, squares,
    ) = spread(
        layer_input.reshape(rows_local, tp_size, piece, depth),
        out_cotangent.reshape(rows_local, tp_size, piece, depth),
        first_values,
        output_weight,
        query_weight,
        key_weight,
        value_weight,
        offsets.astype(jnp.float32).reshape(rows_each * seq_size, 1, local_len),
        frequency[:, None],
        attn_scale,
        sizes,
    )
    output_full = output_full.reshape(tp_size * width, depth)
    source_low = lax.dynamic_index_in_dim(x_rows, me, 2, keepdims=False).reshape(tokens, depth)
    source = source_low.astype(jnp.float32)
    cotangent = lax.dynamic_index_in_dim(cot_all, me, 0, keepdims=False).reshape(tokens, depth)
    cotangent = cotangent.astype(jnp.float32)
    x_rows = x_rows.reshape(rows_each * ROW, depth)
    queries, keys, values = (
        part.reshape(rows_each, ROW, width) for part in (queries, keys, values)
    )
    result, logsum = attend(low, queries, keys, values, starts)
    by_piece = (rows_each, seq_size, tp_size, piece, width)
    by_head = (tp_size, rows_each, seq_size, piece, width)
    (pieces,) = exchange([result.reshape(by_piece)], [by_head], [heads_to_tokens(tp_size)], 1)
    attended = jnp.transpose(pieces.reshape(tp_size, tokens, width), (1, 0, 2)).reshape(tokens, -1)
    middle = source + jnp.dot(attended, output_full, preferred_element_type=jnp.float32)
    unit_feed, inv_feed = norm_rows(middle)
    feed_in = (unit_feed * feed_scale).astype(jnp.bfloat16)
    feed_in_g, out_part, keep, give = feed_forward(
        feed_in, cot_all.reshape(tp_size, tokens, depth), gate_weight.T, up_weight.T, down_weight
    )
    got = lax.ppermute(give, "seq", [(n, n + 1 - 2 * (n % 2)) for n in range(seq_size)])
    middle_extra, feed_gain_part = norm_back(feed_in_g, unit_feed, inv_feed, feed_scale)
    middle_g = cotangent + middle_extra
    branch_g = middle_g.astype(jnp.bfloat16)
    attended_g = jnp.einsum(
        "td,ed->te", branch_g, output_full, preferred_element_type=jnp.float32
    ).astype(jnp.bfloat16)
    (attended_g,) = exchange(
        [jnp.transpose(attended_g.reshape(tokens, tp_size, width), (1, 0, 2)).reshape(by_head)],
        [by_piece],
        [tokens_to_heads(tp_size)],
        2,
    )
    query_g, key_g, value_g = attend_back(
        low, queries, keys, values, result, attended_g.reshape(result.shape), logsum, starts
    )
    squares = jnp.pad(jnp.sum(squares, axis=1)[:2], (0, depth - 2))
    small = jnp.stack([jnp.zeros_like(squares), feed_gain_part, squares])
    layer_output, input_grad, value_own_g, grad_sums, feed_sums, small = tail(
        out_part,
        keep,
        got,
        x_rows,
        query_g,
        key_g,
        value_g,
        cosine,
        sine,
        query_weight,
        key_weight,
        value_weight,
        pieces.reshape(tp_size, tokens, width),
        source_low,
        middle,
        middle_g,
        attn_scale,
        jnp.pad(small, ((0, 5), (0, 0))),
        sizes,
    )
    first_grad = jnp.swapaxes(0.5 * value_own_g.astype(jnp.float32), 1, 2)
    grad_sums = grad_sums.reshape(4 * width, depth).astype(jnp.float32)
    feed_sums = feed_sums.reshape(3, -1, depth).astype(jnp.float32)
    return (
        layer_output.reshape(layer_input.shape),
        input_grad.reshape(layer_input.shape),
        first_grad,
        small[0],
        grad_sums[:width],
        grad_sums[width : 2 * width],
        grad_sums[2 * width : 3 * width],
        grad_sums[3 * width :],
        small[1],
        feed_sums[0].T,
        feed_sums[1].T,
        feed_sums[2],
        jnp.sqrt(small[2, :2]),
    )


def solution(mesh):
    placed = (
        P("tp", "seq", None),
        P(None, "tp", "seq"),
        P(),
        P(),
        P("tp", None),
        P("tp", None),
        P("tp", None),
        P("tp", None),
        P(),
        P(None, "tp"),
        P(None, "tp"),
        P("tp", None),
        P("tp", "seq", None),
    )
    return jax.shard_map(
        shards,
        mesh=mesh,
        in_specs=placed,
        out_specs=(
            P("tp", "seq", None),
            P("tp", "seq", None),
            P(None, "tp", "seq"),
            P(),
            P("tp", None),
            P("tp", None),
            P("tp", None),
            P("tp", None),
            P(),
            P(None, "tp"),
            P(None, "tp"),
            P("tp", None),
            P(),
        ),
        check_vma=False,
    )
```

```python
import functools
import math

import jax
import jax.numpy as jnp
from jax import lax
from jax.experimental import pallas as pl
from jax.experimental.pallas import tpu as pltpu
from jax.sharding import PartitionSpec as P

HD = 64
ROW = 2048
BLOCK = 256
LOG2E = math.log2(math.e)
LN2 = math.log(2.0)
MESH = pl.DeviceIdType.MESH


norm_eps = 1e-06
rope_base = 10000.0
masked_score = -1e30


def doc_layout(doc_lengths):
    doc_ends = jnp.cumsum(doc_lengths, axis=-1)
    places = jnp.arange(ROW, dtype=jnp.int32)
    passed = doc_ends[:, None, :] <= places[None, :, None]
    segment = jnp.sum(passed.astype(jnp.int32), axis=-1)
    starts = jnp.max(jnp.where(passed, doc_ends[:, None, :], 0), axis=-1)
    return (segment, places[None, :] - starts)


def norm_rows(values_in):
    inverse = lax.rsqrt(jnp.mean(values_in * values_in, axis=-1, keepdims=True) + norm_eps)
    return (values_in * inverse, inverse)


def norm_back(grads_in, unit_rows, inverse, gain):
    scaled = grads_in * gain
    extra = inverse * (scaled - unit_rows * jnp.mean(scaled * unit_rows, axis=-1, keepdims=True))
    return (extra, jnp.sum(grads_in * unit_rows, axis=0))


def rows_dot(left, right):
    return lax.dot_general(left, right, (((1,), (1,)), ((), ())), preferred_element_type=jnp.float32)


def plain_dot(left, right):
    return lax.dot_general(left, right, (((1,), (0,)), ((), ())), preferred_element_type=jnp.float32)


def head_masked(block, head, heads):
    if heads == 1:
        return block
    lanes = lax.broadcasted_iota(jnp.int32, block.shape, 1)
    return jnp.where(lanes // HD == head, block, jnp.zeros_like(block))


def lane_group(head, width):
    lanes = min(width, 128)
    return slice(head * HD // lanes * lanes, head * HD // lanes * lanes + lanes), head % (lanes // HD)


def attend_kernel(low_ref, q_ref, k_ref, v_ref, start_ref, o_ref, lse_ref, v_cols):
    row = pl.program_id(0)
    length, width = q_ref.shape[1:]
    heads = width // HD
    together = min(width, 128) // HD
    blocks = length // BLOCK
    for j in range(blocks):
        v_cols[:, j * BLOCK : (j + 1) * BLOCK] = v_ref[0, j * BLOCK : (j + 1) * BLOCK, :].T

    def query_block(i, carry):
        first = pl.multiple_of(i * BLOCK, BLOCK)
        q_heads = []
        for h in range(heads):
            lanes, at = lane_group(h, width)
            q_heads.append(head_masked(q_ref[0, pl.ds(first, BLOCK), lanes], at, together))
        start = start_ref[0, :, pl.ds(first, BLOCK)]
        places = first + lax.broadcasted_iota(jnp.int32, (1, BLOCK), 1)

        def key_block(j, state):
            at = pl.multiple_of(j * BLOCK, BLOCK)
            keys = at + lax.broadcasted_iota(jnp.int32, (BLOCK, BLOCK), 0)
            allowed = (keys >= start) & (keys <= places)
            scores = [
                rows_dot(k_ref[0, pl.ds(at, BLOCK), lane_group(h, width)[0]], q_heads[h])
                for h in range(heads)
            ]
            out = []
            for h in range(heads):
                top, total, acc = state[h]
                masked = jnp.where(allowed, scores[h], masked_score)
                new_top = jnp.maximum(top, jnp.max(masked, axis=0, keepdims=True))
                weights = jnp.exp2(masked - new_top)
                shrink = jnp.exp2(top - new_top)
                total = total * shrink + jnp.sum(weights, axis=0, keepdims=True)
                acc = acc * shrink + plain_dot(
                    v_cols[h * HD : (h + 1) * HD, pl.ds(at, BLOCK)], weights.astype(jnp.bfloat16)
                )
                out.append((new_top, total, acc))
            return tuple(out)

        begin = tuple(
            (
                jnp.full((1, BLOCK), masked_score, jnp.float32),
                jnp.zeros((1, BLOCK), jnp.float32),
                jnp.zeros((HD, BLOCK), jnp.float32),
            )
            for _ in range(heads)
        )
        state = key_block(i, begin)
        state = lax.fori_loop(low_ref[row * blocks + i], i, key_block, state)
        columns = jnp.concatenate([acc / total for _, total, acc in state], axis=0)
        o_ref[0, pl.ds(first, BLOCK), :] = columns.T.astype(jnp.bfloat16)
        for h in range(heads):
            top, total, _ = state[h]
            lse_ref[0, pl.ds(h, 1), pl.ds(first, BLOCK)] = top + jnp.log2(total)
        return carry

    lax.fori_loop(0, blocks, query_block, 0)


def attend(low, queries, keys, values, starts):
    rows, length, width = queries.shape
    heads = width // HD
    wide = pl.BlockSpec((1, length, width), lambda r, low: (r, 0, 0))
    return pl.pallas_call(
        attend_kernel,
        grid_spec=pltpu.PrefetchScalarGridSpec(
            num_scalar_prefetch=1,
            grid=(rows,),
            in_specs=[wide, wide, wide, pl.BlockSpec((1, 1, length), lambda r, low: (r, 0, 0))],
            out_specs=[wide, pl.BlockSpec((1, heads, length), lambda r, low: (r, 0, 0))],
            scratch_shapes=[pltpu.VMEM((width, length), jnp.bfloat16)],
        ),
        out_shape=[
            jax.ShapeDtypeStruct(queries.shape, jnp.bfloat16),
            jax.ShapeDtypeStruct((rows, heads, length), jnp.float32),
        ],
        compiler_params=pltpu.CompilerParams(vmem_limit_bytes=67043328),
        name="attend",
    )(low, queries, keys, values, starts)


def attend_back_kernel(
    low_ref, q_ref, k_ref, v_ref, o_ref, g_ref, lse_ref, start_ref,
    qg_ref, kg_ref, vg_ref, k_cols, k_acc, v_acc,
):
    row = pl.program_id(0)
    length, width = q_ref.shape[1:]
    heads = width // HD
    together = min(width, 128) // HD
    blocks = length // BLOCK
    for j in range(blocks):
        k_cols[:, j * BLOCK : (j + 1) * BLOCK] = k_ref[0, j * BLOCK : (j + 1) * BLOCK, :].T
    k_acc[...] = jnp.zeros_like(k_acc)
    v_acc[...] = jnp.zeros_like(v_acc)
    select = (
        lax.broadcasted_iota(jnp.int32, (8, width), 1) // HD
        == lax.broadcasted_iota(jnp.int32, (8, width), 0)
    ).astype(jnp.float32)

    def query_block(i, carry):
        first = pl.multiple_of(i * BLOCK, BLOCK)
        q_heads, g_heads = [], []
        for h in range(heads):
            lanes, at = lane_group(h, width)
            q_heads.append(head_masked(q_ref[0, pl.ds(first, BLOCK), lanes], at, together))
            g_heads.append(head_masked(g_ref[0, pl.ds(first, BLOCK), lanes], at, together))
        product = g_ref[0, pl.ds(first, BLOCK), :].astype(jnp.float32) * o_ref[
            0, pl.ds(first, BLOCK), :
        ].astype(jnp.float32)
        centre = lax.dot_general(
            select, product, (((1,), (1,)), ((), ())),
            precision=lax.Precision.HIGHEST, preferred_element_type=jnp.float32,
        )
        lse = lse_ref[0, :, pl.ds(first, BLOCK)]
        start = start_ref[0, :, pl.ds(first, BLOCK)]
        places = first + lax.broadcasted_iota(jnp.int32, (1, BLOCK), 1)

        def key_block(j, state):
            at = pl.multiple_of(j * BLOCK, BLOCK)
            keys = at + lax.broadcasted_iota(jnp.int32, (BLOCK, BLOCK), 0)
            allowed = (keys >= start) & (keys <= places)
            scores, prob_gs = [], []
            for h in range(heads):
                lanes, _ = lane_group(h, width)
                scores.append(rows_dot(k_ref[0, pl.ds(at, BLOCK), lanes], q_heads[h]))
                prob_gs.append(rows_dot(v_ref[0, pl.ds(at, BLOCK), lanes], g_heads[h]))
            out = []
            for h in range(heads):
                lanes, _ = lane_group(h, width)
                probs = jnp.exp2(jnp.where(allowed, scores[h], masked_score) - lse[h : h + 1, :])
                score_g = (probs * (prob_gs[h] - centre[h : h + 1, :])).astype(jnp.bfloat16)
                v_acc[pl.ds(at, BLOCK), lanes] += plain_dot(probs.astype(jnp.bfloat16), g_heads[h])
                k_acc[pl.ds(at, BLOCK), lanes] += plain_dot(score_g, q_heads[h])
                out.append(
                    state[h] + plain_dot(k_cols[h * HD : (h + 1) * HD, pl.ds(at, BLOCK)], score_g)
                )
            return tuple(out)

        begin = tuple(jnp.zeros((HD, BLOCK), jnp.float32) for _ in range(heads))
        state = lax.fori_loop(low_ref[row * blocks + i], i + 1, key_block, begin)
        columns = jnp.concatenate(state, axis=0) * HD ** (-0.5)
        qg_ref[0, pl.ds(first, BLOCK), :] = columns.T.astype(jnp.bfloat16)
        return carry

    lax.fori_loop(0, blocks, query_block, 0)
    kg_ref[0] = (k_acc[...] * LN2).astype(jnp.bfloat16)
    vg_ref[0] = v_acc[...].astype(jnp.bfloat16)


def attend_back(low, queries, keys, values, attended, grads, lse, starts):
    rows, length, width = queries.shape
    heads = width // HD
    wide = pl.BlockSpec((1, length, width), lambda r, low: (r, 0, 0))
    return pl.pallas_call(
        attend_back_kernel,
        grid_spec=pltpu.PrefetchScalarGridSpec(
            num_scalar_prefetch=1,
            grid=(rows,),
            in_specs=[wide] * 5
            + [
                pl.BlockSpec((1, heads, length), lambda r, low: (r, 0, 0)),
                pl.BlockSpec((1, 1, length), lambda r, low: (r, 0, 0)),
            ],
            out_specs=[wide] * 3,
            scratch_shapes=[
                pltpu.VMEM((width, length), jnp.bfloat16),
                pltpu.VMEM((length, width), jnp.float32),
                pltpu.VMEM((length, width), jnp.float32),
            ],
        ),
        out_shape=[jax.ShapeDtypeStruct(queries.shape, jnp.bfloat16)] * 3,
        compiler_params=pltpu.CompilerParams(vmem_limit_bytes=67043328),
        name="attend_back",
    )(low, queries, keys, values, attended, grads, lse, starts)


def columns_dot(left, right):
    return lax.dot_general(left, right, (((0,), (0,)), ((), ())), preferred_element_type=jnp.float32)


def feed_kernel(
    chunk, feed_ref, cot_ref, gate_w, up_w, down_w,
    feed_g_ref, out_ref, keep_ref, give_ref,
    feed_all, part, core_in, pair_in, acc,
    feed_send, feed_core, feed_pair, relay_send, part_send, part_core, sum_send, sum_pair,
):
    tokens = feed_ref.shape[0]
    chunks = tokens // chunk
    seq = lax.axis_index("seq")
    me = lax.axis_index("tp")
    pairs = lax.axis_size("tp") // 2
    pair, core = me // 2, lax.rem(me, 2)
    other = pair * 2 + 1 - core

    def peer(offset):
        return lax.rem(pair + offset, pairs) * 2 + core

    def copy(source, target, send, receive, to):
        return pltpu.make_async_remote_copy(
            src_ref=source, dst_ref=target, send_sem=send, recv_sem=receive,
            device_id=(seq, to), device_id_type=MESH,
        )

    barrier = pltpu.get_barrier_semaphore()
    for to in [other] + [peer(offset) for offset in range(1, pairs)]:
        pl.semaphore_signal(barrier, inc=1, device_id=(seq, to), device_id_type=MESH)
    pl.semaphore_wait(barrier, pairs)

    def rows(c):
        return pl.ds(pl.multiple_of(c * chunk, chunk), chunk)

    def feed_to_core(c):
        return copy(
            feed_ref.at[rows(c)], feed_all.at[me, rows(c)],
            feed_send.at[c], feed_core.at[c], other,
        )

    def feed_to_pair(offset, c):
        return copy(
            feed_ref.at[rows(c)], feed_all.at[me, rows(c)],
            feed_send.at[offset * chunks + c],
            feed_pair.at[(pairs - offset) * chunks + c], peer(offset),
        )

    def feed_from_pair(offset, c):
        return copy(
            feed_all.at[peer(offset), rows(c)], feed_all.at[peer(offset), rows(c)],
            feed_send.at[0], feed_pair.at[offset * chunks + c], other,
        )

    def relay(offset, c):
        return copy(
            feed_all.at[peer(offset), rows(c)], feed_all.at[peer(offset), rows(c)],
            relay_send.at[offset * chunks + c], feed_core.at[offset * chunks + c], other,
        )

    def part_to_core(offset, c):
        at = lax.rem(pair + offset, pairs) * 2 + 1 - core
        return copy(
            part.at[at, rows(c)], core_in.at[offset, rows(c)],
            part_send.at[offset * chunks + c], part_core.at[offset * chunks + c], other,
        )

    def sum_to_pair(offset, c):
        return copy(
            part.at[peer(offset), rows(c)], pair_in.at[pairs - offset, rows(c)],
            sum_send.at[offset * chunks + c],
            sum_pair.at[(pairs - offset) * chunks + c], peer(offset),
        )

    for c in range(chunks):
        feed_to_core(c).start()
        for offset in range(1, pairs):
            feed_to_pair(offset, c).start()
    feed_all[me] = feed_ref[...]
    acc[...] = jnp.zeros_like(acc)

    count = chunks * pairs
    early = chunks - 1

    def step(n, carry):
        which = lax.rem(n, 2)
        at = n // 2
        if early:
            at = at + (at + count - early) // count - (at + 1) // count * (count - early)
        c = lax.rem(at, chunks)
        offset = at // chunks
        owner = lax.rem(pair + offset, pairs) * 2 + lax.rem(core + which, 2)

        @pl.when((which == 0) & (offset > 0))
        def _():
            feed_from_pair(offset, c).wait_recv()
            relay(offset, c).start()

        @pl.when(which == 1)
        def _():
            relay(offset, c).wait_recv()

        feed = feed_all[owner, rows(c), :]
        cot = cot_ref[owner, rows(c), :]
        gate = rows_dot(feed, gate_w[...])
        up = rows_dot(feed, up_w[...])
        sigmoid = jax.nn.sigmoid(gate)
        activated = gate * sigmoid
        hidden = (activated * up).astype(jnp.bfloat16)
        hidden_g = rows_dot(cot, down_w[...])
        up_g = (hidden_g * activated).astype(jnp.bfloat16)
        gate_g = (hidden_g * up * sigmoid * (1.0 + gate * (1.0 - sigmoid))).astype(jnp.bfloat16)
        part[owner, rows(c), :] = (
            plain_dot(gate_g, gate_w[...]) + plain_dot(up_g, up_w[...])
        ).astype(jnp.bfloat16)

        @pl.when(which == 1)
        def _():
            part_to_core(offset, c).start()

        out_ref[owner, rows(c), :] = plain_dot(hidden, down_w[...]).astype(jnp.bfloat16)
        acc[0] += columns_dot(gate_g, feed)
        acc[1] += columns_dot(up_g, feed)
        acc[2] += columns_dot(hidden, cot)

        @pl.when((which == 1) & (offset > 0))
        def _():
            part_to_core(offset, c).wait_recv()
            to = peer(offset)
            part[to, rows(c), :] = (
                part[to, rows(c), :].astype(jnp.float32)
                + core_in[offset, rows(c), :].astype(jnp.float32)
            ).astype(jnp.bfloat16)
            sum_to_pair(offset, c).start()

        return carry

    lax.fori_loop(0, 2 * chunks * pairs, step, 0)
    half = acc.shape[1] // 2
    flag = lax.rem(seq, 2)
    for n in range(3):
        keep_ref[n] = acc[n, pl.ds(pl.multiple_of(flag * half, 8), half), :].astype(jnp.bfloat16)
        give_ref[n] = acc[n, pl.ds(pl.multiple_of((1 - flag) * half, 8), half), :].astype(
            jnp.bfloat16
        )
    for c in range(chunks):
        part_to_core(0, c).wait_recv()
        for offset in range(1, pairs):
            sum_to_pair(offset, c).wait_recv()
        total = part[me, rows(c), :].astype(jnp.float32) + core_in[0, rows(c), :].astype(jnp.float32)
        for offset in range(1, pairs):
            total = total + pair_in[offset, rows(c), :].astype(jnp.float32)
        feed_g_ref[rows(c), :] = total
    for c in range(chunks):
        feed_to_core(c).wait_send()
        part_to_core(0, c).wait_send()
        for offset in range(1, pairs):
            feed_to_pair(offset, c).wait_send()
            relay(offset, c).wait_send()
            part_to_core(offset, c).wait_send()
            sum_to_pair(offset, c).wait_send()


def feed_forward(feed_in, cot_all, gate_weight, up_weight, down_weight):
    tokens, width = feed_in.shape
    tp_size = cot_all.shape[0]
    pairs = tp_size // 2
    chunk = min(tokens, 256)
    chunks = tokens // chunk
    hidden = gate_weight.shape[0]
    whole = pl.BlockSpec(memory_space=pltpu.VMEM)
    dma = pltpu.SemaphoreType.DMA
    return pl.pallas_call(
        functools.partial(feed_kernel, chunk),
        out_shape=[
            jax.ShapeDtypeStruct((tokens, width), jnp.float32),
            jax.ShapeDtypeStruct(cot_all.shape, jnp.bfloat16),
            jax.ShapeDtypeStruct((3, hidden // 2, width), jnp.bfloat16),
            jax.ShapeDtypeStruct((3, hidden // 2, width), jnp.bfloat16),
        ],
        in_specs=[whole] * 5,
        out_specs=[whole] * 4,
        scratch_shapes=[
            pltpu.VMEM(cot_all.shape, jnp.bfloat16),
            pltpu.VMEM(cot_all.shape, jnp.bfloat16),
            pltpu.VMEM((pairs, tokens, width), jnp.bfloat16),
            pltpu.VMEM((pairs, tokens, width), jnp.bfloat16),
            pltpu.VMEM((3, hidden, width), jnp.float32),
        ]
        + [dma((pairs * chunks,))] * 8,
        compiler_params=pltpu.CompilerParams(
            collective_id=4, has_side_effects=True, vmem_limit_bytes=67043328
        ),
        name="feed_forward",
    )(feed_in, cot_all, gate_weight, up_weight, down_weight)


def group_of(place, seq_size):
    half = seq_size // 2
    low = place // 2
    return lax.rem(place + low, 2) * half + low


def place_of(group, seq_size):
    half = seq_size // 2
    low = lax.rem(group, half)
    return low * 2 + lax.rem(low + group // half, 2)


def remote(source, target, send, receive, to):
    return pltpu.make_async_remote_copy(
        src_ref=source, dst_ref=target, send_sem=send, recv_sem=receive,
        device_id=to, device_id_type=MESH,
    )


def same(left, right):
    return (left[0] == right[0]) & (left[1] == right[1])


class Exchange:
    def __init__(self, plan, me, source, target, local_sem, send_sem, receive_sem):
        self.me = me
        self.sends, self.receives = plan(*me)
        self.source, self.target = source, target
        self.local_sem, self.send_sem, self.receive_sem = local_sem, send_sem, receive_sem

    def greet(self, barrier):
        for origin, _, _ in self.receives:
            @pl.when(jnp.logical_not(same(origin, self.me)))
            def _():
                pl.semaphore_signal(barrier, inc=1, device_id=origin, device_id_type=MESH)

    def others(self):
        return sum(jnp.where(same(to, self.me), 0, 1) for to, _, _, _ in self.sends)

    def each_send(self, wait):
        for n, (to, source, target, at) in enumerate(self.sends):
            here = same(to, self.me)

            @pl.when(here)
            def _():
                copy = pltpu.make_async_copy(
                    self.source.at[source], self.target.at[target], self.local_sem.at[n]
                )
                copy.wait() if wait else copy.start()

            @pl.when(jnp.logical_not(here))
            def _():
                copy = remote(
                    self.source.at[source], self.target.at[target],
                    self.send_sem.at[n], self.receive_sem.at[at], to,
                )
                copy.wait_send() if wait else copy.start()

    def start(self):
        self.each_send(False)

    def wait_sends(self):
        self.each_send(True)

    def wait_receive(self, origin, target, at):
        @pl.when(jnp.logical_not(same(origin, self.me)))
        def _():
            remote(
                self.target.at[target], self.target.at[target],
                self.send_sem.at[0], self.receive_sem.at[at], origin,
            ).wait_recv()

    def wait_receives(self):
        for receive in self.receives:
            self.wait_receive(*receive)


def exchange(arrays, out_shapes, plans, number):
    count = len(arrays)

    def kernel(*refs):
        me = (lax.axis_index("seq"), lax.axis_index("tp"))
        moves = [
            Exchange(plan, me, refs[n], refs[count + n], *refs[2 * count + 3 * n :][:3])
            for n, plan in enumerate(plans)
        ]
        barrier = pltpu.get_barrier_semaphore()
        for move in moves:
            move.greet(barrier)
        pl.semaphore_wait(barrier, sum(move.others() for move in moves))
        for move in moves:
            move.start()
        for move in moves:
            move.wait_sends()
        for move in moves:
            move.wait_receives()

    semaphores = []
    for plan in plans:
        semaphores += [pltpu.SemaphoreType.DMA((len(plan(0, 0)[0]),))] * 3
    return pl.pallas_call(
        kernel,
        out_shape=[
            jax.ShapeDtypeStruct(shape, array.dtype) for shape, array in zip(out_shapes, arrays)
        ],
        in_specs=[pl.BlockSpec(memory_space=pl.ANY)] * count,
        out_specs=[pl.BlockSpec(memory_space=pl.ANY)] * count,
        scratch_shapes=semaphores,
        compiler_params=pltpu.CompilerParams(collective_id=number, has_side_effects=True),
        name=f"exchange_{number}",
    )(*arrays)


def owner_to_quarter(seq_size, tp_size, rows_each, rows_local, piece_first):
    def plan(s, t):
        sends, receives = [], []
        for slot in range(rows_local):
            row = t * rows_local + slot
            to = place_of(row // rows_each, seq_size)
            j = lax.rem(row, rows_each)
            for i in range(tp_size):
                target = (i, j, s) if piece_first else (j, s, i)
                sends.append(((to, i), (slot, i), target, j * seq_size + s))
        group = group_of(s, seq_size)
        for j in range(rows_each):
            row = group * rows_each + j
            for i in range(seq_size):
                origin = lax.rem(s + i, seq_size)
                target = (t, j, origin) if piece_first else (j, origin, t)
                receives.append(((origin, row // rows_local), target, j * seq_size + origin))
        return sends, receives

    return plan


def quarter_to_owner(seq_size, tp_size, rows_each, rows_local):
    def plan(s, t):
        sends, receives = [], []
        group = group_of(s, seq_size)
        for i in range(seq_size):
            to = lax.rem(s + i, seq_size)
            for j in range(rows_each):
                row = group * rows_each + j
                slot = lax.rem(row, rows_local)
                sends.append(((to, row // rows_local), (j, to), (slot, t), slot * tp_size + t))
        for slot in range(rows_local):
            row = t * rows_local + slot
            for i in range(tp_size):
                receives.append(
                    ((place_of(row // rows_each, seq_size), i), (slot, i), slot * tp_size + i)
                )
        return sends, receives

    return plan


def places_to_rows(seq_size, rows_each):
    def plan(s, t):
        sends, receives = [], []
        for i in range(seq_size):
            to = lax.rem(s + i, seq_size)
            rows = pl.ds(group_of(to, seq_size) * rows_each, rows_each)
            sends.append(((to, t), (rows,), (slice(None), s), s))
            origin = lax.rem(s + seq_size - i, seq_size)
            receives.append(((origin, t), (slice(None), origin), origin))
        return sends, receives

    return plan


def rows_to_places(seq_size, rows_each):
    def plan(s, t):
        sends, receives = [], []
        rows = pl.ds(group_of(s, seq_size) * rows_each, rows_each)
        for i in range(seq_size):
            to = lax.rem(s + i, seq_size)
            sends.append(((to, t), (slice(None), to), (rows,), s))
            origin = lax.rem(s + seq_size - i, seq_size)
            source_rows = pl.ds(group_of(origin, seq_size) * rows_each, rows_each)
            receives.append(((origin, t), (source_rows,), origin))
        return sends, receives

    return plan


def heads_to_tokens(tp_size):
    def plan(s, t):
        sends, receives = [], []
        for i in range(tp_size):
            to = lax.rem(t + i, tp_size)
            sends.append(((s, to), (slice(None), slice(None), to), (t,), t))
            origin = lax.rem(t + tp_size - i, tp_size)
            receives.append(((s, origin), (origin,), origin))
        return sends, receives

    return plan


def tokens_to_heads(tp_size):
    def plan(s, t):
        sends, receives = [], []
        for i in range(tp_size):
            to = lax.rem(t + i, tp_size)
            sends.append(((s, to), (to,), (slice(None), slice(None), t), t))
            origin = lax.rem(t + tp_size - i, tp_size)
            receives.append(((s, origin), (slice(None), slice(None), origin), origin))
        return sends, receives

    return plan


def spread_kernel(
    plans, sizes, x_ref, cot_ref, first_ref, output_ref, q_w, k_w, v_w, offset_ref, frequency_ref,
    gain_ref,
    x_out, cot_out, first_out, output_out, q_ref, k_ref, v_ref, cos_ref, sin_ref, square_ref,
    x_rows, first_rows, q_turned, k_turned,
    x_local, x_send, x_receive, cot_local, cot_send, cot_receive,
    first_local, first_send, first_receive,
    core_send, core_receive, pair_send, pair_receive, relay_send, load_sem, output_sem,
):
    seq_size, tp_size, rows_each, rows_local, parts = sizes
    me = (lax.axis_index("seq"), lax.axis_index("tp"))
    s, t = me
    pairs = tp_size // 2
    pair, core = t // 2, lax.rem(t, 2)
    other = pair * 2 + 1 - core
    each = seq_size // parts

    def peer(offset):
        return lax.rem(pair + offset, pairs) * 2 + core

    x_move = Exchange(plans[0], me, x_ref, x_out, x_local, x_send, x_receive)
    cot_move = Exchange(plans[1], me, cot_ref, cot_out, cot_local, cot_send, cot_receive)
    first_move = Exchange(plans[2], me, first_ref, first_out, first_local, first_send, first_receive)
    moves = (x_move, first_move, cot_move)
    barrier = pltpu.get_barrier_semaphore()
    for move in moves:
        move.greet(barrier)
    for to in [other] + [peer(offset) for offset in range(1, pairs)]:
        pl.semaphore_signal(barrier, inc=1, device_id=(s, to), device_id_type=MESH)
    pl.semaphore_wait(barrier, sum(move.others() for move in moves) + pairs)
    for move in moves:
        move.start()

    def block(out, tensor, piece, part):
        if tensor == 2:
            return out.at[piece]
        span = pl.ds(part * each, each)
        return out.at[:, span, piece] if tensor == 0 else out.at[piece, :, span]

    def number(tensor, offset, part):
        return (tensor * pairs + offset) * parts + part

    def own(out, tensor, part):
        return output_ref if tensor == 2 else block(out, tensor, t, part)

    def to_core(out, tensor, part):
        view, at = block(out, tensor, t, part), number(tensor, 0, part)
        return remote(own(out, tensor, part), view, core_send.at[at], core_receive.at[at], (s, other))

    def to_pair(out, tensor, offset, part):
        view = block(out, tensor, t, part)
        return remote(
            own(out, tensor, part), view, pair_send.at[number(tensor, offset, part)],
            pair_receive.at[number(tensor, pairs - offset, part)], (s, peer(offset)),
        )

    def from_pair(out, tensor, offset, part):
        view, at = block(out, tensor, peer(offset), part), number(tensor, offset, part)
        return remote(view, view, pair_send.at[at], pair_receive.at[at], (s, peer(offset)))

    def relay(out, tensor, offset, part):
        view, at = block(out, tensor, peer(offset), part), number(tensor, offset, part)
        return remote(view, view, relay_send.at[at], core_receive.at[at], (s, other))

    def from_core(out, tensor, offset, part):
        piece = lax.rem(pair + offset, pairs) * 2 + 1 - core
        view, at = block(out, tensor, piece, part), number(tensor, offset, part)
        return remote(view, view, relay_send.at[at], core_receive.at[at], (s, other))

    def forward(move, out, tensor):
        def receive(n, carry):
            part = lax.rem(s // each + n, parts)
            for j in range(rows_each):
                for i in range(each):
                    origin = part * each + i
                    group = group_of(s, seq_size)
                    owner = (origin, (group * rows_each + j) // rows_local)
                    target = (t, j, origin) if tensor else (j, origin, t)
                    move.wait_receive(owner, target, j * seq_size + origin)
                    slot = lax.rem(group * rows_each + j, rows_local)

                    @pl.when(same(owner, me))
                    def _():
                        pltpu.make_async_copy(
                            move.source.at[slot, t], move.target.at[target],
                            move.local_sem.at[slot * tp_size + t],
                        ).wait()
            to_core(out, tensor, part).start()
            for offset in range(1, pairs):
                to_pair(out, tensor, offset, part).start()
            return carry

        def relays(n, carry):
            part = lax.rem(s // each + n, parts)
            for offset in range(1, pairs):
                from_pair(out, tensor, offset, part).wait_recv()
                relay(out, tensor, offset, part).start()
            return carry

        lax.fori_loop(0, parts, receive, 0)
        lax.fori_loop(0, parts, relays, 0)

    def arrive(out, tensor):
        def one(part, carry):
            for offset in range(pairs):
                from_core(out, tensor, offset, part).wait_recv()
            return carry

        lax.fori_loop(0, parts, one, 0)

    def finish(move, out, tensor):
        def one(part, carry):
            to_core(out, tensor, part).wait_send()
            for offset in range(1, pairs):
                to_pair(out, tensor, offset, part).wait_send()
                relay(out, tensor, offset, part).wait_send()
            return carry

        lax.fori_loop(0, parts, one, 0)
        for n, (to, source, target, at) in enumerate(move.sends):
            @pl.when(jnp.logical_not(same(to, me)))
            def _():
                remote(
                    move.source.at[source], move.target.at[target],
                    move.send_sem.at[n], move.receive_sem.at[at], to,
                ).wait_send()

    blocks, _, piece, depth = x_rows.shape
    places = tp_size * piece
    width = q_w.shape[0]
    lanes = cos_ref.shape[2]
    output_copy = pltpu.make_async_copy(output_ref, output_out.at[t], output_sem)
    output_copy.start()
    turn = half_turn(width)
    q_turned[...] = plain_dot(turn, q_w[...]).astype(jnp.bfloat16)
    k_turned[...] = plain_dot(turn, k_w[...]).astype(jnp.bfloat16)
    square_ref[...] = jnp.zeros_like(square_ref)

    def tables(n, carry):
        angles = frequency_ref[...] * offset_ref[n]
        cos_ref[n] = jnp.concatenate([jnp.cos(angles)] * (2 * lanes // HD), axis=0).T
        sin_ref[n] = jnp.concatenate([jnp.sin(angles)] * (2 * lanes // HD), axis=0).T
        return carry

    lax.fori_loop(0, blocks, tables, 0)

    def x_load(n):
        source = x_out.at[n // seq_size, lax.rem(n, seq_size)]
        return pltpu.make_async_copy(source, x_rows.at[n], load_sem.at[n])

    def first_load(n):
        source = first_out.at[n // seq_size, lax.rem(n, seq_size)]
        return pltpu.make_async_copy(source, first_rows.at[n], load_sem.at[n])

    def start_loads(load):
        def one(n, carry):
            load(n).start()
            return carry

        lax.fori_loop(0, blocks, one, 0)

    def query_key(n, carry):
        x_load(n).wait()
        x = x_rows[n].reshape(places, depth).astype(jnp.float32)
        inverse = lax.rsqrt(jnp.mean(x * x, axis=-1, keepdims=True) + norm_eps)
        normed = (x * inverse * gain_ref[...]).astype(jnp.bfloat16)
        cosine, sine = widen(cos_ref[n], width), widen(sin_ref[n], width)
        q_ref[n] = (
            (rows_dot(normed, q_w[...]) * cosine + rows_dot(normed, q_turned[...]) * sine)
            * (HD ** (-0.5) * LOG2E)
        ).astype(jnp.bfloat16)
        k_ref[n] = (
            rows_dot(normed, k_w[...]) * cosine + rows_dot(normed, k_turned[...]) * sine
        ).astype(jnp.bfloat16)
        x_rows[n] = normed.reshape(x_rows.shape[1:])
        return carry

    def mix(n, carry):
        first_load(n).wait()
        first = first_rows[n].astype(jnp.float32)
        value = rows_dot(x_rows[n].reshape(places, depth), v_w[...])
        mixed = (0.5 * value + 0.5 * first.T).astype(jnp.bfloat16)
        v_ref[n] = mixed
        wide = mixed.astype(jnp.float32)
        square_ref[0:1, : first.shape[1]] += jnp.sum(first * first, axis=0, keepdims=True)
        square_ref[1:2, : wide.shape[1]] += jnp.sum(wide * wide, axis=0, keepdims=True)
        return carry

    forward(x_move, x_out, 0)
    to_core(output_out, 2, 0).start()
    for offset in range(1, pairs):
        to_pair(output_out, 2, offset, 0).start()
    arrive(x_out, 0)
    start_loads(x_load)
    lax.fori_loop(0, blocks, query_key, 0)
    first_move.wait_sends()
    first_move.wait_receives()
    start_loads(first_load)
    lax.fori_loop(0, blocks, mix, 0)
    for offset in range(1, pairs):
        from_pair(output_out, 2, offset, 0).wait_recv()
        relay(output_out, 2, offset, 0).start()
    forward(cot_move, cot_out, 1)
    arrive(cot_out, 1)
    for offset in range(pairs):
        from_core(output_out, 2, offset, 0).wait_recv()
    to_core(output_out, 2, 0).wait_send()
    for offset in range(1, pairs):
        to_pair(output_out, 2, offset, 0).wait_send()
        relay(output_out, 2, offset, 0).wait_send()
    finish(x_move, x_out, 0)
    finish(cot_move, cot_out, 1)
    output_copy.wait()


def half_turn(width):
    row = lax.broadcasted_iota(jnp.int32, (width, width), 0)
    column = lax.broadcasted_iota(jnp.int32, (width, width), 1)
    low = lax.rem(row, HD) < HD // 2
    minus = low & (column == row + HD // 2)
    plus = jnp.logical_not(low) & (column == row - HD // 2)
    return jnp.where(plus, 1.0, jnp.where(minus, -1.0, 0.0)).astype(jnp.bfloat16)


def spread(
    layer_input, cotangent, first_values, output_weight, query_weight, key_weight, value_weight,
    offsets, frequency, gain, sizes,
):
    seq_size, tp_size, rows_each, rows_local, parts = sizes
    pieces = layer_input.shape[2:]
    width, depth = query_weight.shape
    features, places = first_values.shape[1:]
    blocks = rows_each * seq_size
    lanes = min(width, 128)
    plans = (
        owner_to_quarter(seq_size, tp_size, rows_each, rows_local, False),
        owner_to_quarter(seq_size, tp_size, rows_each, rows_local, True),
        places_to_rows(seq_size, rows_each),
    )
    dma = pltpu.SemaphoreType.DMA
    quarter = [
        dma((rows_local * tp_size,)), dma((rows_local * tp_size,)), dma((rows_each * seq_size,)),
    ]
    stage = tp_size // 2 * parts * 3
    bf16, f32 = jnp.bfloat16, jnp.float32
    anywhere = pl.BlockSpec(memory_space=pl.ANY)
    vmem = pl.BlockSpec(memory_space=pltpu.VMEM)
    part = jax.ShapeDtypeStruct((blocks, places, width), bf16)
    table = jax.ShapeDtypeStruct((blocks, places, lanes), f32)
    return pl.pallas_call(
        functools.partial(spread_kernel, plans, sizes),
        out_shape=[
            jax.ShapeDtypeStruct((rows_each, seq_size, tp_size) + pieces, bf16),
            jax.ShapeDtypeStruct((tp_size, rows_each, seq_size) + pieces, bf16),
            jax.ShapeDtypeStruct((rows_each, seq_size, features, places), bf16),
            jax.ShapeDtypeStruct((tp_size,) + output_weight.shape, bf16),
            part,
            part,
            part,
            table,
            table,
            jax.ShapeDtypeStruct((8, max(width, places)), f32),
        ],
        in_specs=[anywhere] * 3 + [vmem] * 7,
        out_specs=[anywhere] * 4 + [vmem] * 6,
        scratch_shapes=[
            pltpu.VMEM((blocks, tp_size) + pieces, bf16),
            pltpu.VMEM((blocks, features, places), bf16),
            pltpu.VMEM((width, depth), bf16),
            pltpu.VMEM((width, depth), bf16),
        ]
        + quarter
        + quarter
        + [dma((seq_size,))] * 3
        + [dma((stage,))] * 5
        + [dma((blocks,)), dma],
        compiler_params=pltpu.CompilerParams(
            collective_id=5, has_side_effects=True, vmem_limit_bytes=67043328
        ),
        name="spread",
    )(
        layer_input, cotangent, first_values, output_weight, query_weight, key_weight,
        value_weight, offsets, frequency, gain,
    )


def widen(table, width):
    return jnp.concatenate([table] * (width // table.shape[1]), axis=1)


class Reduce:
    def __init__(self, place, full, core_in, pair_in, chunks, sems):
        self.seq, self.tp, self.pairs = place
        self.pair, self.core = self.tp // 2, lax.rem(self.tp, 2)
        self.other = self.pair * 2 + 1 - self.core
        self.full, self.core_in, self.pair_in = full, core_in, pair_in
        self.chunks = chunks
        self.core_send, self.core_recv, self.pair_send, self.pair_recv = sems

    def peer(self, offset):
        return lax.rem(self.pair + offset, self.pairs) * 2 + self.core

    def cut(self, ref, lead, c):
        return ref.at[lead, :, c]

    def to_core(self, offset, c):
        lead = lax.rem(self.pair + offset, self.pairs) * 2 + 1 - self.core
        at = offset * self.chunks + c
        return remote(
            self.cut(self.full, lead, c), self.cut(self.core_in, offset, c),
            self.core_send.at[at], self.core_recv.at[at], (self.seq, self.other),
        )

    def to_pair(self, offset, c):
        back = self.pairs - offset
        return remote(
            self.cut(self.full, self.peer(offset), c), self.cut(self.pair_in, back - 1, c),
            self.pair_send.at[offset * self.chunks + c],
            self.pair_recv.at[back * self.chunks + c], (self.seq, self.peer(offset)),
        )

    def from_pair(self, offset, c):
        view, at = self.cut(self.pair_in, offset - 1, c), offset * self.chunks + c
        return remote(
            view, view, self.pair_send.at[at], self.pair_recv.at[at], (self.seq, self.peer(offset))
        )

    def start(self, c):
        for offset in list(range(1, self.pairs)) + [0]:
            self.to_core(offset, c).start()

    def pass_on(self, c):
        for offset in range(1, self.pairs):
            self.to_core(offset, c).wait_recv()
            to = self.peer(offset)

            def add(b, carry):
                self.full[to, b, c] = (
                    self.full[to, b, c].astype(jnp.float32)
                    + self.core_in[offset, b, c].astype(jnp.float32)
                ).astype(jnp.bfloat16)
                return carry

            lax.fori_loop(0, self.full.shape[1], add, 0)
            self.to_pair(offset, c).start()

    def arrive(self, c):
        self.to_core(0, c).wait_recv()
        for offset in range(1, self.pairs):
            self.from_pair(offset, c).wait_recv()

    def total(self, b, c):
        value = self.full[self.tp, b, c].astype(jnp.float32)
        value = value + self.core_in[0, b, c].astype(jnp.float32)
        for offset in range(1, self.pairs):
            value = value + self.pair_in[offset - 1, b, c].astype(jnp.float32)
        return value

    def finish(self):
        for c in range(self.chunks):
            for offset in range(self.pairs):
                self.to_core(offset, c).wait_send()
            for offset in range(1, self.pairs):
                self.to_pair(offset, c).wait_send()


class SeqSum:
    def __init__(self, place, steps, done, blocks, held, mine, sums, local_sem, send_sem, recv_sem):
        self.seq, self.tp = place
        self.count, self.done, self.size = steps, done, 1 << steps
        self.blocks, self.held, self.mine, self.sums = blocks, held, mine, sums
        self.local_sem, self.send_sem, self.recv_sem = local_sem, send_sem, recv_sem
        self.flags = [lax.rem(self.seq // (1 << n), 2) for n in range(steps)]
        low, self.lows = 0, [0]
        for n in range(steps):
            low = low + self.flags[n] * (self.size >> (n + 1))
            self.lows.append(low)

    def partner(self, n):
        return (self.seq + (1 - 2 * self.flags[n]) * (1 << n), self.tp)

    def half(self, n):
        return self.size >> (n + 1)

    def begin(self, n):
        return (self.size >> self.done) - (self.size >> n)

    def give(self, n):
        half = self.half(n)
        low = self.lows[n] - self.lows[self.done] + (1 - self.flags[n]) * half
        return remote(
            self.blocks.at[pl.ds(low, half)], self.held.at[pl.ds(self.begin(n), half)],
            self.send_sem.at[n], self.recv_sem.at[n], self.partner(n),
        )

    def take(self, n):
        copy = self.give(n)
        copy.wait_recv()
        copy.wait_send()
        last = n + 1 == self.count

        def add(b, carry):
            at = self.lows[n + 1] - self.lows[self.done] + b
            value = (
                self.blocks[at].astype(jnp.float32)
                + self.held[self.begin(n) + b].astype(jnp.float32)
            ).astype(jnp.bfloat16)
            if last:
                self.mine[b] = value
            else:
                self.blocks[at] = value
            return carry

        lax.fori_loop(0, self.half(n), add, 0)

    def store(self):
        return pltpu.make_async_copy(
            self.mine, self.sums.at[pl.ds(self.lows[self.count], 1)], self.local_sem
        )

    def spread(self, n):
        target = self.sums.at[pl.ds(self.lows[n + 1], self.half(n))]
        source = self.mine if n + 1 == self.count else target
        at = self.count + n
        return remote(source, target, self.send_sem.at[at], self.recv_sem.at[at], self.partner(n))

    def collect(self, n):
        half = self.half(n)
        view = self.sums.at[pl.ds(self.lows[n] + (1 - self.flags[n]) * half, half)]
        at = self.count + n
        remote(view, view, self.send_sem.at[at], self.recv_sem.at[at], self.partner(n)).wait_recv()

    def steps(self):
        self.give(self.done).start()
        yield
        for n in range(self.done, self.count):
            self.take(n)
            if n + 1 < self.count:
                self.give(n + 1).start()
            else:
                self.spread(n).start()
                self.store().start()
            yield
        for n in range(self.count - 1, -1, -1):
            self.collect(n)
            if n + 1 == self.count:
                self.store().wait()
            if n > 0:
                self.spread(n - 1).start()
            yield
        for n in range(self.count):
            self.spread(n).wait_send()


def tail_kernel(
    sizes, dv_plan, out_hbm, keep_hbm, got_hbm, x_hbm, q_hbm, k_hbm, v_hbm, cos_hbm, sin_hbm,
    qw_hbm, kw_hbm, vw_hbm, attended_hbm, source_hbm, middle_hbm, middle_g_hbm, dv_hbm, gain_ref, small_ref,
    out_ref, input_g_ref, first_g_ref, sums_ref, feed_ref, gain_g_ref, feed_gain_g_ref, norms_ref,
    x_rows, q_rows, k_rows, v_rows, cos_rows, sin_rows, weights, attended, grad_acc,
    normed_full, normed_core, normed_pair, proj_full, proj_core, proj_pair,
    out_full, out_core, out_pair, source, middle, middle_g, input_g, result,
    blocks, held, mine, feed_blocks, feed_got, feed_held, feed_mine,
    small, tp_held, tp_sum, seq_held, dv_rows, dv_cols,
    *sems,
):
    seq_size, tp_size, rows_each, rows_local, _ = sizes
    s, t = lax.axis_index("seq"), lax.axis_index("tp")
    me = (s, t)
    pairs = tp_size // 2
    count = seq_size.bit_length() - 1
    normed_sems, proj_sems, out_sems = sems[:4], sems[4:8], sems[8:12]
    dv_sems, back_sems, lo_sems = sems[12:15], sems[15:18], sems[18:21]
    load_sem, x_sem, feed_sem, store_sem, grad_send, grad_recv = sems[21:27]
    feed_send, feed_recv, small_send, tp_sem, seq_sem, first_sem = sems[27:]
    place = (s, t, pairs)
    normed = Reduce(place, normed_full, normed_core, normed_pair, 2, normed_sems)
    proj = Reduce(place, proj_full, proj_core, proj_pair, 1, proj_sems)
    out = Reduce(place, out_full, out_core, out_pair, 2, out_sems)
    dv_move = Exchange(dv_plan, me, dv_hbm, dv_rows, *dv_sems)
    half = source.shape[0]
    places, depth = x_rows.shape[1:]
    width = q_rows.shape[2]

    group = group_of(s, seq_size)
    origins = []
    for slot in range(rows_local):
        row = t * rows_local + slot
        for i in range(tp_size):
            origins.append(((place_of(row // rows_each, seq_size), i), slot, i))

    tp_peers = [lax.rem(t + i, tp_size) for i in range(1, tp_size)]
    seq_peers = [lax.rem(s + i, seq_size) for i in range(1, seq_size)]

    names = (
        (q_hbm, q_rows), (k_hbm, k_rows), (v_hbm, v_rows), (cos_hbm, cos_rows),
        (sin_hbm, sin_rows), (qw_hbm, weights.at[pl.ds(0, width)]),
        (kw_hbm, weights.at[pl.ds(width, width)]), (vw_hbm, weights.at[pl.ds(2 * width, width)]),
        (out_hbm, out_full), (attended_hbm, attended),
        (middle_g_hbm, middle_g), (source_hbm, source), (middle_hbm, middle),
    )
    loads = [
        pltpu.make_async_copy(origin, target, load_sem.at[n])
        for n, (origin, target) in enumerate(names)
    ]
    feed_loads = [
        (
            pltpu.make_async_copy(keep_hbm.at[n], feed_blocks.at[n], feed_sem.at[2 * n]),
            pltpu.make_async_copy(got_hbm.at[n], feed_got.at[n], feed_sem.at[2 * n + 1]),
        )
        for n in range(3)
    ]

    def x_load(n):
        return pltpu.make_async_copy(x_hbm.at[n], x_rows.at[n], x_sem.at[n])

    def ordered(n):
        return 2 * lax.rem(n, half) + n // half

    for pair in feed_loads:
        for copy in pair:
            copy.start()
    loads[8].start()
    for copy in loads[:8]:
        copy.start()
    for n in range(2 * half):
        x_load(ordered(n)).start()
    for copy in loads[9:]:
        copy.start()

    barrier = pltpu.get_barrier_semaphore()
    dv_move.greet(barrier)
    for origin, _, _ in origins:
        @pl.when(jnp.logical_not(same(origin, me)))
        def _():
            pl.semaphore_signal(barrier, inc=1, device_id=origin, device_id_type=MESH)
    for to in tp_peers:
        pl.semaphore_signal(barrier, inc=1, device_id=(s, to), device_id_type=MESH)
    for to in seq_peers:
        pl.semaphore_signal(barrier, inc=1, device_id=(to, t), device_id_type=MESH)
    back_others = sum(
        jnp.where(same((to, (group * rows_each + j) // rows_local), me), 0, 1)
        for j in range(rows_each)
        for to in range(seq_size)
    )
    pl.semaphore_wait(barrier, dv_move.others() + back_others + tp_size + seq_size - 2)

    def seq_sum(n, done, *refs):
        return SeqSum(
            me, count, done, *refs, store_sem.at[n],
            (grad_send if done == 0 else feed_send).at[n if done == 0 else n - 2],
            (grad_recv if done == 0 else feed_recv).at[n if done == 0 else n - 2],
        ).steps()

    sums = [
        seq_sum(n, 0, blocks.at[n], held.at[n], mine.at[n], sums_ref.at[n]) for n in range(2)
    ]
    feeds = [
        seq_sum(
            n + 2, 1, feed_blocks.at[n], feed_held.at[n], feed_mine.at[n], feed_ref.at[n]
        )
        for n in range(3)
    ]

    for n in range(3):
        for copy in feed_loads[n]:
            copy.wait()

        def join(b, carry):
            feed_blocks[n, b] = (
                feed_blocks[n, b].astype(jnp.float32) + feed_got[n, b].astype(jnp.float32)
            ).astype(jnp.bfloat16)
            return carry

        lax.fori_loop(0, feed_blocks.shape[1], join, 0)
        next(feeds[n])
    loads[8].wait()
    out.start(0)
    out.start(1)
    dv_move.start()
    for copy in loads[:8]:
        copy.wait()
    turn = half_turn(width)
    grad_acc[...] = jnp.zeros_like(grad_acc)
    gain = gain_ref[...]

    def project_back(first, last):
        def one(n, carry):
            at = ordered(n)
            x_load(at).wait()
            x = x_rows[at].astype(jnp.float32)
            inverse = lax.rsqrt(jnp.mean(x * x, axis=-1, keepdims=True) + norm_eps)
            rows = (x * inverse * gain).astype(jnp.bfloat16)
            cosine, sine = widen(cos_rows[at], width), widen(sin_rows[at], width)

            def unrotate(grad):
                turned = plain_dot(grad, turn)
                return (grad.astype(jnp.float32) * cosine + turned * sine).astype(jnp.bfloat16)

            stacked = jnp.concatenate(
                [
                    unrotate(q_rows[at]),
                    unrotate(k_rows[at]),
                    (0.5 * v_rows[at].astype(jnp.float32)).astype(jnp.bfloat16),
                ],
                axis=1,
            )
            b, c = at // 2, lax.rem(at, 2)
            product = plain_dot(stacked, weights[...])
            for i in range(tp_size):
                piece = places // tp_size
                normed_full[i, b, c] = product[i * piece : (i + 1) * piece].astype(jnp.bfloat16)
            grad_acc[...] += columns_dot(stacked, rows)
            return carry

        lax.fori_loop(first, last, one, 0)

    quarter = half // 2
    project_back(0, quarter)
    out.pass_on(0)
    out.pass_on(1)
    next(feeds[0])
    project_back(quarter, half)
    normed.start(0)
    next(feeds[1])
    project_back(half, half + quarter)
    normed.pass_on(0)
    next(feeds[2])
    next(feeds[0])
    project_back(half + quarter, 2 * half)
    normed.start(1)
    fine = blocks.shape[2]
    for n in range(3 * seq_size // 2):
        blocks[n // seq_size, n % seq_size] = grad_acc[n * fine : (n + 1) * fine].astype(
            jnp.bfloat16
        )
    next(sums[0])
    next(feeds[1])
    loads[9].wait()
    loads[10].wait()
    branch = middle_g[...].reshape(2 * half * middle_g.shape[2], depth).astype(jnp.bfloat16)
    for i in range(tp_size):
        product = columns_dot(attended[i], branch)
        for n in range(seq_size // 2):
            proj_full[i, n, 0] = product[n * fine : (n + 1) * fine].astype(jnp.bfloat16)
    proj.start(0)
    normed.pass_on(1)
    proj.pass_on(0)
    next(feeds[2])
    next(feeds[0])

    def own_part(target, slot, i):
        piece = source.shape[2]
        return target.at[slot, pl.ds(pl.multiple_of(i * piece, piece), piece)]

    def send_back(source_ref, target, trio, b, c, wait):
        local_sem, send_sem, recv_sem = trio
        flat = 2 * b + c
        j, to = flat // seq_size, lax.rem(flat, seq_size)
        row = group * rows_each + j
        slot = lax.rem(row, rows_local)
        place = (to, row // rows_local)
        here = same(place, me)
        view = own_part(target, slot, t)

        @pl.when(here)
        def _():
            copy = pltpu.make_async_copy(source_ref.at[b, c], view, local_sem.at[flat])
            copy.wait() if wait else copy.start()

        @pl.when(jnp.logical_not(here))
        def _():
            copy = remote(
                source_ref.at[b, c], view, send_sem.at[flat], recv_sem.at[slot * tp_size + t], place
            )
            copy.wait_send() if wait else copy.start()

    small[...] = small_ref[...]

    def back(c):
        normed.arrive(c)

        def one(n, carry):
            b = lax.rem(n + s // 2, half)
            grads = normed.total(b, c)
            x = source[b, c].astype(jnp.float32)
            inverse = lax.rsqrt(jnp.mean(x * x, axis=-1, keepdims=True) + norm_eps)
            unit = x * inverse
            scaled = grads * gain
            extra = inverse * (scaled - unit * jnp.mean(scaled * unit, axis=-1, keepdims=True))
            input_g[b, c] = (middle_g[b, c] + extra).astype(jnp.bfloat16)
            small[0:1, :] += jnp.sum(grads * unit, axis=0, keepdims=True)
            send_back(input_g, input_g_ref, back_sems, b, c, False)
            return carry

        lax.fori_loop(0, half, one, 0)

    def forward(c):
        out.arrive(c)

        def one(n, carry):
            b = lax.rem(n + s // 2, half)
            result[b, c] = (middle[b, c] + out.total(b, c)).astype(jnp.bfloat16)
            send_back(result, out_ref, lo_sems, b, c, False)
            return carry

        lax.fori_loop(0, half, one, 0)

    def tp_copy(n):
        return remote(
            small, tp_held.at[tp_size - n], small_send.at[n],
            tp_sem.at[tp_size - n], (s, tp_peers[n - 1]),
        )

    def seq_copy(n):
        return remote(
            tp_sum, seq_held.at[seq_size - n], small_send.at[tp_size + n],
            seq_sem.at[seq_size - n], (seq_peers[n - 1], t),
        )

    def all_steps(generators):
        for generator in generators:
            next(generator, None)

    loads[12].wait()
    forward(0)
    forward(1)
    next(feeds[1])
    loads[11].wait()
    back(0)
    proj.arrive(0)

    def put(b, carry):
        blocks[1, seq_size // 2 + b] = proj.total(b, 0).astype(jnp.bfloat16)
        return carry

    lax.fori_loop(0, seq_size // 2, put, 0)
    next(sums[1])
    next(sums[0])
    next(feeds[2])
    back(1)
    for n in range(1, tp_size):
        tp_copy(n).start()
    all_steps([feeds[0], sums[0], sums[1]])
    for n in range(1, tp_size):
        tp_copy(n).wait()
    tp_held[0] = small[...]
    total = tp_held[lax.rem(tp_size - t, tp_size)]
    for n in range(1, tp_size):
        total = total + tp_held[lax.rem(n + tp_size - t, tp_size)]
    tp_sum[...] = total
    for n in range(1, seq_size):
        seq_copy(n).start()
    seq_held[0] = total
    dv_move.wait_sends()
    dv_move.wait_receives()

    def first_back(n, carry):
        dv_cols[n] = (0.5 * dv_rows[n].astype(jnp.float32)).T
        return carry

    lax.fori_loop(0, dv_rows.shape[0], first_back, 0)
    first_store = pltpu.make_async_copy(dv_cols, first_g_ref, first_sem)
    first_store.start()
    for _ in range(2 * count):
        all_steps([feeds[1], sums[0], feeds[2], sums[1], feeds[0]])
    for generator in sums + feeds:
        for _ in generator:
            pass
    for n in range(1, seq_size):
        seq_copy(n).wait()
    total = seq_held[lax.rem(seq_size - s, seq_size)]
    for n in range(1, seq_size):
        total = total + seq_held[lax.rem(n + seq_size - s, seq_size)]
    gain_g_ref[...] = total[0:1]
    feed_gain_g_ref[...] = total[1:2]
    norms_ref[...] = jnp.sqrt(total[2:3, :2])

    for reduce in (normed, proj, out):
        reduce.finish()
    for c in range(2):
        def done(b, carry):
            send_back(input_g, input_g_ref, back_sems, b, c, True)
            send_back(result, out_ref, lo_sems, b, c, True)
            return carry

        lax.fori_loop(0, half, done, 0)
    first_store.wait()
    for origin, slot, i in origins:
        @pl.when(jnp.logical_not(same(origin, me)))
        def _():
            for ref, trio in ((input_g_ref, back_sems), (out_ref, lo_sems)):
                view = own_part(ref, slot, i)
                at = slot * tp_size + i
                remote(view, view, trio[1].at[0], trio[2].at[at], origin).wait_recv()


def tail(
    out_part, keep, got, x_rows, query_g, key_g, value_g, cosine, sine, query_weight, key_weight, value_weight,
    attended, source, middle, middle_g, gain, small, sizes,
):
    seq_size, tp_size, rows_each, rows_local, _ = sizes
    pairs = tp_size // 2
    blocks = rows_each * seq_size
    tokens, depth = source.shape
    piece = tokens // blocks
    width = query_g.shape[-1]
    places = x_rows.shape[0] // blocks
    lanes = cosine.shape[2]
    fine = 2 * width // seq_size
    bf16, f32 = jnp.bfloat16, jnp.float32
    shape = (blocks // 2, 2, piece, depth)
    proj_shape = (width // fine, 1, fine, depth)
    hidden = 2 * keep.shape[1] // seq_size
    feed_shape = (3, seq_size // 2, hidden, depth)
    anywhere = pl.BlockSpec(memory_space=pl.ANY)
    vmem = pl.BlockSpec(memory_space=pltpu.VMEM)
    dma = pltpu.SemaphoreType.DMA
    plan = rows_to_places(seq_size, rows_each)
    steps = seq_size.bit_length() - 1
    owned = jax.ShapeDtypeStruct((rows_local, tp_size * piece, depth), bf16)

    def reduce_shapes(part):
        return [
            pltpu.VMEM((tp_size,) + part, bf16),
            pltpu.VMEM((pairs,) + part, bf16),
            pltpu.VMEM((pairs - 1,) + part, bf16),
        ]

    def reduce_sems(chunks):
        return [dma((pairs * chunks,))] * 4

    return pl.pallas_call(
        functools.partial(tail_kernel, sizes, plan),
        out_shape=[
            owned,
            owned,
            jax.ShapeDtypeStruct((blocks, width, places), f32),
            jax.ShapeDtypeStruct((2, seq_size, fine, depth), bf16),
            jax.ShapeDtypeStruct((3, seq_size, hidden, depth), bf16),
            jax.ShapeDtypeStruct((1, depth), f32),
            jax.ShapeDtypeStruct((1, depth), f32),
            jax.ShapeDtypeStruct((1, 2), f32),
        ],
        in_specs=[anywhere] * 17 + [vmem] * 2,
        out_specs=[anywhere] * 5 + [vmem] * 3,
        scratch_shapes=[
            pltpu.VMEM((blocks, places, depth), bf16),
            pltpu.VMEM((blocks, places, width), bf16),
            pltpu.VMEM((blocks, places, width), bf16),
            pltpu.VMEM((blocks, places, width), bf16),
            pltpu.VMEM((blocks, places, lanes), f32),
            pltpu.VMEM((blocks, places, lanes), f32),
            pltpu.VMEM((3 * width, depth), bf16),
            pltpu.VMEM(attended.shape, bf16),
            pltpu.VMEM((3 * width, depth), f32),
        ]
        + reduce_shapes(shape)
        + reduce_shapes(proj_shape)
        + reduce_shapes(shape)
        + [
            pltpu.VMEM(shape, bf16),
            pltpu.VMEM(shape, f32),
            pltpu.VMEM(shape, f32),
            pltpu.VMEM(shape, bf16),
            pltpu.VMEM(shape, bf16),
            pltpu.VMEM((2, seq_size, fine, depth), bf16),
            pltpu.VMEM((2, seq_size, fine, depth), bf16),
            pltpu.VMEM((2, 1, fine, depth), bf16),
            pltpu.VMEM(feed_shape, bf16),
            pltpu.VMEM(feed_shape, bf16),
            pltpu.VMEM(feed_shape, bf16),
            pltpu.VMEM((3, 1, hidden, depth), bf16),
            pltpu.VMEM(small.shape, f32),
            pltpu.VMEM((tp_size,) + small.shape, f32),
            pltpu.VMEM(small.shape, f32),
            pltpu.VMEM((seq_size,) + small.shape, f32),
            pltpu.VMEM((blocks, places, width), bf16),
            pltpu.VMEM((blocks, width, places), f32),
        ]
        + reduce_sems(2)
        + reduce_sems(1)
        + reduce_sems(2)
        + [dma((seq_size,))] * 3
        + ([dma((blocks,))] * 2 + [dma((rows_local * tp_size,))]) * 2
        + [
            dma((13,)),
            dma((blocks,)),
            dma((6,)),
            dma((5,)),
            dma((2, 2 * steps)),
            dma((2, 2 * steps)),
            dma((3, 2 * steps)),
            dma((3, 2 * steps)),
            dma((tp_size + seq_size,)),
            dma((tp_size,)),
            dma((seq_size,)),
            dma,
        ],
        compiler_params=pltpu.CompilerParams(
            collective_id=6, has_side_effects=True, vmem_limit_bytes=67043328
        ),
        name="tail",
    )(
        out_part.reshape((tp_size,) + shape),
        keep.reshape(feed_shape),
        got.reshape(feed_shape),
        x_rows.reshape(blocks, places, depth),
        query_g.reshape(blocks, places, width),
        key_g.reshape(blocks, places, width),
        value_g.reshape(blocks, places, width),
        cosine,
        sine,
        query_weight,
        key_weight,
        value_weight,
        attended,
        source.reshape(shape),
        middle.reshape(shape),
        middle_g.reshape(shape),
        value_g.reshape(rows_each, seq_size, places, width),
        gain,
        small,
    )


def shards(
    layer_input,
    first_values,
    doc_lengths,
    attn_gain,
    query_weight,
    key_weight,
    value_weight,
    output_weight,
    feed_gain,
    gate_weight,
    up_weight,
    down_weight,
    out_cotangent,
):
    seq_size = lax.axis_size("seq")
    tp_size = lax.axis_size("tp")
    rows_local, local_len, depth = layer_input.shape
    row_count = first_values.shape[0]
    width = query_weight.shape[0]
    rows_each = row_count // seq_size
    piece = local_len // tp_size
    tokens = rows_each * seq_size * piece
    sizes = (seq_size, tp_size, rows_each, rows_local, 4)
    me = lax.axis_index("tp")
    my_rows = group_of(lax.axis_index("seq"), seq_size) * rows_each

    _, offsets = doc_layout(doc_lengths)
    offsets = lax.dynamic_slice_in_dim(offsets, my_rows, rows_each, 0)
    starts = jnp.arange(ROW, dtype=jnp.int32)[None, :] - offsets
    low = (starts[:, ::BLOCK] // BLOCK).reshape(-1)
    starts = starts[:, None, :]
    half_dim = HD // 2
    frequency = rope_base ** (-jnp.arange(half_dim, dtype=jnp.float32) * 2.0 / HD)
    attn_scale = attn_gain.astype(jnp.float32)[None, :]
    feed_scale = feed_gain.astype(jnp.float32)[None, :]
    (
        x_rows, cot_all, _, output_full, queries, keys, values, cosine, sine, squares,
    ) = spread(
        layer_input.reshape(rows_local, tp_size, piece, depth),
        out_cotangent.reshape(rows_local, tp_size, piece, depth),
        first_values,
        output_weight,
        query_weight,
        key_weight,
        value_weight,
        offsets.astype(jnp.float32).reshape(rows_each * seq_size, 1, local_len),
        frequency[:, None],
        attn_scale,
        sizes,
    )
    output_full = output_full.reshape(tp_size * width, depth)
    source_low = lax.dynamic_index_in_dim(x_rows, me, 2, keepdims=False).reshape(tokens, depth)
    source = source_low.astype(jnp.float32)
    cotangent = lax.dynamic_index_in_dim(cot_all, me, 0, keepdims=False).reshape(tokens, depth)
    cotangent = cotangent.astype(jnp.float32)
    x_rows = x_rows.reshape(rows_each * ROW, depth)
    queries, keys, values = (
        part.reshape(rows_each, ROW, width) for part in (queries, keys, values)
    )
    result, logsum = attend(low, queries, keys, values, starts)
    by_piece = (rows_each, seq_size, tp_size, piece, width)
    by_head = (tp_size, rows_each, seq_size, piece, width)
    (pieces,) = exchange([result.reshape(by_piece)], [by_head], [heads_to_tokens(tp_size)], 1)
    attended = jnp.transpose(pieces.reshape(tp_size, tokens, width), (1, 0, 2)).reshape(tokens, -1)
    middle = source + jnp.dot(attended, output_full, preferred_element_type=jnp.float32)
    unit_feed, inv_feed = norm_rows(middle)
    feed_in = (unit_feed * feed_scale).astype(jnp.bfloat16)
    feed_in_g, out_part, keep, give = feed_forward(
        feed_in, cot_all.reshape(tp_size, tokens, depth), gate_weight.T, up_weight.T, down_weight
    )
    got = lax.ppermute(give, "seq", [(n, n + 1 - 2 * (n % 2)) for n in range(seq_size)])
    middle_extra, feed_gain_part = norm_back(feed_in_g, unit_feed, inv_feed, feed_scale)
    middle_g = cotangent + middle_extra
    branch_g = middle_g.astype(jnp.bfloat16)
    attended_g = jnp.einsum(
        "td,ed->te", branch_g, output_full, preferred_element_type=jnp.float32
    ).astype(jnp.bfloat16)
    (attended_g,) = exchange(
        [jnp.transpose(attended_g.reshape(tokens, tp_size, width), (1, 0, 2)).reshape(by_head)],
        [by_piece],
        [tokens_to_heads(tp_size)],
        2,
    )
    query_g, key_g, value_g = attend_back(
        low, queries, keys, values, result, attended_g.reshape(result.shape), logsum, starts
    )
    squares = jnp.pad(jnp.sum(squares, axis=1)[:2], (0, depth - 2))
    small = jnp.stack([jnp.zeros_like(squares), feed_gain_part, squares])
    (
        layer_output, input_grad, first_grad, grad_sums, feed_sums,
        gain_grad, feed_gain_grad, norms,
    ) = tail(
        out_part,
        keep,
        got,
        x_rows,
        query_g,
        key_g,
        value_g,
        cosine,
        sine,
        query_weight,
        key_weight,
        value_weight,
        pieces.reshape(tp_size, tokens, width),
        source_low,
        middle,
        middle_g,
        attn_scale,
        jnp.pad(small, ((0, 5), (0, 0))),
        sizes,
    )
    grad_sums = grad_sums.reshape(4, width, depth)
    projections = [grad_sums[n].astype(jnp.float32) for n in range(4)]
    feed_sums = feed_sums.reshape(3, -1, depth).astype(jnp.float32)
    return (
        layer_output,
        input_grad,
        first_grad,
        gain_grad.reshape(depth),
        *projections,
        feed_gain_grad.reshape(depth),
        feed_sums[0].T,
        feed_sums[1].T,
        feed_sums[2],
        norms.reshape(2),
    )


def solution(mesh):
    placed = (
        P("tp", "seq", None),
        P(None, "tp", "seq"),
        P(),
        P(),
        P("tp", None),
        P("tp", None),
        P("tp", None),
        P("tp", None),
        P(),
        P(None, "tp"),
        P(None, "tp"),
        P("tp", None),
        P("tp", "seq", None),
    )
    return jax.shard_map(
        shards,
        mesh=mesh,
        in_specs=placed,
        out_specs=(
            P("tp", "seq", None),
            P("tp", "seq", None),
            P(None, "tp", "seq"),
            P(),
            P("tp", None),
            P("tp", None),
            P("tp", None),
            P("tp", None),
            P(),
            P(None, "tp"),
            P(None, "tp"),
            P("tp", None),
            P(),
        ),
        check_vma=False,
    )
```

```python
import functools
import math

import jax
import jax.numpy as jnp
from jax import lax
from jax.experimental import pallas as pl
from jax.experimental.pallas import tpu as pltpu
from jax.sharding import PartitionSpec as P

HD = 64
ROW = 2048
BLOCK = 256
LOG2E = math.log2(math.e)
LN2 = math.log(2.0)
MESH = pl.DeviceIdType.MESH


norm_eps = 1e-06
rope_base = 10000.0
masked_score = -1e30


def doc_layout(doc_lengths):
    doc_ends = jnp.cumsum(doc_lengths, axis=-1)
    places = jnp.arange(ROW, dtype=jnp.int32)
    passed = doc_ends[:, None, :] <= places[None, :, None]
    segment = jnp.sum(passed.astype(jnp.int32), axis=-1)
    starts = jnp.max(jnp.where(passed, doc_ends[:, None, :], 0), axis=-1)
    return (segment, places[None, :] - starts)


def norm_rows(values_in):
    inverse = lax.rsqrt(jnp.mean(values_in * values_in, axis=-1, keepdims=True) + norm_eps)
    return (values_in * inverse, inverse)


def norm_back(grads_in, unit_rows, inverse, gain):
    scaled = grads_in * gain
    extra = inverse * (scaled - unit_rows * jnp.mean(scaled * unit_rows, axis=-1, keepdims=True))
    return (extra, jnp.sum(grads_in * unit_rows, axis=0))


def rows_dot(left, right):
    return lax.dot_general(left, right, (((1,), (1,)), ((), ())), preferred_element_type=jnp.float32)


def plain_dot(left, right):
    return lax.dot_general(left, right, (((1,), (0,)), ((), ())), preferred_element_type=jnp.float32)


def head_masked(block, head, heads):
    if heads == 1:
        return block
    lanes = lax.broadcasted_iota(jnp.int32, block.shape, 1)
    return jnp.where(lanes // HD == head, block, jnp.zeros_like(block))


def lane_group(head, width):
    lanes = min(width, 128)
    return slice(head * HD // lanes * lanes, head * HD // lanes * lanes + lanes), head % (lanes // HD)


def attend_kernel(low_ref, q_ref, k_ref, v_ref, start_ref, o_ref, lse_ref, v_cols):
    row = pl.program_id(0)
    length, width = q_ref.shape[1:]
    heads = width // HD
    together = min(width, 128) // HD
    blocks = length // BLOCK
    for j in range(blocks):
        v_cols[:, j * BLOCK : (j + 1) * BLOCK] = v_ref[0, j * BLOCK : (j + 1) * BLOCK, :].T

    def query_block(i, carry):
        first = pl.multiple_of(i * BLOCK, BLOCK)
        q_heads = []
        for h in range(heads):
            lanes, at = lane_group(h, width)
            q_heads.append(head_masked(q_ref[0, pl.ds(first, BLOCK), lanes], at, together))
        start = start_ref[0, :, pl.ds(first, BLOCK)]
        places = first + lax.broadcasted_iota(jnp.int32, (1, BLOCK), 1)

        def key_block(j, state):
            at = pl.multiple_of(j * BLOCK, BLOCK)
            keys = at + lax.broadcasted_iota(jnp.int32, (BLOCK, BLOCK), 0)
            allowed = (keys >= start) & (keys <= places)
            scores = [
                rows_dot(k_ref[0, pl.ds(at, BLOCK), lane_group(h, width)[0]], q_heads[h])
                for h in range(heads)
            ]
            out = []
            for h in range(heads):
                top, total, acc = state[h]
                masked = jnp.where(allowed, scores[h], masked_score)
                new_top = jnp.maximum(top, jnp.max(masked, axis=0, keepdims=True))
                weights = jnp.exp2(masked - new_top)
                shrink = jnp.exp2(top - new_top)
                total = total * shrink + jnp.sum(weights, axis=0, keepdims=True)
                acc = acc * shrink + plain_dot(
                    v_cols[h * HD : (h + 1) * HD, pl.ds(at, BLOCK)], weights.astype(jnp.bfloat16)
                )
                out.append((new_top, total, acc))
            return tuple(out)

        begin = tuple(
            (
                jnp.full((1, BLOCK), masked_score, jnp.float32),
                jnp.zeros((1, BLOCK), jnp.float32),
                jnp.zeros((HD, BLOCK), jnp.float32),
            )
            for _ in range(heads)
        )
        state = key_block(i, begin)
        state = lax.fori_loop(low_ref[row * blocks + i], i, key_block, state)
        columns = jnp.concatenate([acc / total for _, total, acc in state], axis=0)
        o_ref[0, pl.ds(first, BLOCK), :] = columns.T.astype(jnp.bfloat16)
        for h in range(heads):
            top, total, _ = state[h]
            lse_ref[0, pl.ds(h, 1), pl.ds(first, BLOCK)] = top + jnp.log2(total)
        return carry

    lax.fori_loop(0, blocks, query_block, 0)


def attend(low, queries, keys, values, starts):
    rows, length, width = queries.shape
    heads = width // HD
    wide = pl.BlockSpec((1, length, width), lambda r, low: (r, 0, 0))
    return pl.pallas_call(
        attend_kernel,
        grid_spec=pltpu.PrefetchScalarGridSpec(
            num_scalar_prefetch=1,
            grid=(rows,),
            in_specs=[wide, wide, wide, pl.BlockSpec((1, 1, length), lambda r, low: (r, 0, 0))],
            out_specs=[wide, pl.BlockSpec((1, heads, length), lambda r, low: (r, 0, 0))],
            scratch_shapes=[pltpu.VMEM((width, length), jnp.bfloat16)],
        ),
        out_shape=[
            jax.ShapeDtypeStruct(queries.shape, jnp.bfloat16),
            jax.ShapeDtypeStruct((rows, heads, length), jnp.float32),
        ],
        compiler_params=pltpu.CompilerParams(vmem_limit_bytes=67043328),
        name="attend",
    )(low, queries, keys, values, starts)


def attend_back_kernel(
    low_ref, q_ref, k_ref, v_ref, o_ref, g_ref, lse_ref, start_ref,
    qg_ref, kg_ref, vg_ref, k_cols, k_acc, v_acc,
):
    row = pl.program_id(0)
    length, width = q_ref.shape[1:]
    heads = width // HD
    together = min(width, 128) // HD
    blocks = length // BLOCK
    for j in range(blocks):
        k_cols[:, j * BLOCK : (j + 1) * BLOCK] = k_ref[0, j * BLOCK : (j + 1) * BLOCK, :].T
    k_acc[...] = jnp.zeros_like(k_acc)
    v_acc[...] = jnp.zeros_like(v_acc)
    select = (
        lax.broadcasted_iota(jnp.int32, (8, width), 1) // HD
        == lax.broadcasted_iota(jnp.int32, (8, width), 0)
    ).astype(jnp.float32)

    def query_block(i, carry):
        first = pl.multiple_of(i * BLOCK, BLOCK)
        q_heads, g_heads = [], []
        for h in range(heads):
            lanes, at = lane_group(h, width)
            q_heads.append(head_masked(q_ref[0, pl.ds(first, BLOCK), lanes], at, together))
            g_heads.append(head_masked(g_ref[0, pl.ds(first, BLOCK), lanes], at, together))
        product = g_ref[0, pl.ds(first, BLOCK), :].astype(jnp.float32) * o_ref[
            0, pl.ds(first, BLOCK), :
        ].astype(jnp.float32)
        centre = lax.dot_general(
            select, product, (((1,), (1,)), ((), ())),
            precision=lax.Precision.HIGHEST, preferred_element_type=jnp.float32,
        )
        lse = lse_ref[0, :, pl.ds(first, BLOCK)]
        start = start_ref[0, :, pl.ds(first, BLOCK)]
        places = first + lax.broadcasted_iota(jnp.int32, (1, BLOCK), 1)

        def key_block(j, state):
            at = pl.multiple_of(j * BLOCK, BLOCK)
            keys = at + lax.broadcasted_iota(jnp.int32, (BLOCK, BLOCK), 0)
            allowed = (keys >= start) & (keys <= places)
            scores, prob_gs = [], []
            for h in range(heads):
                lanes, _ = lane_group(h, width)
                scores.append(rows_dot(k_ref[0, pl.ds(at, BLOCK), lanes], q_heads[h]))
                prob_gs.append(rows_dot(v_ref[0, pl.ds(at, BLOCK), lanes], g_heads[h]))
            out = []
            for h in range(heads):
                lanes, _ = lane_group(h, width)
                probs = jnp.exp2(jnp.where(allowed, scores[h], masked_score) - lse[h : h + 1, :])
                score_g = (probs * (prob_gs[h] - centre[h : h + 1, :])).astype(jnp.bfloat16)
                v_acc[pl.ds(at, BLOCK), lanes] += plain_dot(probs.astype(jnp.bfloat16), g_heads[h])
                k_acc[pl.ds(at, BLOCK), lanes] += plain_dot(score_g, q_heads[h])
                out.append(
                    state[h] + plain_dot(k_cols[h * HD : (h + 1) * HD, pl.ds(at, BLOCK)], score_g)
                )
            return tuple(out)

        begin = tuple(jnp.zeros((HD, BLOCK), jnp.float32) for _ in range(heads))
        state = lax.fori_loop(low_ref[row * blocks + i], i + 1, key_block, begin)
        columns = jnp.concatenate(state, axis=0) * HD ** (-0.5)
        qg_ref[0, pl.ds(first, BLOCK), :] = columns.T.astype(jnp.bfloat16)
        return carry

    lax.fori_loop(0, blocks, query_block, 0)
    kg_ref[0] = (k_acc[...] * LN2).astype(jnp.bfloat16)
    vg_ref[0] = v_acc[...].astype(jnp.bfloat16)


def attend_back(low, queries, keys, values, attended, grads, lse, starts):
    rows, length, width = queries.shape
    heads = width // HD
    wide = pl.BlockSpec((1, length, width), lambda r, low: (r, 0, 0))
    return pl.pallas_call(
        attend_back_kernel,
        grid_spec=pltpu.PrefetchScalarGridSpec(
            num_scalar_prefetch=1,
            grid=(rows,),
            in_specs=[wide] * 5
            + [
                pl.BlockSpec((1, heads, length), lambda r, low: (r, 0, 0)),
                pl.BlockSpec((1, 1, length), lambda r, low: (r, 0, 0)),
            ],
            out_specs=[wide] * 3,
            scratch_shapes=[
                pltpu.VMEM((width, length), jnp.bfloat16),
                pltpu.VMEM((length, width), jnp.float32),
                pltpu.VMEM((length, width), jnp.float32),
            ],
        ),
        out_shape=[jax.ShapeDtypeStruct(queries.shape, jnp.bfloat16)] * 3,
        compiler_params=pltpu.CompilerParams(vmem_limit_bytes=67043328),
        name="attend_back",
    )(low, queries, keys, values, attended, grads, lse, starts)


def columns_dot(left, right):
    return lax.dot_general(left, right, (((0,), (0,)), ((), ())), preferred_element_type=jnp.float32)


def feed_kernel(
    chunk, feed_ref, cot_ref, gate_w, up_w, down_w,
    feed_g_ref, out_ref, keep_ref, give_ref,
    feed_all, part, core_in, pair_in, acc,
    feed_send, feed_core, feed_pair, relay_send, part_send, part_core, sum_send, sum_pair,
):
    tokens = feed_ref.shape[0]
    chunks = tokens // chunk
    seq = lax.axis_index("seq")
    me = lax.axis_index("tp")
    pairs = lax.axis_size("tp") // 2
    pair, core = me // 2, lax.rem(me, 2)
    other = pair * 2 + 1 - core

    def peer(offset):
        return lax.rem(pair + offset, pairs) * 2 + core

    def copy(source, target, send, receive, to):
        return pltpu.make_async_remote_copy(
            src_ref=source, dst_ref=target, send_sem=send, recv_sem=receive,
            device_id=(seq, to), device_id_type=MESH,
        )

    barrier = pltpu.get_barrier_semaphore()
    for to in [other] + [peer(offset) for offset in range(1, pairs)]:
        pl.semaphore_signal(barrier, inc=1, device_id=(seq, to), device_id_type=MESH)
    pl.semaphore_wait(barrier, pairs)

    def rows(c):
        return pl.ds(pl.multiple_of(c * chunk, chunk), chunk)

    def feed_to_core(c):
        return copy(
            feed_ref.at[rows(c)], feed_all.at[me, rows(c)],
            feed_send.at[c], feed_core.at[c], other,
        )

    def feed_to_pair(offset, c):
        return copy(
            feed_ref.at[rows(c)], feed_all.at[me, rows(c)],
            feed_send.at[offset * chunks + c],
            feed_pair.at[(pairs - offset) * chunks + c], peer(offset),
        )

    def feed_from_pair(offset, c):
        return copy(
            feed_all.at[peer(offset), rows(c)], feed_all.at[peer(offset), rows(c)],
            feed_send.at[0], feed_pair.at[offset * chunks + c], other,
        )

    def relay(offset, c):
        return copy(
            feed_all.at[peer(offset), rows(c)], feed_all.at[peer(offset), rows(c)],
            relay_send.at[offset * chunks + c], feed_core.at[offset * chunks + c], other,
        )

    def part_to_core(offset, c):
        at = lax.rem(pair + offset, pairs) * 2 + 1 - core
        return copy(
            part.at[at, rows(c)], core_in.at[offset, rows(c)],
            part_send.at[offset * chunks + c], part_core.at[offset * chunks + c], other,
        )

    def sum_to_pair(offset, c):
        return copy(
            part.at[peer(offset), rows(c)], pair_in.at[pairs - offset, rows(c)],
            sum_send.at[offset * chunks + c],
            sum_pair.at[(pairs - offset) * chunks + c], peer(offset),
        )

    for c in range(chunks):
        feed_to_core(c).start()
        for offset in range(1, pairs):
            feed_to_pair(offset, c).start()
    feed_all[me] = feed_ref[...]
    acc[...] = jnp.zeros_like(acc)

    count = chunks * pairs
    early = chunks - 1

    def step(n, carry):
        which = lax.rem(n, 2)
        at = n // 2
        if early:
            at = at + (at + count - early) // count - (at + 1) // count * (count - early)
        c = lax.rem(at, chunks)
        offset = at // chunks
        owner = lax.rem(pair + offset, pairs) * 2 + lax.rem(core + which, 2)

        @pl.when((which == 0) & (offset > 0))
        def _():
            feed_from_pair(offset, c).wait_recv()
            relay(offset, c).start()

        @pl.when(which == 1)
        def _():
            relay(offset, c).wait_recv()

        feed = feed_all[owner, rows(c), :]
        cot = cot_ref[owner, rows(c), :]
        gate = rows_dot(feed, gate_w[...])
        up = rows_dot(feed, up_w[...])
        sigmoid = jax.nn.sigmoid(gate)
        activated = gate * sigmoid
        hidden = (activated * up).astype(jnp.bfloat16)
        hidden_g = rows_dot(cot, down_w[...])
        up_g = (hidden_g * activated).astype(jnp.bfloat16)
        gate_g = (hidden_g * up * sigmoid * (1.0 + gate * (1.0 - sigmoid))).astype(jnp.bfloat16)
        part[owner, rows(c), :] = (
            plain_dot(gate_g, gate_w[...]) + plain_dot(up_g, up_w[...])
        ).astype(jnp.bfloat16)

        @pl.when(which == 1)
        def _():
            part_to_core(offset, c).start()

        out_ref[owner, rows(c), :] = plain_dot(hidden, down_w[...]).astype(jnp.bfloat16)
        acc[0] += columns_dot(gate_g, feed)
        acc[1] += columns_dot(up_g, feed)
        acc[2] += columns_dot(hidden, cot)

        @pl.when((which == 1) & (offset > 0))
        def _():
            part_to_core(offset, c).wait_recv()
            to = peer(offset)
            part[to, rows(c), :] = (
                part[to, rows(c), :].astype(jnp.float32)
                + core_in[offset, rows(c), :].astype(jnp.float32)
            ).astype(jnp.bfloat16)
            sum_to_pair(offset, c).start()

        return carry

    lax.fori_loop(0, 2 * chunks * pairs, step, 0)
    half = acc.shape[1] // 2
    flag = lax.rem(seq, 2)
    for n in range(3):
        keep_ref[n] = acc[n, pl.ds(pl.multiple_of(flag * half, 8), half), :].astype(jnp.bfloat16)
        give_ref[n] = acc[n, pl.ds(pl.multiple_of((1 - flag) * half, 8), half), :].astype(
            jnp.bfloat16
        )
    for c in range(chunks):
        part_to_core(0, c).wait_recv()
        for offset in range(1, pairs):
            sum_to_pair(offset, c).wait_recv()
        total = part[me, rows(c), :].astype(jnp.float32) + core_in[0, rows(c), :].astype(jnp.float32)
        for offset in range(1, pairs):
            total = total + pair_in[offset, rows(c), :].astype(jnp.float32)
        feed_g_ref[rows(c), :] = total
    for c in range(chunks):
        feed_to_core(c).wait_send()
        part_to_core(0, c).wait_send()
        for offset in range(1, pairs):
            feed_to_pair(offset, c).wait_send()
            relay(offset, c).wait_send()
            part_to_core(offset, c).wait_send()
            sum_to_pair(offset, c).wait_send()


def feed_forward(feed_in, cot_all, gate_weight, up_weight, down_weight):
    tokens, width = feed_in.shape
    tp_size = cot_all.shape[0]
    pairs = tp_size // 2
    chunk = min(tokens, 256)
    chunks = tokens // chunk
    hidden = gate_weight.shape[0]
    whole = pl.BlockSpec(memory_space=pltpu.VMEM)
    dma = pltpu.SemaphoreType.DMA
    return pl.pallas_call(
        functools.partial(feed_kernel, chunk),
        out_shape=[
            jax.ShapeDtypeStruct((tokens, width), jnp.float32),
            jax.ShapeDtypeStruct(cot_all.shape, jnp.bfloat16),
            jax.ShapeDtypeStruct((3, hidden // 2, width), jnp.bfloat16),
            jax.ShapeDtypeStruct((3, hidden // 2, width), jnp.bfloat16),
        ],
        in_specs=[whole] * 5,
        out_specs=[whole] * 4,
        scratch_shapes=[
            pltpu.VMEM(cot_all.shape, jnp.bfloat16),
            pltpu.VMEM(cot_all.shape, jnp.bfloat16),
            pltpu.VMEM((pairs, tokens, width), jnp.bfloat16),
            pltpu.VMEM((pairs, tokens, width), jnp.bfloat16),
            pltpu.VMEM((3, hidden, width), jnp.float32),
        ]
        + [dma((pairs * chunks,))] * 8,
        compiler_params=pltpu.CompilerParams(
            collective_id=4, has_side_effects=True, vmem_limit_bytes=67043328
        ),
        name="feed_forward",
    )(feed_in, cot_all, gate_weight, up_weight, down_weight)


def group_of(place, seq_size):
    half = seq_size // 2
    low = place // 2
    return lax.rem(place + low, 2) * half + low


def place_of(group, seq_size):
    half = seq_size // 2
    low = lax.rem(group, half)
    return low * 2 + lax.rem(low + group // half, 2)


def remote(source, target, send, receive, to):
    return pltpu.make_async_remote_copy(
        src_ref=source, dst_ref=target, send_sem=send, recv_sem=receive,
        device_id=to, device_id_type=MESH,
    )


def same(left, right):
    return (left[0] == right[0]) & (left[1] == right[1])


class Exchange:
    def __init__(self, plan, me, source, target, local_sem, send_sem, receive_sem):
        self.me = me
        self.sends, self.receives = plan(*me)
        self.source, self.target = source, target
        self.local_sem, self.send_sem, self.receive_sem = local_sem, send_sem, receive_sem

    def greet(self, barrier):
        for origin, _, _ in self.receives:
            @pl.when(jnp.logical_not(same(origin, self.me)))
            def _():
                pl.semaphore_signal(barrier, inc=1, device_id=origin, device_id_type=MESH)

    def others(self):
        return sum(jnp.where(same(to, self.me), 0, 1) for to, _, _, _ in self.sends)

    def each_send(self, wait):
        for n, (to, source, target, at) in enumerate(self.sends):
            here = same(to, self.me)

            @pl.when(here)
            def _():
                copy = pltpu.make_async_copy(
                    self.source.at[source], self.target.at[target], self.local_sem.at[n]
                )
                copy.wait() if wait else copy.start()

            @pl.when(jnp.logical_not(here))
            def _():
                copy = remote(
                    self.source.at[source], self.target.at[target],
                    self.send_sem.at[n], self.receive_sem.at[at], to,
                )
                copy.wait_send() if wait else copy.start()

    def start(self):
        self.each_send(False)

    def wait_sends(self):
        self.each_send(True)

    def wait_receive(self, origin, target, at):
        @pl.when(jnp.logical_not(same(origin, self.me)))
        def _():
            remote(
                self.target.at[target], self.target.at[target],
                self.send_sem.at[0], self.receive_sem.at[at], origin,
            ).wait_recv()

    def wait_receives(self):
        for receive in self.receives:
            self.wait_receive(*receive)


def exchange(arrays, out_shapes, plans, number):
    count = len(arrays)

    def kernel(*refs):
        me = (lax.axis_index("seq"), lax.axis_index("tp"))
        moves = [
            Exchange(plan, me, refs[n], refs[count + n], *refs[2 * count + 3 * n :][:3])
            for n, plan in enumerate(plans)
        ]
        barrier = pltpu.get_barrier_semaphore()
        for move in moves:
            move.greet(barrier)
        pl.semaphore_wait(barrier, sum(move.others() for move in moves))
        for move in moves:
            move.start()
        for move in moves:
            move.wait_sends()
        for move in moves:
            move.wait_receives()

    semaphores = []
    for plan in plans:
        semaphores += [pltpu.SemaphoreType.DMA((len(plan(0, 0)[0]),))] * 3
    return pl.pallas_call(
        kernel,
        out_shape=[
            jax.ShapeDtypeStruct(shape, array.dtype) for shape, array in zip(out_shapes, arrays)
        ],
        in_specs=[pl.BlockSpec(memory_space=pl.ANY)] * count,
        out_specs=[pl.BlockSpec(memory_space=pl.ANY)] * count,
        scratch_shapes=semaphores,
        compiler_params=pltpu.CompilerParams(collective_id=number, has_side_effects=True),
        name=f"exchange_{number}",
    )(*arrays)


def owner_to_quarter(seq_size, tp_size, rows_each, rows_local, piece_first):
    def plan(s, t):
        sends, receives = [], []
        for slot in range(rows_local):
            row = t * rows_local + slot
            to = place_of(row // rows_each, seq_size)
            j = lax.rem(row, rows_each)
            for i in range(tp_size):
                target = (i, j, s) if piece_first else (j, s, i)
                sends.append(((to, i), (slot, i), target, j * seq_size + s))
        group = group_of(s, seq_size)
        for j in range(rows_each):
            row = group * rows_each + j
            for i in range(seq_size):
                origin = lax.rem(s + i, seq_size)
                target = (t, j, origin) if piece_first else (j, origin, t)
                receives.append(((origin, row // rows_local), target, j * seq_size + origin))
        return sends, receives

    return plan


def quarter_to_owner(seq_size, tp_size, rows_each, rows_local):
    def plan(s, t):
        sends, receives = [], []
        group = group_of(s, seq_size)
        for i in range(seq_size):
            to = lax.rem(s + i, seq_size)
            for j in range(rows_each):
                row = group * rows_each + j
                slot = lax.rem(row, rows_local)
                sends.append(((to, row // rows_local), (j, to), (slot, t), slot * tp_size + t))
        for slot in range(rows_local):
            row = t * rows_local + slot
            for i in range(tp_size):
                receives.append(
                    ((place_of(row // rows_each, seq_size), i), (slot, i), slot * tp_size + i)
                )
        return sends, receives

    return plan


def places_to_rows(seq_size, rows_each):
    def plan(s, t):
        sends, receives = [], []
        for i in range(seq_size):
            to = lax.rem(s + i, seq_size)
            rows = pl.ds(group_of(to, seq_size) * rows_each, rows_each)
            sends.append(((to, t), (rows,), (slice(None), s), s))
            origin = lax.rem(s + seq_size - i, seq_size)
            receives.append(((origin, t), (slice(None), origin), origin))
        return sends, receives

    return plan


def rows_to_places(seq_size, rows_each):
    def plan(s, t):
        sends, receives = [], []
        rows = pl.ds(group_of(s, seq_size) * rows_each, rows_each)
        for i in range(seq_size):
            to = lax.rem(s + i, seq_size)
            sends.append(((to, t), (slice(None), to), (rows,), s))
            origin = lax.rem(s + seq_size - i, seq_size)
            source_rows = pl.ds(group_of(origin, seq_size) * rows_each, rows_each)
            receives.append(((origin, t), (source_rows,), origin))
        return sends, receives

    return plan


def heads_to_tokens(tp_size):
    def plan(s, t):
        sends, receives = [], []
        for i in range(tp_size):
            to = lax.rem(t + i, tp_size)
            sends.append(((s, to), (slice(None), slice(None), to), (t,), t))
            origin = lax.rem(t + tp_size - i, tp_size)
            receives.append(((s, origin), (origin,), origin))
        return sends, receives

    return plan


def tokens_to_heads(tp_size):
    def plan(s, t):
        sends, receives = [], []
        for i in range(tp_size):
            to = lax.rem(t + i, tp_size)
            sends.append(((s, to), (to,), (slice(None), slice(None), t), t))
            origin = lax.rem(t + tp_size - i, tp_size)
            receives.append(((s, origin), (slice(None), slice(None), origin), origin))
        return sends, receives

    return plan


def spread_kernel(
    plans, sizes, x_ref, cot_ref, first_ref, output_ref, q_w, k_w, v_w, offset_ref, frequency_ref,
    gain_ref,
    x_out, cot_out, first_out, output_out, q_ref, k_ref, v_ref, cos_ref, sin_ref, square_ref,
    x_rows, first_rows, q_turned, k_turned,
    x_local, x_send, x_receive, cot_local, cot_send, cot_receive,
    first_local, first_send, first_receive,
    core_send, core_receive, pair_send, pair_receive, relay_send, load_sem, output_sem,
):
    seq_size, tp_size, rows_each, rows_local, parts = sizes
    me = (lax.axis_index("seq"), lax.axis_index("tp"))
    s, t = me
    pairs = tp_size // 2
    pair, core = t // 2, lax.rem(t, 2)
    other = pair * 2 + 1 - core
    each = seq_size // parts

    def peer(offset):
        return lax.rem(pair + offset, pairs) * 2 + core

    x_move = Exchange(plans[0], me, x_ref, x_out, x_local, x_send, x_receive)
    cot_move = Exchange(plans[1], me, cot_ref, cot_out, cot_local, cot_send, cot_receive)
    first_move = Exchange(plans[2], me, first_ref, first_out, first_local, first_send, first_receive)
    moves = (x_move, first_move, cot_move)
    barrier = pltpu.get_barrier_semaphore()
    for move in moves:
        move.greet(barrier)
    for to in [other] + [peer(offset) for offset in range(1, pairs)]:
        pl.semaphore_signal(barrier, inc=1, device_id=(s, to), device_id_type=MESH)
    pl.semaphore_wait(barrier, sum(move.others() for move in moves) + pairs)
    for move in moves:
        move.start()

    def block(out, tensor, piece, part):
        if tensor == 2:
            return out.at[piece]
        span = pl.ds(part * each, each)
        return out.at[:, span, piece] if tensor == 0 else out.at[piece, :, span]

    def number(tensor, offset, part):
        return (tensor * pairs + offset) * parts + part

    def own(out, tensor, part):
        return output_ref if tensor == 2 else block(out, tensor, t, part)

    def to_core(out, tensor, part):
        view, at = block(out, tensor, t, part), number(tensor, 0, part)
        return remote(own(out, tensor, part), view, core_send.at[at], core_receive.at[at], (s, other))

    def to_pair(out, tensor, offset, part):
        view = block(out, tensor, t, part)
        return remote(
            own(out, tensor, part), view, pair_send.at[number(tensor, offset, part)],
            pair_receive.at[number(tensor, pairs - offset, part)], (s, peer(offset)),
        )

    def from_pair(out, tensor, offset, part):
        view, at = block(out, tensor, peer(offset), part), number(tensor, offset, part)
        return remote(view, view, pair_send.at[at], pair_receive.at[at], (s, peer(offset)))

    def relay(out, tensor, offset, part):
        view, at = block(out, tensor, peer(offset), part), number(tensor, offset, part)
        return remote(view, view, relay_send.at[at], core_receive.at[at], (s, other))

    def from_core(out, tensor, offset, part):
        piece = lax.rem(pair + offset, pairs) * 2 + 1 - core
        view, at = block(out, tensor, piece, part), number(tensor, offset, part)
        return remote(view, view, relay_send.at[at], core_receive.at[at], (s, other))

    def forward(move, out, tensor):
        def receive(n, carry):
            part = lax.rem(s // each + n, parts)
            for j in range(rows_each):
                for i in range(each):
                    origin = part * each + i
                    group = group_of(s, seq_size)
                    owner = (origin, (group * rows_each + j) // rows_local)
                    target = (t, j, origin) if tensor else (j, origin, t)
                    move.wait_receive(owner, target, j * seq_size + origin)
                    slot = lax.rem(group * rows_each + j, rows_local)

                    @pl.when(same(owner, me))
                    def _():
                        pltpu.make_async_copy(
                            move.source.at[slot, t], move.target.at[target],
                            move.local_sem.at[slot * tp_size + t],
                        ).wait()
            to_core(out, tensor, part).start()
            for offset in range(1, pairs):
                to_pair(out, tensor, offset, part).start()
            return carry

        def relays(n, carry):
            part = lax.rem(s // each + n, parts)
            for offset in range(1, pairs):
                from_pair(out, tensor, offset, part).wait_recv()
                relay(out, tensor, offset, part).start()
            return carry

        lax.fori_loop(0, parts, receive, 0)
        lax.fori_loop(0, parts, relays, 0)

    def arrive(out, tensor):
        def one(part, carry):
            for offset in range(pairs):
                from_core(out, tensor, offset, part).wait_recv()
            return carry

        lax.fori_loop(0, parts, one, 0)

    def finish(move, out, tensor):
        def one(part, carry):
            to_core(out, tensor, part).wait_send()
            for offset in range(1, pairs):
                to_pair(out, tensor, offset, part).wait_send()
                relay(out, tensor, offset, part).wait_send()
            return carry

        lax.fori_loop(0, parts, one, 0)
        for n, (to, source, target, at) in enumerate(move.sends):
            @pl.when(jnp.logical_not(same(to, me)))
            def _():
                remote(
                    move.source.at[source], move.target.at[target],
                    move.send_sem.at[n], move.receive_sem.at[at], to,
                ).wait_send()

    blocks, _, piece, depth = x_rows.shape
    places = tp_size * piece
    width = q_w.shape[0]
    lanes = cos_ref.shape[2]
    output_copy = pltpu.make_async_copy(output_ref, output_out.at[t], output_sem)
    output_copy.start()
    turn = half_turn(width)
    q_turned[...] = plain_dot(turn, q_w[...]).astype(jnp.bfloat16)
    k_turned[...] = plain_dot(turn, k_w[...]).astype(jnp.bfloat16)
    square_ref[...] = jnp.zeros_like(square_ref)

    def tables(n, carry):
        angles = frequency_ref[...] * offset_ref[n]
        cos_ref[n] = jnp.concatenate([jnp.cos(angles)] * (2 * lanes // HD), axis=0).T
        sin_ref[n] = jnp.concatenate([jnp.sin(angles)] * (2 * lanes // HD), axis=0).T
        return carry

    lax.fori_loop(0, blocks, tables, 0)

    def x_load(n):
        source = x_out.at[n // seq_size, lax.rem(n, seq_size)]
        return pltpu.make_async_copy(source, x_rows.at[n], load_sem.at[n])

    def first_load(n):
        source = first_out.at[n // seq_size, lax.rem(n, seq_size)]
        return pltpu.make_async_copy(source, first_rows.at[n], load_sem.at[n])

    def start_loads(load):
        def one(n, carry):
            load(n).start()
            return carry

        lax.fori_loop(0, blocks, one, 0)

    def query_key(n, carry):
        x_load(n).wait()
        x = x_rows[n].reshape(places, depth).astype(jnp.float32)
        inverse = lax.rsqrt(jnp.mean(x * x, axis=-1, keepdims=True) + norm_eps)
        normed = (x * inverse * gain_ref[...]).astype(jnp.bfloat16)
        cosine, sine = widen(cos_ref[n], width), widen(sin_ref[n], width)
        q_ref[n] = (
            (rows_dot(normed, q_w[...]) * cosine + rows_dot(normed, q_turned[...]) * sine)
            * (HD ** (-0.5) * LOG2E)
        ).astype(jnp.bfloat16)
        k_ref[n] = (
            rows_dot(normed, k_w[...]) * cosine + rows_dot(normed, k_turned[...]) * sine
        ).astype(jnp.bfloat16)
        x_rows[n] = normed.reshape(x_rows.shape[1:])
        return carry

    def mix(n, carry):
        first_load(n).wait()
        first = first_rows[n].astype(jnp.float32)
        value = rows_dot(x_rows[n].reshape(places, depth), v_w[...])
        mixed = (0.5 * value + 0.5 * first.T).astype(jnp.bfloat16)
        v_ref[n] = mixed
        wide = mixed.astype(jnp.float32)
        square_ref[0:1, : first.shape[1]] += jnp.sum(first * first, axis=0, keepdims=True)
        square_ref[1:2, : wide.shape[1]] += jnp.sum(wide * wide, axis=0, keepdims=True)
        return carry

    forward(x_move, x_out, 0)
    to_core(output_out, 2, 0).start()
    for offset in range(1, pairs):
        to_pair(output_out, 2, offset, 0).start()
    arrive(x_out, 0)
    start_loads(x_load)
    lax.fori_loop(0, blocks, query_key, 0)
    first_move.wait_sends()
    first_move.wait_receives()
    start_loads(first_load)
    lax.fori_loop(0, blocks, mix, 0)
    for offset in range(1, pairs):
        from_pair(output_out, 2, offset, 0).wait_recv()
        relay(output_out, 2, offset, 0).start()
    forward(cot_move, cot_out, 1)
    arrive(cot_out, 1)
    for offset in range(pairs):
        from_core(output_out, 2, offset, 0).wait_recv()
    to_core(output_out, 2, 0).wait_send()
    for offset in range(1, pairs):
        to_pair(output_out, 2, offset, 0).wait_send()
        relay(output_out, 2, offset, 0).wait_send()
    finish(x_move, x_out, 0)
    finish(cot_move, cot_out, 1)
    output_copy.wait()


def half_turn(width):
    row = lax.broadcasted_iota(jnp.int32, (width, width), 0)
    column = lax.broadcasted_iota(jnp.int32, (width, width), 1)
    low = lax.rem(row, HD) < HD // 2
    minus = low & (column == row + HD // 2)
    plus = jnp.logical_not(low) & (column == row - HD // 2)
    return jnp.where(plus, 1.0, jnp.where(minus, -1.0, 0.0)).astype(jnp.bfloat16)


def spread(
    layer_input, cotangent, first_values, output_weight, query_weight, key_weight, value_weight,
    offsets, frequency, gain, sizes,
):
    seq_size, tp_size, rows_each, rows_local, parts = sizes
    pieces = layer_input.shape[2:]
    width, depth = query_weight.shape
    features, places = first_values.shape[1:]
    blocks = rows_each * seq_size
    lanes = min(width, 128)
    plans = (
        owner_to_quarter(seq_size, tp_size, rows_each, rows_local, False),
        owner_to_quarter(seq_size, tp_size, rows_each, rows_local, True),
        places_to_rows(seq_size, rows_each),
    )
    dma = pltpu.SemaphoreType.DMA
    quarter = [
        dma((rows_local * tp_size,)), dma((rows_local * tp_size,)), dma((rows_each * seq_size,)),
    ]
    stage = tp_size // 2 * parts * 3
    bf16, f32 = jnp.bfloat16, jnp.float32
    anywhere = pl.BlockSpec(memory_space=pl.ANY)
    vmem = pl.BlockSpec(memory_space=pltpu.VMEM)
    part = jax.ShapeDtypeStruct((blocks, places, width), bf16)
    table = jax.ShapeDtypeStruct((blocks, places, lanes), f32)
    return pl.pallas_call(
        functools.partial(spread_kernel, plans, sizes),
        out_shape=[
            jax.ShapeDtypeStruct((rows_each, seq_size, tp_size) + pieces, bf16),
            jax.ShapeDtypeStruct((tp_size, rows_each, seq_size) + pieces, bf16),
            jax.ShapeDtypeStruct((rows_each, seq_size, features, places), bf16),
            jax.ShapeDtypeStruct((tp_size,) + output_weight.shape, bf16),
            part,
            part,
            part,
            table,
            table,
            jax.ShapeDtypeStruct((8, max(width, places)), f32),
        ],
        in_specs=[anywhere] * 3 + [vmem] * 7,
        out_specs=[anywhere] * 4 + [vmem] * 6,
        scratch_shapes=[
            pltpu.VMEM((blocks, tp_size) + pieces, bf16),
            pltpu.VMEM((blocks, features, places), bf16),
            pltpu.VMEM((width, depth), bf16),
            pltpu.VMEM((width, depth), bf16),
        ]
        + quarter
        + quarter
        + [dma((seq_size,))] * 3
        + [dma((stage,))] * 5
        + [dma((blocks,)), dma],
        compiler_params=pltpu.CompilerParams(
            collective_id=5, has_side_effects=True, vmem_limit_bytes=67043328
        ),
        name="spread",
    )(
        layer_input, cotangent, first_values, output_weight, query_weight, key_weight,
        value_weight, offsets, frequency, gain,
    )


def widen(table, width):
    return jnp.concatenate([table] * (width // table.shape[1]), axis=1)


class Reduce:
    def __init__(self, place, full, core_in, pair_in, chunks, sems):
        self.seq, self.tp, self.pairs = place
        self.pair, self.core = self.tp // 2, lax.rem(self.tp, 2)
        self.other = self.pair * 2 + 1 - self.core
        self.full, self.core_in, self.pair_in = full, core_in, pair_in
        self.chunks = chunks
        self.core_send, self.core_recv, self.pair_send, self.pair_recv = sems

    def peer(self, offset):
        return lax.rem(self.pair + offset, self.pairs) * 2 + self.core

    def cut(self, ref, lead, c):
        return ref.at[lead, :, c]

    def to_core(self, offset, c):
        lead = lax.rem(self.pair + offset, self.pairs) * 2 + 1 - self.core
        at = offset * self.chunks + c
        return remote(
            self.cut(self.full, lead, c), self.cut(self.core_in, offset, c),
            self.core_send.at[at], self.core_recv.at[at], (self.seq, self.other),
        )

    def to_pair(self, offset, c):
        back = self.pairs - offset
        return remote(
            self.cut(self.full, self.peer(offset), c), self.cut(self.pair_in, back - 1, c),
            self.pair_send.at[offset * self.chunks + c],
            self.pair_recv.at[back * self.chunks + c], (self.seq, self.peer(offset)),
        )

    def from_pair(self, offset, c):
        view, at = self.cut(self.pair_in, offset - 1, c), offset * self.chunks + c
        return remote(
            view, view, self.pair_send.at[at], self.pair_recv.at[at], (self.seq, self.peer(offset))
        )

    def start(self, c):
        for offset in list(range(1, self.pairs)) + [0]:
            self.to_core(offset, c).start()

    def pass_on(self, c):
        for offset in range(1, self.pairs):
            self.to_core(offset, c).wait_recv()
            to = self.peer(offset)

            def add(b, carry):
                self.full[to, b, c] = (
                    self.full[to, b, c].astype(jnp.float32)
                    + self.core_in[offset, b, c].astype(jnp.float32)
                ).astype(jnp.bfloat16)
                return carry

            lax.fori_loop(0, self.full.shape[1], add, 0)
            self.to_pair(offset, c).start()

    def arrive(self, c):
        self.to_core(0, c).wait_recv()
        for offset in range(1, self.pairs):
            self.from_pair(offset, c).wait_recv()

    def total(self, b, c):
        value = self.full[self.tp, b, c].astype(jnp.float32)
        value = value + self.core_in[0, b, c].astype(jnp.float32)
        for offset in range(1, self.pairs):
            value = value + self.pair_in[offset - 1, b, c].astype(jnp.float32)
        return value

    def finish(self):
        for c in range(self.chunks):
            for offset in range(self.pairs):
                self.to_core(offset, c).wait_send()
            for offset in range(1, self.pairs):
                self.to_pair(offset, c).wait_send()


class SeqSum:
    def __init__(self, place, steps, done, blocks, held, mine, sums, local_sem, send_sem, recv_sem):
        self.seq, self.tp = place
        self.count, self.done, self.size = steps, done, 1 << steps
        self.blocks, self.held, self.mine, self.sums = blocks, held, mine, sums
        self.local_sem, self.send_sem, self.recv_sem = local_sem, send_sem, recv_sem
        self.flags = [lax.rem(self.seq // (1 << n), 2) for n in range(steps)]
        low, self.lows = 0, [0]
        for n in range(steps):
            low = low + self.flags[n] * (self.size >> (n + 1))
            self.lows.append(low)

    def partner(self, n):
        return (self.seq + (1 - 2 * self.flags[n]) * (1 << n), self.tp)

    def half(self, n):
        return self.size >> (n + 1)

    def begin(self, n):
        return (self.size >> self.done) - (self.size >> n)

    def give(self, n):
        half = self.half(n)
        low = self.lows[n] - self.lows[self.done] + (1 - self.flags[n]) * half
        return remote(
            self.blocks.at[pl.ds(low, half)], self.held.at[pl.ds(self.begin(n), half)],
            self.send_sem.at[n], self.recv_sem.at[n], self.partner(n),
        )

    def take(self, n):
        copy = self.give(n)
        copy.wait_recv()
        copy.wait_send()
        last = n + 1 == self.count

        def add(b, carry):
            at = self.lows[n + 1] - self.lows[self.done] + b
            value = (
                self.blocks[at].astype(jnp.float32)
                + self.held[self.begin(n) + b].astype(jnp.float32)
            ).astype(jnp.bfloat16)
            if last:
                self.mine[b] = value
            else:
                self.blocks[at] = value
            return carry

        lax.fori_loop(0, self.half(n), add, 0)

    def store(self):
        return pltpu.make_async_copy(
            self.mine, self.sums.at[pl.ds(self.lows[self.count], 1)], self.local_sem
        )

    def spread(self, n):
        target = self.sums.at[pl.ds(self.lows[n + 1], self.half(n))]
        source = self.mine if n + 1 == self.count else target
        at = self.count + n
        return remote(source, target, self.send_sem.at[at], self.recv_sem.at[at], self.partner(n))

    def collect(self, n):
        half = self.half(n)
        view = self.sums.at[pl.ds(self.lows[n] + (1 - self.flags[n]) * half, half)]
        at = self.count + n
        remote(view, view, self.send_sem.at[at], self.recv_sem.at[at], self.partner(n)).wait_recv()

    def steps(self):
        self.give(self.done).start()
        yield
        for n in range(self.done, self.count):
            self.take(n)
            if n + 1 < self.count:
                self.give(n + 1).start()
            else:
                self.spread(n).start()
                self.store().start()
            yield
        for n in range(self.count - 1, -1, -1):
            self.collect(n)
            if n + 1 == self.count:
                self.store().wait()
            if n > 0:
                self.spread(n - 1).start()
            yield
        for n in range(self.count):
            self.spread(n).wait_send()


def tail_kernel(
    sizes, dv_plan, out_hbm, keep_hbm, got_hbm, x_hbm, q_hbm, k_hbm, v_hbm, cos_hbm, sin_hbm,
    qw_hbm, kw_hbm, vw_hbm, attended_hbm, source_hbm, middle_hbm, middle_g_hbm, dv_hbm, gain_ref, small_ref,
    out_ref, input_g_ref, first_g_ref, sums_ref, feed_ref, gain_g_ref, feed_gain_g_ref, norms_ref,
    x_rows, q_rows, k_rows, v_rows, cos_rows, sin_rows, weights, attended, grad_acc,
    normed_full, normed_core, normed_pair, proj_full, proj_core, proj_pair,
    out_full, out_core, out_pair, source, middle, middle_g, input_g, result,
    blocks, held, mine, feed_blocks, feed_got, feed_held, feed_mine,
    small, tp_held, tp_sum, seq_held, dv_rows, dv_cols,
    *sems,
):
    seq_size, tp_size, rows_each, rows_local, _ = sizes
    s, t = lax.axis_index("seq"), lax.axis_index("tp")
    me = (s, t)
    pairs = tp_size // 2
    count = seq_size.bit_length() - 1
    normed_sems, proj_sems, out_sems = sems[:4], sems[4:8], sems[8:12]
    dv_sems, back_sems, lo_sems = sems[12:15], sems[15:18], sems[18:21]
    load_sem, x_sem, feed_sem, store_sem, grad_send, grad_recv = sems[21:27]
    feed_send, feed_recv, small_send, tp_sem, seq_sem, first_sem = sems[27:]
    place = (s, t, pairs)
    normed = Reduce(place, normed_full, normed_core, normed_pair, 2, normed_sems)
    proj = Reduce(place, proj_full, proj_core, proj_pair, 1, proj_sems)
    out = Reduce(place, out_full, out_core, out_pair, 2, out_sems)
    dv_move = Exchange(dv_plan, me, dv_hbm, dv_rows, *dv_sems)
    half = source.shape[0]
    places, depth = x_rows.shape[1:]
    width = q_rows.shape[2]

    group = group_of(s, seq_size)
    origins = []
    for slot in range(rows_local):
        row = t * rows_local + slot
        for i in range(tp_size):
            origins.append(((place_of(row // rows_each, seq_size), i), slot, i))

    tp_peers = [lax.rem(t + i, tp_size) for i in range(1, tp_size)]
    seq_peers = [lax.rem(s + i, seq_size) for i in range(1, seq_size)]

    names = (
        (q_hbm, q_rows), (k_hbm, k_rows), (v_hbm, v_rows), (cos_hbm, cos_rows),
        (sin_hbm, sin_rows), (qw_hbm, weights.at[pl.ds(0, width)]),
        (kw_hbm, weights.at[pl.ds(width, width)]), (vw_hbm, weights.at[pl.ds(2 * width, width)]),
        (out_hbm, out_full), (attended_hbm, attended),
        (middle_g_hbm, middle_g), (source_hbm, source), (middle_hbm, middle),
    )
    loads = [
        pltpu.make_async_copy(origin, target, load_sem.at[n])
        for n, (origin, target) in enumerate(names)
    ]
    feed_loads = [
        (
            pltpu.make_async_copy(keep_hbm.at[n], feed_blocks.at[n], feed_sem.at[2 * n]),
            pltpu.make_async_copy(got_hbm.at[n], feed_got.at[n], feed_sem.at[2 * n + 1]),
        )
        for n in range(3)
    ]

    def x_load(n):
        return pltpu.make_async_copy(x_hbm.at[n], x_rows.at[n], x_sem.at[n])

    def ordered(n):
        return 2 * lax.rem(n, half) + n // half

    for pair in feed_loads:
        for copy in pair:
            copy.start()
    for n in (9, 10, 8):
        loads[n].start()
    for copy in loads[:8]:
        copy.start()
    for n in range(2 * half):
        x_load(ordered(n)).start()
    for copy in loads[11:]:
        copy.start()

    barrier = pltpu.get_barrier_semaphore()
    dv_move.greet(barrier)
    for origin, _, _ in origins:
        @pl.when(jnp.logical_not(same(origin, me)))
        def _():
            pl.semaphore_signal(barrier, inc=1, device_id=origin, device_id_type=MESH)
    for to in tp_peers:
        pl.semaphore_signal(barrier, inc=1, device_id=(s, to), device_id_type=MESH)
    for to in seq_peers:
        pl.semaphore_signal(barrier, inc=1, device_id=(to, t), device_id_type=MESH)
    back_others = sum(
        jnp.where(same((to, (group * rows_each + j) // rows_local), me), 0, 1)
        for j in range(rows_each)
        for to in range(seq_size)
    )
    pl.semaphore_wait(barrier, dv_move.others() + back_others + tp_size + seq_size - 2)

    def seq_sum(n, done, *refs):
        return SeqSum(
            me, count, done, *refs, store_sem.at[n],
            (grad_send if done == 0 else feed_send).at[n if done == 0 else n - 2],
            (grad_recv if done == 0 else feed_recv).at[n if done == 0 else n - 2],
        ).steps()

    sums = [
        seq_sum(n, 0, blocks.at[n], held.at[n], mine.at[n], sums_ref.at[n]) for n in range(2)
    ]
    feeds = [
        seq_sum(
            n + 2, 1, feed_blocks.at[n], feed_held.at[n], feed_mine.at[n], feed_ref.at[n]
        )
        for n in range(3)
    ]

    for n in range(3):
        for copy in feed_loads[n]:
            copy.wait()

        def join(b, carry):
            feed_blocks[n, b] = (
                feed_blocks[n, b].astype(jnp.float32) + feed_got[n, b].astype(jnp.float32)
            ).astype(jnp.bfloat16)
            return carry

        lax.fori_loop(0, feed_blocks.shape[1], join, 0)
        next(feeds[n])
    fine = blocks.shape[2]
    loads[9].wait()
    loads[10].wait()
    branch = middle_g[...].reshape(2 * half * middle_g.shape[2], depth).astype(jnp.bfloat16)
    for i in range(tp_size):
        product = columns_dot(attended[i], branch)
        for n in range(seq_size // 2):
            proj_full[i, n, 0] = product[n * fine : (n + 1) * fine].astype(jnp.bfloat16)
    proj.start(0)
    loads[8].wait()
    out.start(0)
    out.start(1)
    dv_move.start()
    for copy in loads[:8]:
        copy.wait()
    turn = half_turn(width)
    grad_acc[...] = jnp.zeros_like(grad_acc)
    gain = gain_ref[...]

    def project_back(first, last):
        def one(n, carry):
            at = ordered(n)
            x_load(at).wait()
            x = x_rows[at].astype(jnp.float32)
            inverse = lax.rsqrt(jnp.mean(x * x, axis=-1, keepdims=True) + norm_eps)
            rows = (x * inverse * gain).astype(jnp.bfloat16)
            cosine, sine = widen(cos_rows[at], width), widen(sin_rows[at], width)

            def unrotate(grad):
                turned = plain_dot(grad, turn)
                return (grad.astype(jnp.float32) * cosine + turned * sine).astype(jnp.bfloat16)

            stacked = jnp.concatenate(
                [
                    unrotate(q_rows[at]),
                    unrotate(k_rows[at]),
                    (0.5 * v_rows[at].astype(jnp.float32)).astype(jnp.bfloat16),
                ],
                axis=1,
            )
            b, c = at // 2, lax.rem(at, 2)
            product = plain_dot(stacked, weights[...])
            for i in range(tp_size):
                piece = places // tp_size
                normed_full[i, b, c] = product[i * piece : (i + 1) * piece].astype(jnp.bfloat16)
            grad_acc[...] += columns_dot(stacked, rows)
            return carry

        lax.fori_loop(first, last, one, 0)

    quarter = half // 2
    project_back(0, quarter)
    proj.pass_on(0)
    next(feeds[0])
    out.pass_on(0)
    out.pass_on(1)
    project_back(quarter, half)
    normed.start(0)
    next(feeds[1])
    project_back(half, half + quarter)
    normed.pass_on(0)
    next(feeds[2])
    next(feeds[0])
    project_back(half + quarter, 2 * half)
    normed.start(1)
    for n in range(3 * seq_size // 2):
        blocks[n // seq_size, n % seq_size] = grad_acc[n * fine : (n + 1) * fine].astype(
            jnp.bfloat16
        )
    next(sums[0])
    proj.arrive(0)

    def put(b, carry):
        blocks[1, seq_size // 2 + b] = proj.total(b, 0).astype(jnp.bfloat16)
        return carry

    lax.fori_loop(0, seq_size // 2, put, 0)
    next(sums[1])
    normed.pass_on(1)
    next(feeds[1])
    next(feeds[0])
    next(feeds[2])

    def own_part(target, slot, i):
        piece = source.shape[2]
        return target.at[slot, pl.ds(pl.multiple_of(i * piece, piece), piece)]

    def send_back(source_ref, target, trio, b, c, wait):
        local_sem, send_sem, recv_sem = trio
        flat = 2 * b + c
        j, to = flat // seq_size, lax.rem(flat, seq_size)
        row = group * rows_each + j
        slot = lax.rem(row, rows_local)
        place = (to, row // rows_local)
        here = same(place, me)
        view = own_part(target, slot, t)

        @pl.when(here)
        def _():
            copy = pltpu.make_async_copy(source_ref.at[b, c], view, local_sem.at[flat])
            copy.wait() if wait else copy.start()

        @pl.when(jnp.logical_not(here))
        def _():
            copy = remote(
                source_ref.at[b, c], view, send_sem.at[flat], recv_sem.at[slot * tp_size + t], place
            )
            copy.wait_send() if wait else copy.start()

    small[...] = small_ref[...]

    def back(c):
        normed.arrive(c)

        def one(n, carry):
            b = lax.rem(n + s // 2, half)
            grads = normed.total(b, c)
            x = source[b, c].astype(jnp.float32)
            inverse = lax.rsqrt(jnp.mean(x * x, axis=-1, keepdims=True) + norm_eps)
            unit = x * inverse
            scaled = grads * gain
            extra = inverse * (scaled - unit * jnp.mean(scaled * unit, axis=-1, keepdims=True))
            input_g[b, c] = (middle_g[b, c] + extra).astype(jnp.bfloat16)
            small[0:1, :] += jnp.sum(grads * unit, axis=0, keepdims=True)
            send_back(input_g, input_g_ref, back_sems, b, c, False)
            return carry

        lax.fori_loop(0, half, one, 0)

    def forward(c):
        out.arrive(c)

        def one(n, carry):
            b = lax.rem(n + s // 2, half)
            result[b, c] = (middle[b, c] + out.total(b, c)).astype(jnp.bfloat16)
            send_back(result, out_ref, lo_sems, b, c, False)
            return carry

        lax.fori_loop(0, half, one, 0)

    def tp_copy(n):
        return remote(
            small, tp_held.at[tp_size - n], small_send.at[n],
            tp_sem.at[tp_size - n], (s, tp_peers[n - 1]),
        )

    def seq_copy(n):
        return remote(
            tp_sum, seq_held.at[seq_size - n], small_send.at[tp_size + n],
            seq_sem.at[seq_size - n], (seq_peers[n - 1], t),
        )

    def all_steps(generators):
        for generator in generators:
            next(generator, None)

    loads[12].wait()
    forward(0)
    next(feeds[1])
    next(feeds[0])
    next(sums[0])
    forward(1)
    next(feeds[2])
    next(sums[1])
    loads[11].wait()
    back(0)
    next(feeds[1])
    next(sums[0])
    back(1)
    for n in range(1, tp_size):
        tp_copy(n).start()
    all_steps([sums[1], feeds[2], sums[0]])
    for n in range(1, tp_size):
        tp_copy(n).wait()
    tp_held[0] = small[...]
    total = tp_held[lax.rem(tp_size - t, tp_size)]
    for n in range(1, tp_size):
        total = total + tp_held[lax.rem(n + tp_size - t, tp_size)]
    tp_sum[...] = total
    for n in range(1, seq_size):
        seq_copy(n).start()
    seq_held[0] = total
    dv_move.wait_sends()
    dv_move.wait_receives()

    def first_back(n, carry):
        dv_cols[n] = (0.5 * dv_rows[n].astype(jnp.float32)).T
        return carry

    lax.fori_loop(0, dv_rows.shape[0], first_back, 0)
    first_store = pltpu.make_async_copy(dv_cols, first_g_ref, first_sem)
    first_store.start()
    for _ in range(2 * count):
        all_steps([sums[1], sums[0], feeds[0], feeds[1], feeds[2]])
    for generator in sums + feeds:
        for _ in generator:
            pass
    for n in range(1, seq_size):
        seq_copy(n).wait()
    total = seq_held[lax.rem(seq_size - s, seq_size)]
    for n in range(1, seq_size):
        total = total + seq_held[lax.rem(n + seq_size - s, seq_size)]
    gain_g_ref[...] = total[0:1]
    feed_gain_g_ref[...] = total[1:2]
    norms_ref[...] = jnp.sqrt(total[2:3, :2])

    for reduce in (normed, proj, out):
        reduce.finish()
    for c in range(2):
        def done(b, carry):
            send_back(input_g, input_g_ref, back_sems, b, c, True)
            send_back(result, out_ref, lo_sems, b, c, True)
            return carry

        lax.fori_loop(0, half, done, 0)
    first_store.wait()
    for origin, slot, i in origins:
        @pl.when(jnp.logical_not(same(origin, me)))
        def _():
            for ref, trio in ((input_g_ref, back_sems), (out_ref, lo_sems)):
                view = own_part(ref, slot, i)
                at = slot * tp_size + i
                remote(view, view, trio[1].at[0], trio[2].at[at], origin).wait_recv()


def tail(
    out_part, keep, got, x_rows, query_g, key_g, value_g, cosine, sine, query_weight, key_weight, value_weight,
    attended, source, middle, middle_g, gain, small, sizes,
):
    seq_size, tp_size, rows_each, rows_local, _ = sizes
    pairs = tp_size // 2
    blocks = rows_each * seq_size
    tokens, depth = source.shape
    piece = tokens // blocks
    width = query_g.shape[-1]
    places = x_rows.shape[0] // blocks
    lanes = cosine.shape[2]
    fine = 2 * width // seq_size
    bf16, f32 = jnp.bfloat16, jnp.float32
    shape = (blocks // 2, 2, piece, depth)
    proj_shape = (width // fine, 1, fine, depth)
    hidden = 2 * keep.shape[1] // seq_size
    feed_shape = (3, seq_size // 2, hidden, depth)
    anywhere = pl.BlockSpec(memory_space=pl.ANY)
    vmem = pl.BlockSpec(memory_space=pltpu.VMEM)
    dma = pltpu.SemaphoreType.DMA
    plan = rows_to_places(seq_size, rows_each)
    steps = seq_size.bit_length() - 1
    owned = jax.ShapeDtypeStruct((rows_local, tp_size * piece, depth), bf16)

    def reduce_shapes(part):
        return [
            pltpu.VMEM((tp_size,) + part, bf16),
            pltpu.VMEM((pairs,) + part, bf16),
            pltpu.VMEM((pairs - 1,) + part, bf16),
        ]

    def reduce_sems(chunks):
        return [dma((pairs * chunks,))] * 4

    return pl.pallas_call(
        functools.partial(tail_kernel, sizes, plan),
        out_shape=[
            owned,
            owned,
            jax.ShapeDtypeStruct((blocks, width, places), f32),
            jax.ShapeDtypeStruct((2, seq_size, fine, depth), bf16),
            jax.ShapeDtypeStruct((3, seq_size, hidden, depth), bf16),
            jax.ShapeDtypeStruct((1, depth), f32),
            jax.ShapeDtypeStruct((1, depth), f32),
            jax.ShapeDtypeStruct((1, 2), f32),
        ],
        in_specs=[anywhere] * 17 + [vmem] * 2,
        out_specs=[anywhere] * 5 + [vmem] * 3,
        scratch_shapes=[
            pltpu.VMEM((blocks, places, depth), bf16),
            pltpu.VMEM((blocks, places, width), bf16),
            pltpu.VMEM((blocks, places, width), bf16),
            pltpu.VMEM((blocks, places, width), bf16),
            pltpu.VMEM((blocks, places, lanes), f32),
            pltpu.VMEM((blocks, places, lanes), f32),
            pltpu.VMEM((3 * width, depth), bf16),
            pltpu.VMEM(attended.shape, bf16),
            pltpu.VMEM((3 * width, depth), f32),
        ]
        + reduce_shapes(shape)
        + reduce_shapes(proj_shape)
        + reduce_shapes(shape)
        + [
            pltpu.VMEM(shape, bf16),
            pltpu.VMEM(shape, f32),
            pltpu.VMEM(shape, f32),
            pltpu.VMEM(shape, bf16),
            pltpu.VMEM(shape, bf16),
            pltpu.VMEM((2, seq_size, fine, depth), bf16),
            pltpu.VMEM((2, seq_size, fine, depth), bf16),
            pltpu.VMEM((2, 1, fine, depth), bf16),
            pltpu.VMEM(feed_shape, bf16),
            pltpu.VMEM(feed_shape, bf16),
            pltpu.VMEM(feed_shape, bf16),
            pltpu.VMEM((3, 1, hidden, depth), bf16),
            pltpu.VMEM(small.shape, f32),
            pltpu.VMEM((tp_size,) + small.shape, f32),
            pltpu.VMEM(small.shape, f32),
            pltpu.VMEM((seq_size,) + small.shape, f32),
            pltpu.VMEM((blocks, places, width), bf16),
            pltpu.VMEM((blocks, width, places), f32),
        ]
        + reduce_sems(2)
        + reduce_sems(1)
        + reduce_sems(2)
        + [dma((seq_size,))] * 3
        + ([dma((blocks,))] * 2 + [dma((rows_local * tp_size,))]) * 2
        + [
            dma((13,)),
            dma((blocks,)),
            dma((6,)),
            dma((5,)),
            dma((2, 2 * steps)),
            dma((2, 2 * steps)),
            dma((3, 2 * steps)),
            dma((3, 2 * steps)),
            dma((tp_size + seq_size,)),
            dma((tp_size,)),
            dma((seq_size,)),
            dma,
        ],
        compiler_params=pltpu.CompilerParams(
            collective_id=6, has_side_effects=True, vmem_limit_bytes=67043328
        ),
        name="tail",
    )(
        out_part.reshape((tp_size,) + shape),
        keep.reshape(feed_shape),
        got.reshape(feed_shape),
        x_rows.reshape(blocks, places, depth),
        query_g.reshape(blocks, places, width),
        key_g.reshape(blocks, places, width),
        value_g.reshape(blocks, places, width),
        cosine,
        sine,
        query_weight,
        key_weight,
        value_weight,
        attended,
        source.reshape(shape),
        middle.reshape(shape),
        middle_g.reshape(shape),
        value_g.reshape(rows_each, seq_size, places, width),
        gain,
        small,
    )


def shards(
    layer_input,
    first_values,
    doc_lengths,
    attn_gain,
    query_weight,
    key_weight,
    value_weight,
    output_weight,
    feed_gain,
    gate_weight,
    up_weight,
    down_weight,
    out_cotangent,
):
    seq_size = lax.axis_size("seq")
    tp_size = lax.axis_size("tp")
    rows_local, local_len, depth = layer_input.shape
    row_count = first_values.shape[0]
    width = query_weight.shape[0]
    rows_each = row_count // seq_size
    piece = local_len // tp_size
    tokens = rows_each * seq_size * piece
    sizes = (seq_size, tp_size, rows_each, rows_local, 4)
    me = lax.axis_index("tp")
    my_rows = group_of(lax.axis_index("seq"), seq_size) * rows_each

    _, offsets = doc_layout(doc_lengths)
    offsets = lax.dynamic_slice_in_dim(offsets, my_rows, rows_each, 0)
    starts = jnp.arange(ROW, dtype=jnp.int32)[None, :] - offsets
    low = (starts[:, ::BLOCK] // BLOCK).reshape(-1)
    starts = starts[:, None, :]
    half_dim = HD // 2
    frequency = rope_base ** (-jnp.arange(half_dim, dtype=jnp.float32) * 2.0 / HD)
    attn_scale = attn_gain.astype(jnp.float32)[None, :]
    feed_scale = feed_gain.astype(jnp.float32)[None, :]
    (
        x_rows, cot_all, _, output_full, queries, keys, values, cosine, sine, squares,
    ) = spread(
        layer_input.reshape(rows_local, tp_size, piece, depth),
        out_cotangent.reshape(rows_local, tp_size, piece, depth),
        first_values,
        output_weight,
        query_weight,
        key_weight,
        value_weight,
        offsets.astype(jnp.float32).reshape(rows_each * seq_size, 1, local_len),
        frequency[:, None],
        attn_scale,
        sizes,
    )
    output_full = output_full.reshape(tp_size * width, depth)
    source_low = lax.dynamic_index_in_dim(x_rows, me, 2, keepdims=False).reshape(tokens, depth)
    source = source_low.astype(jnp.float32)
    cotangent = lax.dynamic_index_in_dim(cot_all, me, 0, keepdims=False).reshape(tokens, depth)
    cotangent = cotangent.astype(jnp.float32)
    x_rows = x_rows.reshape(rows_each * ROW, depth)
    queries, keys, values = (
        part.reshape(rows_each, ROW, width) for part in (queries, keys, values)
    )
    result, logsum = attend(low, queries, keys, values, starts)
    by_piece = (rows_each, seq_size, tp_size, piece, width)
    by_head = (tp_size, rows_each, seq_size, piece, width)
    (pieces,) = exchange([result.reshape(by_piece)], [by_head], [heads_to_tokens(tp_size)], 1)
    attended = jnp.transpose(pieces.reshape(tp_size, tokens, width), (1, 0, 2)).reshape(tokens, -1)
    middle = source + jnp.dot(attended, output_full, preferred_element_type=jnp.float32)
    unit_feed, inv_feed = norm_rows(middle)
    feed_in = (unit_feed * feed_scale).astype(jnp.bfloat16)
    feed_in_g, out_part, keep, give = feed_forward(
        feed_in, cot_all.reshape(tp_size, tokens, depth), gate_weight.T, up_weight.T, down_weight
    )
    got = lax.ppermute(give, "seq", [(n, n + 1 - 2 * (n % 2)) for n in range(seq_size)])
    middle_extra, feed_gain_part = norm_back(feed_in_g, unit_feed, inv_feed, feed_scale)
    middle_g = cotangent + middle_extra
    branch_g = middle_g.astype(jnp.bfloat16)
    attended_g = jnp.einsum(
        "td,ed->te", branch_g, output_full, preferred_element_type=jnp.float32
    ).astype(jnp.bfloat16)
    (attended_g,) = exchange(
        [jnp.transpose(attended_g.reshape(tokens, tp_size, width), (1, 0, 2)).reshape(by_head)],
        [by_piece],
        [tokens_to_heads(tp_size)],
        2,
    )
    query_g, key_g, value_g = attend_back(
        low, queries, keys, values, result, attended_g.reshape(result.shape), logsum, starts
    )
    squares = jnp.pad(jnp.sum(squares, axis=1)[:2], (0, depth - 2))
    small = jnp.stack([jnp.zeros_like(squares), feed_gain_part, squares])
    (
        layer_output, input_grad, first_grad, grad_sums, feed_sums,
        gain_grad, feed_gain_grad, norms,
    ) = tail(
        out_part,
        keep,
        got,
        x_rows,
        query_g,
        key_g,
        value_g,
        cosine,
        sine,
        query_weight,
        key_weight,
        value_weight,
        pieces.reshape(tp_size, tokens, width),
        source_low,
        middle,
        middle_g,
        attn_scale,
        jnp.pad(small, ((0, 5), (0, 0))),
        sizes,
    )
    grad_sums = grad_sums.reshape(4, width, depth)
    projections = [grad_sums[n].astype(jnp.float32) for n in range(4)]
    feed_sums = feed_sums.reshape(3, -1, depth).astype(jnp.float32)
    return (
        layer_output,
        input_grad,
        first_grad,
        gain_grad.reshape(depth),
        *projections,
        feed_gain_grad.reshape(depth),
        feed_sums[0].T,
        feed_sums[1].T,
        feed_sums[2],
        norms.reshape(2),
    )


def solution(mesh):
    placed = (
        P("tp", "seq", None),
        P(None, "tp", "seq"),
        P(),
        P(),
        P("tp", None),
        P("tp", None),
        P("tp", None),
        P("tp", None),
        P(),
        P(None, "tp"),
        P(None, "tp"),
        P("tp", None),
        P("tp", "seq", None),
    )
    return jax.shard_map(
        shards,
        mesh=mesh,
        in_specs=placed,
        out_specs=(
            P("tp", "seq", None),
            P("tp", "seq", None),
            P(None, "tp", "seq"),
            P(),
            P("tp", None),
            P("tp", None),
            P("tp", None),
            P("tp", None),
            P(),
            P(None, "tp"),
            P(None, "tp"),
            P("tp", None),
            P(),
        ),
        check_vma=False,
    )
```

```python
import functools
import math

import jax
import jax.numpy as jnp
from jax import lax
from jax.experimental import pallas as pl
from jax.experimental.pallas import tpu as pltpu
from jax.sharding import PartitionSpec as P

HD = 64
ROW = 2048
BLOCK = 256
LOG2E = math.log2(math.e)
LN2 = math.log(2.0)
MESH = pl.DeviceIdType.MESH


norm_eps = 1e-06
rope_base = 10000.0
masked_score = -1e30


def doc_layout(doc_lengths):
    doc_ends = jnp.cumsum(doc_lengths, axis=-1)
    places = jnp.arange(ROW, dtype=jnp.int32)
    passed = doc_ends[:, None, :] <= places[None, :, None]
    segment = jnp.sum(passed.astype(jnp.int32), axis=-1)
    starts = jnp.max(jnp.where(passed, doc_ends[:, None, :], 0), axis=-1)
    return (segment, places[None, :] - starts)


def norm_rows(values_in):
    inverse = lax.rsqrt(jnp.mean(values_in * values_in, axis=-1, keepdims=True) + norm_eps)
    return (values_in * inverse, inverse)


def norm_back(grads_in, unit_rows, inverse, gain):
    scaled = grads_in * gain
    extra = inverse * (scaled - unit_rows * jnp.mean(scaled * unit_rows, axis=-1, keepdims=True))
    return (extra, jnp.sum(grads_in * unit_rows, axis=0))


def rows_dot(left, right):
    return lax.dot_general(left, right, (((1,), (1,)), ((), ())), preferred_element_type=jnp.float32)


def plain_dot(left, right):
    return lax.dot_general(left, right, (((1,), (0,)), ((), ())), preferred_element_type=jnp.float32)


def head_masked(block, head, heads):
    if heads == 1:
        return block
    lanes = lax.broadcasted_iota(jnp.int32, block.shape, 1)
    return jnp.where(lanes // HD == head, block, jnp.zeros_like(block))


def lane_group(head, width):
    lanes = min(width, 128)
    return slice(head * HD // lanes * lanes, head * HD // lanes * lanes + lanes), head % (lanes // HD)


def attend_kernel(low_ref, q_ref, k_ref, v_ref, start_ref, o_ref, lse_ref, v_cols):
    row = pl.program_id(0)
    length, width = q_ref.shape[1:]
    heads = width // HD
    together = min(width, 128) // HD
    blocks = length // BLOCK
    for j in range(blocks):
        v_cols[:, j * BLOCK : (j + 1) * BLOCK] = v_ref[0, j * BLOCK : (j + 1) * BLOCK, :].T

    def query_block(i, carry):
        first = pl.multiple_of(i * BLOCK, BLOCK)
        q_heads = []
        for h in range(heads):
            lanes, at = lane_group(h, width)
            q_heads.append(head_masked(q_ref[0, pl.ds(first, BLOCK), lanes], at, together))
        start = start_ref[0, :, pl.ds(first, BLOCK)]
        places = first + lax.broadcasted_iota(jnp.int32, (1, BLOCK), 1)

        def key_block(j, state):
            at = pl.multiple_of(j * BLOCK, BLOCK)
            keys = at + lax.broadcasted_iota(jnp.int32, (BLOCK, BLOCK), 0)
            allowed = (keys >= start) & (keys <= places)
            scores = [
                rows_dot(k_ref[0, pl.ds(at, BLOCK), lane_group(h, width)[0]], q_heads[h])
                for h in range(heads)
            ]
            out = []
            for h in range(heads):
                top, total, acc = state[h]
                masked = jnp.where(allowed, scores[h], masked_score)
                new_top = jnp.maximum(top, jnp.max(masked, axis=0, keepdims=True))
                weights = jnp.exp2(masked - new_top)
                shrink = jnp.exp2(top - new_top)
                total = total * shrink + jnp.sum(weights, axis=0, keepdims=True)
                acc = acc * shrink + plain_dot(
                    v_cols[h * HD : (h + 1) * HD, pl.ds(at, BLOCK)], weights.astype(jnp.bfloat16)
                )
                out.append((new_top, total, acc))
            return tuple(out)

        begin = tuple(
            (
                jnp.full((1, BLOCK), masked_score, jnp.float32),
                jnp.zeros((1, BLOCK), jnp.float32),
                jnp.zeros((HD, BLOCK), jnp.float32),
            )
            for _ in range(heads)
        )
        state = key_block(i, begin)
        state = lax.fori_loop(low_ref[row * blocks + i], i, key_block, state)
        columns = jnp.concatenate([acc / total for _, total, acc in state], axis=0)
        o_ref[0, pl.ds(first, BLOCK), :] = columns.T.astype(jnp.bfloat16)
        for h in range(heads):
            top, total, _ = state[h]
            lse_ref[0, pl.ds(h, 1), pl.ds(first, BLOCK)] = top + jnp.log2(total)
        return carry

    lax.fori_loop(0, blocks, query_block, 0)


def attend(low, queries, keys, values, starts):
    rows, length, width = queries.shape
    heads = width // HD
    wide = pl.BlockSpec((1, length, width), lambda r, low: (r, 0, 0))
    return pl.pallas_call(
        attend_kernel,
        grid_spec=pltpu.PrefetchScalarGridSpec(
            num_scalar_prefetch=1,
            grid=(rows,),
            in_specs=[wide, wide, wide, pl.BlockSpec((1, 1, length), lambda r, low: (r, 0, 0))],
            out_specs=[wide, pl.BlockSpec((1, heads, length), lambda r, low: (r, 0, 0))],
            scratch_shapes=[pltpu.VMEM((width, length), jnp.bfloat16)],
        ),
        out_shape=[
            jax.ShapeDtypeStruct(queries.shape, jnp.bfloat16),
            jax.ShapeDtypeStruct((rows, heads, length), jnp.float32),
        ],
        compiler_params=pltpu.CompilerParams(vmem_limit_bytes=67043328),
        name="attend",
    )(low, queries, keys, values, starts)


def attend_back_kernel(
    low_ref, q_ref, k_ref, v_ref, o_ref, g_ref, lse_ref, start_ref,
    qg_ref, kg_ref, vg_ref, k_cols, k_acc, v_acc,
):
    row = pl.program_id(0)
    length, width = q_ref.shape[1:]
    heads = width // HD
    together = min(width, 128) // HD
    blocks = length // BLOCK
    for j in range(blocks):
        k_cols[:, j * BLOCK : (j + 1) * BLOCK] = k_ref[0, j * BLOCK : (j + 1) * BLOCK, :].T
    k_acc[...] = jnp.zeros_like(k_acc)
    v_acc[...] = jnp.zeros_like(v_acc)
    select = (
        lax.broadcasted_iota(jnp.int32, (8, width), 1) // HD
        == lax.broadcasted_iota(jnp.int32, (8, width), 0)
    ).astype(jnp.float32)

    def query_block(i, carry):
        first = pl.multiple_of(i * BLOCK, BLOCK)
        q_heads, g_heads = [], []
        for h in range(heads):
            lanes, at = lane_group(h, width)
            q_heads.append(head_masked(q_ref[0, pl.ds(first, BLOCK), lanes], at, together))
            g_heads.append(head_masked(g_ref[0, pl.ds(first, BLOCK), lanes], at, together))
        product = g_ref[0, pl.ds(first, BLOCK), :].astype(jnp.float32) * o_ref[
            0, pl.ds(first, BLOCK), :
        ].astype(jnp.float32)
        centre = lax.dot_general(
            select, product, (((1,), (1,)), ((), ())),
            precision=lax.Precision.HIGHEST, preferred_element_type=jnp.float32,
        )
        lse = lse_ref[0, :, pl.ds(first, BLOCK)]
        start = start_ref[0, :, pl.ds(first, BLOCK)]
        places = first + lax.broadcasted_iota(jnp.int32, (1, BLOCK), 1)

        def key_block(j, state):
            at = pl.multiple_of(j * BLOCK, BLOCK)
            keys = at + lax.broadcasted_iota(jnp.int32, (BLOCK, BLOCK), 0)
            allowed = (keys >= start) & (keys <= places)
            scores, prob_gs = [], []
            for h in range(heads):
                lanes, _ = lane_group(h, width)
                scores.append(rows_dot(k_ref[0, pl.ds(at, BLOCK), lanes], q_heads[h]))
                prob_gs.append(rows_dot(v_ref[0, pl.ds(at, BLOCK), lanes], g_heads[h]))
            out = []
            for h in range(heads):
                lanes, _ = lane_group(h, width)
                probs = jnp.exp2(jnp.where(allowed, scores[h], masked_score) - lse[h : h + 1, :])
                score_g = (probs * (prob_gs[h] - centre[h : h + 1, :])).astype(jnp.bfloat16)
                v_acc[pl.ds(at, BLOCK), lanes] += plain_dot(probs.astype(jnp.bfloat16), g_heads[h])
                k_acc[pl.ds(at, BLOCK), lanes] += plain_dot(score_g, q_heads[h])
                out.append(
                    state[h] + plain_dot(k_cols[h * HD : (h + 1) * HD, pl.ds(at, BLOCK)], score_g)
                )
            return tuple(out)

        begin = tuple(jnp.zeros((HD, BLOCK), jnp.float32) for _ in range(heads))
        state = lax.fori_loop(low_ref[row * blocks + i], i + 1, key_block, begin)
        columns = jnp.concatenate(state, axis=0) * HD ** (-0.5)
        qg_ref[0, pl.ds(first, BLOCK), :] = columns.T.astype(jnp.bfloat16)
        return carry

    lax.fori_loop(0, blocks, query_block, 0)
    kg_ref[0] = (k_acc[...] * LN2).astype(jnp.bfloat16)
    vg_ref[0] = v_acc[...].astype(jnp.bfloat16)


def attend_back(low, queries, keys, values, attended, grads, lse, starts):
    rows, length, width = queries.shape
    heads = width // HD
    wide = pl.BlockSpec((1, length, width), lambda r, low: (r, 0, 0))
    return pl.pallas_call(
        attend_back_kernel,
        grid_spec=pltpu.PrefetchScalarGridSpec(
            num_scalar_prefetch=1,
            grid=(rows,),
            in_specs=[wide] * 5
            + [
                pl.BlockSpec((1, heads, length), lambda r, low: (r, 0, 0)),
                pl.BlockSpec((1, 1, length), lambda r, low: (r, 0, 0)),
            ],
            out_specs=[wide] * 3,
            scratch_shapes=[
                pltpu.VMEM((width, length), jnp.bfloat16),
                pltpu.VMEM((length, width), jnp.float32),
                pltpu.VMEM((length, width), jnp.float32),
            ],
        ),
        out_shape=[jax.ShapeDtypeStruct(queries.shape, jnp.bfloat16)] * 3,
        compiler_params=pltpu.CompilerParams(vmem_limit_bytes=67043328),
        name="attend_back",
    )(low, queries, keys, values, attended, grads, lse, starts)


def columns_dot(left, right):
    return lax.dot_general(left, right, (((0,), (0,)), ((), ())), preferred_element_type=jnp.float32)


def feed_kernel(
    chunk, feed_ref, cot_ref, gate_w, up_w, down_w,
    feed_g_ref, out_own_ref, out_give_ref, cot_own_ref, keep_ref, give_ref,
    feed_all, part, core_in, pair_in, acc, out_all, out_in,
    feed_send, feed_core, feed_pair, relay_send, part_send, part_core, sum_send, sum_pair,
    out_send, out_core,
):
    tokens = feed_ref.shape[0]
    chunks = tokens // chunk
    seq = lax.axis_index("seq")
    me = lax.axis_index("tp")
    pairs = lax.axis_size("tp") // 2
    pair, core = me // 2, lax.rem(me, 2)
    other = pair * 2 + 1 - core

    def peer(offset):
        return lax.rem(pair + offset, pairs) * 2 + core

    def copy(source, target, send, receive, to):
        return pltpu.make_async_remote_copy(
            src_ref=source, dst_ref=target, send_sem=send, recv_sem=receive,
            device_id=(seq, to), device_id_type=MESH,
        )

    barrier = pltpu.get_barrier_semaphore()
    for to in [other] + [peer(offset) for offset in range(1, pairs)]:
        pl.semaphore_signal(barrier, inc=1, device_id=(seq, to), device_id_type=MESH)
    pl.semaphore_wait(barrier, pairs)

    def rows(c):
        return pl.ds(pl.multiple_of(c * chunk, chunk), chunk)

    def feed_to_core(c):
        return copy(
            feed_ref.at[rows(c)], feed_all.at[me, rows(c)],
            feed_send.at[c], feed_core.at[c], other,
        )

    def feed_to_pair(offset, c):
        return copy(
            feed_ref.at[rows(c)], feed_all.at[me, rows(c)],
            feed_send.at[offset * chunks + c],
            feed_pair.at[(pairs - offset) * chunks + c], peer(offset),
        )

    def feed_from_pair(offset, c):
        return copy(
            feed_all.at[peer(offset), rows(c)], feed_all.at[peer(offset), rows(c)],
            feed_send.at[0], feed_pair.at[offset * chunks + c], other,
        )

    def relay(offset, c):
        return copy(
            feed_all.at[peer(offset), rows(c)], feed_all.at[peer(offset), rows(c)],
            relay_send.at[offset * chunks + c], feed_core.at[offset * chunks + c], other,
        )

    def part_to_core(offset, c):
        at = lax.rem(pair + offset, pairs) * 2 + 1 - core
        return copy(
            part.at[at, rows(c)], core_in.at[offset, rows(c)],
            part_send.at[offset * chunks + c], part_core.at[offset * chunks + c], other,
        )

    def out_to_core(offset, c):
        at = lax.rem(pair + offset, pairs) * 2 + 1 - core
        return copy(
            out_all.at[at, rows(c)], out_in.at[offset, rows(c)],
            out_send.at[offset * chunks + c], out_core.at[offset * chunks + c], other,
        )

    def out_sum(at, offset, c):
        return (
            out_all[at, rows(c), :].astype(jnp.float32)
            + out_in[offset, rows(c), :].astype(jnp.float32)
        ).astype(jnp.bfloat16)

    def sum_to_pair(offset, c):
        return copy(
            part.at[peer(offset), rows(c)], pair_in.at[pairs - offset, rows(c)],
            sum_send.at[offset * chunks + c],
            sum_pair.at[(pairs - offset) * chunks + c], peer(offset),
        )

    for c in range(chunks):
        feed_to_core(c).start()
        for offset in range(1, pairs):
            feed_to_pair(offset, c).start()
    feed_all[me] = feed_ref[...]
    cot_own_ref[...] = cot_ref[me]
    acc[...] = jnp.zeros_like(acc)

    count = chunks * pairs
    early = chunks - 1

    def step(n, carry):
        which = lax.rem(n, 2)
        at = n // 2
        if early:
            at = at + (at + count - early) // count - (at + 1) // count * (count - early)
        c = lax.rem(at, chunks)
        offset = at // chunks
        owner = lax.rem(pair + offset, pairs) * 2 + lax.rem(core + which, 2)

        @pl.when((which == 0) & (offset > 0))
        def _():
            feed_from_pair(offset, c).wait_recv()
            relay(offset, c).start()

        @pl.when(which == 1)
        def _():
            relay(offset, c).wait_recv()

        feed = feed_all[owner, rows(c), :]
        cot = cot_ref[owner, rows(c), :]
        gate = rows_dot(feed, gate_w[...])
        up = rows_dot(feed, up_w[...])
        sigmoid = jax.nn.sigmoid(gate)
        activated = gate * sigmoid
        hidden = (activated * up).astype(jnp.bfloat16)
        hidden_g = rows_dot(cot, down_w[...])
        up_g = (hidden_g * activated).astype(jnp.bfloat16)
        gate_g = (hidden_g * up * sigmoid * (1.0 + gate * (1.0 - sigmoid))).astype(jnp.bfloat16)
        part[owner, rows(c), :] = (
            plain_dot(gate_g, gate_w[...]) + plain_dot(up_g, up_w[...])
        ).astype(jnp.bfloat16)

        @pl.when(which == 1)
        def _():
            part_to_core(offset, c).start()

        out_all[owner, rows(c), :] = plain_dot(hidden, down_w[...]).astype(jnp.bfloat16)

        @pl.when(which == 1)
        def _():
            out_to_core(offset, c).start()

        acc[0] += columns_dot(gate_g, feed)
        acc[1] += columns_dot(up_g, feed)
        acc[2] += columns_dot(hidden, cot)

        @pl.when((which == 1) & (offset > 0))
        def _():
            part_to_core(offset, c).wait_recv()
            to = peer(offset)
            part[to, rows(c), :] = (
                part[to, rows(c), :].astype(jnp.float32)
                + core_in[offset, rows(c), :].astype(jnp.float32)
            ).astype(jnp.bfloat16)
            sum_to_pair(offset, c).start()
            out_to_core(offset, c).wait_recv()
            out_give_ref[offset - 1, rows(c), :] = out_sum(to, offset, c)

        return carry

    lax.fori_loop(0, 2 * chunks * pairs, step, 0)
    half = acc.shape[1] // 2
    flag = lax.rem(seq, 2)
    for n in range(3):
        keep_ref[n] = acc[n, pl.ds(pl.multiple_of(flag * half, 8), half), :].astype(jnp.bfloat16)
        give_ref[n] = acc[n, pl.ds(pl.multiple_of((1 - flag) * half, 8), half), :].astype(
            jnp.bfloat16
        )
    for c in range(chunks):
        out_to_core(0, c).wait_recv()
        out_own_ref[rows(c), :] = out_sum(me, 0, c)
    for c in range(chunks):
        part_to_core(0, c).wait_recv()
        for offset in range(1, pairs):
            sum_to_pair(offset, c).wait_recv()
        total = part[me, rows(c), :].astype(jnp.float32) + core_in[0, rows(c), :].astype(jnp.float32)
        for offset in range(1, pairs):
            total = total + pair_in[offset, rows(c), :].astype(jnp.float32)
        feed_g_ref[rows(c), :] = total
    for c in range(chunks):
        feed_to_core(c).wait_send()
        part_to_core(0, c).wait_send()
        out_to_core(0, c).wait_send()
        for offset in range(1, pairs):
            feed_to_pair(offset, c).wait_send()
            relay(offset, c).wait_send()
            part_to_core(offset, c).wait_send()
            out_to_core(offset, c).wait_send()
            sum_to_pair(offset, c).wait_send()


def feed_forward(feed_in, cot_all, gate_weight, up_weight, down_weight):
    tokens, width = feed_in.shape
    tp_size = cot_all.shape[0]
    pairs = tp_size // 2
    chunk = min(tokens, 256)
    chunks = tokens // chunk
    hidden = gate_weight.shape[0]
    whole = pl.BlockSpec(memory_space=pltpu.VMEM)
    dma = pltpu.SemaphoreType.DMA
    return pl.pallas_call(
        functools.partial(feed_kernel, chunk),
        out_shape=[
            jax.ShapeDtypeStruct((tokens, width), jnp.float32),
            jax.ShapeDtypeStruct((tokens, width), jnp.bfloat16),
            jax.ShapeDtypeStruct((pairs - 1, tokens, width), jnp.bfloat16),
            jax.ShapeDtypeStruct((tokens, width), jnp.bfloat16),
            jax.ShapeDtypeStruct((3, hidden // 2, width), jnp.bfloat16),
            jax.ShapeDtypeStruct((3, hidden // 2, width), jnp.bfloat16),
        ],
        in_specs=[whole] * 5,
        out_specs=[whole] * 6,
        scratch_shapes=[
            pltpu.VMEM(cot_all.shape, jnp.bfloat16),
            pltpu.VMEM(cot_all.shape, jnp.bfloat16),
            pltpu.VMEM((pairs, tokens, width), jnp.bfloat16),
            pltpu.VMEM((pairs, tokens, width), jnp.bfloat16),
            pltpu.VMEM((3, hidden, width), jnp.float32),
            pltpu.VMEM(cot_all.shape, jnp.bfloat16),
            pltpu.VMEM((pairs, tokens, width), jnp.bfloat16),
        ]
        + [dma((pairs * chunks,))] * 10,
        compiler_params=pltpu.CompilerParams(
            collective_id=4, has_side_effects=True, vmem_limit_bytes=67043328
        ),
        name="feed_forward",
    )(feed_in, cot_all, gate_weight, up_weight, down_weight)


def group_of(place, seq_size):
    half = seq_size // 2
    low = place // 2
    return lax.rem(place + low, 2) * half + low


def place_of(group, seq_size):
    half = seq_size // 2
    low = lax.rem(group, half)
    return low * 2 + lax.rem(low + group // half, 2)


def remote(source, target, send, receive, to):
    return pltpu.make_async_remote_copy(
        src_ref=source, dst_ref=target, send_sem=send, recv_sem=receive,
        device_id=to, device_id_type=MESH,
    )


def same(left, right):
    return (left[0] == right[0]) & (left[1] == right[1])


class Exchange:
    def __init__(self, plan, me, source, target, local_sem, send_sem, receive_sem):
        self.me = me
        self.sends, self.receives = plan(*me)
        self.source, self.target = source, target
        self.local_sem, self.send_sem, self.receive_sem = local_sem, send_sem, receive_sem

    def greet(self, barrier):
        for origin, _, _ in self.receives:
            @pl.when(jnp.logical_not(same(origin, self.me)))
            def _():
                pl.semaphore_signal(barrier, inc=1, device_id=origin, device_id_type=MESH)

    def others(self):
        return sum(jnp.where(same(to, self.me), 0, 1) for to, _, _, _ in self.sends)

    def each_send(self, wait):
        for n, (to, source, target, at) in enumerate(self.sends):
            here = same(to, self.me)

            @pl.when(here)
            def _():
                copy = pltpu.make_async_copy(
                    self.source.at[source], self.target.at[target], self.local_sem.at[n]
                )
                copy.wait() if wait else copy.start()

            @pl.when(jnp.logical_not(here))
            def _():
                copy = remote(
                    self.source.at[source], self.target.at[target],
                    self.send_sem.at[n], self.receive_sem.at[at], to,
                )
                copy.wait_send() if wait else copy.start()

    def start(self):
        self.each_send(False)

    def wait_sends(self):
        self.each_send(True)

    def wait_receive(self, origin, target, at):
        @pl.when(jnp.logical_not(same(origin, self.me)))
        def _():
            remote(
                self.target.at[target], self.target.at[target],
                self.send_sem.at[0], self.receive_sem.at[at], origin,
            ).wait_recv()

    def wait_receives(self):
        for receive in self.receives:
            self.wait_receive(*receive)


def exchange(arrays, out_shapes, plans, number):
    count = len(arrays)

    def kernel(*refs):
        me = (lax.axis_index("seq"), lax.axis_index("tp"))
        moves = [
            Exchange(plan, me, refs[n], refs[count + n], *refs[2 * count + 3 * n :][:3])
            for n, plan in enumerate(plans)
        ]
        barrier = pltpu.get_barrier_semaphore()
        for move in moves:
            move.greet(barrier)
        pl.semaphore_wait(barrier, sum(move.others() for move in moves))
        for move in moves:
            move.start()
        for move in moves:
            move.wait_sends()
        for move in moves:
            move.wait_receives()

    semaphores = []
    for plan in plans:
        semaphores += [pltpu.SemaphoreType.DMA((len(plan(0, 0)[0]),))] * 3
    return pl.pallas_call(
        kernel,
        out_shape=[
            jax.ShapeDtypeStruct(shape, array.dtype) for shape, array in zip(out_shapes, arrays)
        ],
        in_specs=[pl.BlockSpec(memory_space=pl.ANY)] * count,
        out_specs=[pl.BlockSpec(memory_space=pl.ANY)] * count,
        scratch_shapes=semaphores,
        compiler_params=pltpu.CompilerParams(collective_id=number, has_side_effects=True),
        name=f"exchange_{number}",
    )(*arrays)


def owner_to_quarter(seq_size, tp_size, rows_each, rows_local, piece_first):
    def plan(s, t):
        sends, receives = [], []
        for slot in range(rows_local):
            row = t * rows_local + slot
            to = place_of(row // rows_each, seq_size)
            j = lax.rem(row, rows_each)
            for i in range(tp_size):
                target = (i, j, s) if piece_first else (j, s, i)
                sends.append(((to, i), (slot, i), target, j * seq_size + s))
        group = group_of(s, seq_size)
        for j in range(rows_each):
            row = group * rows_each + j
            for i in range(seq_size):
                origin = lax.rem(s + i, seq_size)
                target = (t, j, origin) if piece_first else (j, origin, t)
                receives.append(((origin, row // rows_local), target, j * seq_size + origin))
        return sends, receives

    return plan


def quarter_to_owner(seq_size, tp_size, rows_each, rows_local):
    def plan(s, t):
        sends, receives = [], []
        group = group_of(s, seq_size)
        for i in range(seq_size):
            to = lax.rem(s + i, seq_size)
            for j in range(rows_each):
                row = group * rows_each + j
                slot = lax.rem(row, rows_local)
                sends.append(((to, row // rows_local), (j, to), (slot, t), slot * tp_size + t))
        for slot in range(rows_local):
            row = t * rows_local + slot
            for i in range(tp_size):
                receives.append(
                    ((place_of(row // rows_each, seq_size), i), (slot, i), slot * tp_size + i)
                )
        return sends, receives

    return plan


def places_to_rows(seq_size, rows_each):
    def plan(s, t):
        sends, receives = [], []
        for i in range(seq_size):
            to = lax.rem(s + i, seq_size)
            rows = pl.ds(group_of(to, seq_size) * rows_each, rows_each)
            sends.append(((to, t), (rows,), (slice(None), s), s))
            origin = lax.rem(s + seq_size - i, seq_size)
            receives.append(((origin, t), (slice(None), origin), origin))
        return sends, receives

    return plan


def rows_to_places(seq_size, rows_each):
    def plan(s, t):
        sends, receives = [], []
        rows = pl.ds(group_of(s, seq_size) * rows_each, rows_each)
        for i in range(seq_size):
            to = lax.rem(s + i, seq_size)
            sends.append(((to, t), (slice(None), to), (rows,), s))
            origin = lax.rem(s + seq_size - i, seq_size)
            source_rows = pl.ds(group_of(origin, seq_size) * rows_each, rows_each)
            receives.append(((origin, t), (source_rows,), origin))
        return sends, receives

    return plan


def heads_to_tokens(tp_size):
    def plan(s, t):
        sends, receives = [], []
        for i in range(tp_size):
            to = lax.rem(t + i, tp_size)
            sends.append(((s, to), (slice(None), slice(None), to), (t,), t))
            origin = lax.rem(t + tp_size - i, tp_size)
            receives.append(((s, origin), (origin,), origin))
        return sends, receives

    return plan


def tokens_to_heads(tp_size):
    def plan(s, t):
        sends, receives = [], []
        for i in range(tp_size):
            to = lax.rem(t + i, tp_size)
            sends.append(((s, to), (to,), (slice(None), slice(None), t), t))
            origin = lax.rem(t + tp_size - i, tp_size)
            receives.append(((s, origin), (slice(None), slice(None), origin), origin))
        return sends, receives

    return plan


def spread_kernel(
    plans, sizes, x_ref, cot_ref, first_ref, output_ref, q_w, k_w, v_w, offset_ref, frequency_ref,
    gain_ref,
    x_out, cot_out, first_out, output_out, q_ref, k_ref, v_ref, cos_ref, sin_ref, square_ref,
    x_rows, first_rows, q_turned, k_turned,
    x_local, x_send, x_receive, cot_local, cot_send, cot_receive,
    first_local, first_send, first_receive,
    core_send, core_receive, pair_send, pair_receive, relay_send, load_sem, output_sem,
):
    seq_size, tp_size, rows_each, rows_local, parts = sizes
    me = (lax.axis_index("seq"), lax.axis_index("tp"))
    s, t = me
    pairs = tp_size // 2
    pair, core = t // 2, lax.rem(t, 2)
    other = pair * 2 + 1 - core
    each = seq_size // parts

    def peer(offset):
        return lax.rem(pair + offset, pairs) * 2 + core

    x_move = Exchange(plans[0], me, x_ref, x_out, x_local, x_send, x_receive)
    cot_move = Exchange(plans[1], me, cot_ref, cot_out, cot_local, cot_send, cot_receive)
    first_move = Exchange(plans[2], me, first_ref, first_out, first_local, first_send, first_receive)
    moves = (x_move, first_move, cot_move)
    barrier = pltpu.get_barrier_semaphore()
    for move in moves:
        move.greet(barrier)
    for to in [other] + [peer(offset) for offset in range(1, pairs)]:
        pl.semaphore_signal(barrier, inc=1, device_id=(s, to), device_id_type=MESH)
    pl.semaphore_wait(barrier, sum(move.others() for move in moves) + pairs)
    for move in moves:
        move.start()

    def block(out, tensor, piece, part):
        if tensor == 2:
            return out.at[piece]
        span = pl.ds(part * each, each)
        return out.at[:, span, piece] if tensor == 0 else out.at[piece, :, span]

    def number(tensor, offset, part):
        return (tensor * pairs + offset) * parts + part

    def own(out, tensor, part):
        return output_ref if tensor == 2 else block(out, tensor, t, part)

    def to_core(out, tensor, part):
        view, at = block(out, tensor, t, part), number(tensor, 0, part)
        return remote(own(out, tensor, part), view, core_send.at[at], core_receive.at[at], (s, other))

    def to_pair(out, tensor, offset, part):
        view = block(out, tensor, t, part)
        return remote(
            own(out, tensor, part), view, pair_send.at[number(tensor, offset, part)],
            pair_receive.at[number(tensor, pairs - offset, part)], (s, peer(offset)),
        )

    def from_pair(out, tensor, offset, part):
        view, at = block(out, tensor, peer(offset), part), number(tensor, offset, part)
        return remote(view, view, pair_send.at[at], pair_receive.at[at], (s, peer(offset)))

    def relay(out, tensor, offset, part):
        view, at = block(out, tensor, peer(offset), part), number(tensor, offset, part)
        return remote(view, view, relay_send.at[at], core_receive.at[at], (s, other))

    def from_core(out, tensor, offset, part):
        piece = lax.rem(pair + offset, pairs) * 2 + 1 - core
        view, at = block(out, tensor, piece, part), number(tensor, offset, part)
        return remote(view, view, relay_send.at[at], core_receive.at[at], (s, other))

    def forward(move, out, tensor):
        def receive(n, carry):
            part = lax.rem(s // each + n, parts)
            for j in range(rows_each):
                for i in range(each):
                    origin = part * each + i
                    group = group_of(s, seq_size)
                    owner = (origin, (group * rows_each + j) // rows_local)
                    target = (t, j, origin) if tensor else (j, origin, t)
                    move.wait_receive(owner, target, j * seq_size + origin)
                    slot = lax.rem(group * rows_each + j, rows_local)

                    @pl.when(same(owner, me))
                    def _():
                        pltpu.make_async_copy(
                            move.source.at[slot, t], move.target.at[target],
                            move.local_sem.at[slot * tp_size + t],
                        ).wait()
            to_core(out, tensor, part).start()
            for offset in range(1, pairs):
                to_pair(out, tensor, offset, part).start()
            return carry

        def relays(n, carry):
            part = lax.rem(s // each + n, parts)
            for offset in range(1, pairs):
                from_pair(out, tensor, offset, part).wait_recv()
                relay(out, tensor, offset, part).start()
            return carry

        lax.fori_loop(0, parts, receive, 0)
        lax.fori_loop(0, parts, relays, 0)

    def arrive(out, tensor):
        def one(part, carry):
            for offset in range(pairs):
                from_core(out, tensor, offset, part).wait_recv()
            return carry

        lax.fori_loop(0, parts, one, 0)

    def finish(move, out, tensor):
        def one(part, carry):
            to_core(out, tensor, part).wait_send()
            for offset in range(1, pairs):
                to_pair(out, tensor, offset, part).wait_send()
                relay(out, tensor, offset, part).wait_send()
            return carry

        lax.fori_loop(0, parts, one, 0)
        for n, (to, source, target, at) in enumerate(move.sends):
            @pl.when(jnp.logical_not(same(to, me)))
            def _():
                remote(
                    move.source.at[source], move.target.at[target],
                    move.send_sem.at[n], move.receive_sem.at[at], to,
                ).wait_send()

    blocks, _, piece, depth = x_rows.shape
    places = tp_size * piece
    width = q_w.shape[0]
    lanes = cos_ref.shape[2]
    output_copy = pltpu.make_async_copy(output_ref, output_out.at[t], output_sem)
    output_copy.start()
    turn = half_turn(width)
    q_turned[...] = plain_dot(turn, q_w[...]).astype(jnp.bfloat16)
    k_turned[...] = plain_dot(turn, k_w[...]).astype(jnp.bfloat16)
    square_ref[...] = jnp.zeros_like(square_ref)

    def tables(n, carry):
        angles = frequency_ref[...] * offset_ref[n]
        cos_ref[n] = jnp.concatenate([jnp.cos(angles)] * (2 * lanes // HD), axis=0).T
        sin_ref[n] = jnp.concatenate([jnp.sin(angles)] * (2 * lanes // HD), axis=0).T
        return carry

    lax.fori_loop(0, blocks, tables, 0)

    def x_load(n):
        source = x_out.at[n // seq_size, lax.rem(n, seq_size)]
        return pltpu.make_async_copy(source, x_rows.at[n], load_sem.at[n])

    def first_load(n):
        source = first_out.at[n // seq_size, lax.rem(n, seq_size)]
        return pltpu.make_async_copy(source, first_rows.at[n], load_sem.at[n])

    def start_loads(load):
        def one(n, carry):
            load(n).start()
            return carry

        lax.fori_loop(0, blocks, one, 0)

    def query_key(n, carry):
        x_load(n).wait()
        x = x_rows[n].reshape(places, depth).astype(jnp.float32)
        inverse = lax.rsqrt(jnp.mean(x * x, axis=-1, keepdims=True) + norm_eps)
        normed = (x * inverse * gain_ref[...]).astype(jnp.bfloat16)
        cosine, sine = widen(cos_ref[n], width), widen(sin_ref[n], width)
        q_ref[n] = (
            (rows_dot(normed, q_w[...]) * cosine + rows_dot(normed, q_turned[...]) * sine)
            * (HD ** (-0.5) * LOG2E)
        ).astype(jnp.bfloat16)
        k_ref[n] = (
            rows_dot(normed, k_w[...]) * cosine + rows_dot(normed, k_turned[...]) * sine
        ).astype(jnp.bfloat16)
        x_rows[n] = normed.reshape(x_rows.shape[1:])
        return carry

    def mix(n, carry):
        first_load(n).wait()
        first = first_rows[n].astype(jnp.float32)
        value = rows_dot(x_rows[n].reshape(places, depth), v_w[...])
        mixed = (0.5 * value + 0.5 * first.T).astype(jnp.bfloat16)
        v_ref[n] = mixed
        wide = mixed.astype(jnp.float32)
        square_ref[0:1, : first.shape[1]] += jnp.sum(first * first, axis=0, keepdims=True)
        square_ref[1:2, : wide.shape[1]] += jnp.sum(wide * wide, axis=0, keepdims=True)
        return carry

    forward(x_move, x_out, 0)
    to_core(output_out, 2, 0).start()
    for offset in range(1, pairs):
        to_pair(output_out, 2, offset, 0).start()
    arrive(x_out, 0)
    start_loads(x_load)
    lax.fori_loop(0, blocks, query_key, 0)
    first_move.wait_sends()
    first_move.wait_receives()
    start_loads(first_load)
    lax.fori_loop(0, blocks, mix, 0)
    for offset in range(1, pairs):
        from_pair(output_out, 2, offset, 0).wait_recv()
        relay(output_out, 2, offset, 0).start()
    forward(cot_move, cot_out, 1)
    arrive(cot_out, 1)
    for offset in range(pairs):
        from_core(output_out, 2, offset, 0).wait_recv()
    to_core(output_out, 2, 0).wait_send()
    for offset in range(1, pairs):
        to_pair(output_out, 2, offset, 0).wait_send()
        relay(output_out, 2, offset, 0).wait_send()
    finish(x_move, x_out, 0)
    finish(cot_move, cot_out, 1)
    output_copy.wait()


def half_turn(width):
    row = lax.broadcasted_iota(jnp.int32, (width, width), 0)
    column = lax.broadcasted_iota(jnp.int32, (width, width), 1)
    low = lax.rem(row, HD) < HD // 2
    minus = low & (column == row + HD // 2)
    plus = jnp.logical_not(low) & (column == row - HD // 2)
    return jnp.where(plus, 1.0, jnp.where(minus, -1.0, 0.0)).astype(jnp.bfloat16)


def spread(
    layer_input, cotangent, first_values, output_weight, query_weight, key_weight, value_weight,
    offsets, frequency, gain, sizes,
):
    seq_size, tp_size, rows_each, rows_local, parts = sizes
    pieces = layer_input.shape[2:]
    width, depth = query_weight.shape
    features, places = first_values.shape[1:]
    blocks = rows_each * seq_size
    lanes = min(width, 128)
    plans = (
        owner_to_quarter(seq_size, tp_size, rows_each, rows_local, False),
        owner_to_quarter(seq_size, tp_size, rows_each, rows_local, True),
        places_to_rows(seq_size, rows_each),
    )
    dma = pltpu.SemaphoreType.DMA
    quarter = [
        dma((rows_local * tp_size,)), dma((rows_local * tp_size,)), dma((rows_each * seq_size,)),
    ]
    stage = tp_size // 2 * parts * 3
    bf16, f32 = jnp.bfloat16, jnp.float32
    anywhere = pl.BlockSpec(memory_space=pl.ANY)
    vmem = pl.BlockSpec(memory_space=pltpu.VMEM)
    part = jax.ShapeDtypeStruct((blocks, places, width), bf16)
    table = jax.ShapeDtypeStruct((blocks, places, lanes), f32)
    return pl.pallas_call(
        functools.partial(spread_kernel, plans, sizes),
        out_shape=[
            jax.ShapeDtypeStruct((rows_each, seq_size, tp_size) + pieces, bf16),
            jax.ShapeDtypeStruct((tp_size, rows_each, seq_size) + pieces, bf16),
            jax.ShapeDtypeStruct((rows_each, seq_size, features, places), bf16),
            jax.ShapeDtypeStruct((tp_size,) + output_weight.shape, bf16),
            part,
            part,
            part,
            table,
            table,
            jax.ShapeDtypeStruct((8, max(width, places)), f32),
        ],
        in_specs=[anywhere] * 3 + [vmem] * 7,
        out_specs=[anywhere] * 4 + [vmem] * 6,
        scratch_shapes=[
            pltpu.VMEM((blocks, tp_size) + pieces, bf16),
            pltpu.VMEM((blocks, features, places), bf16),
            pltpu.VMEM((width, depth), bf16),
            pltpu.VMEM((width, depth), bf16),
        ]
        + quarter
        + quarter
        + [dma((seq_size,))] * 3
        + [dma((stage,))] * 5
        + [dma((blocks,)), dma],
        compiler_params=pltpu.CompilerParams(
            collective_id=5, has_side_effects=True, vmem_limit_bytes=67043328
        ),
        name="spread",
    )(
        layer_input, cotangent, first_values, output_weight, query_weight, key_weight,
        value_weight, offsets, frequency, gain,
    )


def widen(table, width):
    return jnp.concatenate([table] * (width // table.shape[1]), axis=1)


class Reduce:
    def __init__(self, place, full, core_in, pair_in, chunks, sems):
        self.seq, self.tp, self.pairs = place
        self.pair, self.core = self.tp // 2, lax.rem(self.tp, 2)
        self.other = self.pair * 2 + 1 - self.core
        self.full, self.core_in, self.pair_in = full, core_in, pair_in
        self.chunks = chunks
        self.core_send, self.core_recv, self.pair_send, self.pair_recv = sems

    def peer(self, offset):
        return lax.rem(self.pair + offset, self.pairs) * 2 + self.core

    def cut(self, ref, lead, c):
        return ref.at[lead, :, c]

    def to_core(self, offset, c):
        lead = lax.rem(self.pair + offset, self.pairs) * 2 + 1 - self.core
        at = offset * self.chunks + c
        return remote(
            self.cut(self.full, lead, c), self.cut(self.core_in, offset, c),
            self.core_send.at[at], self.core_recv.at[at], (self.seq, self.other),
        )

    def to_pair(self, offset, c):
        back = self.pairs - offset
        return remote(
            self.cut(self.full, self.peer(offset), c), self.cut(self.pair_in, back - 1, c),
            self.pair_send.at[offset * self.chunks + c],
            self.pair_recv.at[back * self.chunks + c], (self.seq, self.peer(offset)),
        )

    def from_pair(self, offset, c):
        view, at = self.cut(self.pair_in, offset - 1, c), offset * self.chunks + c
        return remote(
            view, view, self.pair_send.at[at], self.pair_recv.at[at], (self.seq, self.peer(offset))
        )

    def start(self, c):
        for offset in list(range(1, self.pairs)) + [0]:
            self.to_core(offset, c).start()

    def pass_on(self, c):
        for offset in range(1, self.pairs):
            self.to_core(offset, c).wait_recv()
            to = self.peer(offset)

            def add(b, carry):
                self.full[to, b, c] = (
                    self.full[to, b, c].astype(jnp.float32)
                    + self.core_in[offset, b, c].astype(jnp.float32)
                ).astype(jnp.bfloat16)
                return carry

            lax.fori_loop(0, self.full.shape[1], add, 0)
            self.to_pair(offset, c).start()

    def arrive(self, c):
        self.to_core(0, c).wait_recv()
        for offset in range(1, self.pairs):
            self.from_pair(offset, c).wait_recv()

    def total(self, b, c):
        value = self.full[self.tp, b, c].astype(jnp.float32)
        value = value + self.core_in[0, b, c].astype(jnp.float32)
        for offset in range(1, self.pairs):
            value = value + self.pair_in[offset - 1, b, c].astype(jnp.float32)
        return value

    def finish(self):
        for c in range(self.chunks):
            for offset in range(self.pairs):
                self.to_core(offset, c).wait_send()
            for offset in range(1, self.pairs):
                self.to_pair(offset, c).wait_send()


class SeqSum:
    def __init__(self, place, steps, done, blocks, held, mine, sums, local_sem, send_sem, recv_sem):
        self.seq, self.tp = place
        self.count, self.done, self.size = steps, done, 1 << steps
        self.blocks, self.held, self.mine, self.sums = blocks, held, mine, sums
        self.local_sem, self.send_sem, self.recv_sem = local_sem, send_sem, recv_sem
        self.flags = [lax.rem(self.seq // (1 << n), 2) for n in range(steps)]
        low, self.lows = 0, [0]
        for n in range(steps):
            low = low + self.flags[n] * (self.size >> (n + 1))
            self.lows.append(low)

    def partner(self, n):
        return (self.seq + (1 - 2 * self.flags[n]) * (1 << n), self.tp)

    def half(self, n):
        return self.size >> (n + 1)

    def begin(self, n):
        return (self.size >> self.done) - (self.size >> n)

    def give(self, n):
        half = self.half(n)
        low = self.lows[n] - self.lows[self.done] + (1 - self.flags[n]) * half
        return remote(
            self.blocks.at[pl.ds(low, half)], self.held.at[pl.ds(self.begin(n), half)],
            self.send_sem.at[n], self.recv_sem.at[n], self.partner(n),
        )

    def take(self, n):
        copy = self.give(n)
        copy.wait_recv()
        copy.wait_send()
        last = n + 1 == self.count

        def add(b, carry):
            at = self.lows[n + 1] - self.lows[self.done] + b
            value = (
                self.blocks[at].astype(jnp.float32)
                + self.held[self.begin(n) + b].astype(jnp.float32)
            ).astype(jnp.bfloat16)
            if last:
                self.mine[b] = value
            else:
                self.blocks[at] = value
            return carry

        lax.fori_loop(0, self.half(n), add, 0)

    def store(self):
        return pltpu.make_async_copy(
            self.mine, self.sums.at[pl.ds(self.lows[self.count], 1)], self.local_sem
        )

    def spread(self, n):
        target = self.sums.at[pl.ds(self.lows[n + 1], self.half(n))]
        source = self.mine if n + 1 == self.count else target
        at = self.count + n
        return remote(source, target, self.send_sem.at[at], self.recv_sem.at[at], self.partner(n))

    def collect(self, n):
        half = self.half(n)
        view = self.sums.at[pl.ds(self.lows[n] + (1 - self.flags[n]) * half, half)]
        at = self.count + n
        remote(view, view, self.send_sem.at[at], self.recv_sem.at[at], self.partner(n)).wait_recv()

    def steps(self):
        self.give(self.done).start()
        yield
        for n in range(self.done, self.count):
            self.take(n)
            if n + 1 < self.count:
                self.give(n + 1).start()
            else:
                self.spread(n).start()
                self.store().start()
            yield
        for n in range(self.count - 1, -1, -1):
            self.collect(n)
            if n + 1 == self.count:
                self.store().wait()
            if n > 0:
                self.spread(n - 1).start()
            yield
        for n in range(self.count):
            self.spread(n).wait_send()


def tail_kernel(
    sizes, dv_plan, out_own_hbm, out_got_hbm, keep_hbm, got_hbm, x_hbm, q_hbm, k_hbm, v_hbm, cos_hbm, sin_hbm,
    qw_hbm, kw_hbm, vw_hbm, attended_hbm, source_hbm, middle_hbm, middle_g_hbm, dv_hbm, gain_ref, small_ref,
    out_ref, input_g_ref, first_g_ref, sums_ref, feed_ref, gain_g_ref, feed_gain_g_ref, norms_ref,
    x_rows, q_rows, k_rows, v_rows, cos_rows, sin_rows, weights, attended, grad_acc,
    normed_full, normed_core, normed_pair, proj_full, proj_core, proj_pair,
    out_own, out_got, source, middle, middle_g, input_g, result,
    blocks, held, mine, feed_blocks, feed_got, feed_held, feed_mine,
    small, tp_held, tp_sum, seq_held, dv_rows, dv_cols,
    *sems,
):
    seq_size, tp_size, rows_each, rows_local, _ = sizes
    s, t = lax.axis_index("seq"), lax.axis_index("tp")
    me = (s, t)
    pairs = tp_size // 2
    count = seq_size.bit_length() - 1
    normed_sems, proj_sems = sems[:4], sems[4:8]
    dv_sems, back_sems, lo_sems = sems[8:11], sems[11:14], sems[14:17]
    load_sem, x_sem, feed_sem, store_sem, grad_send, grad_recv = sems[17:23]
    feed_send, feed_recv, small_send, tp_sem, seq_sem, first_sem = sems[23:]
    place = (s, t, pairs)
    normed = Reduce(place, normed_full, normed_core, normed_pair, 2, normed_sems)
    proj = Reduce(place, proj_full, proj_core, proj_pair, 1, proj_sems)
    dv_move = Exchange(dv_plan, me, dv_hbm, dv_rows, *dv_sems)
    half = source.shape[0]
    places, depth = x_rows.shape[1:]
    width = q_rows.shape[2]

    group = group_of(s, seq_size)
    origins = []
    for slot in range(rows_local):
        row = t * rows_local + slot
        for i in range(tp_size):
            origins.append(((place_of(row // rows_each, seq_size), i), slot, i))

    tp_peers = [lax.rem(t + i, tp_size) for i in range(1, tp_size)]
    seq_peers = [lax.rem(s + i, seq_size) for i in range(1, seq_size)]

    names = (
        (q_hbm, q_rows), (k_hbm, k_rows), (v_hbm, v_rows), (cos_hbm, cos_rows),
        (sin_hbm, sin_rows), (qw_hbm, weights.at[pl.ds(0, width)]),
        (kw_hbm, weights.at[pl.ds(width, width)]), (vw_hbm, weights.at[pl.ds(2 * width, width)]),
        (out_own_hbm, out_own), (attended_hbm, attended),
        (middle_g_hbm, middle_g), (source_hbm, source), (middle_hbm, middle),
        (out_got_hbm, out_got),
    )
    loads = [
        pltpu.make_async_copy(origin, target, load_sem.at[n])
        for n, (origin, target) in enumerate(names)
    ]
    feed_loads = [
        (
            pltpu.make_async_copy(keep_hbm.at[n], feed_blocks.at[n], feed_sem.at[2 * n]),
            pltpu.make_async_copy(got_hbm.at[n], feed_got.at[n], feed_sem.at[2 * n + 1]),
        )
        for n in range(3)
    ]

    def x_load(n):
        return pltpu.make_async_copy(x_hbm.at[n], x_rows.at[n], x_sem.at[n])

    def ordered(n):
        return 2 * lax.rem(n, half) + n // half

    for pair in feed_loads:
        for copy in pair:
            copy.start()
    for n in (9, 10, 12, 8, 13):
        loads[n].start()
    for copy in loads[:8]:
        copy.start()
    for n in range(2 * half):
        x_load(ordered(n)).start()
    loads[11].start()

    barrier = pltpu.get_barrier_semaphore()
    dv_move.greet(barrier)
    for origin, _, _ in origins:
        @pl.when(jnp.logical_not(same(origin, me)))
        def _():
            pl.semaphore_signal(barrier, inc=1, device_id=origin, device_id_type=MESH)
    for to in tp_peers:
        pl.semaphore_signal(barrier, inc=1, device_id=(s, to), device_id_type=MESH)
    for to in seq_peers:
        pl.semaphore_signal(barrier, inc=1, device_id=(to, t), device_id_type=MESH)
    back_others = sum(
        jnp.where(same((to, (group * rows_each + j) // rows_local), me), 0, 1)
        for j in range(rows_each)
        for to in range(seq_size)
    )
    pl.semaphore_wait(barrier, dv_move.others() + back_others + tp_size + seq_size - 2)

    def seq_sum(n, done, *refs):
        return SeqSum(
            me, count, done, *refs, store_sem.at[n],
            (grad_send if done == 0 else feed_send).at[n if done == 0 else n - 2],
            (grad_recv if done == 0 else feed_recv).at[n if done == 0 else n - 2],
        ).steps()

    sums = [
        seq_sum(n, 0, blocks.at[n], held.at[n], mine.at[n], sums_ref.at[n]) for n in range(2)
    ]
    feeds = [
        seq_sum(
            n + 2, 1, feed_blocks.at[n], feed_held.at[n], feed_mine.at[n], feed_ref.at[n]
        )
        for n in range(3)
    ]

    for n in range(3):
        for copy in feed_loads[n]:
            copy.wait()

        def join(b, carry):
            feed_blocks[n, b] = (
                feed_blocks[n, b].astype(jnp.float32) + feed_got[n, b].astype(jnp.float32)
            ).astype(jnp.bfloat16)
            return carry

        lax.fori_loop(0, feed_blocks.shape[1], join, 0)
        next(feeds[n])
    def own_part(target, slot, i):
        piece = source.shape[2]
        return target.at[slot, pl.ds(pl.multiple_of(i * piece, piece), piece)]

    def send_back(source_ref, target, trio, b, c, wait):
        local_sem, send_sem, recv_sem = trio
        flat = 2 * b + c
        j, to = flat // seq_size, lax.rem(flat, seq_size)
        row = group * rows_each + j
        slot = lax.rem(row, rows_local)
        place = (to, row // rows_local)
        here = same(place, me)
        view = own_part(target, slot, t)

        @pl.when(here)
        def _():
            copy = pltpu.make_async_copy(source_ref.at[b, c], view, local_sem.at[flat])
            copy.wait() if wait else copy.start()

        @pl.when(jnp.logical_not(here))
        def _():
            copy = remote(
                source_ref.at[b, c], view, send_sem.at[flat], recv_sem.at[slot * tp_size + t], place
            )
            copy.wait_send() if wait else copy.start()

    def forward(c):
        def one(n, carry):
            b = lax.rem(n + s // 2, half)
            value = middle[b, c] + out_own[b, c].astype(jnp.float32)
            for offset in range(1, pairs):
                value = value + out_got[offset - 1, b, c].astype(jnp.float32)
            result[b, c] = value.astype(jnp.bfloat16)
            send_back(result, out_ref, lo_sems, b, c, False)
            return carry

        lax.fori_loop(0, half, one, 0)

    fine = blocks.shape[2]
    loads[9].wait()
    loads[10].wait()
    branch = middle_g[...].reshape(2 * half * middle_g.shape[2], depth).astype(jnp.bfloat16)
    for i in range(tp_size):
        product = columns_dot(attended[i], branch)
        for n in range(seq_size // 2):
            proj_full[i, n, 0] = product[n * fine : (n + 1) * fine].astype(jnp.bfloat16)
    proj.start(0)
    for n in (8, 12, 13):
        loads[n].wait()
    forward(0)
    forward(1)
    dv_move.start()
    for copy in loads[:8]:
        copy.wait()
    turn = half_turn(width)
    grad_acc[...] = jnp.zeros_like(grad_acc)
    gain = gain_ref[...]

    def project_back(first, last):
        def one(n, carry):
            at = ordered(n)
            x_load(at).wait()
            x = x_rows[at].astype(jnp.float32)
            inverse = lax.rsqrt(jnp.mean(x * x, axis=-1, keepdims=True) + norm_eps)
            rows = (x * inverse * gain).astype(jnp.bfloat16)
            cosine, sine = widen(cos_rows[at], width), widen(sin_rows[at], width)

            def unrotate(grad):
                turned = plain_dot(grad, turn)
                return (grad.astype(jnp.float32) * cosine + turned * sine).astype(jnp.bfloat16)

            stacked = jnp.concatenate(
                [
                    unrotate(q_rows[at]),
                    unrotate(k_rows[at]),
                    (0.5 * v_rows[at].astype(jnp.float32)).astype(jnp.bfloat16),
                ],
                axis=1,
            )
            b, c = at // 2, lax.rem(at, 2)
            product = plain_dot(stacked, weights[...])
            for i in range(tp_size):
                piece = places // tp_size
                normed_full[i, b, c] = product[i * piece : (i + 1) * piece].astype(jnp.bfloat16)
            grad_acc[...] += columns_dot(stacked, rows)
            return carry

        lax.fori_loop(first, last, one, 0)

    quarter = half // 2
    project_back(0, quarter)
    proj.pass_on(0)
    next(feeds[0])
    project_back(quarter, half)
    normed.start(0)
    next(feeds[1])
    project_back(half, half + quarter)
    normed.pass_on(0)
    next(feeds[2])
    next(feeds[0])
    project_back(half + quarter, 2 * half)
    normed.start(1)
    for n in range(3 * seq_size // 2):
        blocks[n // seq_size, n % seq_size] = grad_acc[n * fine : (n + 1) * fine].astype(
            jnp.bfloat16
        )
    next(sums[0])
    proj.arrive(0)

    def put(b, carry):
        blocks[1, seq_size // 2 + b] = proj.total(b, 0).astype(jnp.bfloat16)
        return carry

    lax.fori_loop(0, seq_size // 2, put, 0)
    next(sums[1])
    normed.pass_on(1)
    next(feeds[1])
    next(feeds[0])
    next(feeds[2])

    small[...] = small_ref[...]

    def back(c):
        normed.arrive(c)

        def one(n, carry):
            b = lax.rem(n + s // 2, half)
            grads = normed.total(b, c)
            x = source[b, c].astype(jnp.float32)
            inverse = lax.rsqrt(jnp.mean(x * x, axis=-1, keepdims=True) + norm_eps)
            unit = x * inverse
            scaled = grads * gain
            extra = inverse * (scaled - unit * jnp.mean(scaled * unit, axis=-1, keepdims=True))
            input_g[b, c] = (middle_g[b, c] + extra).astype(jnp.bfloat16)
            small[0:1, :] += jnp.sum(grads * unit, axis=0, keepdims=True)
            send_back(input_g, input_g_ref, back_sems, b, c, False)
            return carry

        lax.fori_loop(0, half, one, 0)

    def tp_copy(n):
        return remote(
            small, tp_held.at[tp_size - n], small_send.at[n],
            tp_sem.at[tp_size - n], (s, tp_peers[n - 1]),
        )

    def seq_copy(n):
        return remote(
            tp_sum, seq_held.at[seq_size - n], small_send.at[tp_size + n],
            seq_sem.at[seq_size - n], (seq_peers[n - 1], t),
        )

    def all_steps(generators):
        for generator in generators:
            next(generator, None)

    next(feeds[1])
    next(feeds[0])
    next(sums[0])
    next(feeds[2])
    next(sums[1])
    loads[11].wait()
    back(0)
    next(feeds[1])
    next(sums[0])
    back(1)
    for n in range(1, tp_size):
        tp_copy(n).start()
    all_steps([sums[1], feeds[2], sums[0]])
    for n in range(1, tp_size):
        tp_copy(n).wait()
    tp_held[0] = small[...]
    total = tp_held[lax.rem(tp_size - t, tp_size)]
    for n in range(1, tp_size):
        total = total + tp_held[lax.rem(n + tp_size - t, tp_size)]
    tp_sum[...] = total
    for n in range(1, seq_size):
        seq_copy(n).start()
    seq_held[0] = total
    dv_move.wait_sends()
    dv_move.wait_receives()

    def first_back(n, carry):
        dv_cols[n] = (0.5 * dv_rows[n].astype(jnp.float32)).T
        return carry

    lax.fori_loop(0, dv_rows.shape[0], first_back, 0)
    first_store = pltpu.make_async_copy(dv_cols, first_g_ref, first_sem)
    first_store.start()
    for _ in range(2 * count):
        all_steps([sums[1], sums[0], feeds[0], feeds[1], feeds[2]])
    for generator in sums + feeds:
        for _ in generator:
            pass
    for n in range(1, seq_size):
        seq_copy(n).wait()
    total = seq_held[lax.rem(seq_size - s, seq_size)]
    for n in range(1, seq_size):
        total = total + seq_held[lax.rem(n + seq_size - s, seq_size)]
    gain_g_ref[...] = total[0:1]
    feed_gain_g_ref[...] = total[1:2]
    norms_ref[...] = jnp.sqrt(total[2:3, :2])

    for reduce in (normed, proj):
        reduce.finish()
    for c in range(2):
        def done(b, carry):
            send_back(input_g, input_g_ref, back_sems, b, c, True)
            send_back(result, out_ref, lo_sems, b, c, True)
            return carry

        lax.fori_loop(0, half, done, 0)
    first_store.wait()
    for origin, slot, i in origins:
        @pl.when(jnp.logical_not(same(origin, me)))
        def _():
            for ref, trio in ((input_g_ref, back_sems), (out_ref, lo_sems)):
                view = own_part(ref, slot, i)
                at = slot * tp_size + i
                remote(view, view, trio[1].at[0], trio[2].at[at], origin).wait_recv()


def tail(
    out_own, out_got, keep, got, x_rows, query_g, key_g, value_g, cosine, sine, query_weight, key_weight, value_weight,
    attended, source, middle, middle_g, gain, small, sizes,
):
    seq_size, tp_size, rows_each, rows_local, _ = sizes
    pairs = tp_size // 2
    blocks = rows_each * seq_size
    tokens, depth = source.shape
    piece = tokens // blocks
    width = query_g.shape[-1]
    places = x_rows.shape[0] // blocks
    lanes = cosine.shape[2]
    fine = 2 * width // seq_size
    bf16, f32 = jnp.bfloat16, jnp.float32
    shape = (blocks // 2, 2, piece, depth)
    proj_shape = (width // fine, 1, fine, depth)
    hidden = 2 * keep.shape[1] // seq_size
    feed_shape = (3, seq_size // 2, hidden, depth)
    anywhere = pl.BlockSpec(memory_space=pl.ANY)
    vmem = pl.BlockSpec(memory_space=pltpu.VMEM)
    dma = pltpu.SemaphoreType.DMA
    plan = rows_to_places(seq_size, rows_each)
    steps = seq_size.bit_length() - 1
    owned = jax.ShapeDtypeStruct((rows_local, tp_size * piece, depth), bf16)

    def reduce_shapes(part):
        return [
            pltpu.VMEM((tp_size,) + part, bf16),
            pltpu.VMEM((pairs,) + part, bf16),
            pltpu.VMEM((pairs - 1,) + part, bf16),
        ]

    def reduce_sems(chunks):
        return [dma((pairs * chunks,))] * 4

    return pl.pallas_call(
        functools.partial(tail_kernel, sizes, plan),
        out_shape=[
            owned,
            owned,
            jax.ShapeDtypeStruct((blocks, width, places), f32),
            jax.ShapeDtypeStruct((2, seq_size, fine, depth), bf16),
            jax.ShapeDtypeStruct((3, seq_size, hidden, depth), bf16),
            jax.ShapeDtypeStruct((1, depth), f32),
            jax.ShapeDtypeStruct((1, depth), f32),
            jax.ShapeDtypeStruct((1, 2), f32),
        ],
        in_specs=[anywhere] * 18 + [vmem] * 2,
        out_specs=[anywhere] * 5 + [vmem] * 3,
        scratch_shapes=[
            pltpu.VMEM((blocks, places, depth), bf16),
            pltpu.VMEM((blocks, places, width), bf16),
            pltpu.VMEM((blocks, places, width), bf16),
            pltpu.VMEM((blocks, places, width), bf16),
            pltpu.VMEM((blocks, places, lanes), f32),
            pltpu.VMEM((blocks, places, lanes), f32),
            pltpu.VMEM((3 * width, depth), bf16),
            pltpu.VMEM(attended.shape, bf16),
            pltpu.VMEM((3 * width, depth), f32),
        ]
        + reduce_shapes(shape)
        + reduce_shapes(proj_shape)
        + [
            pltpu.VMEM(shape, bf16),
            pltpu.VMEM((pairs - 1,) + shape, bf16),
            pltpu.VMEM(shape, bf16),
            pltpu.VMEM(shape, f32),
            pltpu.VMEM(shape, f32),
            pltpu.VMEM(shape, bf16),
            pltpu.VMEM(shape, bf16),
            pltpu.VMEM((2, seq_size, fine, depth), bf16),
            pltpu.VMEM((2, seq_size, fine, depth), bf16),
            pltpu.VMEM((2, 1, fine, depth), bf16),
            pltpu.VMEM(feed_shape, bf16),
            pltpu.VMEM(feed_shape, bf16),
            pltpu.VMEM(feed_shape, bf16),
            pltpu.VMEM((3, 1, hidden, depth), bf16),
            pltpu.VMEM(small.shape, f32),
            pltpu.VMEM((tp_size,) + small.shape, f32),
            pltpu.VMEM(small.shape, f32),
            pltpu.VMEM((seq_size,) + small.shape, f32),
            pltpu.VMEM((blocks, places, width), bf16),
            pltpu.VMEM((blocks, width, places), f32),
        ]
        + reduce_sems(2)
        + reduce_sems(1)
        + [dma((seq_size,))] * 3
        + ([dma((blocks,))] * 2 + [dma((rows_local * tp_size,))]) * 2
        + [
            dma((14,)),
            dma((blocks,)),
            dma((6,)),
            dma((5,)),
            dma((2, 2 * steps)),
            dma((2, 2 * steps)),
            dma((3, 2 * steps)),
            dma((3, 2 * steps)),
            dma((tp_size + seq_size,)),
            dma((tp_size,)),
            dma((seq_size,)),
            dma,
        ],
        compiler_params=pltpu.CompilerParams(
            collective_id=6, has_side_effects=True, vmem_limit_bytes=67043328
        ),
        name="tail",
    )(
        out_own.reshape(shape),
        out_got.reshape((pairs - 1,) + shape),
        keep.reshape(feed_shape),
        got.reshape(feed_shape),
        x_rows.reshape(blocks, places, depth),
        query_g.reshape(blocks, places, width),
        key_g.reshape(blocks, places, width),
        value_g.reshape(blocks, places, width),
        cosine,
        sine,
        query_weight,
        key_weight,
        value_weight,
        attended,
        source.reshape(shape),
        middle.reshape(shape),
        middle_g.reshape(shape),
        value_g.reshape(rows_each, seq_size, places, width),
        gain,
        small,
    )


def shards(
    layer_input,
    first_values,
    doc_lengths,
    attn_gain,
    query_weight,
    key_weight,
    value_weight,
    output_weight,
    feed_gain,
    gate_weight,
    up_weight,
    down_weight,
    out_cotangent,
):
    seq_size = lax.axis_size("seq")
    tp_size = lax.axis_size("tp")
    rows_local, local_len, depth = layer_input.shape
    row_count = first_values.shape[0]
    width = query_weight.shape[0]
    rows_each = row_count // seq_size
    piece = local_len // tp_size
    tokens = rows_each * seq_size * piece
    sizes = (seq_size, tp_size, rows_each, rows_local, 4)
    me = lax.axis_index("tp")
    my_rows = group_of(lax.axis_index("seq"), seq_size) * rows_each

    _, offsets = doc_layout(doc_lengths)
    offsets = lax.dynamic_slice_in_dim(offsets, my_rows, rows_each, 0)
    starts = jnp.arange(ROW, dtype=jnp.int32)[None, :] - offsets
    low = (starts[:, ::BLOCK] // BLOCK).reshape(-1)
    starts = starts[:, None, :]
    half_dim = HD // 2
    frequency = rope_base ** (-jnp.arange(half_dim, dtype=jnp.float32) * 2.0 / HD)
    attn_scale = attn_gain.astype(jnp.float32)[None, :]
    feed_scale = feed_gain.astype(jnp.float32)[None, :]
    (
        x_rows, cot_all, _, output_full, queries, keys, values, cosine, sine, squares,
    ) = spread(
        layer_input.reshape(rows_local, tp_size, piece, depth),
        out_cotangent.reshape(rows_local, tp_size, piece, depth),
        first_values,
        output_weight,
        query_weight,
        key_weight,
        value_weight,
        offsets.astype(jnp.float32).reshape(rows_each * seq_size, 1, local_len),
        frequency[:, None],
        attn_scale,
        sizes,
    )
    output_full = output_full.reshape(tp_size * width, depth)
    source_low = lax.dynamic_index_in_dim(x_rows, me, 2, keepdims=False).reshape(tokens, depth)
    source = source_low.astype(jnp.float32)
    x_rows = x_rows.reshape(rows_each * ROW, depth)
    queries, keys, values = (
        part.reshape(rows_each, ROW, width) for part in (queries, keys, values)
    )
    result, logsum = attend(low, queries, keys, values, starts)
    by_piece = (rows_each, seq_size, tp_size, piece, width)
    by_head = (tp_size, rows_each, seq_size, piece, width)
    (pieces,) = exchange([result.reshape(by_piece)], [by_head], [heads_to_tokens(tp_size)], 1)
    attended = jnp.transpose(pieces.reshape(tp_size, tokens, width), (1, 0, 2)).reshape(tokens, -1)
    middle = source + jnp.dot(attended, output_full, preferred_element_type=jnp.float32)
    unit_feed, inv_feed = norm_rows(middle)
    feed_in = (unit_feed * feed_scale).astype(jnp.bfloat16)
    feed_in_g, out_own, out_give, cotangent, keep, give = feed_forward(
        feed_in, cot_all.reshape(tp_size, tokens, depth), gate_weight.T, up_weight.T, down_weight
    )
    got = lax.ppermute(give, "seq", [(n, n + 1 - 2 * (n % 2)) for n in range(seq_size)])
    middle_extra, feed_gain_part = norm_back(feed_in_g, unit_feed, inv_feed, feed_scale)
    middle_g = cotangent.astype(jnp.float32) + middle_extra
    branch_g = middle_g.astype(jnp.bfloat16)
    attended_g = jnp.einsum(
        "td,ed->te", branch_g, output_full, preferred_element_type=jnp.float32
    ).astype(jnp.bfloat16)
    (attended_g,) = exchange(
        [jnp.transpose(attended_g.reshape(tokens, tp_size, width), (1, 0, 2)).reshape(by_head)],
        [by_piece],
        [tokens_to_heads(tp_size)],
        2,
    )
    out_give, attended_g = lax.optimization_barrier((out_give, attended_g))
    pairs = tp_size // 2
    out_got = jnp.concatenate(
        [
            lax.ppermute(
                out_give[k - 1 : k], "tp",
                [(n, (n + 2 * k) % tp_size) for n in range(tp_size)],
            )
            for k in range(1, pairs)
        ]
    )
    query_g, key_g, value_g = attend_back(
        low, queries, keys, values, result, attended_g.reshape(result.shape), logsum, starts
    )
    squares = jnp.pad(jnp.sum(squares, axis=1)[:2], (0, depth - 2))
    small = jnp.stack([jnp.zeros_like(squares), feed_gain_part, squares])
    (
        layer_output, input_grad, first_grad, grad_sums, feed_sums,
        gain_grad, feed_gain_grad, norms,
    ) = tail(
        out_own,
        out_got,
        keep,
        got,
        x_rows,
        query_g,
        key_g,
        value_g,
        cosine,
        sine,
        query_weight,
        key_weight,
        value_weight,
        pieces.reshape(tp_size, tokens, width),
        source_low,
        middle,
        middle_g,
        attn_scale,
        jnp.pad(small, ((0, 5), (0, 0))),
        sizes,
    )
    grad_sums = grad_sums.reshape(4, width, depth)
    projections = [grad_sums[n].astype(jnp.float32) for n in range(4)]
    feed_sums = feed_sums.reshape(3, -1, depth).astype(jnp.float32)
    return (
        layer_output,
        input_grad,
        first_grad,
        gain_grad.reshape(depth),
        *projections,
        feed_gain_grad.reshape(depth),
        feed_sums[0].T,
        feed_sums[1].T,
        feed_sums[2],
        norms.reshape(2),
    )


def solution(mesh):
    placed = (
        P("tp", "seq", None),
        P(None, "tp", "seq"),
        P(),
        P(),
        P("tp", None),
        P("tp", None),
        P("tp", None),
        P("tp", None),
        P(),
        P(None, "tp"),
        P(None, "tp"),
        P("tp", None),
        P("tp", "seq", None),
    )
    return jax.shard_map(
        shards,
        mesh=mesh,
        in_specs=placed,
        out_specs=(
            P("tp", "seq", None),
            P("tp", "seq", None),
            P(None, "tp", "seq"),
            P(),
            P("tp", None),
            P("tp", None),
            P("tp", None),
            P("tp", None),
            P(),
            P(None, "tp"),
            P(None, "tp"),
            P("tp", None),
            P(),
        ),
        check_vma=False,
    )
```
